32 devices in a mesh: nodes: 16 (over z, y, x), shard: 2 (over core).
Axes of the slice: x: 2, y: 2, z: 4, core: 2. Of those that a mesh axis runs over, the one named last changes fastest.
Arguments:
- grid_inputs: bfloat16 [32768, 474], P(('nodes', 'shard')), may hold values from -6 to 6
- mesh_static: bfloat16 [32768, 512], P(('nodes', 'shard')), may hold values from -6 to 6
- targets: float32 [32768, 227], P(('nodes', 'shard')), may hold values from -6 to 6
- area_weight: float32 [32768], P(('nodes', 'shard')), may hold values from 0.1 to 1
- valid_rows: int32 [32], P(('nodes', 'shard')), may hold values from 512 to 1024, as said below
- encoder_lists: int32 [32768, 4], P(('nodes', 'shard')), may hold values from 0 to 3071
- mesh_lists: int32 [32768, 4], P(('nodes', 'shard')), may hold values from 0 to 3071
- decoder_lists: int32 [32768, 4], P(('nodes', 'shard')), may hold values from 0 to 3071
- step_count: int32 [1], replicated, may hold values from 1 to 20
- w_in: float32 [474, 512], P(None, ('nodes', 'shard')), may hold values from -0.25 to 0.25
- moment_in: float32 [474, 512], P(None, ('nodes', 'shard')), may hold values from -0.00036621094 to 0.00036621094
- square_in: float32 [474, 512], P(None, ('nodes', 'shard')), may hold values from 5.922408e-10 to 2.3689632e-09
- w_layers: float32 [4, 6, 512, 512], P(None, None, ('nodes', 'shard')), may hold values from -0.25 to 0.25
- moment_layers: float32 [4, 6, 512, 512], P(None, None, ('nodes', 'shard')), may hold values from -0.00036621094 to 0.00036621094
- square_layers: float32 [4, 6, 512, 512], P(None, None, ('nodes', 'shard')), may hold values from 5.922408e-10 to 2.3689632e-09
- norm_gains: float32 [4, 2, 512], P(None, None, ('nodes', 'shard')), may hold values from 0.5 to 1.5
- moment_gains: float32 [4, 2, 512], P(None, None, ('nodes', 'shard')), may hold values from -0.015625 to 0.015625
- square_gains: float32 [4, 2, 512], P(None, None, ('nodes', 'shard')), may hold values from 9.536743e-07 to 3.8146973e-06
- w_out: float32 [512, 227], P(('nodes', 'shard')), may hold values from -0.25 to 0.25
- moment_out: float32 [512, 227], P(('nodes', 'shard')), may hold values from -0.00036621094 to 0.00036621094
- square_out: float32 [512, 227], P(('nodes', 'shard')), may hold values from 5.922408e-10 to 2.3689632e-09
Outputs:
- loss_value: float32 [], replicated
- new_moment_in: float32 [474, 512], P(None, ('nodes', 'shard'))
- new_square_in: float32 [474, 512], P(None, ('nodes', 'shard'))
- new_w_in: float32 [474, 512], P(None, ('nodes', 'shard'))
- new_moment_layers: float32 [4, 6, 512, 512], P(None, None, ('nodes', 'shard'))
- new_square_layers: float32 [4, 6, 512, 512], P(None, None, ('nodes', 'shard'))
- new_w_layers: float32 [4, 6, 512, 512], P(None, None, ('nodes', 'shard'))
- new_moment_gains: float32 [4, 2, 512], P(None, None, ('nodes', 'shard'))
- new_square_gains: float32 [4, 2, 512], P(None, None, ('nodes', 'shard'))
- new_gains: float32 [4, 2, 512], P(None, None, ('nodes', 'shard'))
- new_moment_out: float32 [512, 227], P(('nodes', 'shard'))
- new_square_out: float32 [512, 227], P(('nodes', 'shard'))
- new_w_out: float32 [512, 227], P(('nodes', 'shard'))
The draws below stay inside these ranges and needn't reach their ends.
Inputs may be any that keep to these rules, and one draw needn't show every extreme that they name: `encoder_lists`: entry e names row e mod 1024 of block (p - 1 + e // 1024) mod 32 for a row of block p. `mesh_lists`: entry e names row e mod 1024 of block (p - 1 + e // 1024) mod 32 for a row of block p. `decoder_lists`: entry e names row e mod 1024 of block (p - 1 + e // 1024) mod 32 for a row of block p. `valid_rows`: some block is full and some holds exactly 512 valid cells.
All inputs are finite; a program needn't handle non-finite values.
Results may differ from the reference program's by a relative error of at most 0.0045.
The reference program's roundings to bfloat16 on the way count: a program that leaves them out, or rounds other values in their place, can miss the bound.
Values may be sent and summed in bfloat16 or wider, within the bound.
No kernel may reach another device: no remote copies, remote signals or barrier semaphores. Data moves between devices by JAX's collectives and lax.ppermute only.
A program may use at most 320 MiB of HBM per device.

```python
import math
import jax
import jax.numpy as jnp
from jax import lax

D = 512
OUT = 227
CIN = 474
ND = 1024
K = 4
LAYERS = 4
GRID = 32768


def draw_valid_rows(key, part):
    block_count = GRID // ND
    counts = jax.random.randint(jax.random.fold_in(key, 11), (block_count,), ND // 2, ND + 1)
    full_at = jax.random.randint(jax.random.fold_in(key, 12), (), 0, block_count)
    half_at = (full_at + 1 + jax.random.randint(jax.random.fold_in(key, 13), (), 0, block_count - 1)) % block_count
    return counts.at[full_at].set(ND).at[half_at].set(ND // 2).astype(jnp.int32)


def set_ends(drawn, stream_key, smallest, high):
    spot = [jax.random.randint(jax.random.fold_in(stream_key, axis), (), 0, length) for axis, length in enumerate(drawn.shape)]
    main_axis = drawn.shape.index(max(drawn.shape))
    beside = spot[:main_axis] + [(spot[main_axis] + 1) % drawn.shape[main_axis]] + spot[main_axis + 1:]
    return drawn.at[tuple(spot)].set(smallest).at[tuple(beside)].set(high)


def steps_of(rng, shape, cuts, smallest, high):
    level, own = 1.0, jax.random.fold_in(rng, 6)
    for axis_at, parts in cuts:
        steps = jnp.exp(jax.random.uniform(jax.random.fold_in(own, axis_at), (parts,), jnp.float32, smallest / len(cuts), high / len(cuts)))
        level = level * jnp.repeat(steps, shape[axis_at] // parts).reshape([-1 if axis == axis_at else 1 for axis in range(len(shape))])
    return level


def gaussian(key, dims, deviation, reach, split=(), held_as=jnp.bfloat16):
    level = steps_of(key, dims, split, -0.22, 0.18) if split else 1.0
    array = jax.random.normal(key, dims, jnp.float32) * deviation * level
    return jnp.minimum(jnp.maximum(array, -reach), reach).astype(held_as)


def setup_inputs(seed: int = 0) -> dict:
    key_of = jax.random.split(jax.random.key(seed), 22)
    grid_inputs = gaussian(key_of[0], (GRID, CIN), 1.0, 6.0, ((0, 32),))
    mesh_static = gaussian(key_of[1], (GRID, D), 1.0, 6.0, ((0, 32),))
    targets = gaussian(key_of[2], (GRID, OUT), 1.0, 6.0, ((0, 32),), jnp.float32)
    area_weight = jnp.clip(jnp.exp(math.log(1.0) - 2.3025851 * jax.random.uniform(key_of[3], (GRID,), jnp.float32) ** steps_of(key_of[3], (GRID,), ((0, 32),), -0.2, 0.2)), 0.1, 1.0)
    valid_rows = draw_valid_rows(jax.random.fold_in(key_of[21], 71), 0)
    encoder_lists = set_ends(jax.random.randint(key_of[5], (GRID, K), 0, 3 * ND), jax.random.fold_in(key_of[5], 1), 0, (3 * ND) - 1).astype(jnp.int32)
    mesh_lists = set_ends(jax.random.randint(key_of[6], (GRID, K), 0, 3 * ND), jax.random.fold_in(key_of[6], 1), 0, (3 * ND) - 1).astype(jnp.int32)
    decoder_lists = set_ends(jax.random.randint(key_of[7], (GRID, K), 0, 3 * ND), jax.random.fold_in(key_of[7], 1), 0, (3 * ND) - 1).astype(jnp.int32)
    step_count = jax.random.randint(key_of[8], (1,), 1, 21).astype(jnp.int32)
    w_in = gaussian(key_of[9], (CIN, D), CIN ** -0.5, 0.25, ((1, 32),), jnp.float32)
    moment_in = gaussian(key_of[10], (CIN, D), (1.0 / (OUT * GRID ** 0.5)), 0.00036621094, ((1, 32),), jnp.float32)
    square_in = jnp.clip(jnp.exp(math.log(2.3689632477896794e-09) - 1.3862944 * jax.random.uniform(key_of[11], (CIN, D), jnp.float32) ** steps_of(key_of[11], (CIN, D), ((1, 32),), -0.2, 0.2)), 5.922408119474198e-10, 2.3689632477896794e-09)
    w_layers = gaussian(key_of[12], (LAYERS, 6, D, D), D ** -0.5, 0.25, ((2, 32),), jnp.float32)
    moment_layers = gaussian(key_of[13], (LAYERS, 6, D, D), (1.0 / (OUT * GRID ** 0.5)), 0.00036621094, ((2, 32),), jnp.float32)
    square_layers = jnp.clip(jnp.exp(math.log(2.3689632477896794e-09) - 1.3862944 * jax.random.uniform(key_of[14], (LAYERS, 6, D, D), jnp.float32) ** steps_of(key_of[14], (LAYERS, 6, D, D), ((2, 32),), -0.2, 0.2)), 5.922408119474198e-10, 2.3689632477896794e-09)
    norm_gains = jnp.clip(1.0 + 0.1 * jax.random.normal(key_of[15], (LAYERS, 2, D), jnp.float32), 0.5, 1.5)
    moment_gains = gaussian(key_of[16], (LAYERS, 2, D), (0.5 / D), 0.015625, ((2, 32),), jnp.float32)
    square_gains = jnp.clip(jnp.exp(math.log(3.814697265625e-06) - 1.3862944 * jax.random.uniform(key_of[17], (LAYERS, 2, D), jnp.float32) ** steps_of(key_of[17], (LAYERS, 2, D), ((2, 32),), -0.2, 0.2)), 9.5367431640625e-07, 3.814697265625e-06)
    w_out = gaussian(key_of[18], (D, OUT), D ** -0.5, 0.25, ((0, 32),), jnp.float32)
    moment_out = gaussian(key_of[19], (D, OUT), (1.0 / (OUT * GRID ** 0.5)), 0.00036621094, ((0, 32),), jnp.float32)
    square_out = jnp.clip(jnp.exp(math.log(2.3689632477896794e-09) - 1.3862944 * jax.random.uniform(key_of[20], (D, OUT), jnp.float32) ** steps_of(key_of[20], (D, OUT), ((0, 32),), -0.2, 0.2)), 5.922408119474198e-10, 2.3689632477896794e-09)
    return {"grid_inputs": grid_inputs, "mesh_static": mesh_static, "targets": targets, "area_weight": area_weight, "valid_rows": valid_rows, "encoder_lists": encoder_lists, "mesh_lists": mesh_lists, "decoder_lists": decoder_lists, "step_count": step_count, "w_in": w_in, "moment_in": moment_in, "square_in": square_in, "w_layers": w_layers, "moment_layers": moment_layers, "square_layers": square_layers, "norm_gains": norm_gains, "moment_gains": moment_gains, "square_gains": square_gains, "w_out": w_out, "moment_out": moment_out, "square_out": square_out}


EPS_NORM = 1e-05
BETA_ONE = 0.5
BETA_TWO = 0.5
ADAM_EPS = 1e-08
LEARN_RATE = 0.04
DECAY_RATE = 0.1
PRECISE = lax.Precision.HIGHEST

@jax.custom_vjp
def low(v):
    return lax.optimization_barrier(v.astype(jnp.bfloat16)).astype(jnp.float32)

@jax.custom_vjp
def low_back(v):
    return v

def low_keep(v):
    return (low(v), None)

def low_pass(kept, grad):
    return (grad,)

def back_keep(v):
    return (v, None)

def back_low(kept, grad):
    return (low(grad),)
low.defvjp(low_keep, low_pass)
low_back.defvjp(back_keep, back_low)

def product(left, right):
    return jnp.dot(left, right, precision=PRECISE, preferred_element_type=jnp.float32)

def layer_norm(tensor, gain_row):
    centre = tensor - lax.optimization_barrier(jnp.mean(tensor, axis=-1, keepdims=True))
    spread = lax.optimization_barrier(jnp.mean(centre * centre, axis=-1, keepdims=True))
    return centre * lax.rsqrt(spread + EPS_NORM) * gain_row

def windows(block_count):
    device_ids = jnp.arange(block_count, dtype=jnp.int32)[:, None]
    window_slot = jnp.arange(3 * ND, dtype=jnp.int32)[None, :]
    owner_block = (device_ids - 1 + window_slot // ND) % block_count
    return owner_block * ND + window_slot % ND

def interact(source, target, neighbours, weights, gains, shared_side):
    matrices = low(weights)
    gain_pair = low(gains)
    target_low = low(target)
    source_low = target_low if shared_side else low(source)
    sent_rows = low(low_back(product(source_low, matrices[0])))
    block_count = target.shape[0] // ND
    window = low_back(sent_rows[windows(block_count)])
    flattened = window.reshape(block_count * 3 * ND, sent_rows.shape[1])
    device_ids = jnp.arange(target.shape[0], dtype=jnp.int32) // ND
    slot_index = device_ids[:, None] * (3 * ND) + neighbours
    own_term = low_back(product(target_low, matrices[1]))
    pre_edge = flattened[slot_index] + own_term[:, None, :]
    edge_hidden = low(jax.nn.silu(pre_edge))
    message = low_back(product(edge_hidden.reshape(-1, D), matrices[2])).reshape(pre_edge.shape)
    aggregate = low(lax.optimization_barrier(jnp.sum(layer_norm(message, gain_pair[0]), axis=1)))
    node_mix = low_back(product(target_low, matrices[3]) + product(aggregate, matrices[4]))
    node_hidden = low(jax.nn.silu(node_mix))
    node_out = low_back(product(node_hidden, matrices[5]))
    return target + layer_norm(node_out, gain_pair[1])

def forward(parameters, grid_values, mesh_values, targets, weight_rows, encoder_lists, mesh_lists, decoder_lists):
    w_in, w_layers, norm_gains, w_out = parameters
    checked = jax.checkpoint(interact, static_argnums=(5,))
    grid_latent = low_back(product(grid_values, low(w_in)))
    mesh_latent = checked(grid_latent, mesh_values, encoder_lists, w_layers[0], norm_gains[0], False)
    for layer_id in range(1, LAYERS - 1):
        mesh_latent = checked(mesh_latent, mesh_latent, mesh_lists, w_layers[layer_id], norm_gains[layer_id], True)
    grid_latent = checked(mesh_latent, grid_latent, decoder_lists, w_layers[LAYERS - 1], norm_gains[LAYERS - 1], False)
    prediction = low_back(product(low(grid_latent), low(w_out)))
    error_rows = prediction - targets
    return jnp.sum(weight_rows[:, None] * error_rows * error_rows) / (GRID * OUT)

def adamw_update(weight, moment_one, moment_two, gradient, step_value, decay_rate):
    new_one = BETA_ONE * moment_one + (1.0 - BETA_ONE) * gradient
    new_two = BETA_TWO * moment_two + (1.0 - BETA_TWO) * gradient * gradient
    correct_one = 1.0 - jnp.power(BETA_ONE, step_value)
    correct_two = 1.0 - jnp.power(BETA_TWO, step_value)
    direction = new_one / correct_one / (jnp.sqrt(new_two / correct_two) + ADAM_EPS)
    return (new_one, new_two, weight - LEARN_RATE * (direction + decay_rate * weight))

def reference(grid_inputs, mesh_static, targets, area_weight, valid_rows, encoder_lists, mesh_lists, decoder_lists, step_count, w_in, moment_in, square_in, w_layers, moment_layers, square_layers, norm_gains, moment_gains, square_gains, w_out, moment_out, square_out):
    device_ids = jnp.arange(GRID, dtype=jnp.int32) // ND
    local_rows = jnp.arange(GRID, dtype=jnp.int32) % ND
    weight_rows = area_weight * (local_rows < valid_rows[device_ids]).astype(jnp.float32)
    grid_values = grid_inputs.astype(jnp.float32)
    mesh_values = mesh_static.astype(jnp.float32)

    def loss_for(parameters):
        return forward(parameters, grid_values, mesh_values, targets, weight_rows, encoder_lists, mesh_lists, decoder_lists)
    loss_value, pullback = jax.vjp(loss_for, (w_in, w_layers, norm_gains, w_out))
    gradients, = pullback(jnp.ones_like(loss_value))
    grad_in, grad_layers, grad_gains, grad_out = gradients
    step_value = step_count[0].astype(jnp.float32)
    one_in, two_in, new_in = adamw_update(w_in, moment_in, square_in, grad_in, step_value, DECAY_RATE)
    one_layers, two_layers, new_layers = adamw_update(w_layers, moment_layers, square_layers, grad_layers, step_value, DECAY_RATE)
    one_gains, two_gains, new_gains = adamw_update(norm_gains, moment_gains, square_gains, grad_gains, step_value, 0.0)
    one_out, two_out, new_out = adamw_update(w_out, moment_out, square_out, grad_out, step_value, DECAY_RATE)
    return (loss_value, one_in, two_in, new_in, one_layers, two_layers, new_layers, one_gains, two_gains, new_gains, one_out, two_out, new_out)
```

```python
import functools

import jax
import jax.numpy as jnp
from jax import lax
from jax.experimental import pallas as pl
from jax.experimental.pallas import tpu as pltpu
from jax.sharding import PartitionSpec as P

EPS_NORM = 1e-05
BETA_ONE = 0.5
BETA_TWO = 0.5
ADAM_EPS = 1e-08
LEARN_RATE = 0.04
DECAY_RATE = 0.1

AXES = ("nodes", "shard")
LANES = 128
FORWARD_ROWS = 128
BACKWARD_ROWS = 128
WEIGHT_ROWS = 256
UNROLL = 32
VMEM_BYTES = 56 << 20
LOW = jnp.bfloat16
WIDE = jnp.float32


def product(left, right):
    return jnp.dot(left, right, preferred_element_type=WIDE)


def product_left(left, right):
    return lax.dot_general(left, right, (((0,), (0,)), ((), ())), preferred_element_type=WIDE)


def product_right(left, right):
    return lax.dot_general(left, right, (((1,), (1,)), ((), ())), preferred_element_type=WIDE)


def normalize(tensor):
    centre = tensor - jnp.mean(tensor, axis=-1, keepdims=True)
    inv_scale = lax.rsqrt(jnp.mean(centre * centre, axis=-1, keepdims=True) + EPS_NORM)
    return (centre * inv_scale, inv_scale)


def normal_back(grad_unit, unit_rows, inv_scale):
    centred = grad_unit - jnp.mean(grad_unit, axis=-1, keepdims=True)
    return inv_scale * (
        centred - unit_rows * jnp.mean(grad_unit * unit_rows, axis=-1, keepdims=True)
    )


def sigmoid(tensor):
    return 0.5 * jnp.tanh(0.5 * tensor) + 0.5


def fold_rows(store, base, rows, tensor):
    parts = tensor.shape[1] // LANES
    for part in range(parts):
        store[pl.ds(base * parts + part, rows, stride=parts), :] = tensor[
            :, part * LANES : (part + 1) * LANES
        ]


def unfold_rows(store, base, rows, parts):
    return jnp.concatenate(
        [store[pl.ds(base * parts + part, rows, stride=parts), :] for part in range(parts)],
        axis=1,
    )


def forward_kernel(parts, has_next, *refs):
    if has_next:
        (slots, before, middle, after, low, wide, weights, gains, head) = refs[:9]
        (sent, update, update_low, kept, message, aggregate, mix, out) = refs[9:17]
        window, picked = refs[17:]
    else:
        (slots, before, middle, after, low, wide, weights, gains) = refs[:8]
        (update_low, kept, message, aggregate, mix, out) = refs[8:14]
        window, picked = refs[14:]
    step = pl.program_id(0)
    block_rows = before.shape[0]
    rows, width = low.shape
    fan = kept.shape[0]

    @pl.when(step == 0)
    def _():
        for index, block in enumerate((before, middle, after)):
            fold_rows(window, index * block_rows, block_rows, block[...].astype(WIDE))

    for k in range(fan):

        def pick(trip, carry):
            for lane in range(UNROLL):
                row = trip * UNROLL + lane
                slot = slots[k * block_rows + step * rows + row]
                picked[pl.ds(pl.multiple_of((k * rows + row) * parts, parts), parts), :] = window[
                    pl.ds(pl.multiple_of(slot * parts, parts), parts), :
                ]
            return carry

        lax.fori_loop(0, rows // UNROLL, pick, 0)
    target_low = low[...]
    own_term = product(target_low, weights[1])
    total = jnp.zeros((rows, width), WIDE)
    for k in range(fan):
        sender = unfold_rows(picked, k * rows, rows, parts)
        kept[k] = sender.astype(LOW)
        pre_edge = sender + own_term
        hidden = (pre_edge * sigmoid(pre_edge)).astype(LOW)
        spoken = product(hidden, weights[2])
        message[k] = spoken
        total = total + normalize(spoken)[0] * gains[0:1, :]
    total_low = total.astype(LOW)
    aggregate[...] = total_low
    node_mix = product(target_low, weights[3]) + product(total_low, weights[4])
    mix[...] = node_mix
    node_hidden = (node_mix * sigmoid(node_mix)).astype(LOW)
    node_out = product(node_hidden, weights[5])
    out[...] = node_out
    updated = wide[...].astype(WIDE) + normalize(node_out)[0] * gains[1:2, :]
    updated_low = updated.astype(LOW)
    update_low[...] = updated_low
    if has_next:
        update[...] = updated
        sent[...] = product(updated_low, head[0]).astype(LOW)


def whole(shape):
    zeros = (0,) * len(shape)
    return pl.BlockSpec(shape, lambda step: zeros)


def layer_spec(layer_id, count, width):
    return pl.BlockSpec((None, count, width, width), lambda step: (layer_id, 0, 0, 0))


def tiled(rows, width):
    return pl.BlockSpec((rows, width), lambda step: (step, 0))


def fanned(fan, rows, width):
    return pl.BlockSpec((fan, rows, width), lambda step: (0, step, 0))


def forward_layer(layer_id, has_next, slots, blocks, target_low, target, weights, gains):
    block_rows, width = target_low.shape
    fan = slots.shape[0] // block_rows
    parts = width // LANES
    rows = FORWARD_ROWS
    shape = functools.partial(jax.ShapeDtypeStruct, (block_rows, width))
    fan_shape = functools.partial(jax.ShapeDtypeStruct, (fan, block_rows, width))
    tile = tiled(rows, width)
    in_specs = [pl.BlockSpec(memory_space=pltpu.SMEM)]
    in_specs += [whole((block_rows, width))] * 3 + [tile, tile]
    in_specs += [layer_spec(layer_id, 6, width), whole(gains.shape)]
    out_specs = [tile, fanned(fan, rows, width), fanned(fan, rows, width), tile, tile, tile]
    out_shape = [shape(LOW), fan_shape(LOW), fan_shape(WIDE), shape(LOW), shape(WIDE), shape(WIDE)]
    operands = [slots, *blocks, target_low, target, weights, gains]
    if has_next:
        in_specs += [layer_spec(layer_id + 1, 1, width)]
        operands += [weights]
        out_specs = [tile, tile] + out_specs
        out_shape = [shape(LOW), shape(WIDE)] + out_shape
    return pl.pallas_call(
        functools.partial(forward_kernel, parts, has_next),
        grid=(block_rows // rows,),
        in_specs=in_specs,
        out_specs=out_specs,
        out_shape=out_shape,
        scratch_shapes=[
            pltpu.VMEM((3 * block_rows * parts, LANES), WIDE),
            pltpu.VMEM((fan * rows * parts, LANES), WIDE),
        ],
        compiler_params=pltpu.CompilerParams(vmem_limit_bytes=VMEM_BYTES),
        cost_estimate=pl.CostEstimate(
            flops=2 * (fan + 5) * block_rows * width * width,
            transcendentals=(fan + 1) * block_rows * width,
            bytes_accessed=24 * block_rows * width * 2,
        ),
        name="forward_layer",
    )(*operands)


def backward_kernel(parts, mode, *refs):
    refs = list(refs)
    slots = refs.pop(0)
    if mode != "first":
        returned = [refs.pop(0) for _ in range(3)]
        head = refs.pop(0)
    if mode != "second":
        grad_part = refs.pop(0)
    low, kept, message, mix, out, weights, gains = refs[:7]
    refs = refs[7:]
    if mode != "first":
        sent_grad = refs.pop(0)
        grad_full = refs.pop(0)
    (slot_grad, grad_gains, grad_message, edge_hidden, grad_mix, grad_out, grad_own, hidden) = refs[
        :8
    ]
    sum_even, sum_odd, spread = refs[8:]
    step = pl.program_id(0)
    rows, width = low.shape
    fan = kept.shape[0]
    block_rows = slot_grad.shape[1]

    @pl.when(step == 0)
    def _():
        sum_even[...] = jnp.zeros_like(sum_even)
        sum_odd[...] = jnp.zeros_like(sum_odd)
        grad_gains[...] = jnp.zeros_like(grad_gains)

    if mode == "first":
        grad_new = grad_part[...]
    else:
        sent_low = (
            returned[0][...].astype(WIDE)
            + returned[1][...].reshape(rows, width).astype(WIDE)
            + returned[2][...].astype(WIDE)
        ).astype(LOW)
        sent_grad[...] = sent_low
        grad_new = product_right(sent_low, head[0])
        if mode == "third":
            grad_new = grad_part[...] + grad_new
        grad_full[...] = grad_new
    target_low = low[...]
    out_unit, out_scale = normalize(out[...])
    gain_two = jnp.sum(grad_new * out_unit, axis=0, keepdims=True)
    out_low = normal_back(grad_new * gains[1:2, :], out_unit, out_scale).astype(LOW)
    grad_out[...] = out_low
    node_mix = mix[...]
    gate = sigmoid(node_mix)
    hidden[...] = (node_mix * gate).astype(LOW)
    mix_low = (
        product_right(out_low, weights[5]) * (gate * (1.0 + node_mix * (1.0 - gate)))
    ).astype(LOW)
    grad_mix[...] = mix_low
    grad_sum = product_right(mix_low, weights[4])
    own_term = product(target_low, weights[1])
    grad_unit = grad_sum * gains[0:1, :]
    unit_total = jnp.zeros((rows, width), WIDE)
    own_total = jnp.zeros((rows, width), WIDE)
    for k in range(fan):
        unit_rows, inv_scale = normalize(message[k])
        unit_total = unit_total + unit_rows
        message_low = normal_back(grad_unit, unit_rows, inv_scale).astype(LOW)
        grad_message[k] = message_low
        pre_edge = kept[k].astype(WIDE) + own_term
        edge_gate = sigmoid(pre_edge)
        edge_hidden[k] = (pre_edge * edge_gate).astype(LOW)
        grad_pre = product_right(message_low, weights[2]) * (
            edge_gate * (1.0 + pre_edge * (1.0 - edge_gate))
        )
        own_total = own_total + grad_pre
        fold_rows(spread, k * rows, rows, grad_pre)
    gain_one = jnp.sum(grad_sum * unit_total, axis=0, keepdims=True)
    grad_gains[...] += jnp.concatenate([gain_one, gain_two], axis=0)
    grad_own[...] = own_total.astype(LOW)

    for k in range(fan):

        def add(trip, carry):
            for lane in range(UNROLL // 2):
                places, values = [], []
                for store in (sum_even, sum_odd):
                    row = (trip * (UNROLL // 2) + lane) * 2 + len(places)
                    slot = slots[k * block_rows + step * rows + row]
                    place = pl.ds(pl.multiple_of(slot * parts, parts), parts)
                    value = spread[pl.ds(pl.multiple_of((k * rows + row) * parts, parts), parts), :]
                    places.append(place)
                    values.append(store[place, :] + value)
                sum_even[places[0], :] = values[0]
                sum_odd[places[1], :] = values[1]
            return carry

        lax.fori_loop(0, rows // UNROLL, add, 0)

    @pl.when(step == pl.num_programs(0) - 1)
    def _():
        for index in range(3):
            base = index * block_rows
            slot_grad[index] = (
                unfold_rows(sum_even, base, block_rows, parts)
                + unfold_rows(sum_odd, base, block_rows, parts)
            ).astype(LOW)


def backward_layer(layer_id, slots, above, grad_part, stored, weights, gains):
    target_low, kept, message, mix, out = stored
    block_rows, width = target_low.shape
    fan = kept.shape[0]
    parts = width // LANES
    rows = BACKWARD_ROWS
    tile = tiled(rows, width)
    fan_tile = fanned(fan, rows, width)
    in_specs = [pl.BlockSpec(memory_space=pltpu.SMEM)]
    operands = [slots]
    out_specs, out_shape = [], []
    shape = functools.partial(jax.ShapeDtypeStruct, (block_rows, width))
    fan_shape = functools.partial(jax.ShapeDtypeStruct, (fan, block_rows, width))
    mode = "first" if above is None else ("second" if grad_part is None else "third")
    if above is not None:
        from_before, slot_grad, from_after = above
        in_specs += [
            tile,
            pl.BlockSpec((1, rows, width), lambda step: (1, step, 0)),
            tile,
            layer_spec(layer_id + 1, 1, width),
        ]
        operands += [from_before, slot_grad, from_after, weights]
        out_specs += [tile, tile]
        out_shape += [shape(LOW), shape(WIDE)]
    if grad_part is not None:
        in_specs += [tile]
        operands += [grad_part]
    in_specs += [tile, fan_tile, fan_tile, tile, tile]
    in_specs += [layer_spec(layer_id, 6, width), whole(gains.shape)]
    operands += [target_low, kept, message, mix, out, weights, gains]
    out_specs += [
        whole((3, block_rows, width)),
        whole((2, width)),
        fan_tile,
        fan_tile,
        tile,
        tile,
        tile,
        tile,
    ]
    out_shape += [
        jax.ShapeDtypeStruct((3, block_rows, width), LOW),
        jax.ShapeDtypeStruct((2, width), WIDE),
        fan_shape(LOW),
        fan_shape(LOW),
        shape(LOW),
        shape(LOW),
        shape(LOW),
        shape(LOW),
    ]
    results = pl.pallas_call(
        functools.partial(backward_kernel, parts, mode),
        grid=(block_rows // rows,),
        in_specs=in_specs,
        out_specs=out_specs,
        out_shape=out_shape,
        scratch_shapes=[
            pltpu.VMEM((3 * block_rows * parts, LANES), WIDE),
            pltpu.VMEM((3 * block_rows * parts, LANES), WIDE),
            pltpu.VMEM((fan * rows * parts, LANES), WIDE),
        ],
        compiler_params=pltpu.CompilerParams(vmem_limit_bytes=VMEM_BYTES),
        cost_estimate=pl.CostEstimate(
            flops=2 * (fan + 4) * block_rows * width * width,
            transcendentals=(fan + 1) * block_rows * width,
            bytes_accessed=24 * block_rows * width * 2,
        ),
        name="backward_layer",
    )(*operands)
    if above is None:
        return (None, grad_part, *results)
    return tuple(results)


def weight_kernel(has_above, needs_target, *refs):
    refs = list(refs)
    if has_above:
        source, sent_grad = refs[:2]
        refs = refs[2:]
    low, aggregate, edge_hidden, grad_message, grad_mix, grad_out, grad_own, hidden = refs[:8]
    refs = refs[8:]
    if needs_target:
        grad_new, weights = refs[:2]
        refs = refs[2:]
        grad_matrices, grad_part = refs
    else:
        (grad_matrices,) = refs
    step = pl.program_id(0)
    fan = edge_hidden.shape[0]

    @pl.when(step == 0)
    def _():
        grad_matrices[...] = jnp.zeros_like(grad_matrices)

    target_low = low[...]
    mix_low = grad_mix[...]
    own_low = grad_own[...]
    if has_above:
        grad_matrices[0] += product_left(source[...], sent_grad[...])
    grad_matrices[1] += product_left(target_low, own_low)
    for k in range(fan):
        grad_matrices[2] += product_left(edge_hidden[k], grad_message[k])
    grad_matrices[3] += product_left(target_low, mix_low)
    grad_matrices[4] += product_left(aggregate[...], mix_low)
    grad_matrices[5] += product_left(hidden[...], grad_out[...])
    if needs_target:
        grad_part[...] = (
            grad_new[...]
            + product_right(own_low, weights[1])
            + product_right(mix_low, weights[3])
        )


def weight_layer(layer_id, above, low, aggregate, back, grad_new, weights):
    block_rows, width = low.shape
    rows = WEIGHT_ROWS
    fan = back[1].shape[0]
    tile = tiled(rows, width)
    fan_tile = fanned(fan, rows, width)
    in_specs, operands = [], []
    if above is not None:
        in_specs += [tile, tile]
        operands += list(above)
    in_specs += [tile, tile, fan_tile, fan_tile, tile, tile, tile, tile]
    operands += [low, aggregate, *back]
    out_specs = [whole((6, width, width))]
    out_shape = [jax.ShapeDtypeStruct((6, width, width), WIDE)]
    if grad_new is not None:
        in_specs += [tile, layer_spec(layer_id, 6, width)]
        operands += [grad_new, weights]
        out_specs += [tile]
        out_shape += [jax.ShapeDtypeStruct((block_rows, width), WIDE)]
    return pl.pallas_call(
        functools.partial(weight_kernel, above is not None, grad_new is not None),
        grid=(block_rows // rows,),
        in_specs=in_specs,
        out_specs=out_specs,
        out_shape=out_shape,
        compiler_params=pltpu.CompilerParams(vmem_limit_bytes=VMEM_BYTES),
        cost_estimate=pl.CostEstimate(
            flops=2 * (fan + 6) * block_rows * width * width,
            transcendentals=0,
            bytes_accessed=24 * block_rows * width,
        ),
        name="weight_layer",
    )(*operands)


def shift(cells, count, step):
    return lax.ppermute(cells, AXES, [(i, (i + step) % count) for i in range(count)])


def adamw_update(weight, moment_one, moment_two, gradient, step_value, decay_rate):
    new_one = BETA_ONE * moment_one + (1.0 - BETA_ONE) * gradient
    new_two = BETA_TWO * moment_two + (1.0 - BETA_TWO) * gradient * gradient
    correct_one = 1.0 - jnp.power(BETA_ONE, step_value)
    correct_two = 1.0 - jnp.power(BETA_TWO, step_value)
    direction = new_one / correct_one / (jnp.sqrt(new_two / correct_two) + ADAM_EPS)
    return (new_one, new_two, weight - LEARN_RATE * (direction + decay_rate * weight))


def shards(
    grid_inputs,
    mesh_static,
    targets,
    area_weight,
    valid_rows,
    encoder_lists,
    mesh_lists,
    decoder_lists,
    step_count,
    w_in,
    moment_in,
    square_in,
    w_layers,
    moment_layers,
    square_layers,
    norm_gains,
    moment_gains,
    square_gains,
    w_out,
    moment_out,
    square_out,
):
    row_count = grid_inputs.shape[0]
    layer_total = w_layers.shape[0]
    device_count = lax.axis_size(AXES)
    table_in = lax.all_gather(w_in.astype(LOW), AXES, axis=1, tiled=True)
    table_out = lax.all_gather(w_out.astype(LOW), AXES, axis=0, tiled=True)
    matrices = lax.all_gather(w_layers.astype(LOW), AXES, axis=2, tiled=True)
    gains = lax.all_gather(norm_gains.astype(LOW), AXES, axis=2, tiled=True).astype(WIDE)
    slot_lists = [encoder_lists.T.reshape(-1)]
    slot_lists += [mesh_lists.T.reshape(-1)] * (layer_total - 2)
    slot_lists += [decoder_lists.T.reshape(-1)]
    grid_latent = product(grid_inputs, table_in)
    grid_start = grid_latent.astype(LOW)
    sent = product(grid_start, matrices[0, 0]).astype(LOW)
    target, target_low = mesh_static, mesh_static
    stored_list = []
    for layer_id in range(layer_total):
        blocks = (shift(sent, device_count, 1), sent, shift(sent, device_count, -1))
        last_layer = layer_id == layer_total - 1
        if last_layer:
            source_low = target_low
            target, target_low = grid_latent, grid_start
        else:
            source_low = grid_start if layer_id == 0 else target_low
        results = forward_layer(
            layer_id,
            not last_layer,
            slot_lists[layer_id],
            blocks,
            target_low,
            target,
            matrices,
            gains[layer_id],
        )
        if last_layer:
            grid_low, kept, message, aggregate, mix, out = results
        else:
            sent, updated, updated_low, kept, message, aggregate, mix, out = results
        stored_list.append((source_low, (target_low, kept, message, mix, out), aggregate))
        if not last_layer:
            target, target_low = updated, updated_low
    prediction = product(grid_low, table_out)
    local_rows = jnp.arange(row_count, dtype=jnp.int32)
    weight_rows = area_weight * (local_rows < valid_rows[0]).astype(WIDE)
    error_rows = prediction - targets
    loss_scale = 1.0 / (row_count * device_count * prediction.shape[1])
    loss_local = jnp.sum(weight_rows[:, None] * error_rows * error_rows) * loss_scale
    loss_value = lax.psum(loss_local, AXES)
    grad_pred = (2.0 * loss_scale * weight_rows[:, None] * error_rows).astype(LOW)
    grad_table_out = product_left(grid_low, grad_pred)
    grad_part = product_right(grad_pred, table_out)
    grad_grid = None
    above, above_source = None, None
    layer_grads = [None] * layer_total
    gain_grads = [None] * layer_total
    for layer_id in reversed(range(layer_total)):
        source_low, stored, aggregate = stored_list[layer_id]
        sent_grad, grad_new, slot_grad, grad_gain, *back = backward_layer(
            layer_id, slot_lists[layer_id], above, grad_part, stored, matrices, gains[layer_id]
        )
        from_before = shift(slot_grad[2], device_count, 1)
        from_after = shift(slot_grad[0], device_count, -1)
        back = [back[1], back[0], *back[2:]]
        results = weight_layer(
            layer_id,
            None if above is None else (above_source, sent_grad),
            stored[0],
            aggregate,
            back,
            None if layer_id == 0 else grad_new,
            matrices,
        )
        layer_grads[layer_id] = results[0]
        gain_grads[layer_id] = grad_gain
        if layer_id == layer_total - 1:
            grad_grid, grad_part = results[1], None
        elif layer_id > 0:
            grad_part = results[1]
        above = (from_before, slot_grad, from_after)
        above_source = source_low
    sent_grad = (
        from_before.astype(WIDE) + slot_grad[1].astype(WIDE) + from_after.astype(WIDE)
    ).astype(LOW)
    grad_zero = product_left(above_source, sent_grad)
    grad_grid = grad_grid + product_right(sent_grad, matrices[0, 0])
    grad_table_in = product_left(grid_inputs, grad_grid.astype(LOW))
    grad_stack = jnp.concatenate(
        [grad_zero[None]]
        + [
            part
            for layer_id in range(layer_total)
            for part in (
                [layer_grads[layer_id][1:]]
                + ([layer_grads[layer_id][0:1]] if layer_id < layer_total - 1 else [])
            )
        ],
        axis=0,
    ).reshape(layer_total, 6, *grad_zero.shape)
    grad_layers = lax.psum_scatter(grad_stack, AXES, scatter_dimension=2, tiled=True)
    grad_gain_all = lax.psum_scatter(
        jnp.stack(gain_grads), AXES, scatter_dimension=2, tiled=True
    )
    grad_in = lax.psum_scatter(grad_table_in, AXES, scatter_dimension=1, tiled=True)
    grad_out = lax.psum_scatter(grad_table_out, AXES, scatter_dimension=0, tiled=True)
    step_value = step_count[0].astype(WIDE)
    one_in, two_in, new_in = adamw_update(
        w_in, moment_in, square_in, grad_in, step_value, DECAY_RATE
    )
    one_layers, two_layers, new_layers = adamw_update(
        w_layers, moment_layers, square_layers, grad_layers, step_value, DECAY_RATE
    )
    one_gains, two_gains, new_gains = adamw_update(
        norm_gains, moment_gains, square_gains, grad_gain_all, step_value, 0.0
    )
    one_out, two_out, new_out = adamw_update(
        w_out, moment_out, square_out, grad_out, step_value, DECAY_RATE
    )
    return (
        loss_value,
        one_in,
        two_in,
        new_in,
        one_layers,
        two_layers,
        new_layers,
        one_gains,
        two_gains,
        new_gains,
        one_out,
        two_out,
        new_out,
    )


def solution(mesh):
    rows = P(AXES, None)
    layers = P(None, None, AXES, None)
    gains = P(None, None, AXES)
    columns = P(None, AXES)
    in_specs = (rows, rows, rows, P(AXES), P(AXES), rows, rows, rows, P())
    in_specs += (columns,) * 3 + (layers,) * 3 + (gains,) * 3 + (rows,) * 3
    out_specs = (P(),) + (columns,) * 3 + (layers,) * 3 + (gains,) * 3 + (rows,) * 3
    return jax.shard_map(shards, mesh=mesh, in_specs=in_specs, out_specs=out_specs, check_vma=False)
```

```python
import functools

import jax
import jax.numpy as jnp
from jax import lax
from jax.experimental import pallas as pl
from jax.experimental.pallas import tpu as pltpu
from jax.sharding import PartitionSpec as P

EPS_NORM = 1e-05
BETA_ONE = 0.5
BETA_TWO = 0.5
ADAM_EPS = 1e-08
LEARN_RATE = 0.04
DECAY_RATE = 0.1

AXES = ("nodes", "shard")
LANES = 128
FORWARD_ROWS = 128
BACKWARD_ROWS = 128
WEIGHT_ROWS = 256
UNROLL = 32
VMEM_BYTES = 56 << 20
LOW = jnp.bfloat16
WIDE = jnp.float32
SEND = jnp.float32


def product(left, right):
    return jnp.dot(left, right, preferred_element_type=WIDE)


def product_left(left, right):
    return lax.dot_general(left, right, (((0,), (0,)), ((), ())), preferred_element_type=WIDE)


def product_right(left, right):
    return lax.dot_general(left, right, (((1,), (1,)), ((), ())), preferred_element_type=WIDE)


def normalize(tensor):
    centre = tensor - jnp.mean(tensor, axis=-1, keepdims=True)
    inv_scale = lax.rsqrt(jnp.mean(centre * centre, axis=-1, keepdims=True) + EPS_NORM)
    return (centre * inv_scale, inv_scale)


def normal_back(grad_unit, unit_rows, inv_scale):
    centred = grad_unit - jnp.mean(grad_unit, axis=-1, keepdims=True)
    return inv_scale * (
        centred - unit_rows * jnp.mean(grad_unit * unit_rows, axis=-1, keepdims=True)
    )


def sigmoid(tensor):
    return 0.5 * jnp.tanh(0.5 * tensor) + 0.5


def fold_rows(store, base, rows, tensor):
    parts = tensor.shape[1] // LANES
    for part in range(parts):
        store[pl.ds(base * parts + part, rows, stride=parts), :] = tensor[
            :, part * LANES : (part + 1) * LANES
        ]


def unfold_rows(store, base, rows, parts):
    return jnp.concatenate(
        [store[pl.ds(base * parts + part, rows, stride=parts), :] for part in range(parts)],
        axis=1,
    )


def forward_kernel(parts, has_next, *refs):
    if has_next:
        (slots, before, middle, after, low, wide, weights, gains, head) = refs[:9]
        (sent, update, update_low, kept, message, aggregate, mix, out) = refs[9:17]
        window, picked = refs[17:]
    else:
        (slots, before, middle, after, low, wide, weights, gains) = refs[:8]
        (update_low, kept, message, aggregate, mix, out) = refs[8:14]
        window, picked = refs[14:]
    step = pl.program_id(0)
    block_rows = before.shape[0]
    rows, width = low.shape
    fan = kept.shape[0]

    @pl.when(step == 0)
    def _():
        for index, block in enumerate((before, middle, after)):
            fold_rows(window, index * block_rows, block_rows, block[...].astype(WIDE))

    for k in range(fan):

        def pick(trip, carry):
            for lane in range(UNROLL):
                row = trip * UNROLL + lane
                slot = slots[k * block_rows + step * rows + row]
                picked[pl.ds(pl.multiple_of((k * rows + row) * parts, parts), parts), :] = window[
                    pl.ds(pl.multiple_of(slot * parts, parts), parts), :
                ]
            return carry

        lax.fori_loop(0, rows // UNROLL, pick, 0)
    target_low = low[...]
    own_term = product(target_low, weights[1])
    total = jnp.zeros((rows, width), WIDE)
    for k in range(fan):
        sender = unfold_rows(picked, k * rows, rows, parts)
        kept[k] = sender.astype(LOW)
        pre_edge = sender + own_term
        hidden = (pre_edge * sigmoid(pre_edge)).astype(LOW)
        spoken = product(hidden, weights[2])
        message[k] = spoken
        total = total + normalize(spoken)[0] * gains[0:1, :]
    total_low = total.astype(LOW)
    aggregate[...] = total_low
    node_mix = product(target_low, weights[3]) + product(total_low, weights[4])
    mix[...] = node_mix
    node_hidden = (node_mix * sigmoid(node_mix)).astype(LOW)
    node_out = product(node_hidden, weights[5])
    out[...] = node_out
    updated = wide[...].astype(WIDE) + normalize(node_out)[0] * gains[1:2, :]
    updated_low = updated.astype(LOW)
    update_low[...] = updated_low
    if has_next:
        update[...] = updated
        sent[...] = product(updated_low, head[0]).astype(LOW)


def whole(shape):
    zeros = (0,) * len(shape)
    return pl.BlockSpec(shape, lambda step: zeros)


def matrix_spec(first, count, width):
    return pl.BlockSpec((count, width, width), lambda step: (first // count, 0, 0))


def tiled(rows, width):
    return pl.BlockSpec((rows, width), lambda step: (step, 0))


def fanned(fan, rows, width):
    return pl.BlockSpec((fan, rows, width), lambda step: (0, step, 0))


def forward_layer(slots, blocks, target_low, target, weights, next_weights, gains):
    block_rows, width = target_low.shape
    fan = slots.shape[0] // block_rows
    parts = width // LANES
    rows = FORWARD_ROWS
    has_next = next_weights is not None
    shape = functools.partial(jax.ShapeDtypeStruct, (block_rows, width))
    fan_shape = functools.partial(jax.ShapeDtypeStruct, (fan, block_rows, width))
    tile = tiled(rows, width)
    in_specs = [pl.BlockSpec(memory_space=pltpu.SMEM)]
    in_specs += [whole((block_rows, width))] * 3 + [tile, tile]
    in_specs += [matrix_spec(weights[1], 6, width), whole(gains.shape)]
    out_specs = [tile, fanned(fan, rows, width), fanned(fan, rows, width), tile, tile, tile]
    out_shape = [shape(LOW), fan_shape(LOW), fan_shape(WIDE), shape(LOW), shape(WIDE), shape(WIDE)]
    operands = [slots, *blocks, target_low, target, weights[0], gains]
    if has_next:
        in_specs += [matrix_spec(next_weights[1], 1, width)]
        operands += [next_weights[0]]
        out_specs = [tile, tile] + out_specs
        out_shape = [shape(LOW), shape(WIDE)] + out_shape
    return pl.pallas_call(
        functools.partial(forward_kernel, parts, has_next),
        grid=(block_rows // rows,),
        in_specs=in_specs,
        out_specs=out_specs,
        out_shape=out_shape,
        scratch_shapes=[
            pltpu.VMEM((3 * block_rows * parts, LANES), WIDE),
            pltpu.VMEM((fan * rows * parts, LANES), WIDE),
        ],
        compiler_params=pltpu.CompilerParams(vmem_limit_bytes=VMEM_BYTES),
        cost_estimate=pl.CostEstimate(
            flops=2 * (fan + 5) * block_rows * width * width,
            transcendentals=(fan + 1) * block_rows * width,
            bytes_accessed=24 * block_rows * width * 2,
        ),
        name="forward_layer",
    )(*operands)


def backward_kernel(parts, mode, *refs):
    refs = list(refs)
    slots = refs.pop(0)
    if mode != "first":
        returned = [refs.pop(0) for _ in range(3)]
        head = refs.pop(0)
    if mode != "second":
        grad_part = refs.pop(0)
    low, kept, message, mix, out, weights, gains = refs[:7]
    refs = refs[7:]
    if mode != "first":
        sent_grad = refs.pop(0)
        grad_full = refs.pop(0)
    (slot_grad, grad_gains, grad_message, edge_hidden, grad_mix, grad_out, grad_own, hidden) = refs[
        :8
    ]
    sum_even, sum_odd, spread = refs[8:]
    step = pl.program_id(0)
    rows, width = low.shape
    fan = kept.shape[0]
    block_rows = slot_grad.shape[1]

    @pl.when(step == 0)
    def _():
        sum_even[...] = jnp.zeros_like(sum_even)
        sum_odd[...] = jnp.zeros_like(sum_odd)
        grad_gains[...] = jnp.zeros_like(grad_gains)

    if mode == "first":
        grad_new = grad_part[...]
    else:
        sent_low = (
            returned[0][...].astype(WIDE)
            + returned[1][...].reshape(rows, width).astype(WIDE)
            + returned[2][...].astype(WIDE)
        ).astype(LOW)
        sent_grad[...] = sent_low
        grad_new = product_right(sent_low, head[0])
        if mode == "third":
            grad_new = grad_part[...] + grad_new
        grad_full[...] = grad_new
    target_low = low[...]
    out_unit, out_scale = normalize(out[...])
    gain_two = jnp.sum(grad_new * out_unit, axis=0, keepdims=True)
    out_low = normal_back(grad_new * gains[1:2, :], out_unit, out_scale).astype(LOW)
    grad_out[...] = out_low
    node_mix = mix[...]
    gate = sigmoid(node_mix)
    hidden[...] = (node_mix * gate).astype(LOW)
    mix_low = (
        product_right(out_low, weights[5]) * (gate * (1.0 + node_mix * (1.0 - gate)))
    ).astype(LOW)
    grad_mix[...] = mix_low
    grad_sum = product_right(mix_low, weights[4])
    own_term = product(target_low, weights[1])
    grad_unit = grad_sum * gains[0:1, :]
    unit_total = jnp.zeros((rows, width), WIDE)
    own_total = jnp.zeros((rows, width), WIDE)
    for k in range(fan):
        unit_rows, inv_scale = normalize(message[k])
        unit_total = unit_total + unit_rows
        message_low = normal_back(grad_unit, unit_rows, inv_scale).astype(LOW)
        grad_message[k] = message_low
        pre_edge = kept[k].astype(WIDE) + own_term
        edge_gate = sigmoid(pre_edge)
        edge_hidden[k] = (pre_edge * edge_gate).astype(LOW)
        grad_pre = product_right(message_low, weights[2]) * (
            edge_gate * (1.0 + pre_edge * (1.0 - edge_gate))
        )
        own_total = own_total + grad_pre
        fold_rows(spread, k * rows, rows, grad_pre)
    gain_one = jnp.sum(grad_sum * unit_total, axis=0, keepdims=True)
    grad_gains[...] += jnp.concatenate([gain_one, gain_two], axis=0)
    grad_own[...] = own_total.astype(LOW)

    for k in range(fan):

        def add(trip, carry):
            for lane in range(UNROLL // 2):
                places, values = [], []
                for store in (sum_even, sum_odd):
                    row = (trip * (UNROLL // 2) + lane) * 2 + len(places)
                    slot = slots[k * block_rows + step * rows + row]
                    place = pl.ds(pl.multiple_of(slot * parts, parts), parts)
                    value = spread[pl.ds(pl.multiple_of((k * rows + row) * parts, parts), parts), :]
                    places.append(place)
                    values.append(store[place, :] + value)
                sum_even[places[0], :] = values[0]
                sum_odd[places[1], :] = values[1]
            return carry

        lax.fori_loop(0, rows // UNROLL, add, 0)

    @pl.when(step == pl.num_programs(0) - 1)
    def _():
        for index in range(3):
            base = index * block_rows
            slot_grad[index] = (
                unfold_rows(sum_even, base, block_rows, parts)
                + unfold_rows(sum_odd, base, block_rows, parts)
            ).astype(LOW)


def backward_layer(slots, above, grad_part, stored, weights, gains):
    target_low, kept, message, mix, out = stored
    block_rows, width = target_low.shape
    fan = kept.shape[0]
    parts = width // LANES
    rows = BACKWARD_ROWS
    tile = tiled(rows, width)
    fan_tile = fanned(fan, rows, width)
    in_specs = [pl.BlockSpec(memory_space=pltpu.SMEM)]
    operands = [slots]
    out_specs, out_shape = [], []
    shape = functools.partial(jax.ShapeDtypeStruct, (block_rows, width))
    fan_shape = functools.partial(jax.ShapeDtypeStruct, (fan, block_rows, width))
    mode = "first" if above is None else ("second" if grad_part is None else "third")
    if above is not None:
        from_before, slot_grad, from_after, head = above
        in_specs += [
            tile,
            pl.BlockSpec((1, rows, width), lambda step: (1, step, 0)),
            tile,
            matrix_spec(head[1], 1, width),
        ]
        operands += [from_before, slot_grad, from_after, head[0]]
        out_specs += [tile, tile]
        out_shape += [shape(LOW), shape(WIDE)]
    if grad_part is not None:
        in_specs += [tile]
        operands += [grad_part]
    in_specs += [tile, fan_tile, fan_tile, tile, tile]
    in_specs += [matrix_spec(weights[1], 6, width), whole(gains.shape)]
    operands += [target_low, kept, message, mix, out, weights[0], gains]
    out_specs += [
        whole((3, block_rows, width)),
        whole((2, width)),
        fan_tile,
        fan_tile,
        tile,
        tile,
        tile,
        tile,
    ]
    out_shape += [
        jax.ShapeDtypeStruct((3, block_rows, width), LOW),
        jax.ShapeDtypeStruct((2, width), WIDE),
        fan_shape(LOW),
        fan_shape(LOW),
        shape(LOW),
        shape(LOW),
        shape(LOW),
        shape(LOW),
    ]
    results = pl.pallas_call(
        functools.partial(backward_kernel, parts, mode),
        grid=(block_rows // rows,),
        in_specs=in_specs,
        out_specs=out_specs,
        out_shape=out_shape,
        scratch_shapes=[
            pltpu.VMEM((3 * block_rows * parts, LANES), WIDE),
            pltpu.VMEM((3 * block_rows * parts, LANES), WIDE),
            pltpu.VMEM((fan * rows * parts, LANES), WIDE),
        ],
        compiler_params=pltpu.CompilerParams(vmem_limit_bytes=VMEM_BYTES),
        cost_estimate=pl.CostEstimate(
            flops=2 * (fan + 4) * block_rows * width * width,
            transcendentals=(fan + 1) * block_rows * width,
            bytes_accessed=24 * block_rows * width * 2,
        ),
        name="backward_layer",
    )(*operands)
    if above is None:
        return (None, grad_part, *results)
    return tuple(results)


def deal(self_id, sums, outs):
    keep, send = outs
    share = keep.shape[1] // sums.shape[0]

    def move(node, carry):
        for core, out in enumerate((keep, send)):
            place = pl.multiple_of(((2 * node + core) ^ self_id[0]) * share, share)
            for index in range(sums.shape[0]):
                out[node, index * share : (index + 1) * share, :] = sums[
                    index, pl.ds(place, share), :
                ].astype(out.dtype)
        return carry

    lax.fori_loop(0, keep.shape[0], move, 0)


def weight_kernel(has_above, needs_target, direct, *refs):
    refs = list(refs)
    if direct:
        self_id = refs.pop(0)
    if has_above:
        source, sent_grad = refs[:2]
        refs = refs[2:]
    else:
        extra = refs.pop(0)
    low, aggregate, edge_hidden, grad_message, grad_mix, grad_out, grad_own, hidden = refs[:8]
    refs = refs[8:]
    if needs_target:
        grad_new, weights = refs[:2]
        grad_part = refs[2]
        refs = refs[3:]
    outs, sums = (refs[:2], refs[2]) if direct else (None, refs[0])
    step = pl.program_id(0)
    fan = edge_hidden.shape[0]

    @pl.when(step == 0)
    def _():
        sums[...] = jnp.zeros_like(sums)
        if not has_above:
            sums[0] = extra[...]

    target_low = low[...]
    mix_low = grad_mix[...]
    own_low = grad_own[...]
    if has_above:
        sums[0] += product_left(source[...], sent_grad[...])
    sums[1] += product_left(target_low, own_low)
    for k in range(fan):
        sums[2] += product_left(edge_hidden[k], grad_message[k])
    sums[3] += product_left(target_low, mix_low)
    sums[4] += product_left(aggregate[...], mix_low)
    sums[5] += product_left(hidden[...], grad_out[...])
    if needs_target:
        grad_part[...] = (
            grad_new[...] + product_right(own_low, weights[1]) + product_right(mix_low, weights[3])
        )
    if direct:

        @pl.when(step == pl.num_programs(0) - 1)
        def _():
            deal(self_id, sums, outs)


def share_outputs(count, width, device_count):
    shape = (device_count // 2, count * (width // device_count), width)
    return (
        [whole(shape)] * 2,
        [jax.ShapeDtypeStruct(shape, WIDE), jax.ShapeDtypeStruct(shape, SEND)],
    )


def weight_layer(self_id, device_count, above, extra, low, aggregate, back, grad_new, weights):
    block_rows, width = low.shape
    rows = WEIGHT_ROWS
    fan = back[0].shape[0]
    tile = tiled(rows, width)
    fan_tile = fanned(fan, rows, width)
    in_specs, operands = [], []
    direct = self_id is not None
    if direct:
        in_specs += [pl.BlockSpec(memory_space=pltpu.SMEM)]
        operands += [self_id]
    if above is not None:
        in_specs += [tile, tile]
        operands += list(above)
    else:
        in_specs += [whole((width, width))]
        operands += [extra]
    in_specs += [tile, tile, fan_tile, fan_tile, tile, tile, tile, tile]
    operands += [low, aggregate, *back]
    out_specs, out_shape, scratch = [], [], []
    if grad_new is not None:
        in_specs += [tile, matrix_spec(weights[1], 6, width)]
        operands += [grad_new, weights[0]]
        out_specs += [tile]
        out_shape += [jax.ShapeDtypeStruct((block_rows, width), WIDE)]
    if direct:
        specs, shapes = share_outputs(6, width, device_count)
        out_specs += specs
        out_shape += shapes
        scratch = [pltpu.VMEM((6, width, width), WIDE)]
    else:
        out_specs += [whole((6, width, width))]
        out_shape += [jax.ShapeDtypeStruct((6, width, width), WIDE)]
    results = pl.pallas_call(
        functools.partial(weight_kernel, above is not None, grad_new is not None, direct),
        grid=(block_rows // rows,),
        in_specs=in_specs,
        out_specs=out_specs,
        out_shape=out_shape,
        scratch_shapes=scratch,
        compiler_params=pltpu.CompilerParams(vmem_limit_bytes=VMEM_BYTES),
        cost_estimate=pl.CostEstimate(
            flops=2 * (fan + 6) * block_rows * width * width,
            transcendentals=0,
            bytes_accessed=24 * block_rows * width,
        ),
        name="weight_layer",
    )(*operands)
    if grad_new is None:
        return (None, results)
    return (results[0], results[1:])


def embed_kernel(pieces_count, *refs):
    self_id = refs[0]
    pieces = refs[1 : 1 + pieces_count]
    before, middle, after = refs[1 + pieces_count : 4 + pieces_count]
    weights, latent, latent_low, sent_before, sent_middle, sent_after, table = refs[
        4 + pieces_count :
    ]
    count, width = weights.shape[0], weights.shape[1]
    high = pieces[0].shape[0]
    share = width // (high * pieces_count)

    @pl.when(pl.program_id(0) == 0)
    def _():
        for index, piece in enumerate(pieces):
            core, low_digit = index // (pieces_count // 2), index % (pieces_count // 2)

            def move(digit, carry, piece=piece, core=core, low_digit=low_digit):
                relative = digit * pieces_count + low_digit * 2 + core
                place = pl.multiple_of((relative ^ self_id[0]) * share, share)
                for j in range(count):
                    weights[j, pl.ds(place, share), :] = piece[digit, j * share : (j + 1) * share, :]
                table[pl.ds(place, share), :] = piece[digit, count * share : (count + 1) * share, :]
                return carry

            lax.fori_loop(0, high, move, 0)

    for block, sent in ((before, sent_before), (middle, sent_middle), (after, sent_after)):
        wide = product_right(block[...], table[...])
        low = wide.astype(LOW)
        sent[...] = product(low, weights[0]).astype(LOW)
        if block is middle:
            latent[...] = wide
            latent_low[...] = low


def embed(self_id, pieces, blocks):
    block_rows, width = blocks[1].shape
    rows = WEIGHT_ROWS
    tile = tiled(rows, width)
    shape = functools.partial(jax.ShapeDtypeStruct, (block_rows, width))
    return pl.pallas_call(
        functools.partial(embed_kernel, len(pieces)),
        grid=(block_rows // rows,),
        in_specs=[pl.BlockSpec(memory_space=pltpu.SMEM)]
        + [whole(piece.shape) for piece in pieces]
        + [tile] * 3,
        out_specs=[whole((6, width, width))] + [tile] * 5,
        out_shape=[jax.ShapeDtypeStruct((6, width, width), LOW), shape(WIDE)] + [shape(LOW)] * 4,
        scratch_shapes=[pltpu.VMEM((width, width), LOW)],
        compiler_params=pltpu.CompilerParams(vmem_limit_bytes=VMEM_BYTES),
        cost_estimate=pl.CostEstimate(
            flops=12 * block_rows * width * width,
            transcendentals=0,
            bytes_accessed=24 * block_rows * width,
        ),
        name="embed",
    )(self_id, *pieces, *blocks)


def tail_kernel(self_id, before, middle, after, latent_low, inputs, grad_grid, head, misc, *refs):
    keep, send, sums = refs
    step = pl.program_id(0)
    rows, width = inputs.shape
    share = misc.shape[1]

    @pl.when(step == 0)
    def _():
        sums[...] = jnp.zeros_like(sums)

    sent_low = (
        before[...].astype(WIDE)
        + middle[...].reshape(rows, width).astype(WIDE)
        + after[...].astype(WIDE)
    ).astype(LOW)
    grad_low = (grad_grid[...] + product_right(sent_low, head[0])).astype(LOW)
    sums[0] += product_left(latent_low[...], sent_low)
    sums[1] += product_left(grad_low, inputs[...])

    @pl.when(step == pl.num_programs(0) - 1)
    def _():
        size = sums.shape[0] * (width // misc.shape[0])
        main = [out.at[:, 0:size, :] for out in (keep, send)]
        deal(self_id, sums, main)

        def move(node, carry):
            for core, out in enumerate((keep, send)):
                out[node, size : size + share, :] = misc[(2 * node + core) ^ self_id[0]].astype(
                    out.dtype
                )
            return carry

        lax.fori_loop(0, keep.shape[0], move, 0)


def tail_layer(self_id, from_before, slot_grad, from_after, latent_low, inputs, grad_grid, head, misc):
    block_rows, width = inputs.shape
    device_count = misc.shape[0]
    rows = WEIGHT_ROWS
    tile = tiled(rows, width)
    shape = (device_count // 2, 2 * (width // device_count) + misc.shape[1], width)
    return pl.pallas_call(
        tail_kernel,
        grid=(block_rows // rows,),
        in_specs=[
            pl.BlockSpec(memory_space=pltpu.SMEM),
            tile,
            pl.BlockSpec((1, rows, width), lambda step: (1, step, 0)),
            tile,
            tile,
            tile,
            tile,
            matrix_spec(head[1], 1, width),
            whole(misc.shape),
        ],
        out_specs=[whole(shape)] * 2,
        out_shape=[jax.ShapeDtypeStruct(shape, WIDE), jax.ShapeDtypeStruct(shape, SEND)],
        scratch_shapes=[pltpu.VMEM((2, width, width), WIDE)],
        compiler_params=pltpu.CompilerParams(vmem_limit_bytes=VMEM_BYTES),
        cost_estimate=pl.CostEstimate(
            flops=6 * block_rows * width * width,
            transcendentals=0,
            bytes_accessed=24 * block_rows * width,
        ),
        name="tail_layer",
    )(self_id, from_before, slot_grad, from_after, latent_low, inputs, grad_grid, head[0], misc)


def combine_kernel(count, *refs):
    arrived, outs = refs[:count], refs[count:]
    for digit, out in enumerate(outs):
        total = arrived[0][0, digit].astype(WIDE)
        for part in arrived[1:]:
            total = total + part[0, digit].astype(WIDE)
        out[0] = total.astype(out.dtype)


def combine(arrived, radix):
    _, rows, width = arrived[0].shape
    rest = arrived[0].shape[0] // radix
    arrived = [part.reshape(rest, radix, rows, width) for part in arrived]
    spec = pl.BlockSpec((1, radix, rows, width), lambda step: (step, 0, 0, 0))
    shape = (rest, rows, width)
    return pl.pallas_call(
        functools.partial(combine_kernel, len(arrived)),
        grid=(rest,),
        in_specs=[spec] * len(arrived),
        out_specs=[pl.BlockSpec((1, rows, width), lambda step: (step, 0, 0))] * radix,
        out_shape=[jax.ShapeDtypeStruct(shape, WIDE)]
        + [jax.ShapeDtypeStruct(shape, SEND)] * (radix - 1),
        compiler_params=pltpu.CompilerParams(vmem_limit_bytes=VMEM_BYTES),
        cost_estimate=pl.CostEstimate(
            flops=rest * radix * rows * width * len(arrived),
            transcendentals=0,
            bytes_accessed=4 * rest * radix * rows * width * (len(arrived) + 1),
        ),
        name="combine",
    )(*arrived)


def swap(cells, count, mask):
    return lax.ppermute(cells, AXES, [(i, i ^ mask) for i in range(count)])


def spread_rows(packed, count):
    held = [packed]
    high = 4 * 2
    held += [swap(packed, count, digit * high) for digit in range(1, count // high)]
    column = jnp.stack(held)
    near = [column] + [swap(column, count, digit * 2) for digit in range(1, 4)]
    return near + [swap(piece, count, 1) for piece in near]


def gather_sum(keep, send, count):
    pieces = combine([keep, swap(send, count, 1)], 4)
    arrived = [pieces[0]] + [swap(pieces[digit], count, digit * 2) for digit in range(1, 4)]
    pieces = combine(arrived, count // 8)
    arrived = [pieces[0]]
    arrived += [swap(pieces[digit], count, digit * 8) for digit in range(1, count // 8)]
    total = arrived[0][0]
    for part in arrived[1:]:
        total = total + part[0].astype(WIDE)
    return total


def shift(cells, count, step):
    return lax.ppermute(cells, AXES, [(i, (i + step) % count) for i in range(count)])


def adamw_update(weight, moment_one, moment_two, gradient, step_value, decay_rate):
    new_one = BETA_ONE * moment_one + (1.0 - BETA_ONE) * gradient
    new_two = BETA_TWO * moment_two + (1.0 - BETA_TWO) * gradient * gradient
    correct_one = 1.0 - jnp.power(BETA_ONE, step_value)
    correct_two = 1.0 - jnp.power(BETA_TWO, step_value)
    direction = new_one / correct_one / (jnp.sqrt(new_two / correct_two) + ADAM_EPS)
    return (new_one, new_two, weight - LEARN_RATE * (direction + decay_rate * weight))


def shards(
    grid_inputs,
    mesh_static,
    targets,
    area_weight,
    valid_rows,
    encoder_lists,
    mesh_lists,
    decoder_lists,
    step_count,
    w_in,
    moment_in,
    square_in,
    w_layers,
    moment_layers,
    square_layers,
    norm_gains,
    moment_gains,
    square_gains,
    w_out,
    moment_out,
    square_out,
):
    row_count = grid_inputs.shape[0]
    layer_total = w_layers.shape[0]
    device_count = lax.axis_size(AXES)
    width = mesh_static.shape[1]
    share = w_layers.shape[2]
    channels, outputs = w_in.shape[0], w_out.shape[1]
    direct = share == 16 and device_count % 8 == 0 and device_count & (device_count - 1) == 0
    slot_lists = [encoder_lists.T.reshape(-1)]
    slot_lists += [mesh_lists.T.reshape(-1)] * (layer_total - 2)
    slot_lists += [decoder_lists.T.reshape(-1)]
    if direct:
        self_id = lax.axis_index(AXES).astype(jnp.int32)
        order = jnp.arange(device_count, dtype=jnp.int32) ^ self_id
        self_id = self_id.reshape(1)
        inputs = jnp.pad(grid_inputs, ((0, 0), (0, width - channels)))
        flat_gains = norm_gains.astype(LOW).reshape(1, -1)
        packed = jnp.concatenate(
            [
                w_layers[0].astype(LOW).reshape(-1, width),
                jnp.pad(w_in.astype(LOW).T, ((0, 0), (0, width - channels))),
                jnp.pad(flat_gains, ((0, 7), (0, width - flat_gains.shape[1]))),
            ],
            axis=0,
        )
        rest = jnp.concatenate(
            [
                w_layers[2:].astype(LOW).reshape(-1, share, width),
                jnp.pad(w_out.astype(LOW), ((0, 0), (0, width - outputs)))[None],
            ],
            axis=0,
        )
        input_blocks = (shift(inputs, device_count, 1), inputs, shift(inputs, device_count, -1))
        pieces = spread_rows(packed, device_count)
        second = lax.all_gather(w_layers[1].astype(LOW), AXES, axis=1, tiled=True)
        rest = lax.all_gather(rest, AXES, axis=1, tiled=True)
        first, grid_latent, grid_start, *blocks = embed(self_id, pieces, input_blocks)
        weights = [(first, 0), (second, 0)]
        weights += [(rest, 6 * layer_id) for layer_id in range(layer_total - 2)]
        table_out = rest[6 * (layer_total - 2), :, :outputs]
        gain_rows = jnp.stack(pieces)[:, :, packed.shape[0] - 8, : flat_gains.shape[1]]
        gain_rows = gain_rows.reshape(2, 4, device_count // 8, -1).transpose(2, 1, 0, 3)
        gain_rows = gain_rows.reshape(device_count, -1)[order]
        gains = gain_rows.reshape(device_count, layer_total, 2, share).transpose(1, 2, 0, 3)
        gains = gains.reshape(layer_total, 2, width).astype(WIDE)
    else:
        self_id = None
        table_in = lax.all_gather(w_in.astype(LOW), AXES, axis=1, tiled=True)
        table_out = lax.all_gather(w_out.astype(LOW), AXES, axis=0, tiled=True)
        matrices = lax.all_gather(w_layers.astype(LOW), AXES, axis=2, tiled=True)
        matrices = matrices.reshape(-1, width, width)
        weights = [(matrices, 6 * layer_id) for layer_id in range(layer_total)]
        gains = lax.all_gather(norm_gains.astype(LOW), AXES, axis=2, tiled=True).astype(WIDE)
        grid_latent = product(grid_inputs, table_in)
        grid_start = grid_latent.astype(LOW)
        sent = product(grid_start, matrices[0]).astype(LOW)
        blocks = (shift(sent, device_count, 1), sent, shift(sent, device_count, -1))
    target, target_low = mesh_static, mesh_static
    stored_list = []
    for layer_id in range(layer_total):
        last_layer = layer_id == layer_total - 1
        if last_layer:
            source_low = target_low
            target, target_low = grid_latent, grid_start
        else:
            source_low = grid_start if layer_id == 0 else target_low
        results = forward_layer(
            slot_lists[layer_id],
            blocks,
            target_low,
            target,
            weights[layer_id],
            None if last_layer else weights[layer_id + 1],
            gains[layer_id],
        )
        if last_layer:
            grid_low, kept, message, aggregate, mix, out = results
        else:
            sent, updated, updated_low, kept, message, aggregate, mix, out = results
            blocks = (shift(sent, device_count, 1), sent, shift(sent, device_count, -1))
        stored_list.append((source_low, (target_low, kept, message, mix, out), aggregate))
        if not last_layer:
            target, target_low = updated, updated_low
    prediction = product(grid_low, table_out)
    local_rows = jnp.arange(row_count, dtype=jnp.int32)
    weight_rows = area_weight * (local_rows < valid_rows[0]).astype(WIDE)
    error_rows = prediction - targets
    loss_scale = 1.0 / (row_count * device_count * prediction.shape[1])
    loss_local = jnp.sum(weight_rows[:, None] * error_rows * error_rows) * loss_scale
    grad_pred = (2.0 * loss_scale * weight_rows[:, None] * error_rows).astype(LOW)
    grad_table_out = product_left(grid_low, grad_pred)
    grad_part = product_right(grad_pred, table_out)
    extra = jnp.pad(grad_table_out, ((0, 0), (0, width - outputs)))
    grad_grid = None
    above, above_source = None, None
    layer_grads = [None] * layer_total
    gain_grads = [None] * layer_total
    for layer_id in reversed(range(layer_total)):
        source_low, stored, aggregate = stored_list[layer_id]
        sent_grad, grad_new, slot_grad, grad_gain, *back = backward_layer(
            slot_lists[layer_id], above, grad_part, stored, weights[layer_id], gains[layer_id]
        )
        from_before = shift(slot_grad[2], device_count, 1)
        from_after = shift(slot_grad[0], device_count, -1)
        back = [back[1], back[0], *back[2:]]
        grad_part, sums = weight_layer(
            self_id,
            device_count,
            None if above is None else (above_source, sent_grad),
            extra,
            stored[0],
            aggregate,
            back,
            None if layer_id == 0 else grad_new,
            weights[layer_id],
        )
        if direct:
            total = gather_sum(*sums, device_count)
            layer_grads[layer_id] = total.reshape(6, share, width)
        else:
            layer_grads[layer_id] = sums[0]
        gain_grads[layer_id] = grad_gain
        if layer_id == layer_total - 1:
            grad_grid, grad_part = grad_part, None
        above = (from_before, slot_grad, from_after, weights[layer_id])
        above_source = source_low
    if direct:
        misc = jnp.stack(gain_grads).reshape(-1, device_count, share).transpose(1, 0, 2)
        misc = misc.reshape(device_count, -1)
        misc = jnp.concatenate(
            [misc, jnp.broadcast_to(loss_local.reshape(1, 1), (device_count, 1))], axis=1
        )
        misc = jnp.pad(misc[:, None, :], ((0, 0), (0, 7), (0, width - misc.shape[1])))
        sums = tail_layer(
            self_id,
            from_before,
            slot_grad,
            from_after,
            grid_start,
            inputs,
            grad_grid,
            weights[0],
            misc,
        )
        total = gather_sum(*sums, device_count)
        grad_zero = total[:share]
        grad_in = total[share : 2 * share, :channels].T
        size = layer_total * 2 * share
        grad_gain_all = total[2 * share, :size].reshape(layer_total, 2, share)
        loss_value = total[2 * share, size]
        grad_out = layer_grads[-1][0, :, :outputs]
    else:
        loss_value = lax.psum(loss_local, AXES)
        sent_grad = (
            from_before.astype(WIDE) + slot_grad[1].astype(WIDE) + from_after.astype(WIDE)
        ).astype(LOW)
        grad_zero = product_left(above_source, sent_grad)
        grad_grid = grad_grid + product_right(sent_grad, matrices[0])
        grad_table_in = product_left(grid_inputs, grad_grid.astype(LOW))
        grad_in = lax.psum_scatter(grad_table_in, AXES, scatter_dimension=1, tiled=True)
        grad_out = lax.psum_scatter(grad_table_out, AXES, scatter_dimension=0, tiled=True)
        grad_gain_all = lax.psum_scatter(
            jnp.stack(gain_grads), AXES, scatter_dimension=2, tiled=True
        )
    grad_layers = [grad_zero[None]]
    for layer_id in range(layer_total):
        grad_layers += [layer_grads[layer_id][1:]]
        if layer_id < layer_total - 1:
            grad_layers += [layer_grads[layer_id][0:1]]
    grad_layers = jnp.concatenate(grad_layers, axis=0)
    grad_layers = grad_layers.reshape(layer_total, 6, *grad_layers.shape[1:])
    if not direct:
        grad_layers = lax.psum_scatter(grad_layers, AXES, scatter_dimension=2, tiled=True)
    step_value = step_count[0].astype(WIDE)
    one_in, two_in, new_in = adamw_update(
        w_in, moment_in, square_in, grad_in, step_value, DECAY_RATE
    )
    one_layers, two_layers, new_layers = adamw_update(
        w_layers, moment_layers, square_layers, grad_layers, step_value, DECAY_RATE
    )
    one_gains, two_gains, new_gains = adamw_update(
        norm_gains, moment_gains, square_gains, grad_gain_all, step_value, 0.0
    )
    one_out, two_out, new_out = adamw_update(
        w_out, moment_out, square_out, grad_out, step_value, DECAY_RATE
    )
    return (
        loss_value,
        one_in,
        two_in,
        new_in,
        one_layers,
        two_layers,
        new_layers,
        one_gains,
        two_gains,
        new_gains,
        one_out,
        two_out,
        new_out,
    )


def solution(mesh):
    rows = P(AXES, None)
    layers = P(None, None, AXES, None)
    gains = P(None, None, AXES)
    columns = P(None, AXES)
    in_specs = (rows, rows, rows, P(AXES), P(AXES), rows, rows, rows, P())
    in_specs += (columns,) * 3 + (layers,) * 3 + (gains,) * 3 + (rows,) * 3
    out_specs = (P(),) + (columns,) * 3 + (layers,) * 3 + (gains,) * 3 + (rows,) * 3
    return jax.shard_map(shards, mesh=mesh, in_specs=in_specs, out_specs=out_specs, check_vma=False)
```

```python
import functools

import jax
import jax.numpy as jnp
from jax import lax
from jax.experimental import pallas as pl
from jax.experimental.pallas import tpu as pltpu
from jax.sharding import PartitionSpec as P

EPS_NORM = 1e-05
BETA_ONE = 0.5
BETA_TWO = 0.5
ADAM_EPS = 1e-08
LEARN_RATE = 0.04
DECAY_RATE = 0.1

AXES = ("nodes", "shard")
LANES = 128
FORWARD_ROWS = 256
BACKWARD_ROWS = 256
WEIGHT_ROWS = 256
UNROLL = 32
VMEM_BYTES = 56 << 20
LOW = jnp.bfloat16
WIDE = jnp.float32
SEND = jnp.bfloat16


def product(left, right):
    return jnp.dot(left, right, preferred_element_type=WIDE)


def product_left(left, right):
    return lax.dot_general(left, right, (((0,), (0,)), ((), ())), preferred_element_type=WIDE)


def product_right(left, right):
    return lax.dot_general(left, right, (((1,), (1,)), ((), ())), preferred_element_type=WIDE)


def normalize(tensor):
    centre = tensor - jnp.mean(tensor, axis=-1, keepdims=True)
    inv_scale = lax.rsqrt(jnp.mean(centre * centre, axis=-1, keepdims=True) + EPS_NORM)
    return (centre * inv_scale, inv_scale)


def normal_back(grad_unit, unit_rows, inv_scale):
    centred = grad_unit - jnp.mean(grad_unit, axis=-1, keepdims=True)
    return inv_scale * (
        centred - unit_rows * jnp.mean(grad_unit * unit_rows, axis=-1, keepdims=True)
    )


def silu_parts(tensor):
    half = 0.5 * tensor
    return half, jnp.tanh(half)


def silu(tensor):
    half, bend = silu_parts(tensor)
    return half * (1.0 + bend)


def fold_rows(store, base, rows, tensor):
    parts = tensor.shape[1] // LANES
    for part in range(parts):
        store[pl.ds(base * parts + part, rows, stride=parts), :] = tensor[
            :, part * LANES : (part + 1) * LANES
        ]


def unfold_rows(store, base, rows, parts):
    return jnp.concatenate(
        [store[pl.ds(base * parts + part, rows, stride=parts), :] for part in range(parts)],
        axis=1,
    )


def forward_kernel(parts, has_next, *refs):
    if has_next:
        (slots, before, middle, after, low, wide, weights, gains, head) = refs[:9]
        (sent, update, update_low, kept, message, aggregate, mix, out) = refs[9:17]
        window, picked, hidden = refs[17:]
    else:
        (slots, before, middle, after, low, wide, weights, gains) = refs[:8]
        (update_low, kept, message, aggregate, mix, out) = refs[8:14]
        window, picked, hidden = refs[14:]
    step = pl.program_id(0)
    block_rows = before.shape[0]
    rows, width = low.shape
    fan = kept.shape[0]

    @pl.when(step == 0)
    def _():
        for index, block in enumerate((before, middle, after)):
            fold_rows(window, index * block_rows, block_rows, block[...].astype(WIDE))

    for k in range(fan):

        def pick(trip, carry):
            for lane in range(UNROLL):
                row = trip * UNROLL + lane
                slot = slots[k * block_rows + step * rows + row]
                picked[pl.ds(pl.multiple_of((k * rows + row) * parts, parts), parts), :] = window[
                    pl.ds(pl.multiple_of(slot * parts, parts), parts), :
                ]
            return carry

        lax.fori_loop(0, rows // UNROLL, pick, 0)
    target_low = low[...]
    own_term = product(target_low, weights[1])
    for k in range(fan):
        sender = unfold_rows(picked, k * rows, rows, parts)
        kept[k] = sender.astype(LOW)
        hidden[k * rows : (k + 1) * rows, :] = silu(sender + own_term).astype(LOW)
    message[...] = product(hidden[...], weights[2]).reshape(fan, rows, width)
    total = normalize(message[0])[0]
    for k in range(1, fan):
        total = total + normalize(message[k])[0]
    total_low = (total * gains[0:1, :]).astype(LOW)
    aggregate[...] = total_low
    node_mix = product(target_low, weights[3]) + product(total_low, weights[4])
    mix[...] = node_mix
    node_out = product(silu(node_mix).astype(LOW), weights[5])
    out[...] = node_out
    updated = wide[...].astype(WIDE) + normalize(node_out)[0] * gains[1:2, :]
    updated_low = updated.astype(LOW)
    update_low[...] = updated_low
    if has_next:
        update[...] = updated
        sent[...] = product(updated_low, head[0]).astype(LOW)


def whole(shape):
    zeros = (0,) * len(shape)
    return pl.BlockSpec(shape, lambda step: zeros)


def matrix_spec(first, count, width):
    return pl.BlockSpec((count, width, width), lambda step: (first // count, 0, 0))


def tiled(rows, width):
    return pl.BlockSpec((rows, width), lambda step: (step, 0))


def fanned(fan, rows, width):
    return pl.BlockSpec((fan, rows, width), lambda step: (0, step, 0))


def forward_layer(slots, blocks, target_low, target, weights, next_weights, gains):
    block_rows, width = target_low.shape
    fan = slots.shape[0] // block_rows
    parts = width // LANES
    rows = FORWARD_ROWS
    has_next = next_weights is not None
    shape = functools.partial(jax.ShapeDtypeStruct, (block_rows, width))
    fan_shape = functools.partial(jax.ShapeDtypeStruct, (fan, block_rows, width))
    tile = tiled(rows, width)
    in_specs = [pl.BlockSpec(memory_space=pltpu.SMEM)]
    in_specs += [whole((block_rows, width))] * 3 + [tile, tile]
    in_specs += [matrix_spec(weights[1], 6, width), whole(gains.shape)]
    out_specs = [tile, fanned(fan, rows, width), fanned(fan, rows, width), tile, tile, tile]
    out_shape = [shape(LOW), fan_shape(LOW), fan_shape(WIDE), shape(LOW), shape(WIDE), shape(WIDE)]
    operands = [slots, *blocks, target_low, target, weights[0], gains]
    if has_next:
        in_specs += [matrix_spec(next_weights[1], 1, width)]
        operands += [next_weights[0]]
        out_specs = [tile, tile] + out_specs
        out_shape = [shape(LOW), shape(WIDE)] + out_shape
    return pl.pallas_call(
        functools.partial(forward_kernel, parts, has_next),
        grid=(block_rows // rows,),
        in_specs=in_specs,
        out_specs=out_specs,
        out_shape=out_shape,
        scratch_shapes=[
            pltpu.VMEM((3 * block_rows * parts, LANES), WIDE),
            pltpu.VMEM((fan * rows * parts, LANES), WIDE),
            pltpu.VMEM((fan * rows, width), LOW),
        ],
        compiler_params=pltpu.CompilerParams(vmem_limit_bytes=VMEM_BYTES),
        cost_estimate=pl.CostEstimate(
            flops=2 * (fan + 5) * block_rows * width * width,
            transcendentals=(fan + 1) * block_rows * width,
            bytes_accessed=24 * block_rows * width * 2,
        ),
        name="forward_layer",
    )(*operands)


def backward_kernel(parts, mode, *refs):
    refs = list(refs)
    slots = refs.pop(0)
    if mode != "first":
        returned = [refs.pop(0) for _ in range(3)]
        head = refs.pop(0)
    if mode != "second":
        grad_part = refs.pop(0)
    low, kept, message, mix, out, weights, gains = refs[:7]
    refs = refs[7:]
    if mode != "first":
        sent_grad = refs.pop(0)
        grad_full = refs.pop(0)
    (slot_grad, grad_gains, grad_message, edge_hidden, grad_mix, grad_out, grad_own, hidden) = refs[
        :8
    ]
    sum_even, sum_odd, spread, grad_hidden = refs[8:]
    step = pl.program_id(0)
    rows, width = low.shape
    fan = kept.shape[0]
    block_rows = slot_grad.shape[1]

    @pl.when(step == 0)
    def _():
        sum_even[...] = jnp.zeros_like(sum_even)
        sum_odd[...] = jnp.zeros_like(sum_odd)
        grad_gains[...] = jnp.zeros_like(grad_gains)

    if mode == "first":
        grad_new = grad_part[...]
    else:
        sent_low = (
            returned[0][...].astype(WIDE)
            + returned[1][...].reshape(rows, width).astype(WIDE)
            + returned[2][...].astype(WIDE)
        ).astype(LOW)
        sent_grad[...] = sent_low
        grad_new = product_right(sent_low, head[0])
        if mode == "third":
            grad_new = grad_part[...] + grad_new
        grad_full[...] = grad_new
    target_low = low[...]
    out_unit, out_scale = normalize(out[...])
    gain_two = jnp.sum(grad_new * out_unit, axis=0, keepdims=True)
    out_low = normal_back(grad_new * gains[1:2, :], out_unit, out_scale).astype(LOW)
    grad_out[...] = out_low
    node_mix = mix[...]
    half, bend = silu_parts(node_mix)
    hidden[...] = (half * (1.0 + bend)).astype(LOW)
    mix_low = (
        product_right(out_low, weights[5]) * ((0.5 + 0.5 * bend) * (1.0 + half * (1.0 - bend)))
    ).astype(LOW)
    grad_mix[...] = mix_low
    grad_sum = product_right(mix_low, weights[4])
    own_term = product(target_low, weights[1])
    grad_unit = grad_sum * gains[0:1, :]
    unit_total = None
    for k in range(fan):
        unit_rows, inv_scale = normalize(message[k])
        unit_total = unit_rows if k == 0 else unit_total + unit_rows
        grad_message[k] = normal_back(grad_unit, unit_rows, inv_scale).astype(LOW)
    grad_hidden[...] = product_right(
        grad_message[...].reshape(fan * rows, width), weights[2]
    )
    own_total = None
    for k in range(fan):
        half, bend = silu_parts(kept[k].astype(WIDE) + own_term)
        edge_hidden[k] = (half * (1.0 + bend)).astype(LOW)
        grad_pre = grad_hidden[k * rows : (k + 1) * rows, :] * (
            (0.5 + 0.5 * bend) * (1.0 + half * (1.0 - bend))
        )
        own_total = grad_pre if k == 0 else own_total + grad_pre
        fold_rows(spread, k * rows, rows, grad_pre)
    gain_one = jnp.sum(grad_sum * unit_total, axis=0, keepdims=True)
    grad_gains[...] += jnp.concatenate([gain_one, gain_two], axis=0)
    grad_own[...] = own_total.astype(LOW)

    for k in range(fan):

        def add(trip, carry):
            for lane in range(UNROLL // 2):
                places, values = [], []
                for store in (sum_even, sum_odd):
                    row = (trip * (UNROLL // 2) + lane) * 2 + len(places)
                    slot = slots[k * block_rows + step * rows + row]
                    place = pl.ds(pl.multiple_of(slot * parts, parts), parts)
                    value = spread[pl.ds(pl.multiple_of((k * rows + row) * parts, parts), parts), :]
                    places.append(place)
                    values.append(store[place, :] + value)
                sum_even[places[0], :] = values[0]
                sum_odd[places[1], :] = values[1]
            return carry

        lax.fori_loop(0, rows // UNROLL, add, 0)

    @pl.when(step == pl.num_programs(0) - 1)
    def _():
        for index in range(3):
            base = index * block_rows
            slot_grad[index] = (
                unfold_rows(sum_even, base, block_rows, parts)
                + unfold_rows(sum_odd, base, block_rows, parts)
            ).astype(LOW)


def backward_layer(slots, above, grad_part, stored, weights, gains):
    target_low, kept, message, mix, out = stored
    block_rows, width = target_low.shape
    fan = kept.shape[0]
    parts = width // LANES
    rows = BACKWARD_ROWS
    tile = tiled(rows, width)
    fan_tile = fanned(fan, rows, width)
    in_specs = [pl.BlockSpec(memory_space=pltpu.SMEM)]
    operands = [slots]
    out_specs, out_shape = [], []
    shape = functools.partial(jax.ShapeDtypeStruct, (block_rows, width))
    fan_shape = functools.partial(jax.ShapeDtypeStruct, (fan, block_rows, width))
    mode = "first" if above is None else ("second" if grad_part is None else "third")
    if above is not None:
        from_before, slot_grad, from_after, head = above
        in_specs += [
            tile,
            pl.BlockSpec((1, rows, width), lambda step: (1, step, 0)),
            tile,
            matrix_spec(head[1], 1, width),
        ]
        operands += [from_before, slot_grad, from_after, head[0]]
        out_specs += [tile, tile]
        out_shape += [shape(LOW), shape(WIDE)]
    if grad_part is not None:
        in_specs += [tile]
        operands += [grad_part]
    in_specs += [tile, fan_tile, fan_tile, tile, tile]
    in_specs += [matrix_spec(weights[1], 6, width), whole(gains.shape)]
    operands += [target_low, kept, message, mix, out, weights[0], gains]
    out_specs += [
        whole((3, block_rows, width)),
        whole((2, width)),
        fan_tile,
        fan_tile,
        tile,
        tile,
        tile,
        tile,
    ]
    out_shape += [
        jax.ShapeDtypeStruct((3, block_rows, width), LOW),
        jax.ShapeDtypeStruct((2, width), WIDE),
        fan_shape(LOW),
        fan_shape(LOW),
        shape(LOW),
        shape(LOW),
        shape(LOW),
        shape(LOW),
    ]
    results = pl.pallas_call(
        functools.partial(backward_kernel, parts, mode),
        grid=(block_rows // rows,),
        in_specs=in_specs,
        out_specs=out_specs,
        out_shape=out_shape,
        scratch_shapes=[
            pltpu.VMEM((3 * block_rows * parts, LANES), WIDE),
            pltpu.VMEM((3 * block_rows * parts, LANES), WIDE),
            pltpu.VMEM((fan * rows * parts, LANES), WIDE),
            pltpu.VMEM((fan * rows, width), WIDE),
        ],
        compiler_params=pltpu.CompilerParams(vmem_limit_bytes=VMEM_BYTES),
        cost_estimate=pl.CostEstimate(
            flops=2 * (fan + 4) * block_rows * width * width,
            transcendentals=(fan + 1) * block_rows * width,
            bytes_accessed=24 * block_rows * width * 2,
        ),
        name="backward_layer",
    )(*operands)
    if above is None:
        return (None, grad_part, *results)
    return tuple(results)


def deal(self_id, sums, outs):
    keep, send = outs
    share = keep.shape[1] // sums.shape[0]

    def move(node, carry):
        for core, out in enumerate((keep, send)):
            place = pl.multiple_of(((2 * node + core) ^ self_id[0]) * share, share)
            for index in range(sums.shape[0]):
                out[node, index * share : (index + 1) * share, :] = sums[
                    index, pl.ds(place, share), :
                ].astype(out.dtype)
        return carry

    lax.fori_loop(0, keep.shape[0], move, 0)


def weight_kernel(has_above, needs_target, direct, *refs):
    refs = list(refs)
    if direct:
        self_id = refs.pop(0)
    if has_above:
        source, sent_grad = refs[:2]
        refs = refs[2:]
    else:
        extra = refs.pop(0)
    low, aggregate, edge_hidden, grad_message, grad_mix, grad_out, grad_own, hidden = refs[:8]
    refs = refs[8:]
    if needs_target:
        grad_new, weights = refs[:2]
        grad_part = refs[2]
        refs = refs[3:]
    outs, sums = (refs[:2], refs[2]) if direct else (None, refs[0])
    step = pl.program_id(0)
    fan = edge_hidden.shape[0]

    @pl.when(step == 0)
    def _():
        sums[...] = jnp.zeros_like(sums)
        if not has_above:
            sums[0] = extra[...]

    target_low = low[...]
    mix_low = grad_mix[...]
    own_low = grad_own[...]
    if has_above:
        sums[0] += product_left(source[...], sent_grad[...])
    sums[1] += product_left(target_low, own_low)
    for k in range(fan):
        sums[2] += product_left(edge_hidden[k], grad_message[k])
    sums[3] += product_left(target_low, mix_low)
    sums[4] += product_left(aggregate[...], mix_low)
    sums[5] += product_left(hidden[...], grad_out[...])
    if needs_target:
        grad_part[...] = (
            grad_new[...] + product_right(own_low, weights[1]) + product_right(mix_low, weights[3])
        )
    if direct:

        @pl.when(step == pl.num_programs(0) - 1)
        def _():
            deal(self_id, sums, outs)


def share_outputs(count, width, device_count):
    shape = (device_count // 2, count * (width // device_count), width)
    return (
        [whole(shape)] * 2,
        [jax.ShapeDtypeStruct(shape, WIDE), jax.ShapeDtypeStruct(shape, SEND)],
    )


def weight_layer(self_id, device_count, above, extra, low, aggregate, back, grad_new, weights):
    block_rows, width = low.shape
    rows = WEIGHT_ROWS
    fan = back[0].shape[0]
    tile = tiled(rows, width)
    fan_tile = fanned(fan, rows, width)
    in_specs, operands = [], []
    direct = self_id is not None
    if direct:
        in_specs += [pl.BlockSpec(memory_space=pltpu.SMEM)]
        operands += [self_id]
    if above is not None:
        in_specs += [tile, tile]
        operands += list(above)
    else:
        in_specs += [whole((width, width))]
        operands += [extra]
    in_specs += [tile, tile, fan_tile, fan_tile, tile, tile, tile, tile]
    operands += [low, aggregate, *back]
    out_specs, out_shape, scratch = [], [], []
    if grad_new is not None:
        in_specs += [tile, matrix_spec(weights[1], 6, width)]
        operands += [grad_new, weights[0]]
        out_specs += [tile]
        out_shape += [jax.ShapeDtypeStruct((block_rows, width), WIDE)]
    if direct:
        specs, shapes = share_outputs(6, width, device_count)
        out_specs += specs
        out_shape += shapes
        scratch = [pltpu.VMEM((6, width, width), WIDE)]
    else:
        out_specs += [whole((6, width, width))]
        out_shape += [jax.ShapeDtypeStruct((6, width, width), WIDE)]
    results = pl.pallas_call(
        functools.partial(weight_kernel, above is not None, grad_new is not None, direct),
        grid=(block_rows // rows,),
        in_specs=in_specs,
        out_specs=out_specs,
        out_shape=out_shape,
        scratch_shapes=scratch,
        compiler_params=pltpu.CompilerParams(vmem_limit_bytes=VMEM_BYTES),
        cost_estimate=pl.CostEstimate(
            flops=2 * (fan + 6) * block_rows * width * width,
            transcendentals=0,
            bytes_accessed=24 * block_rows * width,
        ),
        name="weight_layer",
    )(*operands)
    if grad_new is None:
        return (None, results)
    return (results[0], results[1:])


def embed_kernel(pieces_count, *refs):
    self_id = refs[0]
    pieces = refs[1 : 1 + pieces_count]
    before, middle, after = refs[1 + pieces_count : 4 + pieces_count]
    weights, latent, latent_low, sent_before, sent_middle, sent_after, table = refs[
        4 + pieces_count :
    ]
    count, width = weights.shape[0], weights.shape[1]
    high = pieces[0].shape[0]
    share = width // (high * pieces_count)

    @pl.when(pl.program_id(0) == 0)
    def _():
        for index, piece in enumerate(pieces):
            core, low_digit = index // (pieces_count // 2), index % (pieces_count // 2)

            def move(digit, carry, piece=piece, core=core, low_digit=low_digit):
                relative = digit * pieces_count + low_digit * 2 + core
                place = pl.multiple_of((relative ^ self_id[0]) * share, share)
                for j in range(count):
                    weights[j, pl.ds(place, share), :] = piece[digit, j * share : (j + 1) * share, :]
                table[pl.ds(place, share), :] = piece[digit, count * share : (count + 1) * share, :]
                return carry

            lax.fori_loop(0, high, move, 0)

    for block, sent in ((before, sent_before), (middle, sent_middle), (after, sent_after)):
        wide = product_right(block[...], table[...])
        low = wide.astype(LOW)
        sent[...] = product(low, weights[0]).astype(LOW)
        if block is middle:
            latent[...] = wide
            latent_low[...] = low


def embed(self_id, pieces, blocks):
    block_rows, width = blocks[1].shape
    rows = WEIGHT_ROWS
    tile = tiled(rows, width)
    shape = functools.partial(jax.ShapeDtypeStruct, (block_rows, width))
    return pl.pallas_call(
        functools.partial(embed_kernel, len(pieces)),
        grid=(block_rows // rows,),
        in_specs=[pl.BlockSpec(memory_space=pltpu.SMEM)]
        + [whole(piece.shape) for piece in pieces]
        + [tile] * 3,
        out_specs=[whole((6, width, width))] + [tile] * 5,
        out_shape=[jax.ShapeDtypeStruct((6, width, width), LOW), shape(WIDE)] + [shape(LOW)] * 4,
        scratch_shapes=[pltpu.VMEM((width, width), LOW)],
        compiler_params=pltpu.CompilerParams(vmem_limit_bytes=VMEM_BYTES),
        cost_estimate=pl.CostEstimate(
            flops=12 * block_rows * width * width,
            transcendentals=0,
            bytes_accessed=24 * block_rows * width,
        ),
        name="embed",
    )(self_id, *pieces, *blocks)


def tail_kernel(self_id, before, middle, after, latent_low, inputs, grad_grid, head, misc, *refs):
    keep, send, sums = refs
    step = pl.program_id(0)
    rows, width = inputs.shape
    share = misc.shape[1]

    @pl.when(step == 0)
    def _():
        sums[...] = jnp.zeros_like(sums)

    sent_low = (
        before[...].astype(WIDE)
        + middle[...].reshape(rows, width).astype(WIDE)
        + after[...].astype(WIDE)
    ).astype(LOW)
    grad_low = (grad_grid[...] + product_right(sent_low, head[0])).astype(LOW)
    sums[0] += product_left(latent_low[...], sent_low)
    sums[1] += product_left(grad_low, inputs[...])

    @pl.when(step == pl.num_programs(0) - 1)
    def _():
        size = sums.shape[0] * (width // misc.shape[0])
        main = [out.at[:, 0:size, :] for out in (keep, send)]
        deal(self_id, sums, main)

        def move(node, carry):
            for core, out in enumerate((keep, send)):
                out[node, size : size + share, :] = misc[(2 * node + core) ^ self_id[0]].astype(
                    out.dtype
                )
            return carry

        lax.fori_loop(0, keep.shape[0], move, 0)


def tail_layer(self_id, from_before, slot_grad, from_after, latent_low, inputs, grad_grid, head, misc):
    block_rows, width = inputs.shape
    device_count = misc.shape[0]
    rows = WEIGHT_ROWS
    tile = tiled(rows, width)
    shape = (device_count // 2, 2 * (width // device_count) + misc.shape[1], width)
    return pl.pallas_call(
        tail_kernel,
        grid=(block_rows // rows,),
        in_specs=[
            pl.BlockSpec(memory_space=pltpu.SMEM),
            tile,
            pl.BlockSpec((1, rows, width), lambda step: (1, step, 0)),
            tile,
            tile,
            tile,
            tile,
            matrix_spec(head[1], 1, width),
            whole(misc.shape),
        ],
        out_specs=[whole(shape)] * 2,
        out_shape=[jax.ShapeDtypeStruct(shape, WIDE), jax.ShapeDtypeStruct(shape, SEND)],
        scratch_shapes=[pltpu.VMEM((2, width, width), WIDE)],
        compiler_params=pltpu.CompilerParams(vmem_limit_bytes=VMEM_BYTES),
        cost_estimate=pl.CostEstimate(
            flops=6 * block_rows * width * width,
            transcendentals=0,
            bytes_accessed=24 * block_rows * width,
        ),
        name="tail_layer",
    )(self_id, from_before, slot_grad, from_after, latent_low, inputs, grad_grid, head[0], misc)


def combine_kernel(count, *refs):
    arrived, outs = refs[:count], refs[count:]
    for digit, out in enumerate(outs):
        total = arrived[0][0, digit].astype(WIDE)
        for part in arrived[1:]:
            total = total + part[0, digit].astype(WIDE)
        out[0] = total.astype(out.dtype)


def combine(arrived, radix):
    _, rows, width = arrived[0].shape
    rest = arrived[0].shape[0] // radix
    arrived = [part.reshape(rest, radix, rows, width) for part in arrived]
    spec = pl.BlockSpec((1, radix, rows, width), lambda step: (step, 0, 0, 0))
    shape = (rest, rows, width)
    return pl.pallas_call(
        functools.partial(combine_kernel, len(arrived)),
        grid=(rest,),
        in_specs=[spec] * len(arrived),
        out_specs=[pl.BlockSpec((1, rows, width), lambda step: (step, 0, 0))] * radix,
        out_shape=[jax.ShapeDtypeStruct(shape, WIDE)]
        + [jax.ShapeDtypeStruct(shape, SEND)] * (radix - 1),
        compiler_params=pltpu.CompilerParams(vmem_limit_bytes=VMEM_BYTES),
        cost_estimate=pl.CostEstimate(
            flops=rest * radix * rows * width * len(arrived),
            transcendentals=0,
            bytes_accessed=4 * rest * radix * rows * width * (len(arrived) + 1),
        ),
        name="combine",
    )(*arrived)


def swap(cells, count, mask):
    return lax.ppermute(cells, AXES, [(i, i ^ mask) for i in range(count)])


def spread_rows(packed, count):
    held = [packed]
    high = 4 * 2
    held += [swap(packed, count, digit * high) for digit in range(1, count // high)]
    column = jnp.stack(held)
    near = [column] + [swap(column, count, digit * 2) for digit in range(1, 4)]
    return near + [swap(piece, count, 1) for piece in near]


def shift(cells, count, step):
    return lax.ppermute(cells, AXES, [(i, (i + step) % count) for i in range(count)])


def fan_out(pieces, count, unit):
    return [pieces[0]] + [
        swap(pieces[digit], count, digit * unit) for digit in range(1, len(pieces))
    ]


def together(first, second):
    joined = lax.optimization_barrier((tuple(first), tuple(second)))
    return list(joined[0]), list(joined[1])


def add_up(arrived):
    total = arrived[0][0]
    for part in arrived[1:]:
        total = total + part[0].astype(WIDE)
    return total


def adamw_update(weight, moment_one, moment_two, gradient, step_value, decay_rate):
    new_one = BETA_ONE * moment_one + (1.0 - BETA_ONE) * gradient
    new_two = BETA_TWO * moment_two + (1.0 - BETA_TWO) * gradient * gradient
    correct_one = 1.0 - jnp.power(BETA_ONE, step_value)
    correct_two = 1.0 - jnp.power(BETA_TWO, step_value)
    direction = new_one / correct_one / (jnp.sqrt(new_two / correct_two) + ADAM_EPS)
    return (new_one, new_two, weight - LEARN_RATE * (direction + decay_rate * weight))


def shards(
    grid_inputs,
    mesh_static,
    targets,
    area_weight,
    valid_rows,
    encoder_lists,
    mesh_lists,
    decoder_lists,
    step_count,
    w_in,
    moment_in,
    square_in,
    w_layers,
    moment_layers,
    square_layers,
    norm_gains,
    moment_gains,
    square_gains,
    w_out,
    moment_out,
    square_out,
):
    row_count = grid_inputs.shape[0]
    layer_total = w_layers.shape[0]
    device_count = lax.axis_size(AXES)
    width = mesh_static.shape[1]
    share = w_layers.shape[2]
    channels, outputs = w_in.shape[0], w_out.shape[1]
    direct = share == 16 and device_count % 8 == 0 and device_count & (device_count - 1) == 0
    slot_lists = [encoder_lists.T.reshape(-1)]
    slot_lists += [mesh_lists.T.reshape(-1)] * (layer_total - 2)
    slot_lists += [decoder_lists.T.reshape(-1)]
    if direct:
        self_id = lax.axis_index(AXES).astype(jnp.int32)
        order = jnp.arange(device_count, dtype=jnp.int32) ^ self_id
        self_id = self_id.reshape(1)
        inputs = jnp.pad(grid_inputs, ((0, 0), (0, width - channels)))
        flat_gains = norm_gains.astype(LOW).reshape(1, -1)
        packed = jnp.concatenate(
            [
                w_layers[0].astype(LOW).reshape(-1, width),
                jnp.pad(w_in.astype(LOW).T, ((0, 0), (0, width - channels))),
                jnp.pad(flat_gains, ((0, 7), (0, width - flat_gains.shape[1]))),
            ],
            axis=0,
        )
        rest = jnp.concatenate(
            [
                w_layers[2:].astype(LOW).reshape(-1, share, width),
                jnp.pad(w_out.astype(LOW), ((0, 0), (0, width - outputs)))[None],
            ],
            axis=0,
        )
        input_blocks = (shift(inputs, device_count, 1), inputs, shift(inputs, device_count, -1))
        pieces = spread_rows(packed, device_count)
        second = lax.all_gather(w_layers[1].astype(LOW), AXES, axis=1, tiled=True)
        rest = lax.all_gather(rest, AXES, axis=1, tiled=True)
        first, grid_latent, grid_start, *blocks = embed(self_id, pieces, input_blocks)
        weights = [(first, 0), (second, 0)]
        weights += [(rest, 6 * layer_id) for layer_id in range(layer_total - 2)]
        table_out = rest[6 * (layer_total - 2), :, :outputs]
        gain_rows = jnp.stack(pieces)[:, :, packed.shape[0] - 8, : flat_gains.shape[1]]
        gain_rows = gain_rows.reshape(2, 4, device_count // 8, -1).transpose(2, 1, 0, 3)
        gain_rows = gain_rows.reshape(device_count, -1)[order]
        gains = gain_rows.reshape(device_count, layer_total, 2, share).transpose(1, 2, 0, 3)
        gains = gains.reshape(layer_total, 2, width).astype(WIDE)
    else:
        self_id = None
        table_in = lax.all_gather(w_in.astype(LOW), AXES, axis=1, tiled=True)
        table_out = lax.all_gather(w_out.astype(LOW), AXES, axis=0, tiled=True)
        matrices = lax.all_gather(w_layers.astype(LOW), AXES, axis=2, tiled=True)
        matrices = matrices.reshape(-1, width, width)
        weights = [(matrices, 6 * layer_id) for layer_id in range(layer_total)]
        gains = lax.all_gather(norm_gains.astype(LOW), AXES, axis=2, tiled=True).astype(WIDE)
        grid_latent = product(grid_inputs, table_in)
        grid_start = grid_latent.astype(LOW)
        sent = product(grid_start, matrices[0]).astype(LOW)
        blocks = (shift(sent, device_count, 1), sent, shift(sent, device_count, -1))
    target, target_low = mesh_static, mesh_static
    stored_list = []
    for layer_id in range(layer_total):
        last_layer = layer_id == layer_total - 1
        if last_layer:
            source_low = target_low
            target, target_low = grid_latent, grid_start
        else:
            source_low = grid_start if layer_id == 0 else target_low
        results = forward_layer(
            slot_lists[layer_id],
            blocks,
            target_low,
            target,
            weights[layer_id],
            None if last_layer else weights[layer_id + 1],
            gains[layer_id],
        )
        if last_layer:
            grid_low, kept, message, aggregate, mix, out = results
        else:
            sent, updated, updated_low, kept, message, aggregate, mix, out = results
            blocks = (shift(sent, device_count, 1), sent, shift(sent, device_count, -1))
        stored_list.append((source_low, (target_low, kept, message, mix, out), aggregate))
        if not last_layer:
            target, target_low = updated, updated_low
    prediction = product(grid_low, table_out)
    local_rows = jnp.arange(row_count, dtype=jnp.int32)
    weight_rows = area_weight * (local_rows < valid_rows[0]).astype(WIDE)
    error_rows = prediction - targets
    loss_scale = 1.0 / (row_count * device_count * prediction.shape[1])
    loss_local = jnp.sum(weight_rows[:, None] * error_rows * error_rows) * loss_scale
    grad_pred = (2.0 * loss_scale * weight_rows[:, None] * error_rows).astype(LOW)
    grad_table_out = product_left(grid_low, grad_pred)
    grad_part = product_right(grad_pred, table_out)
    extra = jnp.pad(grad_table_out, ((0, 0), (0, width - outputs)))
    grad_grid = None
    above, above_source = None, None
    layer_grads = [None] * layer_total
    gain_grads = [None] * layer_total
    in_plane, in_slice = [], []
    for layer_id in reversed(range(layer_total)):
        source_low, stored, aggregate = stored_list[layer_id]
        sent_grad, grad_new, slot_grad, grad_gain, *back = backward_layer(
            slot_lists[layer_id], above, grad_part, stored, weights[layer_id], gains[layer_id]
        )
        far = []
        if in_plane:
            moved = len(in_plane)
            arrived, (slot_grad,) = together(in_plane + in_slice, [slot_grad])
            if in_slice:
                layer_grads[layer_id + 2] = add_up(arrived[moved:]).reshape(6, share, width)
            far = list(combine(arrived[:moved], device_count // 8))
        from_before = shift(slot_grad[2], device_count, 1)
        from_after = shift(slot_grad[0], device_count, -1)
        back = [back[1], back[0], *back[2:]]
        grad_part, sums = weight_layer(
            self_id,
            device_count,
            None if above is None else (above_source, sent_grad),
            extra,
            stored[0],
            aggregate,
            back,
            None if layer_id == 0 else grad_new,
            weights[layer_id],
        )
        gain_grads[layer_id] = grad_gain
        if direct:
            halo, arrived = together([from_before, from_after], [*sums, *far])
            keep, send, far = arrived[0], arrived[1], arrived[2:]
            in_slice = fan_out(far, device_count, 8) if far else []
            other = swap(send, device_count, 1)
            if layer_id > 0:
                near = list(combine([keep, other], 4))
                halo, near = together(halo, near)
                in_plane = fan_out(near, device_count, 2)
            from_before, from_after = halo
        else:
            layer_grads[layer_id] = sums[0]
        if layer_id == layer_total - 1:
            grad_grid, grad_part = grad_part, None
        above = (from_before, slot_grad, from_after, weights[layer_id])
        above_source = source_low
    if direct:
        misc = jnp.stack(gain_grads).reshape(-1, device_count, share).transpose(1, 0, 2)
        misc = misc.reshape(device_count, -1)
        misc = jnp.concatenate(
            [misc, jnp.broadcast_to(loss_local.reshape(1, 1), (device_count, 1))], axis=1
        )
        misc = jnp.pad(misc[:, None, :], ((0, 0), (0, 7), (0, width - misc.shape[1])))
        sums = tail_layer(
            self_id,
            from_before,
            slot_grad,
            from_after,
            grid_start,
            inputs,
            grad_grid,
            weights[0],
            misc,
        )
        arrived, sums = together([other] + in_slice, sums)
        other, in_slice = arrived[0], arrived[1:]
        near = combine([keep, other], 4)
        layer_grads[1] = add_up(in_slice).reshape(6, share, width)
        far = combine(fan_out(near, device_count, 2), device_count // 8)
        layer_grads[0] = add_up(fan_out(far, device_count, 8)).reshape(6, share, width)
        keep, send = sums
        pieces = combine([keep, swap(send, device_count, 1)], 4)
        pieces = combine(fan_out(pieces, device_count, 2), device_count // 8)
        total = add_up(fan_out(pieces, device_count, 8))
        grad_zero = total[:share]
        grad_in = total[share : 2 * share, :channels].T
        size = layer_total * 2 * share
        grad_gain_all = total[2 * share, :size].reshape(layer_total, 2, share)
        loss_value = total[2 * share, size]
        grad_out = layer_grads[-1][0, :, :outputs]
    else:
        loss_value = lax.psum(loss_local, AXES)
        sent_grad = (
            from_before.astype(WIDE) + slot_grad[1].astype(WIDE) + from_after.astype(WIDE)
        ).astype(LOW)
        grad_zero = product_left(above_source, sent_grad)
        grad_grid = grad_grid + product_right(sent_grad, matrices[0])
        grad_table_in = product_left(grid_inputs, grad_grid.astype(LOW))
        grad_in = lax.psum_scatter(grad_table_in, AXES, scatter_dimension=1, tiled=True)
        grad_out = lax.psum_scatter(grad_table_out, AXES, scatter_dimension=0, tiled=True)
        grad_gain_all = lax.psum_scatter(
            jnp.stack(gain_grads), AXES, scatter_dimension=2, tiled=True
        )
    grad_layers = [grad_zero[None]]
    for layer_id in range(layer_total):
        grad_layers += [layer_grads[layer_id][1:]]
        if layer_id < layer_total - 1:
            grad_layers += [layer_grads[layer_id][0:1]]
    grad_layers = jnp.concatenate(grad_layers, axis=0)
    grad_layers = grad_layers.reshape(layer_total, 6, *grad_layers.shape[1:])
    if not direct:
        grad_layers = lax.psum_scatter(grad_layers, AXES, scatter_dimension=2, tiled=True)
    step_value = step_count[0].astype(WIDE)
    one_in, two_in, new_in = adamw_update(
        w_in, moment_in, square_in, grad_in, step_value, DECAY_RATE
    )
    one_layers, two_layers, new_layers = adamw_update(
        w_layers, moment_layers, square_layers, grad_layers, step_value, DECAY_RATE
    )
    one_gains, two_gains, new_gains = adamw_update(
        norm_gains, moment_gains, square_gains, grad_gain_all, step_value, 0.0
    )
    one_out, two_out, new_out = adamw_update(
        w_out, moment_out, square_out, grad_out, step_value, DECAY_RATE
    )
    return (
        loss_value,
        one_in,
        two_in,
        new_in,
        one_layers,
        two_layers,
        new_layers,
        one_gains,
        two_gains,
        new_gains,
        one_out,
        two_out,
        new_out,
    )


def solution(mesh):
    rows = P(AXES, None)
    layers = P(None, None, AXES, None)
    gains = P(None, None, AXES)
    columns = P(None, AXES)
    in_specs = (rows, rows, rows, P(AXES), P(AXES), rows, rows, rows, P())
    in_specs += (columns,) * 3 + (layers,) * 3 + (gains,) * 3 + (rows,) * 3
    out_specs = (P(),) + (columns,) * 3 + (layers,) * 3 + (gains,) * 3 + (rows,) * 3
    return jax.shard_map(shards, mesh=mesh, in_specs=in_specs, out_specs=out_specs, check_vma=False)
```

```python
import functools

import jax
import jax.numpy as jnp
from jax import lax
from jax.experimental import pallas as pl
from jax.experimental.pallas import tpu as pltpu
from jax.sharding import PartitionSpec as P

EPS_NORM = 1e-05
BETA_ONE = 0.5
BETA_TWO = 0.5
ADAM_EPS = 1e-08
LEARN_RATE = 0.04
DECAY_RATE = 0.1

AXES = ("nodes", "shard")
LANES = 128
FORWARD_ROWS = 256
BACKWARD_ROWS = 256
WEIGHT_ROWS = 256
UNROLL = 32
LOW = jnp.bfloat16
WIDE = jnp.float32
SEND = jnp.bfloat16


def product(left, right):
    return jnp.dot(left, right, preferred_element_type=WIDE)


def product_left(left, right):
    return lax.dot_general(left, right, (((0,), (0,)), ((), ())), preferred_element_type=WIDE)


def product_right(left, right):
    return lax.dot_general(left, right, (((1,), (1,)), ((), ())), preferred_element_type=WIDE)


def normalize(tensor):
    centre = tensor - jnp.mean(tensor, axis=-1, keepdims=True)
    inv_scale = lax.rsqrt(jnp.mean(centre * centre, axis=-1, keepdims=True) + EPS_NORM)
    return (centre * inv_scale, inv_scale)


def normal_back(grad_unit, unit_rows, inv_scale):
    centred = grad_unit - jnp.mean(grad_unit, axis=-1, keepdims=True)
    return inv_scale * (
        centred - unit_rows * jnp.mean(grad_unit * unit_rows, axis=-1, keepdims=True)
    )


def silu_parts(tensor):
    half = 0.5 * tensor
    return half, jnp.tanh(half)


def silu(tensor):
    half, bend = silu_parts(tensor)
    return half * (1.0 + bend)


def fold_rows(store, base, rows, tensor):
    parts = tensor.shape[1] // LANES
    for part in range(parts):
        store[pl.ds(base * parts + part, rows, stride=parts), :] = tensor[
            :, part * LANES : (part + 1) * LANES
        ]


def unfold_rows(store, base, rows, parts):
    return jnp.concatenate(
        [store[pl.ds(base * parts + part, rows, stride=parts), :] for part in range(parts)],
        axis=1,
    )


def forward_kernel(parts, has_next, *refs):
    if has_next:
        (slots, before, middle, after, low, wide, weights, gains, head) = refs[:9]
        (sent, update, update_low, kept, aggregate) = refs[9:14]
        window, picked, hidden, message = refs[14:]
    else:
        (slots, before, middle, after, low, wide, weights, gains) = refs[:8]
        (update_low, kept, aggregate) = refs[8:11]
        window, picked, hidden, message = refs[11:]
    step = pl.program_id(0)
    block_rows = before.shape[0]
    rows, width = low.shape
    fan = kept.shape[0]

    @pl.when(step == 0)
    def _():
        for index, block in enumerate((before, middle, after)):
            fold_rows(window, index * block_rows, block_rows, block[...].astype(WIDE))

    for k in range(fan):

        def pick(trip, carry):
            for lane in range(UNROLL):
                row = trip * UNROLL + lane
                slot = slots[k * block_rows + step * rows + row]
                picked[pl.ds(pl.multiple_of((k * rows + row) * parts, parts), parts), :] = window[
                    pl.ds(pl.multiple_of(slot * parts, parts), parts), :
                ]
            return carry

        lax.fori_loop(0, rows // UNROLL, pick, 0)
    target_low = low[...]
    own_term = product(target_low, weights[1])
    for k in range(fan):
        sender = unfold_rows(picked, k * rows, rows, parts)
        kept[k] = sender.astype(LOW)
        hidden[k * rows : (k + 1) * rows, :] = silu(sender + own_term).astype(LOW)
    message[...] = product(hidden[...], weights[2])
    total = normalize(message[0:rows, :])[0]
    for k in range(1, fan):
        total = total + normalize(message[k * rows : (k + 1) * rows, :])[0]
    total_low = (total * gains[0:1, :]).astype(LOW)
    aggregate[...] = total_low
    node_mix = product(target_low, weights[3]) + product(total_low, weights[4])
    node_out = product(silu(node_mix).astype(LOW), weights[5])
    updated = wide[...].astype(WIDE) + normalize(node_out)[0] * gains[1:2, :]
    updated_low = updated.astype(LOW)
    update_low[...] = updated_low
    if has_next:
        update[...] = updated
        sent[...] = product(updated_low, head[0]).astype(LOW)


def whole(shape):
    zeros = (0,) * len(shape)
    return pl.BlockSpec(shape, lambda step: zeros, pipeline_mode=pl.Buffered(1))


def matrix_spec(first, count, width):
    return pl.BlockSpec(
        (count, width, width), lambda step: (first // count, 0, 0), pipeline_mode=pl.Buffered(1)
    )


def tiled(rows, width):
    return pl.BlockSpec((rows, width), lambda step: (step, 0))


def fanned(fan, rows, width):
    return pl.BlockSpec((fan, rows, width), lambda step: (0, step, 0))


def forward_layer(slots, blocks, target_low, target, weights, next_weights, gains):
    block_rows, width = target_low.shape
    fan = slots.shape[0] // block_rows
    parts = width // LANES
    rows = FORWARD_ROWS
    has_next = next_weights is not None
    shape = functools.partial(jax.ShapeDtypeStruct, (block_rows, width))
    fan_shape = functools.partial(jax.ShapeDtypeStruct, (fan, block_rows, width))
    tile = tiled(rows, width)
    in_specs = [pl.BlockSpec(memory_space=pltpu.SMEM)]
    in_specs += [whole((block_rows, width))] * 3 + [tile, tile]
    in_specs += [matrix_spec(weights[1], 6, width), whole(gains.shape)]
    out_specs = [tile, fanned(fan, rows, width), tile]
    out_shape = [shape(LOW), fan_shape(LOW), shape(LOW)]
    operands = [slots, *blocks, target_low, target, weights[0], gains]
    if has_next:
        in_specs += [matrix_spec(next_weights[1], 1, width)]
        operands += [next_weights[0]]
        out_specs = [tile, tile] + out_specs
        out_shape = [shape(LOW), shape(WIDE)] + out_shape
    return pl.pallas_call(
        functools.partial(forward_kernel, parts, has_next),
        grid=(block_rows // rows,),
        in_specs=in_specs,
        out_specs=out_specs,
        out_shape=out_shape,
        scratch_shapes=[
            pltpu.VMEM((3 * block_rows * parts, LANES), WIDE),
            pltpu.VMEM((fan * rows * parts, LANES), WIDE),
            pltpu.VMEM((fan * rows, width), LOW),
            pltpu.VMEM((fan * rows, width), WIDE),
        ],
        compiler_params=pltpu.CompilerParams(vmem_limit_bytes=28 << 20),
        cost_estimate=pl.CostEstimate(
            flops=2 * (fan + 5) * block_rows * width * width,
            transcendentals=(fan + 1) * block_rows * width,
            bytes_accessed=24 * block_rows * width * 2,
        ),
        name="forward_layer",
    )(*operands)


def backward_kernel(parts, mode, *refs):
    refs = list(refs)
    slots = refs.pop(0)
    if mode != "first":
        returned = [refs.pop(0) for _ in range(3)]
        head = refs.pop(0)
    if mode != "second":
        grad_part = refs.pop(0)
    low, kept, aggregate, weights, gains = refs[:5]
    refs = refs[5:]
    if mode != "first":
        sent_grad = refs.pop(0)
        grad_full = refs.pop(0)
    slot_grads = refs[:3]
    (grad_gains, grad_message, edge_hidden, grad_mix, grad_out, grad_own, hidden) = refs[3:10]
    sum_even, sum_odd, spread, stage = refs[10:]
    step = pl.program_id(0)
    rows, width = low.shape
    fan = kept.shape[0]
    block_rows = slot_grads[0].shape[0]

    @pl.when(step == 0)
    def _():
        sum_even[...] = jnp.zeros_like(sum_even)
        sum_odd[...] = jnp.zeros_like(sum_odd)
        grad_gains[...] = jnp.zeros_like(grad_gains)

    if mode == "first":
        grad_new = grad_part[...]
    else:
        sent_low = (
            returned[0][...].astype(WIDE)
            + returned[1][...].astype(WIDE)
            + returned[2][...].astype(WIDE)
        ).astype(LOW)
        sent_grad[...] = sent_low
        grad_new = product_right(sent_low, head[0])
        if mode == "third":
            grad_new = grad_part[...] + grad_new
        grad_full[...] = grad_new
    target_low = low[...]
    own_term = product(target_low, weights[1])
    node_mix = product(target_low, weights[3]) + product(aggregate[...], weights[4])
    for k in range(fan):
        edge_hidden[k] = silu(kept[k].astype(WIDE) + own_term).astype(LOW)
    stage[...] = product(edge_hidden[...].reshape(fan * rows, width), weights[2])
    half, bend = silu_parts(node_mix)
    node_hidden = (half * (1.0 + bend)).astype(LOW)
    hidden[...] = node_hidden
    out_unit, out_scale = normalize(product(node_hidden, weights[5]))
    gain_two = jnp.sum(grad_new * out_unit, axis=0, keepdims=True)
    out_low = normal_back(grad_new * gains[1:2, :], out_unit, out_scale).astype(LOW)
    grad_out[...] = out_low
    mix_low = (
        product_right(out_low, weights[5]) * ((0.5 + 0.5 * bend) * (1.0 + half * (1.0 - bend)))
    ).astype(LOW)
    grad_mix[...] = mix_low
    grad_sum = product_right(mix_low, weights[4])
    grad_unit = grad_sum * gains[0:1, :]
    unit_total = None
    for k in range(fan):
        unit_rows, inv_scale = normalize(stage[k * rows : (k + 1) * rows, :])
        unit_total = unit_rows if k == 0 else unit_total + unit_rows
        grad_message[k] = normal_back(grad_unit, unit_rows, inv_scale).astype(LOW)
    stage[...] = product_right(grad_message[...].reshape(fan * rows, width), weights[2])
    own_total = None
    for k in range(fan):
        half, bend = silu_parts(kept[k].astype(WIDE) + own_term)
        grad_pre = stage[k * rows : (k + 1) * rows, :] * (
            (0.5 + 0.5 * bend) * (1.0 + half * (1.0 - bend))
        )
        own_total = grad_pre if k == 0 else own_total + grad_pre
        fold_rows(spread, k * rows, rows, grad_pre)
    gain_one = jnp.sum(grad_sum * unit_total, axis=0, keepdims=True)
    grad_gains[...] += jnp.concatenate([gain_one, gain_two], axis=0)
    grad_own[...] = own_total.astype(LOW)

    for k in range(fan):

        def add(trip, carry):
            for lane in range(UNROLL // 2):
                places, values = [], []
                for store in (sum_even, sum_odd):
                    row = (trip * (UNROLL // 2) + lane) * 2 + len(places)
                    slot = slots[k * block_rows + step * rows + row]
                    place = pl.ds(pl.multiple_of(slot * parts, parts), parts)
                    value = spread[pl.ds(pl.multiple_of((k * rows + row) * parts, parts), parts), :]
                    places.append(place)
                    values.append(store[place, :] + value)
                sum_even[places[0], :] = values[0]
                sum_odd[places[1], :] = values[1]
            return carry

        lax.fori_loop(0, rows // UNROLL, add, 0)

    @pl.when(step == pl.num_programs(0) - 1)
    def _():
        for index in range(3):
            base = index * block_rows
            slot_grads[index][...] = (
                unfold_rows(sum_even, base, block_rows, parts)
                + unfold_rows(sum_odd, base, block_rows, parts)
            ).astype(LOW)


def backward_layer(slots, above, grad_part, stored, weights, gains):
    target_low, kept, aggregate = stored
    block_rows, width = target_low.shape
    fan = kept.shape[0]
    parts = width // LANES
    rows = BACKWARD_ROWS
    tile = tiled(rows, width)
    fan_tile = fanned(fan, rows, width)
    in_specs = [pl.BlockSpec(memory_space=pltpu.SMEM)]
    operands = [slots]
    out_specs, out_shape = [], []
    shape = functools.partial(jax.ShapeDtypeStruct, (block_rows, width))
    fan_shape = functools.partial(jax.ShapeDtypeStruct, (fan, block_rows, width))
    mode = "first" if above is None else ("second" if grad_part is None else "third")
    if above is not None:
        from_before, slot_grad, from_after, head = above
        in_specs += [
            tile,
            tile,
            tile,
            matrix_spec(head[1], 1, width),
        ]
        operands += [from_before, slot_grad, from_after, head[0]]
        out_specs += [tile, tile]
        out_shape += [shape(LOW), shape(WIDE)]
    if grad_part is not None:
        in_specs += [tile]
        operands += [grad_part]
    in_specs += [tile, fan_tile, tile]
    in_specs += [matrix_spec(weights[1], 6, width), whole(gains.shape)]
    operands += [target_low, kept, aggregate, weights[0], gains]
    out_specs += [
        whole((block_rows, width)),
        whole((block_rows, width)),
        whole((block_rows, width)),
        whole((2, width)),
        fan_tile,
        fan_tile,
        tile,
        tile,
        tile,
        tile,
    ]
    out_shape += [
        shape(LOW),
        shape(LOW),
        shape(LOW),
        jax.ShapeDtypeStruct((2, width), WIDE),
        fan_shape(LOW),
        fan_shape(LOW),
        shape(LOW),
        shape(LOW),
        shape(LOW),
        shape(LOW),
    ]
    results = pl.pallas_call(
        functools.partial(backward_kernel, parts, mode),
        grid=(block_rows // rows,),
        in_specs=in_specs,
        out_specs=out_specs,
        out_shape=out_shape,
        scratch_shapes=[
            pltpu.VMEM((3 * block_rows * parts, LANES), WIDE),
            pltpu.VMEM((3 * block_rows * parts, LANES), WIDE),
            pltpu.VMEM((fan * rows * parts, LANES), WIDE),
            pltpu.VMEM((fan * rows, width), WIDE),
        ],
        compiler_params=pltpu.CompilerParams(vmem_limit_bytes=38 << 20),
        cost_estimate=pl.CostEstimate(
            flops=2 * (fan + 4) * block_rows * width * width,
            transcendentals=(fan + 1) * block_rows * width,
            bytes_accessed=24 * block_rows * width * 2,
        ),
        name="backward_layer",
    )(*operands)
    if above is None:
        return (None, grad_part, *results)
    return tuple(results)


def deal(self_id, sums, outs):
    keep, send = outs
    share = keep.shape[1] // sums.shape[0]

    def move(node, carry):
        for core, out in enumerate((keep, send)):
            place = pl.multiple_of(((2 * node + core) ^ self_id[0]) * share, share)
            for index in range(sums.shape[0]):
                out[node, index * share : (index + 1) * share, :] = sums[
                    index, pl.ds(place, share), :
                ].astype(out.dtype)
        return carry

    lax.fori_loop(0, keep.shape[0], move, 0)


def weight_kernel(has_above, needs_target, direct, *refs):
    refs = list(refs)
    if direct:
        self_id = refs.pop(0)
    if has_above:
        source, sent_grad = refs[:2]
        refs = refs[2:]
    else:
        extra = refs.pop(0)
    low, aggregate, edge_hidden, grad_message, grad_mix, grad_out, grad_own, hidden = refs[:8]
    refs = refs[8:]
    if needs_target:
        grad_new, weights = refs[:2]
        grad_part = refs[2]
        refs = refs[3:]
    outs, sums = (refs[:2], refs[2]) if direct else (None, refs[0])
    step = pl.program_id(0)
    fan = edge_hidden.shape[0]

    @pl.when(step == 0)
    def _():
        sums[...] = jnp.zeros_like(sums)
        if not has_above:
            sums[0] = extra[...]

    target_low = low[...]
    mix_low = grad_mix[...]
    own_low = grad_own[...]
    if has_above:
        sums[0] += product_left(source[...], sent_grad[...])
    sums[1] += product_left(target_low, own_low)
    for k in range(fan):
        sums[2] += product_left(edge_hidden[k], grad_message[k])
    sums[3] += product_left(target_low, mix_low)
    sums[4] += product_left(aggregate[...], mix_low)
    sums[5] += product_left(hidden[...], grad_out[...])
    if needs_target:
        grad_part[...] = (
            grad_new[...] + product_right(own_low, weights[1]) + product_right(mix_low, weights[3])
        )
    if direct:

        @pl.when(step == pl.num_programs(0) - 1)
        def _():
            deal(self_id, sums, outs)


def share_outputs(count, width, device_count):
    shape = (device_count // 2, count * (width // device_count), width)
    return (
        [whole(shape)] * 2,
        [jax.ShapeDtypeStruct(shape, WIDE), jax.ShapeDtypeStruct(shape, SEND)],
    )


def weight_layer(self_id, device_count, above, extra, low, aggregate, back, grad_new, weights):
    block_rows, width = low.shape
    rows = WEIGHT_ROWS
    fan = back[0].shape[0]
    tile = tiled(rows, width)
    fan_tile = fanned(fan, rows, width)
    in_specs, operands = [], []
    direct = self_id is not None
    if direct:
        in_specs += [pl.BlockSpec(memory_space=pltpu.SMEM)]
        operands += [self_id]
    if above is not None:
        in_specs += [tile, tile]
        operands += list(above)
    else:
        in_specs += [whole((width, width))]
        operands += [extra]
    in_specs += [tile, tile, fan_tile, fan_tile, tile, tile, tile, tile]
    operands += [low, aggregate, *back]
    out_specs, out_shape, scratch = [], [], []
    if grad_new is not None:
        in_specs += [tile, matrix_spec(weights[1], 6, width)]
        operands += [grad_new, weights[0]]
        out_specs += [tile]
        out_shape += [jax.ShapeDtypeStruct((block_rows, width), WIDE)]
    if direct:
        specs, shapes = share_outputs(6, width, device_count)
        out_specs += specs
        out_shape += shapes
        scratch = [pltpu.VMEM((6, width, width), WIDE)]
    else:
        out_specs += [whole((6, width, width))]
        out_shape += [jax.ShapeDtypeStruct((6, width, width), WIDE)]
    results = pl.pallas_call(
        functools.partial(weight_kernel, above is not None, grad_new is not None, direct),
        grid=(block_rows // rows,),
        in_specs=in_specs,
        out_specs=out_specs,
        out_shape=out_shape,
        scratch_shapes=scratch,
        compiler_params=pltpu.CompilerParams(vmem_limit_bytes=28 << 20),
        cost_estimate=pl.CostEstimate(
            flops=2 * (fan + 6) * block_rows * width * width,
            transcendentals=0,
            bytes_accessed=24 * block_rows * width,
        ),
        name="weight_layer",
    )(*operands)
    if grad_new is None:
        return (None, results)
    return (results[0], results[1:])


def embed_kernel(pieces_count, *refs):
    self_id = refs[0]
    pieces = refs[1 : 1 + pieces_count]
    before, middle, after = refs[1 + pieces_count : 4 + pieces_count]
    weights, latent, latent_low, sent_before, sent_middle, sent_after, table = refs[
        4 + pieces_count :
    ]
    count, width = weights.shape[0], weights.shape[1]
    high = pieces[0].shape[0]
    share = width // (high * pieces_count)

    @pl.when(pl.program_id(0) == 0)
    def _():
        for index, piece in enumerate(pieces):
            core, low_digit = index // (pieces_count // 2), index % (pieces_count // 2)

            def move(digit, carry, piece=piece, core=core, low_digit=low_digit):
                relative = digit * pieces_count + low_digit * 2 + core
                place = pl.multiple_of((relative ^ self_id[0]) * share, share)
                for j in range(count):
                    weights[j, pl.ds(place, share), :] = piece[digit, j * share : (j + 1) * share, :]
                table[pl.ds(place, share), :] = piece[digit, count * share : (count + 1) * share, :]
                return carry

            lax.fori_loop(0, high, move, 0)

    for block, sent in ((before, sent_before), (middle, sent_middle), (after, sent_after)):
        wide = product_right(block[...], table[...])
        low = wide.astype(LOW)
        sent[...] = product(low, weights[0]).astype(LOW)
        if block is middle:
            latent[...] = wide
            latent_low[...] = low


def embed(self_id, pieces, blocks):
    block_rows, width = blocks[1].shape
    rows = WEIGHT_ROWS
    tile = tiled(rows, width)
    shape = functools.partial(jax.ShapeDtypeStruct, (block_rows, width))
    return pl.pallas_call(
        functools.partial(embed_kernel, len(pieces)),
        grid=(block_rows // rows,),
        in_specs=[pl.BlockSpec(memory_space=pltpu.SMEM)]
        + [whole(piece.shape) for piece in pieces]
        + [tile] * 3,
        out_specs=[whole((7, width, width))] + [tile] * 5,
        out_shape=[jax.ShapeDtypeStruct((7, width, width), LOW), shape(WIDE)] + [shape(LOW)] * 4,
        scratch_shapes=[pltpu.VMEM((width, width), LOW)],
        compiler_params=pltpu.CompilerParams(vmem_limit_bytes=20 << 20),
        cost_estimate=pl.CostEstimate(
            flops=12 * block_rows * width * width,
            transcendentals=0,
            bytes_accessed=24 * block_rows * width,
        ),
        name="embed",
    )(self_id, *pieces, *blocks)


def tail_kernel(self_id, before, middle, after, latent_low, inputs, grad_grid, head, misc, *refs):
    keep, send, sums = refs
    step = pl.program_id(0)
    rows, width = inputs.shape
    share = misc.shape[1]

    @pl.when(step == 0)
    def _():
        sums[...] = jnp.zeros_like(sums)

    sent_low = (
        before[...].astype(WIDE)
        + middle[...].astype(WIDE)
        + after[...].astype(WIDE)
    ).astype(LOW)
    grad_low = (grad_grid[...] + product_right(sent_low, head[0])).astype(LOW)
    sums[0] += product_left(latent_low[...], sent_low)
    sums[1] += product_left(grad_low, inputs[...])

    @pl.when(step == pl.num_programs(0) - 1)
    def _():
        size = sums.shape[0] * (width // misc.shape[0])
        main = [out.at[:, 0:size, :] for out in (keep, send)]
        deal(self_id, sums, main)

        def move(node, carry):
            for core, out in enumerate((keep, send)):
                out[node, size : size + share, :] = misc[(2 * node + core) ^ self_id[0]].astype(
                    out.dtype
                )
            return carry

        lax.fori_loop(0, keep.shape[0], move, 0)


def tail_layer(self_id, from_before, slot_grad, from_after, latent_low, inputs, grad_grid, head, misc):
    block_rows, width = inputs.shape
    device_count = misc.shape[0]
    rows = WEIGHT_ROWS
    tile = tiled(rows, width)
    shape = (device_count // 2, 2 * (width // device_count) + misc.shape[1], width)
    return pl.pallas_call(
        tail_kernel,
        grid=(block_rows // rows,),
        in_specs=[
            pl.BlockSpec(memory_space=pltpu.SMEM),
            tile,
            tile,
            tile,
            tile,
            tile,
            tile,
            matrix_spec(head[1], 1, width),
            whole(misc.shape),
        ],
        out_specs=[whole(shape)] * 2,
        out_shape=[jax.ShapeDtypeStruct(shape, WIDE), jax.ShapeDtypeStruct(shape, SEND)],
        scratch_shapes=[pltpu.VMEM((2, width, width), WIDE)],
        compiler_params=pltpu.CompilerParams(vmem_limit_bytes=20 << 20),
        cost_estimate=pl.CostEstimate(
            flops=6 * block_rows * width * width,
            transcendentals=0,
            bytes_accessed=24 * block_rows * width,
        ),
        name="tail_layer",
    )(self_id, from_before, slot_grad, from_after, latent_low, inputs, grad_grid, head[0], misc)


def combine_kernel(count, *refs):
    arrived, outs = refs[:count], refs[count:]
    for digit, out in enumerate(outs):
        total = arrived[0][0, digit].astype(WIDE)
        for part in arrived[1:]:
            total = total + part[0, digit].astype(WIDE)
        out[0] = total.astype(out.dtype)


def combine(arrived, radix):
    _, rows, width = arrived[0].shape
    rest = arrived[0].shape[0] // radix
    arrived = [part.reshape(rest, radix, rows, width) for part in arrived]
    spec = pl.BlockSpec((1, radix, rows, width), lambda step: (step, 0, 0, 0))
    shape = (rest, rows, width)
    return pl.pallas_call(
        functools.partial(combine_kernel, len(arrived)),
        grid=(rest,),
        in_specs=[spec] * len(arrived),
        out_specs=[pl.BlockSpec((1, rows, width), lambda step: (step, 0, 0))] * radix,
        out_shape=[jax.ShapeDtypeStruct(shape, WIDE)]
        + [jax.ShapeDtypeStruct(shape, SEND)] * (radix - 1),
        compiler_params=pltpu.CompilerParams(vmem_limit_bytes=12 << 20),
        cost_estimate=pl.CostEstimate(
            flops=rest * radix * rows * width * len(arrived),
            transcendentals=0,
            bytes_accessed=4 * rest * radix * rows * width * (len(arrived) + 1),
        ),
        name="combine",
    )(*arrived)


def swap(cells, count, mask):
    return lax.ppermute(cells, AXES, [(i, i ^ mask) for i in range(count)])


def spread_column(packed, count):
    high = 4 * 2
    return [packed] + [swap(packed, count, digit * high) for digit in range(1, count // high)]


def spread_rows(held, count):
    column = jnp.stack(held)
    near = [column] + [swap(column, count, digit * 2) for digit in range(1, 4)]
    return near + [swap(piece, count, 1) for piece in near]


def shift(cells, count, step):
    return lax.ppermute(cells, AXES, [(i, (i + step) % count) for i in range(count)])


def fan_out(pieces, count, unit):
    return [pieces[0]] + [
        swap(pieces[digit], count, digit * unit) for digit in range(1, len(pieces))
    ]


def together(first, second):
    joined = lax.optimization_barrier((tuple(first), tuple(second)))
    return list(joined[0]), list(joined[1])


def add_up(arrived):
    total = arrived[0][0]
    for part in arrived[1:]:
        total = total + part[0].astype(WIDE)
    return total


def adamw_update(weight, moment_one, moment_two, gradient, step_value, decay_rate):
    new_one = BETA_ONE * moment_one + (1.0 - BETA_ONE) * gradient
    new_two = BETA_TWO * moment_two + (1.0 - BETA_TWO) * gradient * gradient
    correct_one = 1.0 - jnp.power(BETA_ONE, step_value)
    correct_two = 1.0 - jnp.power(BETA_TWO, step_value)
    direction = new_one / correct_one / (jnp.sqrt(new_two / correct_two) + ADAM_EPS)
    return (new_one, new_two, weight - LEARN_RATE * (direction + decay_rate * weight))


def shards(
    grid_inputs,
    mesh_static,
    targets,
    area_weight,
    valid_rows,
    encoder_lists,
    mesh_lists,
    decoder_lists,
    step_count,
    w_in,
    moment_in,
    square_in,
    w_layers,
    moment_layers,
    square_layers,
    norm_gains,
    moment_gains,
    square_gains,
    w_out,
    moment_out,
    square_out,
):
    row_count = grid_inputs.shape[0]
    layer_total = w_layers.shape[0]
    device_count = lax.axis_size(AXES)
    width = mesh_static.shape[1]
    share = w_layers.shape[2]
    channels, outputs = w_in.shape[0], w_out.shape[1]
    direct = share == 16 and device_count % 8 == 0 and device_count & (device_count - 1) == 0
    slot_lists = [encoder_lists.T.reshape(-1)]
    slot_lists += [mesh_lists.T.reshape(-1)] * (layer_total - 2)
    slot_lists += [decoder_lists.T.reshape(-1)]
    if direct:
        self_id = lax.axis_index(AXES).astype(jnp.int32)
        order = jnp.arange(device_count, dtype=jnp.int32) ^ self_id
        self_id = self_id.reshape(1)
        inputs = jnp.pad(grid_inputs, ((0, 0), (0, width - channels)))
        flat_gains = norm_gains.astype(LOW).reshape(1, -1)
        packed = jnp.concatenate(
            [
                w_layers[0].astype(LOW).reshape(-1, width),
                w_layers[1, 0].astype(LOW),
                jnp.pad(w_in.astype(LOW).T, ((0, 0), (0, width - channels))),
                jnp.pad(flat_gains, ((0, 7), (0, width - flat_gains.shape[1]))),
            ],
            axis=0,
        )
        second = jnp.concatenate([w_layers[2, :1], w_layers[1, 1:]], axis=0).astype(LOW)
        rest = jnp.concatenate(
            [
                jnp.pad(w_out.astype(LOW), ((0, 0), (0, width - outputs)))[None],
                w_layers[2, 1:].astype(LOW),
                w_layers[3:].astype(LOW).reshape(-1, share, width),
            ],
            axis=0,
        )
        held = spread_column(packed, device_count)
        sides = [shift(inputs, device_count, 1), shift(inputs, device_count, -1)]
        held, sides = together(held, [*sides, second])
        second = lax.all_gather(sides[2], AXES, axis=1, tiled=True)
        pieces = spread_rows(held, device_count)
        pieces, (rest,) = together(pieces, [rest])
        rest = lax.all_gather(rest, AXES, axis=1, tiled=True)
        first, grid_latent, grid_start, *blocks = embed(
            self_id, pieces, (sides[0], inputs, sides[1])
        )
        weights = [(first, 0), (second, 0)]
        weights += [(rest, 6 * layer_id) for layer_id in range(layer_total - 2)]
        heads = [(first, 0), (first, 6), (second, 0)]
        heads += weights[3:]
        table_out = rest[0, :, :outputs]
        gain_rows = jnp.stack(pieces)[:, :, packed.shape[0] - 8, : flat_gains.shape[1]]
        gain_rows = gain_rows.reshape(2, 4, device_count // 8, -1).transpose(2, 1, 0, 3)
        gain_rows = gain_rows.reshape(device_count, -1)[order]
        gains = gain_rows.reshape(device_count, layer_total, 2, share).transpose(1, 2, 0, 3)
        gains = gains.reshape(layer_total, 2, width).astype(WIDE)
    else:
        self_id = None
        table_in = lax.all_gather(w_in.astype(LOW), AXES, axis=1, tiled=True)
        table_out = lax.all_gather(w_out.astype(LOW), AXES, axis=0, tiled=True)
        matrices = lax.all_gather(w_layers.astype(LOW), AXES, axis=2, tiled=True)
        matrices = matrices.reshape(-1, width, width)
        weights = [(matrices, 6 * layer_id) for layer_id in range(layer_total)]
        heads = weights
        gains = lax.all_gather(norm_gains.astype(LOW), AXES, axis=2, tiled=True).astype(WIDE)
        grid_latent = product(grid_inputs, table_in)
        grid_start = grid_latent.astype(LOW)
        sent = product(grid_start, matrices[0]).astype(LOW)
        blocks = (shift(sent, device_count, 1), sent, shift(sent, device_count, -1))
    target, target_low = mesh_static, mesh_static
    stored_list = []
    for layer_id in range(layer_total):
        last_layer = layer_id == layer_total - 1
        if last_layer:
            source_low = target_low
            target, target_low = grid_latent, grid_start
        else:
            source_low = grid_start if layer_id == 0 else target_low
        results = forward_layer(
            slot_lists[layer_id],
            blocks,
            target_low,
            target,
            weights[layer_id],
            None if last_layer else heads[layer_id + 1],
            gains[layer_id],
        )
        if last_layer:
            grid_low, kept, aggregate = results
        else:
            sent, updated, updated_low, kept, aggregate = results
            blocks = (shift(sent, device_count, 1), sent, shift(sent, device_count, -1))
        stored_list.append((source_low, (target_low, kept, aggregate), aggregate))
        if not last_layer:
            target, target_low = updated, updated_low
    prediction = product(grid_low, table_out)
    local_rows = jnp.arange(row_count, dtype=jnp.int32)
    weight_rows = area_weight * (local_rows < valid_rows[0]).astype(WIDE)
    error_rows = prediction - targets
    loss_scale = 1.0 / (row_count * device_count * prediction.shape[1])
    loss_local = jnp.sum(weight_rows[:, None] * error_rows * error_rows) * loss_scale
    grad_pred = (2.0 * loss_scale * weight_rows[:, None] * error_rows).astype(LOW)
    grad_table_out = product_left(grid_low, grad_pred)
    grad_part = product_right(grad_pred, table_out)
    extra = jnp.pad(grad_table_out, ((0, 0), (0, width - outputs)))
    grad_grid = None
    above, above_source = None, None
    layer_grads = [None] * layer_total
    gain_grads = [None] * layer_total
    in_plane, in_slice = [], []
    for layer_id in reversed(range(layer_total)):
        source_low, stored, aggregate = stored_list[layer_id]
        sent_grad, grad_new, *slot_grads, grad_gain, grad_message, edge_hidden, b0, b1, b2, b3 = backward_layer(
            slot_lists[layer_id], above, grad_part, stored, weights[layer_id], gains[layer_id]
        )
        far = []
        if in_plane:
            moved = len(in_plane)
            arrived, slot_grads = together(in_plane + in_slice, slot_grads)
            if in_slice:
                layer_grads[layer_id + 2] = add_up(arrived[moved:]).reshape(6, share, width)
            far = list(combine(arrived[:moved], device_count // 8))
        from_before = shift(slot_grads[2], device_count, 1)
        from_after = shift(slot_grads[0], device_count, -1)
        back = [edge_hidden, grad_message, b0, b1, b2, b3]
        grad_part, sums = weight_layer(
            self_id,
            device_count,
            None if above is None else (above_source, sent_grad),
            extra,
            stored[0],
            aggregate,
            back,
            None if layer_id == 0 else grad_new,
            weights[layer_id],
        )
        gain_grads[layer_id] = grad_gain
        if direct:
            halo, arrived = together([from_before, from_after], [*sums, *far])
            keep, send, far = arrived[0], arrived[1], arrived[2:]
            in_slice = fan_out(far, device_count, 8) if far else []
            other = swap(send, device_count, 1)
            if layer_id > 0:
                near = list(combine([keep, other], 4))
                halo, near = together(halo, near)
                in_plane = fan_out(near, device_count, 2)
            from_before, from_after = halo
        else:
            layer_grads[layer_id] = sums[0]
        if layer_id == layer_total - 1:
            grad_grid, grad_part = grad_part, None
        above = (from_before, slot_grads[1], from_after, heads[layer_id])
        above_source = source_low
    if direct:
        misc = jnp.stack(gain_grads).reshape(-1, device_count, share).transpose(1, 0, 2)
        misc = misc.reshape(device_count, -1)
        misc = jnp.concatenate(
            [misc, jnp.broadcast_to(loss_local.reshape(1, 1), (device_count, 1))], axis=1
        )
        misc = jnp.pad(misc[:, None, :], ((0, 0), (0, 7), (0, width - misc.shape[1])))
        sums = tail_layer(
            self_id,
            from_before,
            slot_grads[1],
            from_after,
            grid_start,
            inputs,
            grad_grid,
            heads[0],
            misc,
        )
        arrived, sums = together([other] + in_slice, sums)
        other, in_slice = arrived[0], arrived[1:]
        near = combine([keep, other], 4)
        layer_grads[1] = add_up(in_slice).reshape(6, share, width)
        far = combine(fan_out(near, device_count, 2), device_count // 8)
        layer_grads[0] = add_up(fan_out(far, device_count, 8)).reshape(6, share, width)
        keep, send = sums
        pieces = combine([keep, swap(send, device_count, 1)], 4)
        pieces = combine(fan_out(pieces, device_count, 2), device_count // 8)
        total = add_up(fan_out(pieces, device_count, 8))
        grad_zero = total[:share]
        grad_in = total[share : 2 * share, :channels].T
        size = layer_total * 2 * share
        grad_gain_all = total[2 * share, :size].reshape(layer_total, 2, share)
        loss_value = total[2 * share, size]
        grad_out = layer_grads[-1][0, :, :outputs]
    else:
        loss_value = lax.psum(loss_local, AXES)
        sent_grad = (
            from_before.astype(WIDE) + slot_grads[1].astype(WIDE) + from_after.astype(WIDE)
        ).astype(LOW)
        grad_zero = product_left(above_source, sent_grad)
        grad_grid = grad_grid + product_right(sent_grad, matrices[0])
        grad_table_in = product_left(grid_inputs, grad_grid.astype(LOW))
        grad_in = lax.psum_scatter(grad_table_in, AXES, scatter_dimension=1, tiled=True)
        grad_out = lax.psum_scatter(grad_table_out, AXES, scatter_dimension=0, tiled=True)
        grad_gain_all = lax.psum_scatter(
            jnp.stack(gain_grads), AXES, scatter_dimension=2, tiled=True
        )
    grad_layers = [grad_zero[None]]
    for layer_id in range(layer_total):
        grad_layers += [layer_grads[layer_id][1:]]
        if layer_id < layer_total - 1:
            grad_layers += [layer_grads[layer_id][0:1]]
    grad_layers = jnp.concatenate(grad_layers, axis=0)
    grad_layers = grad_layers.reshape(layer_total, 6, *grad_layers.shape[1:])
    if not direct:
        grad_layers = lax.psum_scatter(grad_layers, AXES, scatter_dimension=2, tiled=True)
    step_value = step_count[0].astype(WIDE)
    one_in, two_in, new_in = adamw_update(
        w_in, moment_in, square_in, grad_in, step_value, DECAY_RATE
    )
    one_layers, two_layers, new_layers = adamw_update(
        w_layers, moment_layers, square_layers, grad_layers, step_value, DECAY_RATE
    )
    one_gains, two_gains, new_gains = adamw_update(
        norm_gains, moment_gains, square_gains, grad_gain_all, step_value, 0.0
    )
    one_out, two_out, new_out = adamw_update(
        w_out, moment_out, square_out, grad_out, step_value, DECAY_RATE
    )
    return (
        loss_value,
        one_in,
        two_in,
        new_in,
        one_layers,
        two_layers,
        new_layers,
        one_gains,
        two_gains,
        new_gains,
        one_out,
        two_out,
        new_out,
    )


def solution(mesh):
    rows = P(AXES, None)
    layers = P(None, None, AXES, None)
    gains = P(None, None, AXES)
    columns = P(None, AXES)
    in_specs = (rows, rows, rows, P(AXES), P(AXES), rows, rows, rows, P())
    in_specs += (columns,) * 3 + (layers,) * 3 + (gains,) * 3 + (rows,) * 3
    out_specs = (P(),) + (columns,) * 3 + (layers,) * 3 + (gains,) * 3 + (rows,) * 3
    return jax.shard_map(shards, mesh=mesh, in_specs=in_specs, out_specs=out_specs, check_vma=False)
```

```python
import functools

import jax
import jax.numpy as jnp
from jax import lax
from jax.experimental import pallas as pl
from jax.experimental.pallas import tpu as pltpu
from jax.sharding import PartitionSpec as P

EPS_NORM = 1e-05
BETA_ONE = 0.5
BETA_TWO = 0.5
ADAM_EPS = 1e-08
LEARN_RATE = 0.04
DECAY_RATE = 0.1

AXES = ("nodes", "shard")
LANES = 128
FORWARD_ROWS = 256
BACKWARD_ROWS = 256
WEIGHT_ROWS = 256
UNROLL = 32
LOW = jnp.bfloat16
WIDE = jnp.float32
SEND = jnp.bfloat16


def product(left, right):
    return jnp.dot(left, right, preferred_element_type=WIDE)


def product_left(left, right):
    return lax.dot_general(left, right, (((0,), (0,)), ((), ())), preferred_element_type=WIDE)


def product_right(left, right):
    return lax.dot_general(left, right, (((1,), (1,)), ((), ())), preferred_element_type=WIDE)


def normalize(tensor):
    centre = tensor - jnp.mean(tensor, axis=-1, keepdims=True)
    inv_scale = lax.rsqrt(jnp.mean(centre * centre, axis=-1, keepdims=True) + EPS_NORM)
    return (centre * inv_scale, inv_scale)


def normal_back(grad_unit, unit_rows, inv_scale):
    centred = grad_unit - jnp.mean(grad_unit, axis=-1, keepdims=True)
    return inv_scale * (
        centred - unit_rows * jnp.mean(grad_unit * unit_rows, axis=-1, keepdims=True)
    )


def silu_parts(tensor):
    half = 0.5 * tensor
    return half, jnp.tanh(half)


def silu(tensor):
    half, bend = silu_parts(tensor)
    return half * (1.0 + bend)


def fold_rows(store, base, rows, tensor):
    parts = tensor.shape[1] // LANES
    for part in range(parts):
        store[pl.ds(base * parts + part, rows, stride=parts), :] = tensor[
            :, part * LANES : (part + 1) * LANES
        ]


def unfold_rows(store, base, rows, parts):
    return jnp.concatenate(
        [store[pl.ds(base * parts + part, rows, stride=parts), :] for part in range(parts)],
        axis=1,
    )


def forward_kernel(parts, has_next, *refs):
    if has_next:
        (slots, before, middle, after, low, wide, weights, gains, head) = refs[:9]
        (sent, update, update_low, kept, aggregate) = refs[9:14]
        window, picked, hidden, message = refs[14:]
    else:
        (slots, before, middle, after, low, wide, weights, gains) = refs[:8]
        (update_low, kept, aggregate) = refs[8:11]
        window, picked, hidden, message = refs[11:]
    step = pl.program_id(0)
    block_rows = before.shape[0]
    rows, width = low.shape
    fan = kept.shape[0]

    @pl.when(step == 0)
    def _():
        for index, block in enumerate((before, middle, after)):
            fold_rows(window, index * block_rows, block_rows, block[...].astype(WIDE))

    for k in range(fan):

        def pick(trip, carry):
            for lane in range(UNROLL):
                row = trip * UNROLL + lane
                slot = slots[k * block_rows + step * rows + row]
                picked[pl.ds(pl.multiple_of((k * rows + row) * parts, parts), parts), :] = window[
                    pl.ds(pl.multiple_of(slot * parts, parts), parts), :
                ]
            return carry

        lax.fori_loop(0, rows // UNROLL, pick, 0)
    target_low = low[...]
    own_term = product(target_low, weights[1])
    for k in range(fan):
        sender = unfold_rows(picked, k * rows, rows, parts)
        kept[k] = sender.astype(LOW)
        hidden[k * rows : (k + 1) * rows, :] = silu(sender + own_term).astype(LOW)
    message[...] = product(hidden[...], weights[2])
    total = normalize(message[0:rows, :])[0]
    for k in range(1, fan):
        total = total + normalize(message[k * rows : (k + 1) * rows, :])[0]
    total_low = (total * gains[0:1, :]).astype(LOW)
    aggregate[...] = total_low
    node_mix = product(target_low, weights[3]) + product(total_low, weights[4])
    node_out = product(silu(node_mix).astype(LOW), weights[5])
    updated = wide[...].astype(WIDE) + normalize(node_out)[0] * gains[1:2, :]
    updated_low = updated.astype(LOW)
    update_low[...] = updated_low
    if has_next:
        update[...] = updated
        sent[...] = product(updated_low, head[0]).astype(LOW)


def in_hbm(shape, dtype):
    return pltpu.MemorySpace.HBM(shape, dtype)


def on_chip(shape, dtype):
    return pltpu.MemorySpace.VMEM(shape, dtype)


def kept_on_chip(array):
    return pltpu.with_memory_space_constraint(array, pltpu.MemorySpace.VMEM)


def pinned(array):
    return pltpu.with_memory_space_constraint(array, pltpu.MemorySpace.HBM)


def whole(shape):
    zeros = (0,) * len(shape)
    return pl.BlockSpec(shape, lambda step: zeros, pipeline_mode=pl.Buffered(1))


def matrix_spec(first, count, width):
    return pl.BlockSpec(
        (count, width, width), lambda step: (first // count, 0, 0), pipeline_mode=pl.Buffered(1)
    )


def tiled(rows, width):
    return pl.BlockSpec((rows, width), lambda step: (step, 0))


def fanned(fan, rows, width):
    return pl.BlockSpec((fan, rows, width), lambda step: (0, step, 0))


def forward_layer(slots, blocks, target_low, target, weights, next_weights, gains):
    block_rows, width = target_low.shape
    fan = slots.shape[0] // block_rows
    parts = width // LANES
    rows = FORWARD_ROWS
    has_next = next_weights is not None
    shape = functools.partial(in_hbm, (block_rows, width))
    fan_shape = functools.partial(in_hbm, (fan, block_rows, width))
    tile = tiled(rows, width)
    in_specs = [pl.BlockSpec(memory_space=pltpu.SMEM)]
    in_specs += [whole((block_rows, width))] * 3 + [tile, tile]
    in_specs += [matrix_spec(weights[1], 6, width), whole(gains.shape)]
    out_specs = [tile, fanned(fan, rows, width), tile]
    out_shape = [shape(LOW), fan_shape(LOW), shape(LOW)]
    operands = [slots, *blocks, target_low, target, weights[0], gains]
    if has_next:
        in_specs += [matrix_spec(next_weights[1], 1, width)]
        operands += [next_weights[0]]
        out_specs = [tile, tile] + out_specs
        out_shape = [shape(LOW), shape(WIDE)] + out_shape
    return pl.pallas_call(
        functools.partial(forward_kernel, parts, has_next),
        grid=(block_rows // rows,),
        in_specs=in_specs,
        out_specs=out_specs,
        out_shape=out_shape,
        scratch_shapes=[
            pltpu.VMEM((3 * block_rows * parts, LANES), WIDE),
            pltpu.VMEM((fan * rows * parts, LANES), WIDE),
            pltpu.VMEM((fan * rows, width), LOW),
            pltpu.VMEM((fan * rows, width), WIDE),
        ],
        compiler_params=pltpu.CompilerParams(vmem_limit_bytes=54 << 20),
        cost_estimate=pl.CostEstimate(
            flops=2 * (fan + 5) * block_rows * width * width,
            transcendentals=(fan + 1) * block_rows * width,
            bytes_accessed=24 * block_rows * width * 2,
        ),
        name="forward_layer",
    )(
        operands[0],
        kept_on_chip(operands[1]),
        pinned(operands[2]),
        kept_on_chip(operands[3]),
        *map(pinned, operands[4:]),
    )


def backward_kernel(parts, mode, *refs):
    refs = list(refs)
    slots = refs.pop(0)
    if mode != "first":
        returned = [refs.pop(0) for _ in range(3)]
        head = refs.pop(0)
    if mode != "second":
        grad_part = refs.pop(0)
    low, kept, aggregate, weights, gains = refs[:5]
    refs = refs[5:]
    if mode != "first":
        sent_grad = refs.pop(0)
        grad_full = refs.pop(0)
    slot_grads = refs[:3]
    (grad_gains, grad_message, edge_hidden, grad_mix, grad_out, grad_own, hidden) = refs[3:10]
    sum_even, sum_odd, spread, stage = refs[10:]
    step = pl.program_id(0)
    rows, width = low.shape
    fan = kept.shape[0]
    block_rows = slot_grads[0].shape[0]

    @pl.when(step == 0)
    def _():
        sum_even[...] = jnp.zeros_like(sum_even)
        sum_odd[...] = jnp.zeros_like(sum_odd)
        grad_gains[...] = jnp.zeros_like(grad_gains)

    if mode == "first":
        grad_new = grad_part[...]
    else:
        sent_low = (
            returned[0][...].astype(WIDE)
            + returned[1][...].astype(WIDE)
            + returned[2][...].astype(WIDE)
        ).astype(LOW)
        sent_grad[...] = sent_low
        grad_new = product_right(sent_low, head[0])
        if mode == "third":
            grad_new = grad_part[...] + grad_new
        grad_full[...] = grad_new
    target_low = low[...]
    own_term = product(target_low, weights[1])
    node_mix = product(target_low, weights[3]) + product(aggregate[...], weights[4])
    for k in range(fan):
        edge_hidden[k] = silu(kept[k].astype(WIDE) + own_term).astype(LOW)
    stage[...] = product(edge_hidden[...].reshape(fan * rows, width), weights[2])
    half, bend = silu_parts(node_mix)
    node_hidden = (half * (1.0 + bend)).astype(LOW)
    hidden[...] = node_hidden
    out_unit, out_scale = normalize(product(node_hidden, weights[5]))
    gain_two = jnp.sum(grad_new * out_unit, axis=0, keepdims=True)
    out_low = normal_back(grad_new * gains[1:2, :], out_unit, out_scale).astype(LOW)
    grad_out[...] = out_low
    mix_low = (
        product_right(out_low, weights[5]) * ((0.5 + 0.5 * bend) * (1.0 + half * (1.0 - bend)))
    ).astype(LOW)
    grad_mix[...] = mix_low
    grad_sum = product_right(mix_low, weights[4])
    grad_unit = grad_sum * gains[0:1, :]
    unit_total = None
    for k in range(fan):
        unit_rows, inv_scale = normalize(stage[k * rows : (k + 1) * rows, :])
        unit_total = unit_rows if k == 0 else unit_total + unit_rows
        grad_message[k] = normal_back(grad_unit, unit_rows, inv_scale).astype(LOW)
    stage[...] = product_right(grad_message[...].reshape(fan * rows, width), weights[2])
    own_total = None
    for k in range(fan):
        half, bend = silu_parts(kept[k].astype(WIDE) + own_term)
        grad_pre = stage[k * rows : (k + 1) * rows, :] * (
            (0.5 + 0.5 * bend) * (1.0 + half * (1.0 - bend))
        )
        own_total = grad_pre if k == 0 else own_total + grad_pre
        fold_rows(spread, k * rows, rows, grad_pre)
    gain_one = jnp.sum(grad_sum * unit_total, axis=0, keepdims=True)
    grad_gains[...] += jnp.concatenate([gain_one, gain_two], axis=0)
    grad_own[...] = own_total.astype(LOW)

    for k in range(fan):

        def add(trip, carry):
            for lane in range(UNROLL // 2):
                places, values = [], []
                for store in (sum_even, sum_odd):
                    row = (trip * (UNROLL // 2) + lane) * 2 + len(places)
                    slot = slots[k * block_rows + step * rows + row]
                    place = pl.ds(pl.multiple_of(slot * parts, parts), parts)
                    value = spread[pl.ds(pl.multiple_of((k * rows + row) * parts, parts), parts), :]
                    places.append(place)
                    values.append(store[place, :] + value)
                sum_even[places[0], :] = values[0]
                sum_odd[places[1], :] = values[1]
            return carry

        lax.fori_loop(0, rows // UNROLL, add, 0)

    @pl.when(step == pl.num_programs(0) - 1)
    def _():
        for index in range(3):
            base = index * block_rows
            slot_grads[index][...] = (
                unfold_rows(sum_even, base, block_rows, parts)
                + unfold_rows(sum_odd, base, block_rows, parts)
            ).astype(LOW)


def backward_layer(slots, above, grad_part, stored, weights, gains):
    target_low, kept, aggregate = stored
    block_rows, width = target_low.shape
    fan = kept.shape[0]
    parts = width // LANES
    rows = BACKWARD_ROWS
    tile = tiled(rows, width)
    fan_tile = fanned(fan, rows, width)
    in_specs = [pl.BlockSpec(memory_space=pltpu.SMEM)]
    operands = [slots]
    out_specs, out_shape = [], []
    shape = functools.partial(on_chip, (block_rows, width))
    fan_shape = functools.partial(on_chip, (fan, block_rows, width))
    mode = "first" if above is None else ("second" if grad_part is None else "third")
    if above is not None:
        from_before, slot_grad, from_after, head = above
        in_specs += [
            tile,
            tile,
            tile,
            matrix_spec(head[1], 1, width),
        ]
        operands += [from_before, slot_grad, from_after, head[0]]
        out_specs += [tile, tile]
        out_shape += [shape(LOW), shape(WIDE)]
    if grad_part is not None:
        in_specs += [tile]
        operands += [grad_part]
    in_specs += [tile, fan_tile, tile]
    in_specs += [matrix_spec(weights[1], 6, width), whole(gains.shape)]
    operands += [target_low, kept, aggregate, weights[0], gains]
    out_specs += [
        whole((block_rows, width)),
        whole((block_rows, width)),
        whole((block_rows, width)),
        whole((2, width)),
        fan_tile,
        fan_tile,
        tile,
        tile,
        tile,
        tile,
    ]
    out_shape += [
        in_hbm((block_rows, width), LOW),
        in_hbm((block_rows, width), LOW),
        in_hbm((block_rows, width), LOW),
        jax.ShapeDtypeStruct((2, width), WIDE),
        fan_shape(LOW),
        fan_shape(LOW),
        shape(LOW),
        shape(LOW),
        shape(LOW),
        shape(LOW),
    ]
    results = pl.pallas_call(
        functools.partial(backward_kernel, parts, mode),
        grid=(block_rows // rows,),
        in_specs=in_specs,
        out_specs=out_specs,
        out_shape=out_shape,
        scratch_shapes=[
            pltpu.VMEM((3 * block_rows * parts, LANES), WIDE),
            pltpu.VMEM((3 * block_rows * parts, LANES), WIDE),
            pltpu.VMEM((fan * rows * parts, LANES), WIDE),
            pltpu.VMEM((fan * rows, width), WIDE),
        ],
        compiler_params=pltpu.CompilerParams(vmem_limit_bytes=38 << 20),
        cost_estimate=pl.CostEstimate(
            flops=2 * (fan + 4) * block_rows * width * width,
            transcendentals=(fan + 1) * block_rows * width,
            bytes_accessed=24 * block_rows * width * 2,
        ),
        name="backward_layer",
    )(operands[0], *map(pinned, operands[1:]))
    if above is None:
        return (None, grad_part, *results)
    return tuple(results)


def deal(self_id, sums, outs):
    keep, send = outs
    share = keep.shape[1] // sums.shape[0]

    def move(node, carry):
        for core, out in enumerate((keep, send)):
            place = pl.multiple_of(((2 * node + core) ^ self_id[0]) * share, share)
            for index in range(sums.shape[0]):
                out[node, index * share : (index + 1) * share, :] = sums[
                    index, pl.ds(place, share), :
                ].astype(out.dtype)
        return carry

    lax.fori_loop(0, keep.shape[0], move, 0)


def weight_kernel(has_above, needs_target, direct, *refs):
    refs = list(refs)
    if direct:
        self_id = refs.pop(0)
    if has_above:
        source, sent_grad = refs[:2]
        refs = refs[2:]
    else:
        extra = refs.pop(0)
    low, aggregate, edge_hidden, grad_message, grad_mix, grad_out, grad_own, hidden = refs[:8]
    refs = refs[8:]
    if needs_target:
        grad_new, weights = refs[:2]
        grad_part = refs[2]
        refs = refs[3:]
    outs, sums = (refs[:2], refs[2]) if direct else (None, refs[0])
    step = pl.program_id(0)
    fan = edge_hidden.shape[0]

    @pl.when(step == 0)
    def _():
        sums[...] = jnp.zeros_like(sums)
        if not has_above:
            sums[0] = extra[...]

    target_low = low[...]
    mix_low = grad_mix[...]
    own_low = grad_own[...]
    if has_above:
        sums[0] += product_left(source[...], sent_grad[...])
    sums[1] += product_left(target_low, own_low)
    for k in range(fan):
        sums[2] += product_left(edge_hidden[k], grad_message[k])
    sums[3] += product_left(target_low, mix_low)
    sums[4] += product_left(aggregate[...], mix_low)
    sums[5] += product_left(hidden[...], grad_out[...])
    if needs_target:
        grad_part[...] = (
            grad_new[...] + product_right(own_low, weights[1]) + product_right(mix_low, weights[3])
        )
    if direct:

        @pl.when(step == pl.num_programs(0) - 1)
        def _():
            deal(self_id, sums, outs)


def share_outputs(count, width, device_count):
    shape = (device_count // 2, count * (width // device_count), width)
    return (
        [whole(shape)] * 2,
        [on_chip(shape, WIDE), on_chip(shape, SEND)],
    )


def weight_layer(self_id, device_count, above, extra, low, aggregate, back, grad_new, weights):
    block_rows, width = low.shape
    rows = WEIGHT_ROWS
    fan = back[0].shape[0]
    tile = tiled(rows, width)
    fan_tile = fanned(fan, rows, width)
    in_specs, operands = [], []
    direct = self_id is not None
    if direct:
        in_specs += [pl.BlockSpec(memory_space=pltpu.SMEM)]
        operands += [self_id]
    if above is not None:
        in_specs += [tile, tile]
        operands += [pinned(above[0]), kept_on_chip(above[1])]
    else:
        in_specs += [whole((width, width))]
        operands += [extra]
    in_specs += [tile, tile, fan_tile, fan_tile, tile, tile, tile, tile]
    operands += [pinned(low), pinned(aggregate), *map(kept_on_chip, back)]
    out_specs, out_shape, scratch = [], [], []
    if grad_new is not None:
        in_specs += [tile, matrix_spec(weights[1], 6, width)]
        operands += [kept_on_chip(grad_new), pinned(weights[0])]
        out_specs += [tile]
        out_shape += [in_hbm((block_rows, width), WIDE)]
    if direct:
        specs, shapes = share_outputs(6, width, device_count)
        out_specs += specs
        out_shape += shapes
        scratch = [pltpu.VMEM((6, width, width), WIDE)]
    else:
        out_specs += [whole((6, width, width))]
        out_shape += [jax.ShapeDtypeStruct((6, width, width), WIDE)]
    results = pl.pallas_call(
        functools.partial(weight_kernel, above is not None, grad_new is not None, direct),
        grid=(block_rows // rows,),
        in_specs=in_specs,
        out_specs=out_specs,
        out_shape=out_shape,
        scratch_shapes=scratch,
        compiler_params=pltpu.CompilerParams(vmem_limit_bytes=30 << 20),
        cost_estimate=pl.CostEstimate(
            flops=2 * (fan + 6) * block_rows * width * width,
            transcendentals=0,
            bytes_accessed=24 * block_rows * width,
        ),
        name="weight_layer",
    )(*operands)
    if grad_new is None:
        return (None, results)
    return (results[0], results[1:])


def embed_kernel(pieces_count, *refs):
    self_id = refs[0]
    pieces = refs[1 : 1 + pieces_count]
    before, middle, after = refs[1 + pieces_count : 4 + pieces_count]
    weights, latent, latent_low, sent_before, sent_middle, sent_after, table = refs[
        4 + pieces_count :
    ]
    count, width = weights.shape[0], weights.shape[1]
    high = pieces[0].shape[0]
    share = width // (high * pieces_count)

    @pl.when(pl.program_id(0) == 0)
    def _():
        for index, piece in enumerate(pieces):
            core, low_digit = index // (pieces_count // 2), index % (pieces_count // 2)

            def move(digit, carry, piece=piece, core=core, low_digit=low_digit):
                relative = digit * pieces_count + low_digit * 2 + core
                place = pl.multiple_of((relative ^ self_id[0]) * share, share)
                for j in range(count):
                    weights[j, pl.ds(place, share), :] = piece[digit, j * share : (j + 1) * share, :]
                table[pl.ds(place, share), :] = piece[digit, count * share : (count + 1) * share, :]
                return carry

            lax.fori_loop(0, high, move, 0)

    for block, sent in ((before, sent_before), (middle, sent_middle), (after, sent_after)):
        wide = product_right(block[...], table[...])
        low = wide.astype(LOW)
        sent[...] = product(low, weights[0]).astype(LOW)
        if block is middle:
            latent[...] = wide
            latent_low[...] = low


def embed(self_id, pieces, blocks):
    block_rows, width = blocks[1].shape
    rows = WEIGHT_ROWS
    tile = tiled(rows, width)
    return pl.pallas_call(
        functools.partial(embed_kernel, len(pieces)),
        grid=(block_rows // rows,),
        in_specs=[pl.BlockSpec(memory_space=pltpu.SMEM)]
        + [whole(piece.shape) for piece in pieces]
        + [tile] * 3,
        out_specs=[whole((7, width, width))] + [tile] * 5,
        out_shape=[
            in_hbm((7, width, width), LOW),
            in_hbm((block_rows, width), WIDE),
            in_hbm((block_rows, width), LOW),
            on_chip((block_rows, width), LOW),
            in_hbm((block_rows, width), LOW),
            on_chip((block_rows, width), LOW),
        ],
        scratch_shapes=[pltpu.VMEM((width, width), LOW)],
        compiler_params=pltpu.CompilerParams(vmem_limit_bytes=50 << 20),
        cost_estimate=pl.CostEstimate(
            flops=12 * block_rows * width * width,
            transcendentals=0,
            bytes_accessed=24 * block_rows * width,
        ),
        name="embed",
    )(self_id, *pieces, *blocks)


def tail_kernel(self_id, before, middle, after, latent_low, inputs, grad_grid, head, misc, *refs):
    keep, send, sums = refs
    step = pl.program_id(0)
    rows, width = inputs.shape
    share = misc.shape[1]

    @pl.when(step == 0)
    def _():
        sums[...] = jnp.zeros_like(sums)

    sent_low = (
        before[...].astype(WIDE)
        + middle[...].astype(WIDE)
        + after[...].astype(WIDE)
    ).astype(LOW)
    grad_low = (grad_grid[...] + product_right(sent_low, head[0])).astype(LOW)
    sums[0] += product_left(latent_low[...], sent_low)
    sums[1] += product_left(grad_low, inputs[...])

    @pl.when(step == pl.num_programs(0) - 1)
    def _():
        size = sums.shape[0] * (width // misc.shape[0])
        main = [out.at[:, 0:size, :] for out in (keep, send)]
        deal(self_id, sums, main)

        def move(node, carry):
            for core, out in enumerate((keep, send)):
                out[node, size : size + share, :] = misc[(2 * node + core) ^ self_id[0]].astype(
                    out.dtype
                )
            return carry

        lax.fori_loop(0, keep.shape[0], move, 0)


def tail_layer(self_id, from_before, slot_grad, from_after, latent_low, inputs, grad_grid, head, misc):
    block_rows, width = inputs.shape
    device_count = misc.shape[0]
    rows = WEIGHT_ROWS
    tile = tiled(rows, width)
    shape = (device_count // 2, 2 * (width // device_count) + misc.shape[1], width)
    return pl.pallas_call(
        tail_kernel,
        grid=(block_rows // rows,),
        in_specs=[
            pl.BlockSpec(memory_space=pltpu.SMEM),
            tile,
            tile,
            tile,
            tile,
            tile,
            tile,
            matrix_spec(head[1], 1, width),
            whole(misc.shape),
        ],
        out_specs=[whole(shape)] * 2,
        out_shape=[on_chip(shape, WIDE), on_chip(shape, SEND)],
        scratch_shapes=[pltpu.VMEM((2, width, width), WIDE)],
        compiler_params=pltpu.CompilerParams(vmem_limit_bytes=56 << 20),
        cost_estimate=pl.CostEstimate(
            flops=6 * block_rows * width * width,
            transcendentals=0,
            bytes_accessed=24 * block_rows * width,
        ),
        name="tail_layer",
    )(
        self_id,
        *map(pinned, (from_before, slot_grad, from_after, latent_low, inputs, grad_grid, head[0])),
        misc,
    )


def combine_kernel(count, *refs):
    arrived, outs = refs[:count], refs[count:]
    for digit, out in enumerate(outs):
        total = arrived[0][0, digit].astype(WIDE)
        for part in arrived[1:]:
            total = total + part[0, digit].astype(WIDE)
        out[0] = total.astype(out.dtype)


def combine(arrived, radix):
    _, rows, width = arrived[0].shape
    rest = arrived[0].shape[0] // radix
    arrived = [part.reshape(rest, radix, rows, width) for part in arrived]
    spec = pl.BlockSpec((1, radix, rows, width), lambda step: (step, 0, 0, 0))
    shape = (rest, rows, width)
    return pl.pallas_call(
        functools.partial(combine_kernel, len(arrived)),
        grid=(rest,),
        in_specs=[spec] * len(arrived),
        out_specs=[pl.BlockSpec((1, rows, width), lambda step: (step, 0, 0))] * radix,
        out_shape=[on_chip(shape, WIDE)] + [on_chip(shape, SEND)] * (radix - 1),
        compiler_params=pltpu.CompilerParams(vmem_limit_bytes=20 << 20),
        cost_estimate=pl.CostEstimate(
            flops=rest * radix * rows * width * len(arrived),
            transcendentals=0,
            bytes_accessed=4 * rest * radix * rows * width * (len(arrived) + 1),
        ),
        name="combine",
    )(*map(kept_on_chip, arrived))


def swap(cells, count, mask):
    return lax.ppermute(cells, AXES, [(i, i ^ mask) for i in range(count)])


def spread_column(packed, count):
    high = 4 * 2
    return [packed] + [swap(packed, count, digit * high) for digit in range(1, count // high)]


def spread_rows(held, count):
    column = jnp.stack(held)
    near = [column] + [swap(column, count, digit * 2) for digit in range(1, 4)]
    return near + [swap(piece, count, 1) for piece in near]


def shift(cells, count, step):
    return lax.ppermute(cells, AXES, [(i, (i + step) % count) for i in range(count)])


def fan_out(pieces, count, unit):
    return [pieces[0]] + [
        swap(pieces[digit], count, digit * unit) for digit in range(1, len(pieces))
    ]


def together(first, second):
    joined = lax.optimization_barrier((tuple(first), tuple(second)))
    return list(joined[0]), list(joined[1])


def add_up(arrived):
    total = arrived[0][0]
    for part in arrived[1:]:
        total = total + part[0].astype(WIDE)
    return total


def adamw_update(weight, moment_one, moment_two, gradient, step_value, decay_rate):
    new_one = BETA_ONE * moment_one + (1.0 - BETA_ONE) * gradient
    new_two = BETA_TWO * moment_two + (1.0 - BETA_TWO) * gradient * gradient
    correct_one = 1.0 - jnp.power(BETA_ONE, step_value)
    correct_two = 1.0 - jnp.power(BETA_TWO, step_value)
    direction = new_one / correct_one / (jnp.sqrt(new_two / correct_two) + ADAM_EPS)
    return (new_one, new_two, weight - LEARN_RATE * (direction + decay_rate * weight))


def shards(
    grid_inputs,
    mesh_static,
    targets,
    area_weight,
    valid_rows,
    encoder_lists,
    mesh_lists,
    decoder_lists,
    step_count,
    w_in,
    moment_in,
    square_in,
    w_layers,
    moment_layers,
    square_layers,
    norm_gains,
    moment_gains,
    square_gains,
    w_out,
    moment_out,
    square_out,
):
    row_count = grid_inputs.shape[0]
    layer_total = w_layers.shape[0]
    device_count = lax.axis_size(AXES)
    width = mesh_static.shape[1]
    share = w_layers.shape[2]
    channels, outputs = w_in.shape[0], w_out.shape[1]
    direct = share == 16 and device_count % 8 == 0 and device_count & (device_count - 1) == 0
    slot_lists = [encoder_lists.T.reshape(-1)]
    slot_lists += [mesh_lists.T.reshape(-1)] * (layer_total - 2)
    slot_lists += [decoder_lists.T.reshape(-1)]
    if direct:
        self_id = lax.axis_index(AXES).astype(jnp.int32)
        order = jnp.arange(device_count, dtype=jnp.int32) ^ self_id
        self_id = self_id.reshape(1)
        inputs = jnp.pad(grid_inputs, ((0, 0), (0, width - channels)))
        flat_gains = norm_gains.astype(LOW).reshape(1, -1)
        packed = jnp.concatenate(
            [
                w_layers[0].astype(LOW).reshape(-1, width),
                w_layers[1, 0].astype(LOW),
                jnp.pad(w_in.astype(LOW).T, ((0, 0), (0, width - channels))),
                jnp.pad(flat_gains, ((0, 7), (0, width - flat_gains.shape[1]))),
            ],
            axis=0,
        )
        second = jnp.concatenate([w_layers[2, :1], w_layers[1, 1:]], axis=0).astype(LOW)
        rest = jnp.concatenate(
            [
                jnp.pad(w_out.astype(LOW), ((0, 0), (0, width - outputs)))[None],
                w_layers[2, 1:].astype(LOW),
                w_layers[3:].astype(LOW).reshape(-1, share, width),
            ],
            axis=0,
        )
        held = spread_column(packed, device_count)
        sides = [shift(inputs, device_count, 1), shift(inputs, device_count, -1)]
        held, sides = together(held, [*sides, second])
        second = lax.all_gather(sides[2], AXES, axis=1, tiled=True)
        pieces = spread_rows(held, device_count)
        pieces, (rest,) = together(pieces, [rest])
        rest = lax.all_gather(rest, AXES, axis=1, tiled=True)
        first, grid_latent, grid_start, *blocks = embed(
            self_id, pieces, (sides[0], inputs, sides[1])
        )
        weights = [(first, 0), (second, 0)]
        weights += [(rest, 6 * layer_id) for layer_id in range(layer_total - 2)]
        heads = [(first, 0), (first, 6), (second, 0)]
        heads += weights[3:]
        table_out = rest[0, :, :outputs]
        gain_rows = jnp.stack(pieces)[:, :, packed.shape[0] - 8, : flat_gains.shape[1]]
        gain_rows = gain_rows.reshape(2, 4, device_count // 8, -1).transpose(2, 1, 0, 3)
        gain_rows = gain_rows.reshape(device_count, -1)[order]
        gains = gain_rows.reshape(device_count, layer_total, 2, share).transpose(1, 2, 0, 3)
        gains = gains.reshape(layer_total, 2, width).astype(WIDE)
    else:
        self_id = None
        table_in = lax.all_gather(w_in.astype(LOW), AXES, axis=1, tiled=True)
        table_out = lax.all_gather(w_out.astype(LOW), AXES, axis=0, tiled=True)
        matrices = lax.all_gather(w_layers.astype(LOW), AXES, axis=2, tiled=True)
        matrices = matrices.reshape(-1, width, width)
        weights = [(matrices, 6 * layer_id) for layer_id in range(layer_total)]
        heads = weights
        gains = lax.all_gather(norm_gains.astype(LOW), AXES, axis=2, tiled=True).astype(WIDE)
        grid_latent = product(grid_inputs, table_in)
        grid_start = grid_latent.astype(LOW)
        sent = product(grid_start, matrices[0]).astype(LOW)
        blocks = (shift(sent, device_count, 1), sent, shift(sent, device_count, -1))
    target, target_low = mesh_static, mesh_static
    stored_list = []
    for layer_id in range(layer_total):
        last_layer = layer_id == layer_total - 1
        if last_layer:
            source_low = target_low
            target, target_low = grid_latent, grid_start
        else:
            source_low = grid_start if layer_id == 0 else target_low
        results = forward_layer(
            slot_lists[layer_id],
            blocks,
            target_low,
            target,
            weights[layer_id],
            None if last_layer else heads[layer_id + 1],
            gains[layer_id],
        )
        if last_layer:
            grid_low, kept, aggregate = results
        else:
            sent, updated, updated_low, kept, aggregate = results
            blocks = (shift(sent, device_count, 1), sent, shift(sent, device_count, -1))
        stored_list.append((source_low, (target_low, kept, aggregate), aggregate))
        if not last_layer:
            target, target_low = updated, updated_low
    prediction = product(grid_low, table_out)
    local_rows = jnp.arange(row_count, dtype=jnp.int32)
    weight_rows = area_weight * (local_rows < valid_rows[0]).astype(WIDE)
    error_rows = prediction - targets
    loss_scale = 1.0 / (row_count * device_count * prediction.shape[1])
    loss_local = jnp.sum(weight_rows[:, None] * error_rows * error_rows) * loss_scale
    grad_pred = (2.0 * loss_scale * weight_rows[:, None] * error_rows).astype(LOW)
    grad_table_out = product_left(grid_low, grad_pred)
    grad_part = product_right(grad_pred, table_out)
    extra = jnp.pad(grad_table_out, ((0, 0), (0, width - outputs)))
    grad_grid = None
    above, above_source = None, None
    layer_grads = [None] * layer_total
    gain_grads = [None] * layer_total
    in_plane, in_slice = [], []
    for layer_id in reversed(range(layer_total)):
        source_low, stored, aggregate = stored_list[layer_id]
        sent_grad, grad_new, *slot_grads, grad_gain, grad_message, edge_hidden, b0, b1, b2, b3 = backward_layer(
            slot_lists[layer_id], above, grad_part, stored, weights[layer_id], gains[layer_id]
        )
        far = []
        if in_plane:
            moved = len(in_plane)
            arrived, slot_grads = together(in_plane + in_slice, slot_grads)
            if in_slice:
                layer_grads[layer_id + 2] = add_up(arrived[moved:]).reshape(6, share, width)
            far = list(combine(arrived[:moved], device_count // 8))
        from_before = shift(slot_grads[2], device_count, 1)
        from_after = shift(slot_grads[0], device_count, -1)
        back = [edge_hidden, grad_message, b0, b1, b2, b3]
        grad_part, sums = weight_layer(
            self_id,
            device_count,
            None if above is None else (above_source, sent_grad),
            extra,
            stored[0],
            aggregate,
            back,
            None if layer_id == 0 else grad_new,
            weights[layer_id],
        )
        gain_grads[layer_id] = grad_gain
        if direct:
            halo, arrived = together([from_before, from_after], [*sums, *far])
            keep, send, far = arrived[0], arrived[1], arrived[2:]
            in_slice = fan_out(far, device_count, 8) if far else []
            other = swap(send, device_count, 1)
            if layer_id > 0:
                near = list(combine([keep, other], 4))
                halo, near = together(halo, near)
                in_plane = fan_out(near, device_count, 2)
            from_before, from_after = halo
        else:
            layer_grads[layer_id] = sums[0]
        if layer_id == layer_total - 1:
            grad_grid, grad_part = grad_part, None
        above = (from_before, slot_grads[1], from_after, heads[layer_id])
        above_source = source_low
    if direct:
        misc = jnp.stack(gain_grads).reshape(-1, device_count, share).transpose(1, 0, 2)
        misc = misc.reshape(device_count, -1)
        misc = jnp.concatenate(
            [misc, jnp.broadcast_to(loss_local.reshape(1, 1), (device_count, 1))], axis=1
        )
        misc = jnp.pad(misc[:, None, :], ((0, 0), (0, 7), (0, width - misc.shape[1])))
        sums = tail_layer(
            self_id,
            from_before,
            slot_grads[1],
            from_after,
            grid_start,
            inputs,
            grad_grid,
            heads[0],
            misc,
        )
        arrived, sums = together([other] + in_slice, sums)
        other, in_slice = arrived[0], arrived[1:]
        near = combine([keep, other], 4)
        layer_grads[1] = add_up(in_slice).reshape(6, share, width)
        far = combine(fan_out(near, device_count, 2), device_count // 8)
        layer_grads[0] = add_up(fan_out(far, device_count, 8)).reshape(6, share, width)
        keep, send = sums
        pieces = combine([keep, swap(send, device_count, 1)], 4)
        pieces = combine(fan_out(pieces, device_count, 2), device_count // 8)
        total = add_up(fan_out(pieces, device_count, 8))
        grad_zero = total[:share]
        grad_in = total[share : 2 * share, :channels].T
        size = layer_total * 2 * share
        grad_gain_all = total[2 * share, :size].reshape(layer_total, 2, share)
        loss_value = total[2 * share, size]
        grad_out = layer_grads[-1][0, :, :outputs]
    else:
        loss_value = lax.psum(loss_local, AXES)
        sent_grad = (
            from_before.astype(WIDE) + slot_grads[1].astype(WIDE) + from_after.astype(WIDE)
        ).astype(LOW)
        grad_zero = product_left(above_source, sent_grad)
        grad_grid = grad_grid + product_right(sent_grad, matrices[0])
        grad_table_in = product_left(grid_inputs, grad_grid.astype(LOW))
        grad_in = lax.psum_scatter(grad_table_in, AXES, scatter_dimension=1, tiled=True)
        grad_out = lax.psum_scatter(grad_table_out, AXES, scatter_dimension=0, tiled=True)
        grad_gain_all = lax.psum_scatter(
            jnp.stack(gain_grads), AXES, scatter_dimension=2, tiled=True
        )
    grad_layers = [grad_zero[None]]
    for layer_id in range(layer_total):
        grad_layers += [layer_grads[layer_id][1:]]
        if layer_id < layer_total - 1:
            grad_layers += [layer_grads[layer_id][0:1]]
    grad_layers = jnp.concatenate(grad_layers, axis=0)
    grad_layers = grad_layers.reshape(layer_total, 6, *grad_layers.shape[1:])
    if not direct:
        grad_layers = lax.psum_scatter(grad_layers, AXES, scatter_dimension=2, tiled=True)
    step_value = step_count[0].astype(WIDE)
    one_in, two_in, new_in = adamw_update(
        w_in, moment_in, square_in, grad_in, step_value, DECAY_RATE
    )
    one_layers, two_layers, new_layers = adamw_update(
        w_layers, moment_layers, square_layers, grad_layers, step_value, DECAY_RATE
    )
    one_gains, two_gains, new_gains = adamw_update(
        norm_gains, moment_gains, square_gains, grad_gain_all, step_value, 0.0
    )
    one_out, two_out, new_out = adamw_update(
        w_out, moment_out, square_out, grad_out, step_value, DECAY_RATE
    )
    return (
        loss_value,
        one_in,
        two_in,
        new_in,
        one_layers,
        two_layers,
        new_layers,
        one_gains,
        two_gains,
        new_gains,
        one_out,
        two_out,
        new_out,
    )


def solution(mesh):
    rows = P(AXES, None)
    layers = P(None, None, AXES, None)
    gains = P(None, None, AXES)
    columns = P(None, AXES)
    in_specs = (rows, rows, rows, P(AXES), P(AXES), rows, rows, rows, P())
    in_specs += (columns,) * 3 + (layers,) * 3 + (gains,) * 3 + (rows,) * 3
    out_specs = (P(),) + (columns,) * 3 + (layers,) * 3 + (gains,) * 3 + (rows,) * 3
    return jax.shard_map(shards, mesh=mesh, in_specs=in_specs, out_specs=out_specs, check_vma=False)
```

```python
import functools

import jax
import jax.numpy as jnp
from jax import lax
from jax.experimental import pallas as pl
from jax.experimental.pallas import tpu as pltpu
from jax.sharding import PartitionSpec as P

EPS_NORM = 1e-05
BETA_ONE = 0.5
BETA_TWO = 0.5
ADAM_EPS = 1e-08
LEARN_RATE = 0.04
DECAY_RATE = 0.1

AXES = ("nodes", "shard")
LANES = 128
FORWARD_ROWS = 256
BACKWARD_ROWS = 256
WEIGHT_ROWS = 256
UNROLL = 32
LOW = jnp.bfloat16
WIDE = jnp.float32
SEND = jnp.bfloat16


def product(left, right):
    return jnp.dot(left, right, preferred_element_type=WIDE)


def product_left(left, right):
    return lax.dot_general(left, right, (((0,), (0,)), ((), ())), preferred_element_type=WIDE)


def product_right(left, right):
    return lax.dot_general(left, right, (((1,), (1,)), ((), ())), preferred_element_type=WIDE)


def normalize(tensor):
    centre = tensor - jnp.mean(tensor, axis=-1, keepdims=True)
    inv_scale = lax.rsqrt(jnp.mean(centre * centre, axis=-1, keepdims=True) + EPS_NORM)
    return (centre * inv_scale, inv_scale)


def normal_back(grad_unit, unit_rows, inv_scale):
    centred = grad_unit - jnp.mean(grad_unit, axis=-1, keepdims=True)
    return inv_scale * (
        centred - unit_rows * jnp.mean(grad_unit * unit_rows, axis=-1, keepdims=True)
    )


def silu_parts(tensor):
    half = 0.5 * tensor
    return half, jnp.tanh(half)


def silu(tensor):
    half, bend = silu_parts(tensor)
    return half * (1.0 + bend)


def fold_rows(store, base, rows, tensor):
    parts = tensor.shape[1] // LANES
    for part in range(parts):
        store[pl.ds(base * parts + part, rows, stride=parts), :] = tensor[
            :, part * LANES : (part + 1) * LANES
        ]


def unfold_rows(store, base, rows, parts):
    return jnp.concatenate(
        [store[pl.ds(base * parts + part, rows, stride=parts), :] for part in range(parts)],
        axis=1,
    )


def forward_kernel(parts, has_next, *refs):
    if has_next:
        (slots, before, middle, after, low, wide, weights, gains, head) = refs[:9]
        (sent, update, update_low, kept, aggregate) = refs[9:14]
        window, picked, hidden, message = refs[14:]
    else:
        (slots, before, middle, after, low, wide, weights, gains) = refs[:8]
        (update_low, kept, aggregate) = refs[8:11]
        window, picked, hidden, message = refs[11:]
    step = pl.program_id(0)
    block_rows = before.shape[0]
    rows, width = low.shape
    fan = kept.shape[0]

    @pl.when(step == 0)
    def _():
        for index, block in enumerate((before, middle, after)):
            fold_rows(window, index * block_rows, block_rows, block[...].astype(WIDE))

    for k in range(fan):

        def pick(trip, carry):
            for lane in range(UNROLL):
                row = trip * UNROLL + lane
                slot = slots[k * block_rows + step * rows + row]
                picked[pl.ds(pl.multiple_of((k * rows + row) * parts, parts), parts), :] = window[
                    pl.ds(pl.multiple_of(slot * parts, parts), parts), :
                ]
            return carry

        lax.fori_loop(0, rows // UNROLL, pick, 0)
    target_low = low[...]
    own_term = product(target_low, weights[1])
    for k in range(fan):
        sender = unfold_rows(picked, k * rows, rows, parts)
        kept[k] = sender.astype(LOW)
        hidden[k * rows : (k + 1) * rows, :] = silu(sender + own_term).astype(LOW)
    message[...] = product(hidden[...], weights[2])
    total = normalize(message[0:rows, :])[0]
    for k in range(1, fan):
        total = total + normalize(message[k * rows : (k + 1) * rows, :])[0]
    total_low = (total * gains[0:1, :]).astype(LOW)
    aggregate[...] = total_low
    node_mix = product(target_low, weights[3]) + product(total_low, weights[4])
    node_out = product(silu(node_mix).astype(LOW), weights[5])
    updated = wide[...].astype(WIDE) + normalize(node_out)[0] * gains[1:2, :]
    updated_low = updated.astype(LOW)
    update_low[...] = updated_low
    if has_next:
        update[...] = updated
        sent[...] = product(updated_low, head[0]).astype(LOW)


def in_hbm(shape, dtype):
    return pltpu.MemorySpace.HBM(shape, dtype)


def on_chip(shape, dtype):
    return pltpu.MemorySpace.VMEM(shape, dtype)


def kept_on_chip(array):
    return pltpu.with_memory_space_constraint(array, pltpu.MemorySpace.VMEM)


def pinned(array):
    return pltpu.with_memory_space_constraint(array, pltpu.MemorySpace.HBM)


def whole(shape):
    zeros = (0,) * len(shape)
    return pl.BlockSpec(shape, lambda step: zeros, pipeline_mode=pl.Buffered(1))


def matrix_spec(first, count, width):
    return pl.BlockSpec(
        (count, width, width), lambda step: (first // count, 0, 0), pipeline_mode=pl.Buffered(1)
    )


def tiled(rows, width):
    return pl.BlockSpec((rows, width), lambda step: (step, 0))


def fanned(fan, rows, width):
    return pl.BlockSpec((fan, rows, width), lambda step: (0, step, 0))


def forward_layer(slots, blocks, target_low, target, weights, next_weights, gains):
    block_rows, width = target_low.shape
    fan = slots.shape[0] // block_rows
    parts = width // LANES
    rows = FORWARD_ROWS
    has_next = next_weights is not None
    shape = functools.partial(in_hbm, (block_rows, width))
    fan_shape = functools.partial(in_hbm, (fan, block_rows, width))
    tile = tiled(rows, width)
    in_specs = [pl.BlockSpec(memory_space=pltpu.SMEM)]
    in_specs += [whole((block_rows, width))] * 3 + [tile, tile]
    in_specs += [matrix_spec(weights[1], 6, width), whole(gains.shape)]
    out_specs = [tile, fanned(fan, rows, width), tile]
    out_shape = [shape(LOW), fan_shape(LOW), shape(LOW)]
    operands = [slots, *blocks, target_low, target, weights[0], gains]
    if has_next:
        in_specs += [matrix_spec(next_weights[1], 1, width)]
        operands += [next_weights[0]]
        out_specs = [tile, tile] + out_specs
        out_shape = [shape(LOW), shape(WIDE)] + out_shape
    return pl.pallas_call(
        functools.partial(forward_kernel, parts, has_next),
        grid=(block_rows // rows,),
        in_specs=in_specs,
        out_specs=out_specs,
        out_shape=out_shape,
        scratch_shapes=[
            pltpu.VMEM((3 * block_rows * parts, LANES), WIDE),
            pltpu.VMEM((fan * rows * parts, LANES), WIDE),
            pltpu.VMEM((fan * rows, width), LOW),
            pltpu.VMEM((fan * rows, width), WIDE),
        ],
        compiler_params=pltpu.CompilerParams(vmem_limit_bytes=54 << 20),
        cost_estimate=pl.CostEstimate(
            flops=2 * (fan + 5) * block_rows * width * width,
            transcendentals=(fan + 1) * block_rows * width,
            bytes_accessed=24 * block_rows * width * 2,
        ),
        name="forward_layer",
    )(
        operands[0],
        kept_on_chip(operands[1]),
        pinned(operands[2]),
        kept_on_chip(operands[3]),
        *map(pinned, operands[4:]),
    )


def backward_kernel(parts, mode, *refs):
    refs = list(refs)
    slots = refs.pop(0)
    if mode != "first":
        returned = [refs.pop(0) for _ in range(3)]
        head = refs.pop(0)
    if mode != "second":
        grad_part = refs.pop(0)
    low, kept, aggregate, weights, gains = refs[:5]
    refs = refs[5:]
    if mode != "first":
        sent_grad = refs.pop(0)
        grad_full = refs.pop(0)
    slot_grads = refs[:3]
    (grad_gains, grad_message, edge_hidden, grad_mix, grad_out, grad_own, hidden) = refs[3:10]
    sum_even, sum_odd, spread, stage = refs[10:]
    step = pl.program_id(0)
    rows, width = low.shape
    fan = kept.shape[0]
    block_rows = slot_grads[0].shape[0]

    @pl.when(step == 0)
    def _():
        sum_even[...] = jnp.zeros_like(sum_even)
        sum_odd[...] = jnp.zeros_like(sum_odd)
        grad_gains[...] = jnp.zeros_like(grad_gains)

    if mode == "first":
        grad_new = grad_part[...]
    else:
        sent_low = (
            returned[0][...].astype(WIDE)
            + returned[1][...].astype(WIDE)
            + returned[2][...].astype(WIDE)
        ).astype(LOW)
        sent_grad[...] = sent_low
        grad_new = product_right(sent_low, head[0])
        if mode == "third":
            grad_new = grad_part[...] + grad_new
        grad_full[...] = grad_new
    target_low = low[...]
    own_term = product(target_low, weights[1])
    node_mix = product(target_low, weights[3]) + product(aggregate[...], weights[4])
    for k in range(fan):
        edge_hidden[k] = silu(kept[k].astype(WIDE) + own_term).astype(LOW)
    stage[...] = product(edge_hidden[...].reshape(fan * rows, width), weights[2])
    half, bend = silu_parts(node_mix)
    node_hidden = (half * (1.0 + bend)).astype(LOW)
    hidden[...] = node_hidden
    out_unit, out_scale = normalize(product(node_hidden, weights[5]))
    gain_two = jnp.sum(grad_new * out_unit, axis=0, keepdims=True)
    out_low = normal_back(grad_new * gains[1:2, :], out_unit, out_scale).astype(LOW)
    grad_out[...] = out_low
    mix_low = (
        product_right(out_low, weights[5]) * ((0.5 + 0.5 * bend) * (1.0 + half * (1.0 - bend)))
    ).astype(LOW)
    grad_mix[...] = mix_low
    grad_sum = product_right(mix_low, weights[4])
    grad_unit = grad_sum * gains[0:1, :]
    unit_total = None
    for k in range(fan):
        unit_rows, inv_scale = normalize(stage[k * rows : (k + 1) * rows, :])
        unit_total = unit_rows if k == 0 else unit_total + unit_rows
        grad_message[k] = normal_back(grad_unit, unit_rows, inv_scale).astype(LOW)
    stage[...] = product_right(grad_message[...].reshape(fan * rows, width), weights[2])
    own_total = None
    for k in range(fan):
        half, bend = silu_parts(kept[k].astype(WIDE) + own_term)
        grad_pre = stage[k * rows : (k + 1) * rows, :] * (
            (0.5 + 0.5 * bend) * (1.0 + half * (1.0 - bend))
        )
        own_total = grad_pre if k == 0 else own_total + grad_pre
        fold_rows(spread, k * rows, rows, grad_pre)
    gain_one = jnp.sum(grad_sum * unit_total, axis=0, keepdims=True)
    grad_gains[...] += jnp.concatenate([gain_one, gain_two], axis=0)
    grad_own[...] = own_total.astype(LOW)

    for k in range(fan):

        def add(trip, carry):
            for lane in range(UNROLL // 2):
                places, values = [], []
                for store in (sum_even, sum_odd):
                    row = (trip * (UNROLL // 2) + lane) * 2 + len(places)
                    slot = slots[k * block_rows + step * rows + row]
                    place = pl.ds(pl.multiple_of(slot * parts, parts), parts)
                    value = spread[pl.ds(pl.multiple_of((k * rows + row) * parts, parts), parts), :]
                    places.append(place)
                    values.append(store[place, :] + value)
                sum_even[places[0], :] = values[0]
                sum_odd[places[1], :] = values[1]
            return carry

        lax.fori_loop(0, rows // UNROLL, add, 0)

    @pl.when(step == pl.num_programs(0) - 1)
    def _():
        for index in range(3):
            base = index * block_rows
            slot_grads[index][...] = (
                unfold_rows(sum_even, base, block_rows, parts)
                + unfold_rows(sum_odd, base, block_rows, parts)
            ).astype(LOW)


def backward_layer(slots, above, grad_part, stored, weights, gains):
    target_low, kept, aggregate = stored
    block_rows, width = target_low.shape
    fan = kept.shape[0]
    parts = width // LANES
    rows = BACKWARD_ROWS
    tile = tiled(rows, width)
    fan_tile = fanned(fan, rows, width)
    in_specs = [pl.BlockSpec(memory_space=pltpu.SMEM)]
    operands = [slots]
    out_specs, out_shape = [], []
    shape = functools.partial(on_chip, (block_rows, width))
    fan_shape = functools.partial(on_chip, (fan, block_rows, width))
    mode = "first" if above is None else ("second" if grad_part is None else "third")
    if above is not None:
        from_before, slot_grad, from_after, head = above
        in_specs += [
            tile,
            tile,
            tile,
            matrix_spec(head[1], 1, width),
        ]
        operands += [from_before, slot_grad, from_after, head[0]]
        out_specs += [tile, tile]
        out_shape += [shape(LOW), shape(WIDE)]
    if grad_part is not None:
        in_specs += [tile]
        operands += [grad_part]
    in_specs += [tile, fan_tile, tile]
    in_specs += [matrix_spec(weights[1], 6, width), whole(gains.shape)]
    operands += [target_low, kept, aggregate, weights[0], gains]
    out_specs += [
        whole((block_rows, width)),
        whole((block_rows, width)),
        whole((block_rows, width)),
        whole((2, width)),
        fan_tile,
        fan_tile,
        tile,
        tile,
        tile,
        tile,
    ]
    out_shape += [
        in_hbm((block_rows, width), LOW),
        in_hbm((block_rows, width), LOW),
        in_hbm((block_rows, width), LOW),
        jax.ShapeDtypeStruct((2, width), WIDE),
        fan_shape(LOW),
        fan_shape(LOW),
        shape(LOW),
        shape(LOW),
        shape(LOW),
        shape(LOW),
    ]
    results = pl.pallas_call(
        functools.partial(backward_kernel, parts, mode),
        grid=(block_rows // rows,),
        in_specs=in_specs,
        out_specs=out_specs,
        out_shape=out_shape,
        scratch_shapes=[
            pltpu.VMEM((3 * block_rows * parts, LANES), WIDE),
            pltpu.VMEM((3 * block_rows * parts, LANES), WIDE),
            pltpu.VMEM((fan * rows * parts, LANES), WIDE),
            pltpu.VMEM((fan * rows, width), WIDE),
        ],
        compiler_params=pltpu.CompilerParams(vmem_limit_bytes=38 << 20),
        cost_estimate=pl.CostEstimate(
            flops=2 * (fan + 4) * block_rows * width * width,
            transcendentals=(fan + 1) * block_rows * width,
            bytes_accessed=24 * block_rows * width * 2,
        ),
        name="backward_layer",
    )(operands[0], *map(pinned, operands[1:]))
    if above is None:
        return (None, grad_part, *results)
    return tuple(results)


def deal(self_id, sums, outs):
    keep, send = outs
    share = keep.shape[1] // sums.shape[0]

    def move(node, carry):
        for core, out in enumerate((keep, send)):
            place = pl.multiple_of(((2 * node + core) ^ self_id[0]) * share, share)
            for index in range(sums.shape[0]):
                out[node, index * share : (index + 1) * share, :] = sums[
                    index, pl.ds(place, share), :
                ].astype(out.dtype)
        return carry

    lax.fori_loop(0, keep.shape[0], move, 0)


def weight_kernel(has_above, needs_target, direct, *refs):
    refs = list(refs)
    if direct:
        self_id = refs.pop(0)
    if has_above:
        source, sent_grad = refs[:2]
        refs = refs[2:]
    else:
        extra = refs.pop(0)
    low, aggregate, edge_hidden, grad_message, grad_mix, grad_out, grad_own, hidden = refs[:8]
    refs = refs[8:]
    if needs_target:
        grad_new, weights = refs[:2]
        grad_part = refs[2]
        refs = refs[3:]
    outs, sums = (refs[:2], refs[2]) if direct else (None, refs[0])
    step = pl.program_id(0)
    fan = edge_hidden.shape[0]

    @pl.when(step == 0)
    def _():
        sums[...] = jnp.zeros_like(sums)
        if not has_above:
            sums[0] = extra[...]

    target_low = low[...]
    mix_low = grad_mix[...]
    own_low = grad_own[...]
    if has_above:
        sums[0] += product_left(source[...], sent_grad[...])
    sums[1] += product_left(target_low, own_low)
    for k in range(fan):
        sums[2] += product_left(edge_hidden[k], grad_message[k])
    sums[3] += product_left(target_low, mix_low)
    sums[4] += product_left(aggregate[...], mix_low)
    sums[5] += product_left(hidden[...], grad_out[...])
    if needs_target:
        grad_part[...] = (
            grad_new[...] + product_right(own_low, weights[1]) + product_right(mix_low, weights[3])
        )
    if direct:

        @pl.when(step == pl.num_programs(0) - 1)
        def _():
            deal(self_id, sums, outs)


def share_outputs(count, width, device_count):
    shape = (device_count // 2, count * (width // device_count), width)
    return (
        [whole(shape)] * 2,
        [on_chip(shape, WIDE), on_chip(shape, SEND)],
    )


def weight_layer(self_id, device_count, above, extra, low, aggregate, back, grad_new, weights):
    block_rows, width = low.shape
    rows = WEIGHT_ROWS
    fan = back[0].shape[0]
    tile = tiled(rows, width)
    fan_tile = fanned(fan, rows, width)
    in_specs, operands = [], []
    direct = self_id is not None
    if direct:
        in_specs += [pl.BlockSpec(memory_space=pltpu.SMEM)]
        operands += [self_id]
    if above is not None:
        in_specs += [tile, tile]
        operands += [pinned(above[0]), kept_on_chip(above[1])]
    else:
        in_specs += [whole((width, width))]
        operands += [extra]
    in_specs += [tile, tile, fan_tile, fan_tile, tile, tile, tile, tile]
    operands += [pinned(low), pinned(aggregate), *map(kept_on_chip, back)]
    out_specs, out_shape, scratch = [], [], []
    if grad_new is not None:
        in_specs += [tile, matrix_spec(weights[1], 6, width)]
        operands += [kept_on_chip(grad_new), pinned(weights[0])]
        out_specs += [tile]
        out_shape += [in_hbm((block_rows, width), WIDE)]
    if direct:
        specs, shapes = share_outputs(6, width, device_count)
        out_specs += specs
        out_shape += shapes
        scratch = [pltpu.VMEM((6, width, width), WIDE)]
    else:
        out_specs += [whole((6, width, width))]
        out_shape += [jax.ShapeDtypeStruct((6, width, width), WIDE)]
    results = pl.pallas_call(
        functools.partial(weight_kernel, above is not None, grad_new is not None, direct),
        grid=(block_rows // rows,),
        in_specs=in_specs,
        out_specs=out_specs,
        out_shape=out_shape,
        scratch_shapes=scratch,
        compiler_params=pltpu.CompilerParams(vmem_limit_bytes=30 << 20),
        cost_estimate=pl.CostEstimate(
            flops=2 * (fan + 6) * block_rows * width * width,
            transcendentals=0,
            bytes_accessed=24 * block_rows * width,
        ),
        name="weight_layer",
    )(*operands)
    if grad_new is None:
        return (None, results)
    return (results[0], results[1:])


def embed_kernel(pieces_count, *refs):
    self_id = refs[0]
    pieces = refs[1 : 1 + pieces_count]
    before, middle, after = refs[1 + pieces_count : 4 + pieces_count]
    weights, latent, latent_low, sent_before, sent_middle, sent_after, table = refs[
        4 + pieces_count :
    ]
    count, width = weights.shape[0], weights.shape[1]
    high = pieces[0].shape[0]
    share = width // (high * pieces_count)

    @pl.when(pl.program_id(0) == 0)
    def _():
        for index, piece in enumerate(pieces):
            base = (index // 2) + (index % 2) * 4

            def move(digit, carry, piece=piece, base=base):
                relative = (digit // 2) * 8 + (digit % 2) * 2 + base
                place = pl.multiple_of((relative ^ self_id[0]) * share, share)
                for j in range(count):
                    weights[j, pl.ds(place, share), :] = piece[digit, j * share : (j + 1) * share, :]
                table[pl.ds(place, share), :] = piece[digit, count * share : (count + 1) * share, :]
                return carry

            lax.fori_loop(0, high, move, 0)

    for block, sent in ((before, sent_before), (middle, sent_middle), (after, sent_after)):
        wide = product_right(block[...], table[...])
        low = wide.astype(LOW)
        sent[...] = product(low, weights[0]).astype(LOW)
        if block is middle:
            latent[...] = wide
            latent_low[...] = low


def embed(self_id, pieces, blocks):
    block_rows, width = blocks[1].shape
    rows = WEIGHT_ROWS
    tile = tiled(rows, width)
    return pl.pallas_call(
        functools.partial(embed_kernel, len(pieces)),
        grid=(block_rows // rows,),
        in_specs=[pl.BlockSpec(memory_space=pltpu.SMEM)]
        + [whole(piece.shape) for piece in pieces]
        + [tile] * 3,
        out_specs=[whole((7, width, width))] + [tile] * 5,
        out_shape=[
            in_hbm((7, width, width), LOW),
            in_hbm((block_rows, width), WIDE),
            in_hbm((block_rows, width), LOW),
            on_chip((block_rows, width), LOW),
            in_hbm((block_rows, width), LOW),
            on_chip((block_rows, width), LOW),
        ],
        scratch_shapes=[pltpu.VMEM((width, width), LOW)],
        compiler_params=pltpu.CompilerParams(vmem_limit_bytes=50 << 20),
        cost_estimate=pl.CostEstimate(
            flops=12 * block_rows * width * width,
            transcendentals=0,
            bytes_accessed=24 * block_rows * width,
        ),
        name="embed",
    )(self_id, *pieces, *blocks)


def tail_kernel(self_id, loss, before, middle, after, latent_low, inputs, grad_grid, head, *refs):
    gains = refs[:-3]
    keep, send, sums = refs[-3:]
    step = pl.program_id(0)
    rows, width = inputs.shape
    share = width // (2 * keep.shape[0])
    gain_count = 2 * len(gains)

    @pl.when(step == 0)
    def _():
        sums[...] = jnp.zeros_like(sums)

    sent_low = (
        before[...].astype(WIDE)
        + middle[...].astype(WIDE)
        + after[...].astype(WIDE)
    ).astype(LOW)
    grad_low = (grad_grid[...] + product_right(sent_low, head[0])).astype(LOW)
    sums[0] += product_left(latent_low[...], sent_low)
    sums[1] += product_left(grad_low, inputs[...])

    @pl.when(step == pl.num_programs(0) - 1)
    def _():
        size = sums.shape[0] * share
        main = [out.at[:, 0:size, :] for out in (keep, send)]
        deal(self_id, sums, main)
        gain_rows = jnp.concatenate([gain[...] for gain in gains], axis=0)
        lane = lax.broadcasted_iota(jnp.int32, gain_rows.shape, 1)

        def move(node, carry):
            for core, out in enumerate((keep, send)):
                device = (2 * node + core) ^ self_id[0]
                turned = pltpu.roll(gain_rows, width - device * share, axis=1)
                out[node, size : size + gain_count, :] = jnp.where(
                    lane == share, loss[0], turned
                ).astype(out.dtype)
            return carry

        lax.fori_loop(0, keep.shape[0], move, 0)


def tail_layer(
    self_id, device_count, loss, from_before, slot_grad, from_after, latent_low, inputs, grad_grid, head, gains
):
    block_rows, width = inputs.shape
    rows = WEIGHT_ROWS
    tile = tiled(rows, width)
    gain_count = 2 * len(gains)
    shape = (device_count // 2, 2 * (width // device_count) + gain_count, width)
    return pl.pallas_call(
        tail_kernel,
        grid=(block_rows // rows,),
        in_specs=[pl.BlockSpec(memory_space=pltpu.SMEM)] * 2
        + [tile] * 6
        + [matrix_spec(head[1], 1, width)]
        + [whole((2, width))] * len(gains),
        out_specs=[whole(shape)] * 2,
        out_shape=[on_chip(shape, WIDE), on_chip(shape, SEND)],
        scratch_shapes=[pltpu.VMEM((2, width, width), WIDE)],
        compiler_params=pltpu.CompilerParams(vmem_limit_bytes=56 << 20),
        cost_estimate=pl.CostEstimate(
            flops=6 * block_rows * width * width,
            transcendentals=0,
            bytes_accessed=24 * block_rows * width,
        ),
        name="tail_layer",
    )(
        self_id,
        loss,
        *map(pinned, (from_before, slot_grad, from_after, latent_low, inputs, grad_grid, head[0])),
        *gains,
    )


def combine_kernel(count, *refs):
    arrived, outs = refs[:count], refs[count:]
    for digit, out in enumerate(outs):
        total = arrived[0][0, digit].astype(WIDE)
        for part in arrived[1:]:
            total = total + part[0, digit].astype(WIDE)
        out[0] = total.astype(out.dtype)


def combine(arrived, radix):
    _, rows, width = arrived[0].shape
    rest = arrived[0].shape[0] // radix
    arrived = [part.reshape(rest, radix, rows, width) for part in arrived]
    spec = pl.BlockSpec((1, radix, rows, width), lambda step: (step, 0, 0, 0))
    shape = (rest, rows, width)
    return pl.pallas_call(
        functools.partial(combine_kernel, len(arrived)),
        grid=(rest,),
        in_specs=[spec] * len(arrived),
        out_specs=[pl.BlockSpec((1, rows, width), lambda step: (step, 0, 0))] * radix,
        out_shape=[on_chip(shape, WIDE)] + [on_chip(shape, SEND)] * (radix - 1),
        compiler_params=pltpu.CompilerParams(vmem_limit_bytes=20 << 20),
        cost_estimate=pl.CostEstimate(
            flops=rest * radix * rows * width * len(arrived),
            transcendentals=0,
            bytes_accessed=4 * rest * radix * rows * width * (len(arrived) + 1),
        ),
        name="combine",
    )(*map(kept_on_chip, arrived))


def swap(cells, count, mask):
    return lax.ppermute(cells, AXES, [(i, i ^ mask) for i in range(count)])


def spread_rows(row_pair, count, first_bulk, second_bulk):
    pair = jnp.stack(row_pair)
    column = [pair] + [swap(pair, count, digit * 8) for digit in range(1, count // 8)]
    column, first_bulk = together(column, first_bulk)
    plane = jnp.concatenate(column)
    near = [plane, swap(plane, count, 4)]
    near, second_bulk = together(near, second_bulk)
    return near + [swap(piece, count, 1) for piece in near], first_bulk, second_bulk


def home(block, direct):
    return block ^ (((block >> 2) & 1) << 1) if direct else block


def bring(cells, count, step, direct):
    return lax.ppermute(cells, AXES, [(i, home((i + step) % count, direct)) for i in range(count)])


def shift(cells, count, step, direct):
    pairs = [(home(i, direct), home((i + step) % count, direct)) for i in range(count)]
    return lax.ppermute(cells, AXES, pairs)


def fan_out(pieces, count, unit):
    return [pieces[0]] + [
        swap(pieces[digit], count, digit * unit) for digit in range(1, len(pieces))
    ]


def together(first, second):
    joined = lax.optimization_barrier((tuple(first), tuple(second)))
    return list(joined[0]), list(joined[1])


def add_up(arrived):
    total = arrived[0][0]
    for part in arrived[1:]:
        total = total + part[0].astype(WIDE)
    return total


def adamw_update(weight, moment_one, moment_two, gradient, step_value, decay_rate):
    new_one = BETA_ONE * moment_one + (1.0 - BETA_ONE) * gradient
    new_two = BETA_TWO * moment_two + (1.0 - BETA_TWO) * gradient * gradient
    correct_one = 1.0 - jnp.power(BETA_ONE, step_value)
    correct_two = 1.0 - jnp.power(BETA_TWO, step_value)
    direction = new_one / correct_one / (jnp.sqrt(new_two / correct_two) + ADAM_EPS)
    return (new_one, new_two, weight - LEARN_RATE * (direction + decay_rate * weight))


def shards(
    grid_inputs,
    mesh_static,
    targets,
    area_weight,
    valid_rows,
    encoder_lists,
    mesh_lists,
    decoder_lists,
    step_count,
    w_in,
    moment_in,
    square_in,
    w_layers,
    moment_layers,
    square_layers,
    norm_gains,
    moment_gains,
    square_gains,
    w_out,
    moment_out,
    square_out,
):
    row_count = grid_inputs.shape[0]
    layer_total = w_layers.shape[0]
    device_count = lax.axis_size(AXES)
    width = mesh_static.shape[1]
    share = w_layers.shape[2]
    channels, outputs = w_in.shape[0], w_out.shape[1]
    direct = share == 16 and device_count % 8 == 0 and device_count & (device_count - 1) == 0
    slot_lists = [encoder_lists.T.reshape(-1), mesh_lists.T.reshape(-1), decoder_lists.T.reshape(-1)]
    local_rows = jnp.arange(row_count, dtype=jnp.int32)
    weight_rows = area_weight * (local_rows < valid_rows[0]).astype(WIDE)
    if direct:
        self_id = lax.axis_index(AXES).astype(jnp.int32)
        order = jnp.arange(device_count, dtype=jnp.int32) ^ self_id
        self_id = self_id.reshape(1)
        inputs = jnp.pad(grid_inputs, ((0, 0), (0, width - channels)))
        flat_gains = norm_gains.astype(LOW).reshape(1, -1)
        packed = jnp.concatenate(
            [
                w_layers[0].astype(LOW).reshape(-1, width),
                w_layers[1, 0].astype(LOW),
                jnp.pad(w_in.astype(LOW).T, ((0, 0), (0, width - channels))),
                jnp.pad(flat_gains, ((0, 7), (0, width - flat_gains.shape[1]))),
            ],
            axis=0,
        )
        second = jnp.concatenate([w_layers[2, :1], w_layers[1, 1:]], axis=0).astype(LOW)
        rest = jnp.concatenate(
            [
                jnp.pad(w_out.astype(LOW), ((0, 0), (0, width - outputs)))[None],
                w_layers[2, 1:].astype(LOW),
                w_layers[3:].astype(LOW).reshape(-1, share, width),
            ],
            axis=0,
        )
        lists = jnp.concatenate(slot_lists).reshape(-1, LANES)
        lists = bring(lists, device_count, 0, direct)
        goals = jnp.concatenate([targets, weight_rows[:, None]], axis=1)
        goals = jnp.pad(goals, ((0, 0), (0, -goals.shape[1] % LANES)))
        row_pair = [packed, swap(packed, device_count, 2)]
        sides = [bring(inputs, device_count, step, direct) for step in (1, 0, -1)]
        mesh_rows = bring(mesh_static, device_count, 0, direct)
        second = lax.all_gather(second, AXES, axis=1, tiled=True)
        pieces, (mesh_rows, before, after, lists), (own,) = spread_rows(
            row_pair, device_count, [mesh_rows, sides[0], sides[2], lists], [sides[1]]
        )
        sides = [before, own, after]
        pieces, (rest, goals) = together(pieces, [rest, goals])
        rest = lax.all_gather(rest, AXES, axis=1, tiled=True)
        inputs = own
        lists = lists.reshape(len(slot_lists), -1)
        slot_lists = [lists[index] for index in range(len(slot_lists))]
        first, grid_latent, grid_start, *blocks = embed(
            self_id, pieces, sides
        )
        first, goals = lax.optimization_barrier((first, goals))
        goals = bring(goals, device_count, 0, direct)
        targets, weight_rows = goals[:, :outputs], goals[:, outputs]
        weights = [(first, 0), (second, 0)]
        weights += [(rest, 6 * layer_id) for layer_id in range(layer_total - 2)]
        heads = [(first, 0), (first, 6), (second, 0)]
        heads += weights[3:]
        table_out = rest[0, :, :outputs]
        gain_rows = jnp.stack(pieces)[:, :, packed.shape[0] - 8, : flat_gains.shape[1]]
        gain_rows = gain_rows.reshape(2, 2, device_count // 8, 2, -1).transpose(2, 1, 3, 0, 4)
        gain_rows = gain_rows.reshape(device_count, -1)[order]
        gains = gain_rows.reshape(device_count, layer_total, 2, share).transpose(1, 2, 0, 3)
        gains = gains.reshape(layer_total, 2, width).astype(WIDE)
    else:
        self_id = None
        table_in = lax.all_gather(w_in.astype(LOW), AXES, axis=1, tiled=True)
        table_out = lax.all_gather(w_out.astype(LOW), AXES, axis=0, tiled=True)
        matrices = lax.all_gather(w_layers.astype(LOW), AXES, axis=2, tiled=True)
        matrices = matrices.reshape(-1, width, width)
        weights = [(matrices, 6 * layer_id) for layer_id in range(layer_total)]
        heads = weights
        gains = lax.all_gather(norm_gains.astype(LOW), AXES, axis=2, tiled=True).astype(WIDE)
        grid_latent = product(grid_inputs, table_in)
        grid_start = grid_latent.astype(LOW)
        sent = product(grid_start, matrices[0]).astype(LOW)
        blocks = (shift(sent, device_count, 1, direct), sent, shift(sent, device_count, -1, direct))
        mesh_rows = mesh_static
    slot_lists = [slot_lists[0]] + [slot_lists[1]] * (layer_total - 2) + [slot_lists[2]]
    target, target_low = mesh_rows, mesh_rows
    stored_list = []
    for layer_id in range(layer_total):
        last_layer = layer_id == layer_total - 1
        if last_layer:
            source_low = target_low
            target, target_low = grid_latent, grid_start
        else:
            source_low = grid_start if layer_id == 0 else target_low
        results = forward_layer(
            slot_lists[layer_id],
            blocks,
            target_low,
            target,
            weights[layer_id],
            None if last_layer else heads[layer_id + 1],
            gains[layer_id],
        )
        if last_layer:
            grid_low, kept, aggregate = results
        else:
            sent, updated, updated_low, kept, aggregate = results
            blocks = (shift(sent, device_count, 1, direct), sent, shift(sent, device_count, -1, direct))
        stored_list.append((source_low, (target_low, kept, aggregate), aggregate))
        if not last_layer:
            target, target_low = updated, updated_low
    prediction = product(grid_low, table_out)
    error_rows = prediction - targets
    loss_scale = 1.0 / (row_count * device_count * prediction.shape[1])
    loss_local = jnp.sum(weight_rows[:, None] * error_rows * error_rows) * loss_scale
    grad_pred = (2.0 * loss_scale * weight_rows[:, None] * error_rows).astype(LOW)
    grad_table_out = product_left(grid_low, grad_pred)
    grad_part = product_right(grad_pred, table_out)
    extra = jnp.pad(grad_table_out, ((0, 0), (0, width - outputs)))
    grad_grid = None
    above, above_source = None, None
    layer_grads = [None] * layer_total
    gain_grads = [None] * layer_total
    in_plane, in_slice = [], []
    for layer_id in reversed(range(layer_total)):
        source_low, stored, aggregate = stored_list[layer_id]
        sent_grad, grad_new, *slot_grads, grad_gain, grad_message, edge_hidden, b0, b1, b2, b3 = backward_layer(
            slot_lists[layer_id], above, grad_part, stored, weights[layer_id], gains[layer_id]
        )
        far = []
        if in_plane:
            moved = len(in_plane)
            arrived, slot_grads = together(in_plane + in_slice, slot_grads)
            if in_slice:
                layer_grads[layer_id + 2] = add_up(arrived[moved:]).reshape(6, share, width)
            far = list(combine(arrived[:moved], device_count // 8))
        from_before = shift(slot_grads[2], device_count, 1, direct)
        from_after = shift(slot_grads[0], device_count, -1, direct)
        back = [edge_hidden, grad_message, b0, b1, b2, b3]
        grad_part, sums = weight_layer(
            self_id,
            device_count,
            None if above is None else (above_source, sent_grad),
            extra,
            stored[0],
            aggregate,
            back,
            None if layer_id == 0 else grad_new,
            weights[layer_id],
        )
        gain_grads[layer_id] = grad_gain
        if direct:
            halo, arrived = together([from_before, from_after], [*sums, *far])
            keep, send, far = arrived[0], arrived[1], arrived[2:]
            in_slice = fan_out(far, device_count, 8) if far else []
            other = swap(send, device_count, 1)
            if layer_id > 0:
                near = list(combine([keep, other], 4))
                halo, near = together(halo, near)
                in_plane = fan_out(near, device_count, 2)
            from_before, from_after = halo
        else:
            layer_grads[layer_id] = sums[0]
        if layer_id == layer_total - 1:
            grad_grid, grad_part = grad_part, None
        above = (from_before, slot_grads[1], from_after, heads[layer_id])
        above_source = source_low
    if direct:
        sums = tail_layer(
            self_id,
            device_count,
            loss_local.reshape(1),
            from_before,
            slot_grads[1],
            from_after,
            grid_start,
            inputs,
            grad_grid,
            heads[0],
            gain_grads,
        )
        arrived, sums = together([other] + in_slice, sums)
        other, in_slice = arrived[0], arrived[1:]
        near = combine([keep, other], 4)
        layer_grads[1] = add_up(in_slice).reshape(6, share, width)
        far = combine(fan_out(near, device_count, 2), device_count // 8)
        layer_grads[0] = add_up(fan_out(far, device_count, 8)).reshape(6, share, width)
        keep, send = sums
        pieces = combine([keep, swap(send, device_count, 1)], 4)
        pieces = combine(fan_out(pieces, device_count, 2), device_count // 8)
        total = add_up(fan_out(pieces, device_count, 8))
        grad_zero = total[:share]
        grad_in = total[share : 2 * share, :channels].T
        grad_gain_all = total[2 * share :, :share].reshape(layer_total, 2, share)
        loss_value = total[2 * share, share]
        grad_out = layer_grads[-1][0, :, :outputs]
    else:
        loss_value = lax.psum(loss_local, AXES)
        sent_grad = (
            from_before.astype(WIDE) + slot_grads[1].astype(WIDE) + from_after.astype(WIDE)
        ).astype(LOW)
        grad_zero = product_left(above_source, sent_grad)
        grad_grid = grad_grid + product_right(sent_grad, matrices[0])
        grad_table_in = product_left(grid_inputs, grad_grid.astype(LOW))
        grad_in = lax.psum_scatter(grad_table_in, AXES, scatter_dimension=1, tiled=True)
        grad_out = lax.psum_scatter(grad_table_out, AXES, scatter_dimension=0, tiled=True)
        grad_gain_all = lax.psum_scatter(
            jnp.stack(gain_grads), AXES, scatter_dimension=2, tiled=True
        )
    grad_layers = [grad_zero[None]]
    for layer_id in range(layer_total):
        grad_layers += [layer_grads[layer_id][1:]]
        if layer_id < layer_total - 1:
            grad_layers += [layer_grads[layer_id][0:1]]
    grad_layers = jnp.concatenate(grad_layers, axis=0)
    grad_layers = grad_layers.reshape(layer_total, 6, *grad_layers.shape[1:])
    if not direct:
        grad_layers = lax.psum_scatter(grad_layers, AXES, scatter_dimension=2, tiled=True)
    step_value = step_count[0].astype(WIDE)
    one_in, two_in, new_in = adamw_update(
        w_in, moment_in, square_in, grad_in, step_value, DECAY_RATE
    )
    one_layers, two_layers, new_layers = adamw_update(
        w_layers, moment_layers, square_layers, grad_layers, step_value, DECAY_RATE
    )
    one_gains, two_gains, new_gains = adamw_update(
        norm_gains, moment_gains, square_gains, grad_gain_all, step_value, 0.0
    )
    one_out, two_out, new_out = adamw_update(
        w_out, moment_out, square_out, grad_out, step_value, DECAY_RATE
    )
    return (
        loss_value,
        one_in,
        two_in,
        new_in,
        one_layers,
        two_layers,
        new_layers,
        one_gains,
        two_gains,
        new_gains,
        one_out,
        two_out,
        new_out,
    )


def solution(mesh):
    rows = P(AXES, None)
    layers = P(None, None, AXES, None)
    gains = P(None, None, AXES)
    columns = P(None, AXES)
    in_specs = (rows, rows, rows, P(AXES), P(AXES), rows, rows, rows, P())
    in_specs += (columns,) * 3 + (layers,) * 3 + (gains,) * 3 + (rows,) * 3
    out_specs = (P(),) + (columns,) * 3 + (layers,) * 3 + (gains,) * 3 + (rows,) * 3
    return jax.shard_map(shards, mesh=mesh, in_specs=in_specs, out_specs=out_specs, check_vma=False)
```

```python
import functools

import jax
import jax.numpy as jnp
from jax import lax
from jax.experimental import pallas as pl
from jax.experimental.pallas import tpu as pltpu
from jax.sharding import PartitionSpec as P

EPS_NORM = 1e-05
BETA_ONE = 0.5
BETA_TWO = 0.5
ADAM_EPS = 1e-08
LEARN_RATE = 0.04
DECAY_RATE = 0.1

AXES = ("nodes", "shard")
LANES = 128
FORWARD_ROWS = 256
BACKWARD_ROWS = 256
WEIGHT_ROWS = 256
UNROLL = 32
LOW = jnp.bfloat16
WIDE = jnp.float32
SEND = jnp.bfloat16


def product(left, right):
    return jnp.dot(left, right, preferred_element_type=WIDE)


def product_left(left, right):
    return lax.dot_general(left, right, (((0,), (0,)), ((), ())), preferred_element_type=WIDE)


def product_right(left, right):
    return lax.dot_general(left, right, (((1,), (1,)), ((), ())), preferred_element_type=WIDE)


def normalize(tensor):
    centre = tensor - jnp.mean(tensor, axis=-1, keepdims=True)
    inv_scale = lax.rsqrt(jnp.mean(centre * centre, axis=-1, keepdims=True) + EPS_NORM)
    return (centre * inv_scale, inv_scale)


def normal_back(grad_unit, unit_rows, inv_scale):
    centred = grad_unit - jnp.mean(grad_unit, axis=-1, keepdims=True)
    return inv_scale * (
        centred - unit_rows * jnp.mean(grad_unit * unit_rows, axis=-1, keepdims=True)
    )


def silu_parts(tensor):
    half = 0.5 * tensor
    return half, jnp.tanh(half)


def silu(tensor):
    half, bend = silu_parts(tensor)
    return half * (1.0 + bend)


def fold_rows(store, base, rows, tensor):
    parts = tensor.shape[1] // LANES
    for part in range(parts):
        store[pl.ds(base * parts + part, rows, stride=parts), :] = tensor[
            :, part * LANES : (part + 1) * LANES
        ]


def unfold_rows(store, base, rows, parts):
    return jnp.concatenate(
        [store[pl.ds(base * parts + part, rows, stride=parts), :] for part in range(parts)],
        axis=1,
    )


def forward_kernel(parts, has_next, *refs):
    if has_next:
        (slots, before, middle, after, low, wide, weights, gains, head) = refs[:9]
        (sent, update, update_low, kept, aggregate) = refs[9:14]
        window, picked, hidden, message = refs[14:]
    else:
        (slots, before, middle, after, low, wide, weights, gains) = refs[:8]
        (update_low, kept, aggregate) = refs[8:11]
        window, picked, hidden, message = refs[11:]
    step = pl.program_id(0)
    block_rows = before.shape[0]
    rows, width = low.shape
    fan = kept.shape[0]

    @pl.when(step == 0)
    def _():
        for index, block in enumerate((before, middle, after)):
            fold_rows(window, index * block_rows, block_rows, block[...].astype(WIDE))

    for k in range(fan):

        def pick(trip, carry):
            for lane in range(UNROLL):
                row = trip * UNROLL + lane
                slot = slots[k * block_rows + step * rows + row]
                picked[pl.ds(pl.multiple_of((k * rows + row) * parts, parts), parts), :] = window[
                    pl.ds(pl.multiple_of(slot * parts, parts), parts), :
                ]
            return carry

        lax.fori_loop(0, rows // UNROLL, pick, 0)
    target_low = low[...]
    own_term = product(target_low, weights[1])
    for k in range(fan):
        sender = unfold_rows(picked, k * rows, rows, parts)
        kept[k] = sender.astype(LOW)
        hidden[k * rows : (k + 1) * rows, :] = silu(sender + own_term).astype(LOW)
    message[...] = product(hidden[...], weights[2])
    total = normalize(message[0:rows, :])[0]
    for k in range(1, fan):
        total = total + normalize(message[k * rows : (k + 1) * rows, :])[0]
    total_low = (total * gains[0:1, :]).astype(LOW)
    aggregate[...] = total_low
    node_mix = product(target_low, weights[3]) + product(total_low, weights[4])
    node_out = product(silu(node_mix).astype(LOW), weights[5])
    updated = wide[...].astype(WIDE) + normalize(node_out)[0] * gains[1:2, :]
    updated_low = updated.astype(LOW)
    update_low[...] = updated_low
    if has_next:
        update[...] = updated
        sent[...] = product(updated_low, head[0]).astype(LOW)


def in_hbm(shape, dtype):
    return pltpu.MemorySpace.HBM(shape, dtype)


def on_chip(shape, dtype):
    return pltpu.MemorySpace.VMEM(shape, dtype)


def kept_on_chip(array):
    return pltpu.with_memory_space_constraint(array, pltpu.MemorySpace.VMEM)


def pinned(array):
    return pltpu.with_memory_space_constraint(array, pltpu.MemorySpace.HBM)


def whole(shape):
    zeros = (0,) * len(shape)
    return pl.BlockSpec(shape, lambda step: zeros, pipeline_mode=pl.Buffered(1))


def matrix_spec(first, count, width):
    return pl.BlockSpec(
        (count, width, width), lambda step: (first // count, 0, 0), pipeline_mode=pl.Buffered(1)
    )


def tiled(rows, width):
    return pl.BlockSpec((rows, width), lambda step: (step, 0))


def fanned(fan, rows, width):
    return pl.BlockSpec((fan, rows, width), lambda step: (0, step, 0))


def forward_layer(slots, blocks, target_low, target, weights, next_weights, gains):
    block_rows, width = target_low.shape
    fan = slots.shape[0] // block_rows
    parts = width // LANES
    rows = FORWARD_ROWS
    has_next = next_weights is not None
    shape = functools.partial(in_hbm, (block_rows, width))
    fan_shape = functools.partial(in_hbm, (fan, block_rows, width))
    tile = tiled(rows, width)
    in_specs = [pl.BlockSpec(memory_space=pltpu.SMEM)]
    in_specs += [whole((block_rows, width))] * 3 + [tile, tile]
    in_specs += [matrix_spec(weights[1], 6, width), whole(gains.shape)]
    out_specs = [tile, fanned(fan, rows, width), tile]
    out_shape = [shape(LOW), fan_shape(LOW), shape(LOW)]
    operands = [slots, *blocks, target_low, target, weights[0], gains]
    if has_next:
        in_specs += [matrix_spec(next_weights[1], 1, width)]
        operands += [next_weights[0]]
        out_specs = [tile, tile] + out_specs
        out_shape = [shape(LOW), shape(WIDE)] + out_shape
    return pl.pallas_call(
        functools.partial(forward_kernel, parts, has_next),
        grid=(block_rows // rows,),
        in_specs=in_specs,
        out_specs=out_specs,
        out_shape=out_shape,
        scratch_shapes=[
            pltpu.VMEM((3 * block_rows * parts, LANES), WIDE),
            pltpu.VMEM((fan * rows * parts, LANES), WIDE),
            pltpu.VMEM((fan * rows, width), LOW),
            pltpu.VMEM((fan * rows, width), WIDE),
        ],
        compiler_params=pltpu.CompilerParams(vmem_limit_bytes=54 << 20),
        cost_estimate=pl.CostEstimate(
            flops=2 * (fan + 5) * block_rows * width * width,
            transcendentals=(fan + 1) * block_rows * width,
            bytes_accessed=24 * block_rows * width * 2,
        ),
        name="forward_layer",
    )(
        operands[0],
        kept_on_chip(operands[1]),
        pinned(operands[2]),
        kept_on_chip(operands[3]),
        *map(pinned, operands[4:]),
    )


def backward_kernel(parts, mode, *refs):
    refs = list(refs)
    slots = refs.pop(0)
    if mode != "first":
        returned = [refs.pop(0) for _ in range(3)]
        head = refs.pop(0)
    if mode != "second":
        grad_part = refs.pop(0)
    low, kept, aggregate, weights, gains = refs[:5]
    refs = refs[5:]
    if mode != "first":
        sent_grad = refs.pop(0)
        grad_full = refs.pop(0)
    slot_grads = refs[:3]
    (grad_gains, grad_message, edge_hidden, grad_mix, grad_out, grad_own, hidden) = refs[3:10]
    sum_even, sum_odd, spread, stage = refs[10:]
    step = pl.program_id(0)
    rows, width = low.shape
    fan = kept.shape[0]
    block_rows = slot_grads[0].shape[0]

    @pl.when(step == 0)
    def _():
        sum_even[...] = jnp.zeros_like(sum_even)
        sum_odd[...] = jnp.zeros_like(sum_odd)
        grad_gains[...] = jnp.zeros_like(grad_gains)

    if mode == "first":
        grad_new = grad_part[...]
    else:
        sent_low = (
            returned[0][...].astype(WIDE)
            + returned[1][...].astype(WIDE)
            + returned[2][...].astype(WIDE)
        ).astype(LOW)
        sent_grad[...] = sent_low
        grad_new = product_right(sent_low, head[0])
        if mode == "third":
            grad_new = grad_part[...] + grad_new
        grad_full[...] = grad_new
    target_low = low[...]
    own_term = product(target_low, weights[1])
    node_mix = product(target_low, weights[3]) + product(aggregate[...], weights[4])
    for k in range(fan):
        edge_hidden[k] = silu(kept[k].astype(WIDE) + own_term).astype(LOW)
    stage[...] = product(edge_hidden[...].reshape(fan * rows, width), weights[2])
    half, bend = silu_parts(node_mix)
    node_hidden = (half * (1.0 + bend)).astype(LOW)
    hidden[...] = node_hidden
    out_unit, out_scale = normalize(product(node_hidden, weights[5]))
    gain_two = jnp.sum(grad_new * out_unit, axis=0, keepdims=True)
    out_low = normal_back(grad_new * gains[1:2, :], out_unit, out_scale).astype(LOW)
    grad_out[...] = out_low
    mix_low = (
        product_right(out_low, weights[5]) * ((0.5 + 0.5 * bend) * (1.0 + half * (1.0 - bend)))
    ).astype(LOW)
    grad_mix[...] = mix_low
    grad_sum = product_right(mix_low, weights[4])
    grad_unit = grad_sum * gains[0:1, :]
    unit_total = None
    for k in range(fan):
        unit_rows, inv_scale = normalize(stage[k * rows : (k + 1) * rows, :])
        unit_total = unit_rows if k == 0 else unit_total + unit_rows
        grad_message[k] = normal_back(grad_unit, unit_rows, inv_scale).astype(LOW)
    stage[...] = product_right(grad_message[...].reshape(fan * rows, width), weights[2])
    own_total = None
    for k in range(fan):
        half, bend = silu_parts(kept[k].astype(WIDE) + own_term)
        grad_pre = stage[k * rows : (k + 1) * rows, :] * (
            (0.5 + 0.5 * bend) * (1.0 + half * (1.0 - bend))
        )
        own_total = grad_pre if k == 0 else own_total + grad_pre
        fold_rows(spread, k * rows, rows, grad_pre)
    gain_one = jnp.sum(grad_sum * unit_total, axis=0, keepdims=True)
    grad_gains[...] += jnp.concatenate([gain_one, gain_two], axis=0)
    grad_own[...] = own_total.astype(LOW)

    for k in range(fan):

        def add(trip, carry):
            for lane in range(UNROLL // 2):
                places, values = [], []
                for store in (sum_even, sum_odd):
                    row = (trip * (UNROLL // 2) + lane) * 2 + len(places)
                    slot = slots[k * block_rows + step * rows + row]
                    place = pl.ds(pl.multiple_of(slot * parts, parts), parts)
                    value = spread[pl.ds(pl.multiple_of((k * rows + row) * parts, parts), parts), :]
                    places.append(place)
                    values.append(store[place, :] + value)
                sum_even[places[0], :] = values[0]
                sum_odd[places[1], :] = values[1]
            return carry

        lax.fori_loop(0, rows // UNROLL, add, 0)

    @pl.when(step == pl.num_programs(0) - 1)
    def _():
        for index in range(3):
            base = index * block_rows
            slot_grads[index][...] = (
                unfold_rows(sum_even, base, block_rows, parts)
                + unfold_rows(sum_odd, base, block_rows, parts)
            ).astype(LOW)


def backward_layer(slots, above, grad_part, stored, weights, gains):
    target_low, kept, aggregate = stored
    block_rows, width = target_low.shape
    fan = kept.shape[0]
    parts = width // LANES
    rows = BACKWARD_ROWS
    tile = tiled(rows, width)
    fan_tile = fanned(fan, rows, width)
    in_specs = [pl.BlockSpec(memory_space=pltpu.SMEM)]
    operands = [slots]
    out_specs, out_shape = [], []
    shape = functools.partial(on_chip, (block_rows, width))
    fan_shape = functools.partial(on_chip, (fan, block_rows, width))
    mode = "first" if above is None else ("second" if grad_part is None else "third")
    if above is not None:
        from_before, slot_grad, from_after, head = above
        in_specs += [
            tile,
            tile,
            tile,
            matrix_spec(head[1], 1, width),
        ]
        operands += [from_before, slot_grad, from_after, head[0]]
        out_specs += [tile, tile]
        out_shape += [shape(LOW), shape(WIDE)]
    if grad_part is not None:
        in_specs += [tile]
        operands += [grad_part]
    in_specs += [tile, fan_tile, tile]
    in_specs += [matrix_spec(weights[1], 6, width), whole(gains.shape)]
    operands += [target_low, kept, aggregate, weights[0], gains]
    out_specs += [
        whole((block_rows, width)),
        whole((block_rows, width)),
        whole((block_rows, width)),
        whole((2, width)),
        fan_tile,
        fan_tile,
        tile,
        tile,
        tile,
        tile,
    ]
    out_shape += [
        in_hbm((block_rows, width), LOW),
        in_hbm((block_rows, width), LOW),
        in_hbm((block_rows, width), LOW),
        jax.ShapeDtypeStruct((2, width), WIDE),
        fan_shape(LOW),
        fan_shape(LOW),
        shape(LOW),
        shape(LOW),
        shape(LOW),
        shape(LOW),
    ]
    results = pl.pallas_call(
        functools.partial(backward_kernel, parts, mode),
        grid=(block_rows // rows,),
        in_specs=in_specs,
        out_specs=out_specs,
        out_shape=out_shape,
        scratch_shapes=[
            pltpu.VMEM((3 * block_rows * parts, LANES), WIDE),
            pltpu.VMEM((3 * block_rows * parts, LANES), WIDE),
            pltpu.VMEM((fan * rows * parts, LANES), WIDE),
            pltpu.VMEM((fan * rows, width), WIDE),
        ],
        compiler_params=pltpu.CompilerParams(vmem_limit_bytes=38 << 20),
        cost_estimate=pl.CostEstimate(
            flops=2 * (fan + 4) * block_rows * width * width,
            transcendentals=(fan + 1) * block_rows * width,
            bytes_accessed=24 * block_rows * width * 2,
        ),
        name="backward_layer",
    )(operands[0], *map(pinned, operands[1:]))
    if above is None:
        return (None, grad_part, *results)
    return tuple(results)


def deal(self_id, sums, outs):
    keep, send = outs
    share = keep.shape[1] // sums.shape[0]

    def move(node, carry):
        for core, out in enumerate((keep, send)):
            place = pl.multiple_of(((2 * node + core) ^ self_id[0]) * share, share)
            for index in range(sums.shape[0]):
                out[node, index * share : (index + 1) * share, :] = sums[
                    index, pl.ds(place, share), :
                ].astype(out.dtype)
        return carry

    lax.fori_loop(0, keep.shape[0], move, 0)


def weight_kernel(has_above, needs_target, direct, *refs):
    refs = list(refs)
    if direct:
        self_id = refs.pop(0)
    if has_above:
        source, sent_grad = refs[:2]
        refs = refs[2:]
    else:
        extra = refs.pop(0)
    low, aggregate, edge_hidden, grad_message, grad_mix, grad_out, grad_own, hidden = refs[:8]
    refs = refs[8:]
    if needs_target:
        grad_new, weights = refs[:2]
        grad_part = refs[2]
        refs = refs[3:]
    outs, sums = (refs[:2], refs[2]) if direct else (None, refs[0])
    step = pl.program_id(0)
    fan = edge_hidden.shape[0]

    @pl.when(step == 0)
    def _():
        sums[...] = jnp.zeros_like(sums)
        if not has_above:
            sums[0] = extra[...]

    target_low = low[...]
    mix_low = grad_mix[...]
    own_low = grad_own[...]
    if has_above:
        sums[0] += product_left(source[...], sent_grad[...])
    sums[1] += product_left(target_low, own_low)
    for k in range(fan):
        sums[2] += product_left(edge_hidden[k], grad_message[k])
    sums[3] += product_left(target_low, mix_low)
    sums[4] += product_left(aggregate[...], mix_low)
    sums[5] += product_left(hidden[...], grad_out[...])
    if needs_target:
        grad_part[...] = (
            grad_new[...] + product_right(own_low, weights[1]) + product_right(mix_low, weights[3])
        )
    if direct:

        @pl.when(step == pl.num_programs(0) - 1)
        def _():
            deal(self_id, sums, outs)


def share_outputs(count, width, device_count):
    shape = (device_count // 2, count * (width // device_count), width)
    return (
        [whole(shape)] * 2,
        [on_chip(shape, WIDE), on_chip(shape, SEND)],
    )


def weight_layer(self_id, device_count, above, extra, low, aggregate, back, grad_new, weights):
    block_rows, width = low.shape
    rows = WEIGHT_ROWS
    fan = back[0].shape[0]
    tile = tiled(rows, width)
    fan_tile = fanned(fan, rows, width)
    in_specs, operands = [], []
    direct = self_id is not None
    if direct:
        in_specs += [pl.BlockSpec(memory_space=pltpu.SMEM)]
        operands += [self_id]
    if above is not None:
        in_specs += [tile, tile]
        operands += [pinned(above[0]), kept_on_chip(above[1])]
    else:
        in_specs += [whole((width, width))]
        operands += [extra]
    in_specs += [tile, tile, fan_tile, fan_tile, tile, tile, tile, tile]
    operands += [pinned(low), pinned(aggregate), *map(kept_on_chip, back)]
    out_specs, out_shape, scratch = [], [], []
    if grad_new is not None:
        in_specs += [tile, matrix_spec(weights[1], 6, width)]
        operands += [kept_on_chip(grad_new), pinned(weights[0])]
        out_specs += [tile]
        out_shape += [in_hbm((block_rows, width), WIDE)]
    if direct:
        specs, shapes = share_outputs(6, width, device_count)
        out_specs += specs
        out_shape += shapes
        scratch = [pltpu.VMEM((6, width, width), WIDE)]
    else:
        out_specs += [whole((6, width, width))]
        out_shape += [jax.ShapeDtypeStruct((6, width, width), WIDE)]
    results = pl.pallas_call(
        functools.partial(weight_kernel, above is not None, grad_new is not None, direct),
        grid=(block_rows // rows,),
        in_specs=in_specs,
        out_specs=out_specs,
        out_shape=out_shape,
        scratch_shapes=scratch,
        compiler_params=pltpu.CompilerParams(vmem_limit_bytes=30 << 20),
        cost_estimate=pl.CostEstimate(
            flops=2 * (fan + 6) * block_rows * width * width,
            transcendentals=0,
            bytes_accessed=24 * block_rows * width,
        ),
        name="weight_layer",
    )(*operands)
    if grad_new is None:
        return (None, results)
    return (results[0], results[1:])


def embed_kernel(pieces_count, *refs):
    self_id = refs[0]
    pieces = refs[1 : 1 + pieces_count]
    before, middle, after = refs[1 + pieces_count : 4 + pieces_count]
    weights, latent, latent_low, sent_before, sent_middle, sent_after, table = refs[
        4 + pieces_count :
    ]
    count, width = weights.shape[0], weights.shape[1]
    high = pieces[0].shape[0]
    share = width // (high * pieces_count)

    @pl.when(pl.program_id(0) == 0)
    def _():
        for index, piece in enumerate(pieces):
            base = (index // 2) + (index % 2) * 4

            def move(digit, carry, piece=piece, base=base):
                relative = (digit // 2) * 8 + (digit % 2) * 2 + base
                place = pl.multiple_of((relative ^ self_id[0]) * share, share)
                for j in range(count):
                    weights[j, pl.ds(place, share), :] = piece[digit, j * share : (j + 1) * share, :]
                table[pl.ds(place, share), :] = piece[digit, count * share : (count + 1) * share, :]
                return carry

            lax.fori_loop(0, high, move, 0)

    for block, sent in ((before, sent_before), (middle, sent_middle), (after, sent_after)):
        wide = product_right(block[...], table[...])
        low = wide.astype(LOW)
        sent[...] = product(low, weights[0]).astype(LOW)
        if block is middle:
            latent[...] = wide
            latent_low[...] = low


def embed(self_id, pieces, blocks):
    block_rows, width = blocks[1].shape
    rows = WEIGHT_ROWS
    tile = tiled(rows, width)
    return pl.pallas_call(
        functools.partial(embed_kernel, len(pieces)),
        grid=(block_rows // rows,),
        in_specs=[pl.BlockSpec(memory_space=pltpu.SMEM)]
        + [whole(piece.shape) for piece in pieces]
        + [tile] * 3,
        out_specs=[whole((7, width, width))] + [tile] * 5,
        out_shape=[
            in_hbm((7, width, width), LOW),
            in_hbm((block_rows, width), WIDE),
            in_hbm((block_rows, width), LOW),
            on_chip((block_rows, width), LOW),
            in_hbm((block_rows, width), LOW),
            on_chip((block_rows, width), LOW),
        ],
        scratch_shapes=[pltpu.VMEM((width, width), LOW)],
        compiler_params=pltpu.CompilerParams(vmem_limit_bytes=50 << 20),
        cost_estimate=pl.CostEstimate(
            flops=12 * block_rows * width * width,
            transcendentals=0,
            bytes_accessed=24 * block_rows * width,
        ),
        name="embed",
    )(self_id, *pieces, *blocks)


def tail_kernel(self_id, loss, before, middle, after, latent_low, inputs, grad_grid, head, *refs):
    gains = refs[:-3]
    keep, send, sums = refs[-3:]
    step = pl.program_id(0)
    rows, width = inputs.shape
    share = width // (2 * keep.shape[0])
    gain_count = 2 * len(gains)

    @pl.when(step == 0)
    def _():
        sums[...] = jnp.zeros_like(sums)

    sent_low = (
        before[...].astype(WIDE)
        + middle[...].astype(WIDE)
        + after[...].astype(WIDE)
    ).astype(LOW)
    grad_low = (grad_grid[...] + product_right(sent_low, head[0])).astype(LOW)
    sums[0] += product_left(latent_low[...], sent_low)
    sums[1] += product_left(grad_low, inputs[...])

    @pl.when(step == pl.num_programs(0) - 1)
    def _():
        size = sums.shape[0] * share
        main = [out.at[:, 0:size, :] for out in (keep, send)]
        deal(self_id, sums, main)
        gain_rows = jnp.concatenate([gain[...] for gain in gains], axis=0)
        lane = lax.broadcasted_iota(jnp.int32, gain_rows.shape, 1)

        def move(node, carry):
            for core, out in enumerate((keep, send)):
                device = (2 * node + core) ^ self_id[0]
                turned = pltpu.roll(gain_rows, width - device * share, axis=1)
                out[node, size : size + gain_count, :] = jnp.where(
                    lane == share, loss[0], turned
                ).astype(out.dtype)
            return carry

        lax.fori_loop(0, keep.shape[0], move, 0)


def tail_layer(
    self_id, device_count, loss, from_before, slot_grad, from_after, latent_low, inputs, grad_grid, head, gains
):
    block_rows, width = inputs.shape
    rows = WEIGHT_ROWS
    tile = tiled(rows, width)
    gain_count = 2 * len(gains)
    shape = (device_count // 2, 2 * (width // device_count) + gain_count, width)
    return pl.pallas_call(
        tail_kernel,
        grid=(block_rows // rows,),
        in_specs=[pl.BlockSpec(memory_space=pltpu.SMEM)] * 2
        + [tile] * 6
        + [matrix_spec(head[1], 1, width)]
        + [whole((2, width))] * len(gains),
        out_specs=[whole(shape)] * 2,
        out_shape=[on_chip(shape, WIDE), on_chip(shape, SEND)],
        scratch_shapes=[pltpu.VMEM((2, width, width), WIDE)],
        compiler_params=pltpu.CompilerParams(vmem_limit_bytes=56 << 20),
        cost_estimate=pl.CostEstimate(
            flops=6 * block_rows * width * width,
            transcendentals=0,
            bytes_accessed=24 * block_rows * width,
        ),
        name="tail_layer",
    )(
        self_id,
        loss,
        *map(pinned, (from_before, slot_grad, from_after, latent_low, inputs, grad_grid, head[0])),
        *gains,
    )


def combine_kernel(count, *refs):
    arrived, outs = refs[:count], refs[count:]
    for digit, out in enumerate(outs):
        total = arrived[0][0, digit].astype(WIDE)
        for part in arrived[1:]:
            total = total + part[0, digit].astype(WIDE)
        out[0] = total.astype(out.dtype)


def combine(arrived, radix):
    _, rows, width = arrived[0].shape
    rest = arrived[0].shape[0] // radix
    arrived = [part.reshape(rest, radix, rows, width) for part in arrived]
    spec = pl.BlockSpec((1, radix, rows, width), lambda step: (step, 0, 0, 0))
    shape = (rest, rows, width)
    return pl.pallas_call(
        functools.partial(combine_kernel, len(arrived)),
        grid=(rest,),
        in_specs=[spec] * len(arrived),
        out_specs=[pl.BlockSpec((1, rows, width), lambda step: (step, 0, 0))] * radix,
        out_shape=[on_chip(shape, WIDE)] + [on_chip(shape, SEND)] * (radix - 1),
        compiler_params=pltpu.CompilerParams(vmem_limit_bytes=20 << 20),
        cost_estimate=pl.CostEstimate(
            flops=rest * radix * rows * width * len(arrived),
            transcendentals=0,
            bytes_accessed=4 * rest * radix * rows * width * (len(arrived) + 1),
        ),
        name="combine",
    )(*map(kept_on_chip, arrived))


def swap(cells, count, mask):
    return lax.ppermute(cells, AXES, [(i, i ^ mask) for i in range(count)])


def spread_rows(row_pair, count, first_bulk, second_bulk):
    pair = jnp.stack(row_pair)
    column = [pair] + [swap(pair, count, digit * 8) for digit in range(1, count // 8)]
    column, first_bulk = together(column, first_bulk)
    plane = jnp.concatenate(column)
    near = [plane, swap(plane, count, 4)]
    near, second_bulk = together(near, second_bulk)
    return near + [swap(piece, count, 1) for piece in near], first_bulk, second_bulk


def home(block, direct):
    return block ^ (((block >> 2) & 1) << 1) if direct else block


def bring(cells, count, step, direct):
    return lax.ppermute(cells, AXES, [(i, home((i + step) % count, direct)) for i in range(count)])


def shift(cells, count, step, direct):
    pairs = [(home(i, direct), home((i + step) % count, direct)) for i in range(count)]
    return lax.ppermute(cells, AXES, pairs)


def fan_out(pieces, count, unit):
    return [pieces[0]] + [
        swap(pieces[digit], count, digit * unit) for digit in range(1, len(pieces))
    ]


def together(first, second):
    joined = lax.optimization_barrier((tuple(first), tuple(second)))
    return list(joined[0]), list(joined[1])


def add_up(arrived):
    total = arrived[0][0]
    for part in arrived[1:]:
        total = total + part[0].astype(WIDE)
    return total


def adamw_update(weight, moment_one, moment_two, gradient, step_value, decay_rate):
    new_one = BETA_ONE * moment_one + (1.0 - BETA_ONE) * gradient
    new_two = BETA_TWO * moment_two + (1.0 - BETA_TWO) * gradient * gradient
    correct_one = 1.0 - jnp.power(BETA_ONE, step_value)
    correct_two = 1.0 - jnp.power(BETA_TWO, step_value)
    direction = new_one / correct_one / (jnp.sqrt(new_two / correct_two) + ADAM_EPS)
    return (new_one, new_two, weight - LEARN_RATE * (direction + decay_rate * weight))


def shards(
    grid_inputs,
    mesh_static,
    targets,
    area_weight,
    valid_rows,
    encoder_lists,
    mesh_lists,
    decoder_lists,
    step_count,
    w_in,
    moment_in,
    square_in,
    w_layers,
    moment_layers,
    square_layers,
    norm_gains,
    moment_gains,
    square_gains,
    w_out,
    moment_out,
    square_out,
):
    row_count = grid_inputs.shape[0]
    layer_total = w_layers.shape[0]
    device_count = lax.axis_size(AXES)
    width = mesh_static.shape[1]
    share = w_layers.shape[2]
    channels, outputs = w_in.shape[0], w_out.shape[1]
    direct = share == 16 and device_count % 8 == 0 and device_count & (device_count - 1) == 0
    slot_lists = [encoder_lists.T.reshape(-1), mesh_lists.T.reshape(-1), decoder_lists.T.reshape(-1)]
    local_rows = jnp.arange(row_count, dtype=jnp.int32)
    weight_rows = area_weight * (local_rows < valid_rows[0]).astype(WIDE)
    if direct:
        self_id = lax.axis_index(AXES).astype(jnp.int32)
        order = jnp.arange(device_count, dtype=jnp.int32) ^ self_id
        self_id = self_id.reshape(1)
        inputs = jnp.pad(grid_inputs, ((0, 0), (0, width - channels)))
        flat_gains = norm_gains.astype(LOW).reshape(1, -1)
        packed = jnp.concatenate(
            [
                w_layers[0].astype(LOW).reshape(-1, width),
                w_layers[1, 0].astype(LOW),
                jnp.pad(w_in.astype(LOW).T, ((0, 0), (0, width - channels))),
                jnp.pad(flat_gains, ((0, 7), (0, width - flat_gains.shape[1]))),
            ],
            axis=0,
        )
        second = jnp.concatenate([w_layers[2, :1], w_layers[1, 1:]], axis=0).astype(LOW)
        rest = jnp.concatenate(
            [
                jnp.pad(w_out.astype(LOW), ((0, 0), (0, width - outputs)))[None],
                w_layers[2, 1:].astype(LOW),
                w_layers[3:].astype(LOW).reshape(-1, share, width),
            ],
            axis=0,
        )
        lists = jnp.concatenate(slot_lists).reshape(-1, LANES)
        goals = jnp.concatenate([targets, weight_rows[:, None]], axis=1)
        goals = jnp.pad(goals, ((0, 0), (0, -goals.shape[1] % LANES)))
        row_pair = [packed, swap(packed, device_count, 2)]
        row_pair, bulk = together(row_pair, [inputs, mesh_static, lists])
        inputs, mesh_static, lists = bulk
        lists = bring(lists, device_count, 0, direct)
        sides = [bring(inputs, device_count, step, direct) for step in (1, 0, -1)]
        mesh_rows = bring(mesh_static, device_count, 0, direct)
        second = lax.all_gather(second, AXES, axis=1, tiled=True)
        pieces, (mesh_rows, before, after, lists), (own,) = spread_rows(
            row_pair, device_count, [mesh_rows, sides[0], sides[2], lists], [sides[1]]
        )
        sides = [before, own, after]
        pieces, (rest, goals) = together(pieces, [rest, goals])
        rest = lax.all_gather(rest, AXES, axis=1, tiled=True)
        inputs = own
        lists = lists.reshape(len(slot_lists), -1)
        slot_lists = [lists[index] for index in range(len(slot_lists))]
        first, grid_latent, grid_start, *blocks = embed(
            self_id, pieces, sides
        )
        first, goals = lax.optimization_barrier((first, goals))
        goals = bring(goals, device_count, 0, direct)
        targets, weight_rows = goals[:, :outputs], goals[:, outputs]
        weights = [(first, 0), (second, 0)]
        weights += [(rest, 6 * layer_id) for layer_id in range(layer_total - 2)]
        heads = [(first, 0), (first, 6), (second, 0)]
        heads += weights[3:]
        table_out = rest[0, :, :outputs]
        gain_rows = jnp.stack(pieces)[:, :, packed.shape[0] - 8, : flat_gains.shape[1]]
        gain_rows = gain_rows.reshape(2, 2, device_count // 8, 2, -1).transpose(2, 1, 3, 0, 4)
        gain_rows = gain_rows.reshape(device_count, -1)[order]
        gains = gain_rows.reshape(device_count, layer_total, 2, share).transpose(1, 2, 0, 3)
        gains = gains.reshape(layer_total, 2, width).astype(WIDE)
    else:
        self_id = None
        table_in = lax.all_gather(w_in.astype(LOW), AXES, axis=1, tiled=True)
        table_out = lax.all_gather(w_out.astype(LOW), AXES, axis=0, tiled=True)
        matrices = lax.all_gather(w_layers.astype(LOW), AXES, axis=2, tiled=True)
        matrices = matrices.reshape(-1, width, width)
        weights = [(matrices, 6 * layer_id) for layer_id in range(layer_total)]
        heads = weights
        gains = lax.all_gather(norm_gains.astype(LOW), AXES, axis=2, tiled=True).astype(WIDE)
        grid_latent = product(grid_inputs, table_in)
        grid_start = grid_latent.astype(LOW)
        sent = product(grid_start, matrices[0]).astype(LOW)
        blocks = (shift(sent, device_count, 1, direct), sent, shift(sent, device_count, -1, direct))
        mesh_rows = mesh_static
    slot_lists = [slot_lists[0]] + [slot_lists[1]] * (layer_total - 2) + [slot_lists[2]]
    target, target_low = mesh_rows, mesh_rows
    stored_list = []
    for layer_id in range(layer_total):
        last_layer = layer_id == layer_total - 1
        if last_layer:
            source_low = target_low
            target, target_low = grid_latent, grid_start
        else:
            source_low = grid_start if layer_id == 0 else target_low
        results = forward_layer(
            slot_lists[layer_id],
            blocks,
            target_low,
            target,
            weights[layer_id],
            None if last_layer else heads[layer_id + 1],
            gains[layer_id],
        )
        if last_layer:
            grid_low, kept, aggregate = results
        else:
            sent, updated, updated_low, kept, aggregate = results
            blocks = (shift(sent, device_count, 1, direct), sent, shift(sent, device_count, -1, direct))
        stored_list.append((source_low, (target_low, kept, aggregate), aggregate))
        if not last_layer:
            target, target_low = updated, updated_low
    prediction = product(grid_low, table_out)
    error_rows = prediction - targets
    loss_scale = 1.0 / (row_count * device_count * prediction.shape[1])
    loss_local = jnp.sum(weight_rows[:, None] * error_rows * error_rows) * loss_scale
    grad_pred = (2.0 * loss_scale * weight_rows[:, None] * error_rows).astype(LOW)
    grad_table_out = product_left(grid_low, grad_pred)
    grad_part = product_right(grad_pred, table_out)
    extra = jnp.pad(grad_table_out, ((0, 0), (0, width - outputs)))
    grad_grid = None
    above, above_source = None, None
    layer_grads = [None] * layer_total
    gain_grads = [None] * layer_total
    in_plane, in_slice = [], []
    for layer_id in reversed(range(layer_total)):
        source_low, stored, aggregate = stored_list[layer_id]
        sent_grad, grad_new, *slot_grads, grad_gain, grad_message, edge_hidden, b0, b1, b2, b3 = backward_layer(
            slot_lists[layer_id], above, grad_part, stored, weights[layer_id], gains[layer_id]
        )
        far = []
        if in_plane:
            moved = len(in_plane)
            arrived, slot_grads = together(in_plane + in_slice, slot_grads)
            if in_slice:
                layer_grads[layer_id + 2] = add_up(arrived[moved:]).reshape(6, share, width)
            far = list(combine(arrived[:moved], device_count // 8))
        from_before = shift(slot_grads[2], device_count, 1, direct)
        from_after = shift(slot_grads[0], device_count, -1, direct)
        back = [edge_hidden, grad_message, b0, b1, b2, b3]
        grad_part, sums = weight_layer(
            self_id,
            device_count,
            None if above is None else (above_source, sent_grad),
            extra,
            stored[0],
            aggregate,
            back,
            None if layer_id == 0 else grad_new,
            weights[layer_id],
        )
        gain_grads[layer_id] = grad_gain
        if direct:
            halo, arrived = together([from_before, from_after], [*sums, *far])
            keep, send, far = arrived[0], arrived[1], arrived[2:]
            in_slice = fan_out(far, device_count, 8) if far else []
            other = swap(send, device_count, 1)
            if layer_id > 0:
                near = list(combine([keep, other], 4))
                halo, near = together(halo, near)
                in_plane = fan_out(near, device_count, 2)
            from_before, from_after = halo
        else:
            layer_grads[layer_id] = sums[0]
        if layer_id == layer_total - 1:
            grad_grid, grad_part = grad_part, None
        above = (from_before, slot_grads[1], from_after, heads[layer_id])
        above_source = source_low
    if direct:
        sums = tail_layer(
            self_id,
            device_count,
            loss_local.reshape(1),
            from_before,
            slot_grads[1],
            from_after,
            grid_start,
            inputs,
            grad_grid,
            heads[0],
            gain_grads,
        )
        arrived, sums = together([other] + in_slice, sums)
        other, in_slice = arrived[0], arrived[1:]
        near = combine([keep, other], 4)
        layer_grads[1] = add_up(in_slice).reshape(6, share, width)
        far = combine(fan_out(near, device_count, 2), device_count // 8)
        layer_grads[0] = add_up(fan_out(far, device_count, 8)).reshape(6, share, width)
        keep, send = sums
        pieces = combine([keep, swap(send, device_count, 1)], 4)
        pieces = combine(fan_out(pieces, device_count, 2), device_count // 8)
        total = add_up(fan_out(pieces, device_count, 8))
        grad_zero = total[:share]
        grad_in = total[share : 2 * share, :channels].T
        grad_gain_all = total[2 * share :, :share].reshape(layer_total, 2, share)
        loss_value = total[2 * share, share]
        grad_out = layer_grads[-1][0, :, :outputs]
    else:
        loss_value = lax.psum(loss_local, AXES)
        sent_grad = (
            from_before.astype(WIDE) + slot_grads[1].astype(WIDE) + from_after.astype(WIDE)
        ).astype(LOW)
        grad_zero = product_left(above_source, sent_grad)
        grad_grid = grad_grid + product_right(sent_grad, matrices[0])
        grad_table_in = product_left(grid_inputs, grad_grid.astype(LOW))
        grad_in = lax.psum_scatter(grad_table_in, AXES, scatter_dimension=1, tiled=True)
        grad_out = lax.psum_scatter(grad_table_out, AXES, scatter_dimension=0, tiled=True)
        grad_gain_all = lax.psum_scatter(
            jnp.stack(gain_grads), AXES, scatter_dimension=2, tiled=True
        )
    grad_layers = [grad_zero[None]]
    for layer_id in range(layer_total):
        grad_layers += [layer_grads[layer_id][1:]]
        if layer_id < layer_total - 1:
            grad_layers += [layer_grads[layer_id][0:1]]
    grad_layers = jnp.concatenate(grad_layers, axis=0)
    grad_layers = grad_layers.reshape(layer_total, 6, *grad_layers.shape[1:])
    if not direct:
        grad_layers = lax.psum_scatter(grad_layers, AXES, scatter_dimension=2, tiled=True)
    step_value = step_count[0].astype(WIDE)
    one_in, two_in, new_in = adamw_update(
        w_in, moment_in, square_in, grad_in, step_value, DECAY_RATE
    )
    one_layers, two_layers, new_layers = adamw_update(
        w_layers, moment_layers, square_layers, grad_layers, step_value, DECAY_RATE
    )
    one_gains, two_gains, new_gains = adamw_update(
        norm_gains, moment_gains, square_gains, grad_gain_all, step_value, 0.0
    )
    one_out, two_out, new_out = adamw_update(
        w_out, moment_out, square_out, grad_out, step_value, DECAY_RATE
    )
    return (
        loss_value,
        one_in,
        two_in,
        new_in,
        one_layers,
        two_layers,
        new_layers,
        one_gains,
        two_gains,
        new_gains,
        one_out,
        two_out,
        new_out,
    )


def solution(mesh):
    rows = P(AXES, None)
    layers = P(None, None, AXES, None)
    gains = P(None, None, AXES)
    columns = P(None, AXES)
    in_specs = (rows, rows, rows, P(AXES), P(AXES), rows, rows, rows, P())
    in_specs += (columns,) * 3 + (layers,) * 3 + (gains,) * 3 + (rows,) * 3
    out_specs = (P(),) + (columns,) * 3 + (layers,) * 3 + (gains,) * 3 + (rows,) * 3
    return jax.shard_map(shards, mesh=mesh, in_specs=in_specs, out_specs=out_specs, check_vma=False)
```

```python
import functools

import jax
import jax.numpy as jnp
from jax import lax
from jax.experimental import pallas as pl
from jax.experimental.pallas import tpu as pltpu
from jax.sharding import PartitionSpec as P

EPS_NORM = 1e-05
BETA_ONE = 0.5
BETA_TWO = 0.5
ADAM_EPS = 1e-08
LEARN_RATE = 0.04
DECAY_RATE = 0.1

AXES = ("nodes", "shard")
LANES = 128
FORWARD_ROWS = 256
BACKWARD_ROWS = 256
WEIGHT_ROWS = 256
UNROLL = 32
LOW = jnp.bfloat16
WIDE = jnp.float32
SEND = jnp.bfloat16


def product(left, right):
    return jnp.dot(left, right, preferred_element_type=WIDE)


def product_left(left, right):
    return lax.dot_general(left, right, (((0,), (0,)), ((), ())), preferred_element_type=WIDE)


def product_right(left, right):
    return lax.dot_general(left, right, (((1,), (1,)), ((), ())), preferred_element_type=WIDE)


def normalize(tensor):
    centre = tensor - jnp.mean(tensor, axis=-1, keepdims=True)
    inv_scale = lax.rsqrt(jnp.mean(centre * centre, axis=-1, keepdims=True) + EPS_NORM)
    return (centre * inv_scale, inv_scale)


def normal_back(grad_unit, unit_rows, inv_scale):
    centred = grad_unit - jnp.mean(grad_unit, axis=-1, keepdims=True)
    return inv_scale * (
        centred - unit_rows * jnp.mean(grad_unit * unit_rows, axis=-1, keepdims=True)
    )


def silu_parts(tensor):
    half = 0.5 * tensor
    return half, jnp.tanh(half)


def silu(tensor):
    half, bend = silu_parts(tensor)
    return half * (1.0 + bend)


def fold_rows(store, base, rows, tensor):
    parts = tensor.shape[1] // LANES
    for part in range(parts):
        store[pl.ds(base * parts + part, rows, stride=parts), :] = tensor[
            :, part * LANES : (part + 1) * LANES
        ]


def unfold_rows(store, base, rows, parts):
    return jnp.concatenate(
        [store[pl.ds(base * parts + part, rows, stride=parts), :] for part in range(parts)],
        axis=1,
    )


def forward_kernel(parts, has_next, *refs):
    if has_next:
        (slots, before, middle, after, low, wide, weights, gains, head) = refs[:9]
        (sent, update, update_low, kept, aggregate) = refs[9:14]
        window, picked, hidden, message = refs[14:]
    else:
        (slots, before, middle, after, low, wide, weights, gains) = refs[:8]
        (update_low, kept, aggregate) = refs[8:11]
        window, picked, hidden, message = refs[11:]
    step = pl.program_id(0)
    block_rows = before.shape[0]
    rows, width = low.shape
    fan = kept.shape[0]

    @pl.when(step == 0)
    def _():
        for index, block in enumerate((before, middle, after)):
            fold_rows(window, index * block_rows, block_rows, block[...].astype(WIDE))

    for k in range(fan):

        def pick(trip, carry):
            for lane in range(UNROLL):
                row = trip * UNROLL + lane
                slot = slots[k * block_rows + step * rows + row]
                picked[pl.ds(pl.multiple_of((k * rows + row) * parts, parts), parts), :] = window[
                    pl.ds(pl.multiple_of(slot * parts, parts), parts), :
                ]
            return carry

        lax.fori_loop(0, rows // UNROLL, pick, 0)
    target_low = low[...]
    own_term = product(target_low, weights[1])
    for k in range(fan):
        sender = unfold_rows(picked, k * rows, rows, parts)
        kept[k] = sender.astype(LOW)
        hidden[k * rows : (k + 1) * rows, :] = silu(sender + own_term).astype(LOW)
    message[...] = product(hidden[...], weights[2])
    total = normalize(message[0:rows, :])[0]
    for k in range(1, fan):
        total = total + normalize(message[k * rows : (k + 1) * rows, :])[0]
    total_low = (total * gains[0:1, :]).astype(LOW)
    aggregate[...] = total_low
    node_mix = product(target_low, weights[3]) + product(total_low, weights[4])
    node_out = product(silu(node_mix).astype(LOW), weights[5])
    updated = wide[...].astype(WIDE) + normalize(node_out)[0] * gains[1:2, :]
    updated_low = updated.astype(LOW)
    update_low[...] = updated_low
    if has_next:
        update[...] = updated
        sent[...] = product(updated_low, head[0]).astype(LOW)


def in_hbm(shape, dtype):
    return pltpu.MemorySpace.HBM(shape, dtype)


def on_chip(shape, dtype):
    return pltpu.MemorySpace.VMEM(shape, dtype)


def kept_on_chip(array):
    return pltpu.with_memory_space_constraint(array, pltpu.MemorySpace.VMEM)


def pinned(array):
    return pltpu.with_memory_space_constraint(array, pltpu.MemorySpace.HBM)


def whole(shape):
    zeros = (0,) * len(shape)
    return pl.BlockSpec(shape, lambda step: zeros, pipeline_mode=pl.Buffered(1))


def matrix_spec(first, count, width):
    return pl.BlockSpec(
        (count, width, width), lambda step: (first // count, 0, 0), pipeline_mode=pl.Buffered(1)
    )


def tiled(rows, width):
    return pl.BlockSpec((rows, width), lambda step: (step, 0))


def fanned(fan, rows, width):
    return pl.BlockSpec((fan, rows, width), lambda step: (0, step, 0))


def forward_layer(slots, blocks, target_low, target, weights, next_weights, gains):
    block_rows, width = target_low.shape
    fan = slots.shape[0] // block_rows
    parts = width // LANES
    rows = FORWARD_ROWS
    has_next = next_weights is not None
    shape = functools.partial(in_hbm, (block_rows, width))
    fan_shape = functools.partial(in_hbm, (fan, block_rows, width))
    tile = tiled(rows, width)
    in_specs = [pl.BlockSpec(memory_space=pltpu.SMEM)]
    in_specs += [whole((block_rows, width))] * 3 + [tile, tile]
    in_specs += [matrix_spec(weights[1], 6, width), whole(gains.shape)]
    out_specs = [tile, fanned(fan, rows, width), tile]
    out_shape = [shape(LOW), fan_shape(LOW), shape(LOW)]
    operands = [slots, *blocks, target_low, target, weights[0], gains]
    if has_next:
        in_specs += [matrix_spec(next_weights[1], 1, width)]
        operands += [next_weights[0]]
        out_specs = [tile, tile] + out_specs
        out_shape = [shape(LOW), shape(WIDE)] + out_shape
    return pl.pallas_call(
        functools.partial(forward_kernel, parts, has_next),
        grid=(block_rows // rows,),
        in_specs=in_specs,
        out_specs=out_specs,
        out_shape=out_shape,
        scratch_shapes=[
            pltpu.VMEM((3 * block_rows * parts, LANES), WIDE),
            pltpu.VMEM((fan * rows * parts, LANES), WIDE),
            pltpu.VMEM((fan * rows, width), LOW),
            pltpu.VMEM((fan * rows, width), WIDE),
        ],
        compiler_params=pltpu.CompilerParams(vmem_limit_bytes=54 << 20),
        cost_estimate=pl.CostEstimate(
            flops=2 * (fan + 5) * block_rows * width * width,
            transcendentals=(fan + 1) * block_rows * width,
            bytes_accessed=24 * block_rows * width * 2,
        ),
        name="forward_layer",
    )(
        operands[0],
        kept_on_chip(operands[1]),
        pinned(operands[2]),
        kept_on_chip(operands[3]),
        *map(pinned, operands[4:]),
    )


def backward_kernel(parts, mode, *refs):
    refs = list(refs)
    slots = refs.pop(0)
    if mode != "first":
        returned = [refs.pop(0) for _ in range(3)]
        head = refs.pop(0)
    if mode != "second":
        grad_part = refs.pop(0)
    low, kept, aggregate, weights, gains = refs[:5]
    refs = refs[5:]
    if mode != "first":
        sent_grad = refs.pop(0)
        grad_full = refs.pop(0)
    slot_grads = refs[:3]
    (grad_gains, grad_message, edge_hidden, grad_mix, grad_out, grad_own, hidden) = refs[3:10]
    sum_even, sum_odd, spread, stage = refs[10:]
    step = pl.program_id(0)
    rows, width = low.shape
    fan = kept.shape[0]
    block_rows = slot_grads[0].shape[0]

    @pl.when(step == 0)
    def _():
        sum_even[...] = jnp.zeros_like(sum_even)
        sum_odd[...] = jnp.zeros_like(sum_odd)
        grad_gains[...] = jnp.zeros_like(grad_gains)

    if mode == "first":
        grad_new = grad_part[...]
    else:
        sent_low = (
            returned[0][...].astype(WIDE)
            + returned[1][...].astype(WIDE)
            + returned[2][...].astype(WIDE)
        ).astype(LOW)
        sent_grad[...] = sent_low
        grad_new = product_right(sent_low, head[0])
        if mode == "third":
            grad_new = grad_part[...] + grad_new
        grad_full[...] = grad_new
    target_low = low[...]
    own_term = product(target_low, weights[1])
    node_mix = product(target_low, weights[3]) + product(aggregate[...], weights[4])
    for k in range(fan):
        edge_hidden[k] = silu(kept[k].astype(WIDE) + own_term).astype(LOW)
    stage[...] = product(edge_hidden[...].reshape(fan * rows, width), weights[2])
    half, bend = silu_parts(node_mix)
    node_hidden = (half * (1.0 + bend)).astype(LOW)
    hidden[...] = node_hidden
    out_unit, out_scale = normalize(product(node_hidden, weights[5]))
    gain_two = jnp.sum(grad_new * out_unit, axis=0, keepdims=True)
    out_low = normal_back(grad_new * gains[1:2, :], out_unit, out_scale).astype(LOW)
    grad_out[...] = out_low
    mix_low = (
        product_right(out_low, weights[5]) * ((0.5 + 0.5 * bend) * (1.0 + half * (1.0 - bend)))
    ).astype(LOW)
    grad_mix[...] = mix_low
    grad_sum = product_right(mix_low, weights[4])
    grad_unit = grad_sum * gains[0:1, :]
    unit_total = None
    for k in range(fan):
        unit_rows, inv_scale = normalize(stage[k * rows : (k + 1) * rows, :])
        unit_total = unit_rows if k == 0 else unit_total + unit_rows
        grad_message[k] = normal_back(grad_unit, unit_rows, inv_scale).astype(LOW)
    stage[...] = product_right(grad_message[...].reshape(fan * rows, width), weights[2])
    own_total = None
    for k in range(fan):
        half, bend = silu_parts(kept[k].astype(WIDE) + own_term)
        grad_pre = stage[k * rows : (k + 1) * rows, :] * (
            (0.5 + 0.5 * bend) * (1.0 + half * (1.0 - bend))
        )
        own_total = grad_pre if k == 0 else own_total + grad_pre
        fold_rows(spread, k * rows, rows, grad_pre)
    gain_one = jnp.sum(grad_sum * unit_total, axis=0, keepdims=True)
    grad_gains[...] += jnp.concatenate([gain_one, gain_two], axis=0)
    grad_own[...] = own_total.astype(LOW)

    for k in range(fan):

        def add(trip, carry):
            for lane in range(UNROLL // 2):
                places, values = [], []
                for store in (sum_even, sum_odd):
                    row = (trip * (UNROLL // 2) + lane) * 2 + len(places)
                    slot = slots[k * block_rows + step * rows + row]
                    place = pl.ds(pl.multiple_of(slot * parts, parts), parts)
                    value = spread[pl.ds(pl.multiple_of((k * rows + row) * parts, parts), parts), :]
                    places.append(place)
                    values.append(store[place, :] + value)
                sum_even[places[0], :] = values[0]
                sum_odd[places[1], :] = values[1]
            return carry

        lax.fori_loop(0, rows // UNROLL, add, 0)

    @pl.when(step == pl.num_programs(0) - 1)
    def _():
        for index in range(3):
            base = index * block_rows
            slot_grads[index][...] = (
                unfold_rows(sum_even, base, block_rows, parts)
                + unfold_rows(sum_odd, base, block_rows, parts)
            ).astype(LOW)


def backward_layer(slots, above, grad_part, stored, weights, gains, first_layer):
    target_low, kept, aggregate = stored
    block_rows, width = target_low.shape
    fan = kept.shape[0]
    parts = width // LANES
    rows = BACKWARD_ROWS
    tile = tiled(rows, width)
    fan_tile = fanned(fan, rows, width)
    in_specs = [pl.BlockSpec(memory_space=pltpu.SMEM)]
    operands = [slots]
    out_specs, out_shape = [], []
    shape = functools.partial(on_chip, (block_rows, width))
    fan_shape = functools.partial(on_chip, (fan, block_rows, width))
    mode = "first" if above is None else ("second" if grad_part is None else "third")
    if above is not None:
        from_before, slot_grad, from_after, head = above
        in_specs += [
            tile,
            tile,
            tile,
            matrix_spec(head[1], 1, width),
        ]
        operands += [from_before, slot_grad, from_after, head[0]]
        out_specs += [tile, tile]
        out_shape += [shape(LOW), shape(WIDE)]
    if grad_part is not None:
        in_specs += [tile]
        operands += [grad_part]
    in_specs += [tile, fan_tile, tile]
    in_specs += [matrix_spec(weights[1], 6, width), whole(gains.shape)]
    operands += [target_low, kept, aggregate, weights[0], gains]
    out_specs += [
        whole((block_rows, width)),
        whole((block_rows, width)),
        whole((block_rows, width)),
        whole((2, width)),
        fan_tile,
        fan_tile,
        tile,
        tile,
        tile,
        tile,
    ]
    out_shape += [
        in_hbm((block_rows, width), LOW),
        in_hbm((block_rows, width), LOW),
        in_hbm((block_rows, width), LOW),
        jax.ShapeDtypeStruct((2, width), WIDE),
        fan_shape(LOW),
        in_hbm((fan, block_rows, width), LOW) if first_layer else fan_shape(LOW),
        shape(LOW),
        shape(LOW),
        shape(LOW),
        shape(LOW),
    ]
    results = pl.pallas_call(
        functools.partial(backward_kernel, parts, mode),
        grid=(block_rows // rows,),
        in_specs=in_specs,
        out_specs=out_specs,
        out_shape=out_shape,
        scratch_shapes=[
            pltpu.VMEM((3 * block_rows * parts, LANES), WIDE),
            pltpu.VMEM((3 * block_rows * parts, LANES), WIDE),
            pltpu.VMEM((fan * rows * parts, LANES), WIDE),
            pltpu.VMEM((fan * rows, width), WIDE),
        ],
        compiler_params=pltpu.CompilerParams(vmem_limit_bytes=38 << 20),
        cost_estimate=pl.CostEstimate(
            flops=2 * (fan + 4) * block_rows * width * width,
            transcendentals=(fan + 1) * block_rows * width,
            bytes_accessed=24 * block_rows * width * 2,
        ),
        name="backward_layer",
    )(operands[0], *map(pinned, operands[1:]))
    if above is None:
        return (None, grad_part, *results)
    return tuple(results)


def deal(self_id, sums, outs):
    keep, send = outs
    share = keep.shape[1] // sums.shape[0]

    def move(node, carry):
        for core, out in enumerate((keep, send)):
            place = pl.multiple_of(((2 * node + core) ^ self_id[0]) * share, share)
            for index in range(sums.shape[0]):
                out[node, index * share : (index + 1) * share, :] = sums[
                    index, pl.ds(place, share), :
                ].astype(out.dtype)
        return carry

    lax.fori_loop(0, keep.shape[0], move, 0)


def weight_kernel(has_above, needs_target, direct, *refs):
    refs = list(refs)
    if direct:
        self_id = refs.pop(0)
    if has_above:
        source, sent_grad = refs[:2]
        refs = refs[2:]
    else:
        extra = refs.pop(0)
    low, aggregate, edge_hidden, grad_message, grad_mix, grad_out, grad_own, hidden = refs[:8]
    refs = refs[8:]
    if needs_target:
        grad_new, weights = refs[:2]
        grad_part = refs[2]
        refs = refs[3:]
    outs, sums = (refs[:2], refs[2]) if direct else (None, refs[0])
    step = pl.program_id(0)
    fan = edge_hidden.shape[0]

    @pl.when(step == 0)
    def _():
        sums[...] = jnp.zeros_like(sums)
        if not has_above:
            sums[0] = extra[...]

    target_low = low[...]
    mix_low = grad_mix[...]
    own_low = grad_own[...]
    if has_above:
        sums[0] += product_left(source[...], sent_grad[...])
    sums[1] += product_left(target_low, own_low)
    for k in range(fan):
        sums[2] += product_left(edge_hidden[k], grad_message[k])
    sums[3] += product_left(target_low, mix_low)
    sums[4] += product_left(aggregate[...], mix_low)
    sums[5] += product_left(hidden[...], grad_out[...])
    if needs_target:
        grad_part[...] = (
            grad_new[...] + product_right(own_low, weights[1]) + product_right(mix_low, weights[3])
        )
    if direct:

        @pl.when(step == pl.num_programs(0) - 1)
        def _():
            deal(self_id, sums, outs)


def share_outputs(count, width, device_count):
    shape = (device_count // 2, count * (width // device_count), width)
    return (
        [whole(shape)] * 2,
        [on_chip(shape, WIDE), on_chip(shape, SEND)],
    )


def weight_layer(self_id, device_count, above, extra, low, aggregate, back, grad_new, weights):
    block_rows, width = low.shape
    rows = WEIGHT_ROWS
    fan = back[0].shape[0]
    tile = tiled(rows, width)
    fan_tile = fanned(fan, rows, width)
    in_specs, operands = [], []
    direct = self_id is not None
    if direct:
        in_specs += [pl.BlockSpec(memory_space=pltpu.SMEM)]
        operands += [self_id]
    if above is not None:
        in_specs += [tile, tile]
        operands += [pinned(above[0]), kept_on_chip(above[1])]
    else:
        in_specs += [whole((width, width))]
        operands += [extra]
    in_specs += [tile, tile, fan_tile, fan_tile, tile, tile, tile, tile]
    place = pinned if grad_new is None else kept_on_chip
    operands += [pinned(low), pinned(aggregate), place(back[0]), *map(kept_on_chip, back[1:])]
    out_specs, out_shape, scratch = [], [], []
    if grad_new is not None:
        in_specs += [tile, matrix_spec(weights[1], 6, width)]
        operands += [kept_on_chip(grad_new), pinned(weights[0])]
        out_specs += [tile]
        out_shape += [in_hbm((block_rows, width), WIDE)]
    if direct:
        specs, shapes = share_outputs(6, width, device_count)
        out_specs += specs
        out_shape += shapes
        scratch = [pltpu.VMEM((6, width, width), WIDE)]
    else:
        out_specs += [whole((6, width, width))]
        out_shape += [jax.ShapeDtypeStruct((6, width, width), WIDE)]
    results = pl.pallas_call(
        functools.partial(weight_kernel, above is not None, grad_new is not None, direct),
        grid=(block_rows // rows,),
        in_specs=in_specs,
        out_specs=out_specs,
        out_shape=out_shape,
        scratch_shapes=scratch,
        compiler_params=pltpu.CompilerParams(vmem_limit_bytes=30 << 20),
        cost_estimate=pl.CostEstimate(
            flops=2 * (fan + 6) * block_rows * width * width,
            transcendentals=0,
            bytes_accessed=24 * block_rows * width,
        ),
        name="weight_layer",
    )(*operands)
    if grad_new is None:
        return (None, results)
    return (results[0], results[1:])


def place_rows(self_id, pieces, targets, width):
    share = width // (pieces[0].shape[0] * len(pieces))
    for index, piece in enumerate(pieces):
        base = (index // 2) + (index % 2) * 4

        def move(digit, carry, piece=piece, base=base):
            relative = (digit // 2) * 8 + (digit % 2) * 2 + base
            place = pl.multiple_of((relative ^ self_id[0]) * share, share)
            for j, target in enumerate(targets):
                target[pl.ds(place, share), :] = piece[digit, j * share : (j + 1) * share, :]
            return carry

        lax.fori_loop(0, piece.shape[0], move, 0)


def assemble_kernel(pieces_count, *refs):
    matrices = refs[-1]
    targets = [matrices.at[j] for j in range(matrices.shape[0])]
    place_rows(refs[0], refs[1 : 1 + pieces_count], targets, matrices.shape[1])


def assemble(self_id, pieces):
    digits, rows, width = pieces[0].shape
    count = rows * digits * len(pieces) // width
    return pl.pallas_call(
        functools.partial(assemble_kernel, len(pieces)),
        grid=(1,),
        in_specs=[pl.BlockSpec(memory_space=pltpu.SMEM)] + [whole(piece.shape) for piece in pieces],
        out_specs=whole((count, width, width)),
        out_shape=in_hbm((count, width, width), LOW),
        compiler_params=pltpu.CompilerParams(vmem_limit_bytes=20 << 20),
        cost_estimate=pl.CostEstimate(
            flops=0, transcendentals=0, bytes_accessed=4 * count * width * width
        ),
        name="assemble",
    )(self_id, *pieces)


def embed_kernel(pieces_count, *refs):
    self_id = refs[0]
    pieces = refs[1 : 1 + pieces_count]
    before, middle, after = refs[1 + pieces_count : 4 + pieces_count]
    weights, latent, latent_low, sent_before, sent_middle, sent_after, table = refs[
        4 + pieces_count :
    ]

    @pl.when(pl.program_id(0) == 0)
    def _():
        targets = [weights.at[j] for j in range(weights.shape[0])] + [table]
        place_rows(self_id, pieces, targets, weights.shape[1])

    for block, sent in ((before, sent_before), (middle, sent_middle), (after, sent_after)):
        wide = product_right(block[...], table[...])
        low = wide.astype(LOW)
        sent[...] = product(low, weights[0]).astype(LOW)
        if block is middle:
            latent[...] = wide
            latent_low[...] = low


def embed(self_id, pieces, blocks):
    block_rows, width = blocks[1].shape
    rows = WEIGHT_ROWS
    tile = tiled(rows, width)
    return pl.pallas_call(
        functools.partial(embed_kernel, len(pieces)),
        grid=(block_rows // rows,),
        in_specs=[pl.BlockSpec(memory_space=pltpu.SMEM)]
        + [whole(piece.shape) for piece in pieces]
        + [tile] * 3,
        out_specs=[whole((7, width, width))] + [tile] * 5,
        out_shape=[
            in_hbm((7, width, width), LOW),
            in_hbm((block_rows, width), WIDE),
            in_hbm((block_rows, width), LOW),
            on_chip((block_rows, width), LOW),
            in_hbm((block_rows, width), LOW),
            on_chip((block_rows, width), LOW),
        ],
        scratch_shapes=[pltpu.VMEM((width, width), LOW)],
        compiler_params=pltpu.CompilerParams(vmem_limit_bytes=50 << 20),
        cost_estimate=pl.CostEstimate(
            flops=12 * block_rows * width * width,
            transcendentals=0,
            bytes_accessed=24 * block_rows * width,
        ),
        name="embed",
    )(self_id, *pieces, *blocks)


def tail_kernel(self_id, loss, before, middle, after, latent_low, inputs, grad_grid, head, *refs):
    gains = refs[:-3]
    keep, send, sums = refs[-3:]
    step = pl.program_id(0)
    rows, width = inputs.shape
    share = width // (2 * keep.shape[0])
    gain_count = 2 * len(gains)

    @pl.when(step == 0)
    def _():
        sums[...] = jnp.zeros_like(sums)

    sent_low = (
        before[...].astype(WIDE)
        + middle[...].astype(WIDE)
        + after[...].astype(WIDE)
    ).astype(LOW)
    grad_low = (grad_grid[...] + product_right(sent_low, head[0])).astype(LOW)
    sums[0] += product_left(latent_low[...], sent_low)
    sums[1] += product_left(grad_low, inputs[...])

    @pl.when(step == pl.num_programs(0) - 1)
    def _():
        size = sums.shape[0] * share
        main = [out.at[:, 0:size, :] for out in (keep, send)]
        deal(self_id, sums, main)
        gain_rows = jnp.concatenate([gain[...] for gain in gains], axis=0)
        lane = lax.broadcasted_iota(jnp.int32, gain_rows.shape, 1)

        def move(node, carry):
            for core, out in enumerate((keep, send)):
                device = (2 * node + core) ^ self_id[0]
                turned = pltpu.roll(gain_rows, width - device * share, axis=1)
                out[node, size : size + gain_count, :] = jnp.where(
                    lane == share, loss[0], turned
                ).astype(out.dtype)
            return carry

        lax.fori_loop(0, keep.shape[0], move, 0)


def tail_layer(
    self_id, device_count, loss, from_before, slot_grad, from_after, latent_low, inputs, grad_grid, head, gains
):
    block_rows, width = inputs.shape
    rows = WEIGHT_ROWS
    tile = tiled(rows, width)
    gain_count = 2 * len(gains)
    shape = (device_count // 2, 2 * (width // device_count) + gain_count, width)
    return pl.pallas_call(
        tail_kernel,
        grid=(block_rows // rows,),
        in_specs=[pl.BlockSpec(memory_space=pltpu.SMEM)] * 2
        + [tile] * 6
        + [matrix_spec(head[1], 1, width)]
        + [whole((2, width))] * len(gains),
        out_specs=[whole(shape)] * 2,
        out_shape=[on_chip(shape, WIDE), on_chip(shape, SEND)],
        scratch_shapes=[pltpu.VMEM((2, width, width), WIDE)],
        compiler_params=pltpu.CompilerParams(vmem_limit_bytes=56 << 20),
        cost_estimate=pl.CostEstimate(
            flops=6 * block_rows * width * width,
            transcendentals=0,
            bytes_accessed=24 * block_rows * width,
        ),
        name="tail_layer",
    )(
        self_id,
        loss,
        *map(pinned, (from_before, slot_grad, from_after, latent_low, inputs, grad_grid, head[0])),
        *gains,
    )


def combine_kernel(count, *refs):
    arrived, outs = refs[:count], refs[count:]
    for digit, out in enumerate(outs):
        total = arrived[0][0, digit].astype(WIDE)
        for part in arrived[1:]:
            total = total + part[0, digit].astype(WIDE)
        out[0] = total.astype(out.dtype)


def combine(arrived, radix):
    _, rows, width = arrived[0].shape
    rest = arrived[0].shape[0] // radix
    arrived = [part.reshape(rest, radix, rows, width) for part in arrived]
    spec = pl.BlockSpec((1, radix, rows, width), lambda step: (step, 0, 0, 0))
    shape = (rest, rows, width)
    return pl.pallas_call(
        functools.partial(combine_kernel, len(arrived)),
        grid=(rest,),
        in_specs=[spec] * len(arrived),
        out_specs=[pl.BlockSpec((1, rows, width), lambda step: (step, 0, 0))] * radix,
        out_shape=[on_chip(shape, WIDE)] + [on_chip(shape, SEND)] * (radix - 1),
        compiler_params=pltpu.CompilerParams(vmem_limit_bytes=20 << 20),
        cost_estimate=pl.CostEstimate(
            flops=rest * radix * rows * width * len(arrived),
            transcendentals=0,
            bytes_accessed=4 * rest * radix * rows * width * (len(arrived) + 1),
        ),
        name="combine",
    )(*map(kept_on_chip, arrived))


def swap(cells, count, mask):
    return lax.ppermute(cells, AXES, [(i, i ^ mask) for i in range(count)])


def spread_high(rows, count):
    return [rows] + [swap(rows, count, digit * 8) for digit in range(1, count // 8)]


def home(block, direct):
    return block ^ (((block >> 2) & 1) << 1) if direct else block


def bring(cells, count, step, direct):
    return lax.ppermute(cells, AXES, [(i, home((i + step) % count, direct)) for i in range(count)])


def shift(cells, count, step, direct):
    pairs = [(home(i, direct), home((i + step) % count, direct)) for i in range(count)]
    return lax.ppermute(cells, AXES, pairs)


def fan_out(pieces, count, unit):
    return [pieces[0]] + [
        swap(pieces[digit], count, digit * unit) for digit in range(1, len(pieces))
    ]


def together(first, second):
    joined = lax.optimization_barrier((tuple(first), tuple(second)))
    return list(joined[0]), list(joined[1])


def add_up(arrived):
    total = arrived[0][0]
    for part in arrived[1:]:
        total = total + part[0].astype(WIDE)
    return total


def adamw_update(weight, moment_one, moment_two, gradient, step_value, decay_rate):
    new_one = BETA_ONE * moment_one + (1.0 - BETA_ONE) * gradient
    new_two = BETA_TWO * moment_two + (1.0 - BETA_TWO) * gradient * gradient
    correct_one = 1.0 - jnp.power(BETA_ONE, step_value)
    correct_two = 1.0 - jnp.power(BETA_TWO, step_value)
    direction = new_one / correct_one / (jnp.sqrt(new_two / correct_two) + ADAM_EPS)
    return (new_one, new_two, weight - LEARN_RATE * (direction + decay_rate * weight))


def shards(
    grid_inputs,
    mesh_static,
    targets,
    area_weight,
    valid_rows,
    encoder_lists,
    mesh_lists,
    decoder_lists,
    step_count,
    w_in,
    moment_in,
    square_in,
    w_layers,
    moment_layers,
    square_layers,
    norm_gains,
    moment_gains,
    square_gains,
    w_out,
    moment_out,
    square_out,
):
    row_count = grid_inputs.shape[0]
    layer_total = w_layers.shape[0]
    device_count = lax.axis_size(AXES)
    width = mesh_static.shape[1]
    share = w_layers.shape[2]
    channels, outputs = w_in.shape[0], w_out.shape[1]
    direct = share == 16 and device_count % 8 == 0 and device_count & (device_count - 1) == 0
    slot_lists = [encoder_lists.T.reshape(-1), mesh_lists.T.reshape(-1), decoder_lists.T.reshape(-1)]
    local_rows = jnp.arange(row_count, dtype=jnp.int32)
    weight_rows = area_weight * (local_rows < valid_rows[0]).astype(WIDE)
    if direct:
        self_id = lax.axis_index(AXES).astype(jnp.int32)
        order = jnp.arange(device_count, dtype=jnp.int32) ^ self_id
        self_id = self_id.reshape(1)
        inputs = jnp.pad(grid_inputs, ((0, 0), (0, width - channels)))
        flat_gains = norm_gains.astype(LOW).reshape(1, -1)
        packed = jnp.concatenate(
            [
                w_layers[0].astype(LOW).reshape(-1, width),
                w_layers[1, 0].astype(LOW),
                jnp.pad(w_in.astype(LOW).T, ((0, 0), (0, width - channels))),
                jnp.pad(flat_gains, ((0, 7), (0, width - flat_gains.shape[1]))),
            ],
            axis=0,
        )
        second = jnp.concatenate([w_layers[2, :1], w_layers[1, 1:]], axis=0)
        second = second.astype(LOW).reshape(-1, width)
        rest = jnp.concatenate(
            [
                jnp.pad(w_out.astype(LOW), ((0, 0), (0, width - outputs)))[None],
                w_layers[2, 1:].astype(LOW),
                w_layers[3:].astype(LOW).reshape(-1, share, width),
            ],
            axis=0,
        )
        lists = jnp.concatenate(slot_lists).reshape(-1, LANES)
        goals = jnp.concatenate([targets, weight_rows[:, None]], axis=1)
        goals = jnp.pad(goals, ((0, 0), (0, -goals.shape[1] % LANES)))
        barrier = lax.optimization_barrier
        pairs = ((packed, swap(packed, device_count, 2)), (second, swap(second, device_count, 2)))
        lists = bring(lists, device_count, 0, direct)
        pairs, lists, inputs, mesh_static = barrier((pairs, lists, inputs, mesh_static))
        sides = [bring(inputs, device_count, step, direct) for step in (1, -1)]
        mesh_rows = bring(mesh_static, device_count, 0, direct)
        pair, second_pair = (jnp.stack(rows) for rows in pairs)
        column, sides, mesh_rows, inputs, second_pair = barrier(
            (spread_high(pair, device_count), sides, mesh_rows, inputs, second_pair)
        )
        own = bring(inputs, device_count, 0, direct)
        second_column = spread_high(second_pair, device_count)
        plane = jnp.concatenate(column)
        near, own, second_column, rest, goals = barrier(
            ((plane, swap(plane, device_count, 4)), own, second_column, rest, goals)
        )
        pieces = [*near, *(swap(piece, device_count, 1) for piece in near)]
        sides = [sides[0], own, sides[1]]
        rest = lax.all_gather(rest, AXES, axis=1, tiled=True)
        inputs = own
        lists = lists.reshape(len(slot_lists), -1)
        slot_lists = [lists[index] for index in range(len(slot_lists))]
        first, grid_latent, grid_start, *blocks = embed(
            self_id, pieces, sides
        )
        first, goals = barrier((first, goals))
        second_plane = jnp.concatenate(second_column)
        second_near = (second_plane, swap(second_plane, device_count, 4))
        goals = bring(goals, device_count, 0, direct)
        targets, weight_rows = goals[:, :outputs], goals[:, outputs]
        weights = [(first, 0), None]
        weights += [(rest, 6 * layer_id) for layer_id in range(layer_total - 2)]
        heads = [(first, 0), (first, 6), None]
        heads += weights[3:]
        table_out = rest[0, :, :outputs]
        gain_rows = jnp.stack(pieces)[:, :, packed.shape[0] - 8, : flat_gains.shape[1]]
        gain_rows = gain_rows.reshape(2, 2, device_count // 8, 2, -1).transpose(2, 1, 3, 0, 4)
        gain_rows = gain_rows.reshape(device_count, -1)[order]
        gains = gain_rows.reshape(device_count, layer_total, 2, share).transpose(1, 2, 0, 3)
        gains = gains.reshape(layer_total, 2, width).astype(WIDE)
    else:
        self_id = None
        table_in = lax.all_gather(w_in.astype(LOW), AXES, axis=1, tiled=True)
        table_out = lax.all_gather(w_out.astype(LOW), AXES, axis=0, tiled=True)
        matrices = lax.all_gather(w_layers.astype(LOW), AXES, axis=2, tiled=True)
        matrices = matrices.reshape(-1, width, width)
        weights = [(matrices, 6 * layer_id) for layer_id in range(layer_total)]
        heads = weights
        gains = lax.all_gather(norm_gains.astype(LOW), AXES, axis=2, tiled=True).astype(WIDE)
        grid_latent = product(grid_inputs, table_in)
        grid_start = grid_latent.astype(LOW)
        sent = product(grid_start, matrices[0]).astype(LOW)
        blocks = (shift(sent, device_count, 1, direct), sent, shift(sent, device_count, -1, direct))
        mesh_rows = mesh_static
    slot_lists = [slot_lists[0]] + [slot_lists[1]] * (layer_total - 2) + [slot_lists[2]]
    target, target_low = mesh_rows, mesh_rows
    stored_list = []
    for layer_id in range(layer_total):
        if direct and layer_id == 1:
            second_near, target = lax.optimization_barrier((second_near, target))
            second_pieces = [*second_near, *(swap(piece, device_count, 1) for piece in second_near)]
            second = assemble(self_id, second_pieces)
            weights[1] = heads[2] = (second, 0)
        last_layer = layer_id == layer_total - 1
        if last_layer:
            source_low = target_low
            target, target_low = grid_latent, grid_start
        else:
            source_low = grid_start if layer_id == 0 else target_low
        results = forward_layer(
            slot_lists[layer_id],
            blocks,
            target_low,
            target,
            weights[layer_id],
            None if last_layer else heads[layer_id + 1],
            gains[layer_id],
        )
        if last_layer:
            grid_low, kept, aggregate = results
        else:
            sent, updated, updated_low, kept, aggregate = results
            blocks = (shift(sent, device_count, 1, direct), sent, shift(sent, device_count, -1, direct))
        stored_list.append((source_low, (target_low, kept, aggregate), aggregate))
        if not last_layer:
            target, target_low = updated, updated_low
    prediction = product(grid_low, table_out)
    error_rows = prediction - targets
    loss_scale = 1.0 / (row_count * device_count * prediction.shape[1])
    loss_local = jnp.sum(weight_rows[:, None] * error_rows * error_rows) * loss_scale
    grad_pred = (2.0 * loss_scale * weight_rows[:, None] * error_rows).astype(LOW)
    grad_table_out = product_left(grid_low, grad_pred)
    grad_part = product_right(grad_pred, table_out)
    extra = jnp.pad(grad_table_out, ((0, 0), (0, width - outputs)))
    grad_grid = None
    above, above_source = None, None
    layer_grads = [None] * layer_total
    gain_grads = [None] * layer_total
    in_plane, in_slice = [], []
    for layer_id in reversed(range(layer_total)):
        source_low, stored, aggregate = stored_list[layer_id]
        sent_grad, grad_new, *slot_grads, grad_gain, grad_message, edge_hidden, b0, b1, b2, b3 = backward_layer(
            slot_lists[layer_id], above, grad_part, stored, weights[layer_id], gains[layer_id], layer_id == 0
        )
        far = []
        if in_plane:
            moved = len(in_plane)
            arrived, slot_grads = together(in_plane + in_slice, slot_grads)
            if in_slice:
                layer_grads[layer_id + 2] = add_up(arrived[moved:]).reshape(6, share, width)
            far = list(combine(arrived[:moved], device_count // 8))
        from_before = shift(slot_grads[2], device_count, 1, direct)
        from_after = shift(slot_grads[0], device_count, -1, direct)
        back = [edge_hidden, grad_message, b0, b1, b2, b3]
        grad_part, sums = weight_layer(
            self_id,
            device_count,
            None if above is None else (above_source, sent_grad),
            extra,
            stored[0],
            aggregate,
            back,
            None if layer_id == 0 else grad_new,
            weights[layer_id],
        )
        gain_grads[layer_id] = grad_gain
        if direct:
            halo, arrived = together([from_before, from_after], [*sums, *far])
            keep, send, far = arrived[0], arrived[1], arrived[2:]
            in_slice = fan_out(far, device_count, 8) if far else []
            other = swap(send, device_count, 1)
            if layer_id > 0:
                near = list(combine([keep, other], 4))
                halo, near = together(halo, near)
                in_plane = fan_out(near, device_count, 2)
            from_before, from_after = halo
        else:
            layer_grads[layer_id] = sums[0]
        if layer_id == layer_total - 1:
            grad_grid, grad_part = grad_part, None
        above = (from_before, slot_grads[1], from_after, heads[layer_id])
        above_source = source_low
    if direct:
        sums = tail_layer(
            self_id,
            device_count,
            loss_local.reshape(1),
            from_before,
            slot_grads[1],
            from_after,
            grid_start,
            inputs,
            grad_grid,
            heads[0],
            gain_grads,
        )
        arrived, sums = together([other] + in_slice, sums)
        other, in_slice = arrived[0], arrived[1:]
        near = combine([keep, other], 4)
        layer_grads[1] = add_up(in_slice).reshape(6, share, width)
        far = combine(fan_out(near, device_count, 2), device_count // 8)
        layer_grads[0] = add_up(fan_out(far, device_count, 8)).reshape(6, share, width)
        keep, send = sums
        pieces = combine([keep, swap(send, device_count, 1)], 4)
        pieces = combine(fan_out(pieces, device_count, 2), device_count // 8)
        total = add_up(fan_out(pieces, device_count, 8))
        grad_zero = total[:share]
        grad_in = total[share : 2 * share, :channels].T
        grad_gain_all = total[2 * share :, :share].reshape(layer_total, 2, share)
        loss_value = total[2 * share, share]
        grad_out = layer_grads[-1][0, :, :outputs]
    else:
        loss_value = lax.psum(loss_local, AXES)
        sent_grad = (
            from_before.astype(WIDE) + slot_grads[1].astype(WIDE) + from_after.astype(WIDE)
        ).astype(LOW)
        grad_zero = product_left(above_source, sent_grad)
        grad_grid = grad_grid + product_right(sent_grad, matrices[0])
        grad_table_in = product_left(grid_inputs, grad_grid.astype(LOW))
        grad_in = lax.psum_scatter(grad_table_in, AXES, scatter_dimension=1, tiled=True)
        grad_out = lax.psum_scatter(grad_table_out, AXES, scatter_dimension=0, tiled=True)
        grad_gain_all = lax.psum_scatter(
            jnp.stack(gain_grads), AXES, scatter_dimension=2, tiled=True
        )
    grad_layers = [grad_zero[None]]
    for layer_id in range(layer_total):
        grad_layers += [layer_grads[layer_id][1:]]
        if layer_id < layer_total - 1:
            grad_layers += [layer_grads[layer_id][0:1]]
    grad_layers = jnp.concatenate(grad_layers, axis=0)
    grad_layers = grad_layers.reshape(layer_total, 6, *grad_layers.shape[1:])
    if not direct:
        grad_layers = lax.psum_scatter(grad_layers, AXES, scatter_dimension=2, tiled=True)
    step_value = step_count[0].astype(WIDE)
    one_in, two_in, new_in = adamw_update(
        w_in, moment_in, square_in, grad_in, step_value, DECAY_RATE
    )
    one_layers, two_layers, new_layers = adamw_update(
        w_layers, moment_layers, square_layers, grad_layers, step_value, DECAY_RATE
    )
    one_gains, two_gains, new_gains = adamw_update(
        norm_gains, moment_gains, square_gains, grad_gain_all, step_value, 0.0
    )
    one_out, two_out, new_out = adamw_update(
        w_out, moment_out, square_out, grad_out, step_value, DECAY_RATE
    )
    return (
        loss_value,
        one_in,
        two_in,
        new_in,
        one_layers,
        two_layers,
        new_layers,
        one_gains,
        two_gains,
        new_gains,
        one_out,
        two_out,
        new_out,
    )


def solution(mesh):
    rows = P(AXES, None)
    layers = P(None, None, AXES, None)
    gains = P(None, None, AXES)
    columns = P(None, AXES)
    in_specs = (rows, rows, rows, P(AXES), P(AXES), rows, rows, rows, P())
    in_specs += (columns,) * 3 + (layers,) * 3 + (gains,) * 3 + (rows,) * 3
    out_specs = (P(),) + (columns,) * 3 + (layers,) * 3 + (gains,) * 3 + (rows,) * 3
    return jax.shard_map(shards, mesh=mesh, in_specs=in_specs, out_specs=out_specs, check_vma=False)
```

```python
import functools

import jax
import jax.numpy as jnp
from jax import lax
from jax.experimental import pallas as pl
from jax.experimental.pallas import tpu as pltpu
from jax.sharding import PartitionSpec as P

EPS_NORM = 1e-05
BETA_ONE = 0.5
BETA_TWO = 0.5
ADAM_EPS = 1e-08
LEARN_RATE = 0.04
DECAY_RATE = 0.1

AXES = ("nodes", "shard")
LANES = 128
FORWARD_ROWS = 256
BACKWARD_ROWS = 256
WEIGHT_ROWS = 256
UNROLL = 256
LOW = jnp.bfloat16
WIDE = jnp.float32
SEND = jnp.bfloat16


def product(left, right):
    return jnp.dot(left, right, preferred_element_type=WIDE)


def product_left(left, right):
    return lax.dot_general(left, right, (((0,), (0,)), ((), ())), preferred_element_type=WIDE)


def product_right(left, right):
    return lax.dot_general(left, right, (((1,), (1,)), ((), ())), preferred_element_type=WIDE)


def normalize(tensor):
    centre = tensor - jnp.mean(tensor, axis=-1, keepdims=True)
    inv_scale = lax.rsqrt(jnp.mean(centre * centre, axis=-1, keepdims=True) + EPS_NORM)
    return (centre * inv_scale, inv_scale)


def normal_back(grad_unit, unit_rows, inv_scale):
    centred = grad_unit - jnp.mean(grad_unit, axis=-1, keepdims=True)
    return inv_scale * (
        centred - unit_rows * jnp.mean(grad_unit * unit_rows, axis=-1, keepdims=True)
    )


def silu_parts(tensor):
    half = 0.5 * tensor
    return half, jnp.tanh(half)


def silu(tensor):
    half, bend = silu_parts(tensor)
    return half * (1.0 + bend)


def fold_rows(store, base, rows, tensor):
    parts = tensor.shape[1] // LANES
    for part in range(parts):
        store[pl.ds(base * parts + part, rows, stride=parts), :] = tensor[
            :, part * LANES : (part + 1) * LANES
        ]


def unfold_rows(store, base, rows, parts):
    return jnp.concatenate(
        [store[pl.ds(base * parts + part, rows, stride=parts), :] for part in range(parts)],
        axis=1,
    )


def forward_kernel(parts, has_next, *refs):
    if has_next:
        (slots, before, middle, after, low, wide, weights, gains, head) = refs[:9]
        (sent, update, update_low, kept, aggregate) = refs[9:14]
        window, picked, hidden, message = refs[14:]
    else:
        (slots, before, middle, after, low, wide, weights, gains) = refs[:8]
        (update_low, kept, aggregate) = refs[8:11]
        window, picked, hidden, message = refs[11:]
    step = pl.program_id(0)
    block_rows = before.shape[0]
    rows, width = low.shape
    fan = kept.shape[0]

    @pl.when(step == 0)
    def _():
        for index, block in enumerate((before, middle, after)):
            fold_rows(window, index * block_rows, block_rows, block[...].astype(WIDE))

    for k in range(fan):

        def pick(trip, carry):
            for lane in range(UNROLL):
                row = trip * UNROLL + lane
                slot = slots[k * block_rows + step * rows + row]
                picked[pl.ds(pl.multiple_of((k * rows + row) * parts, parts), parts), :] = window[
                    pl.ds(pl.multiple_of(slot * parts, parts), parts), :
                ]
            return carry

        lax.fori_loop(0, rows // UNROLL, pick, 0)
    target_low = low[...]
    own_term = product(target_low, weights[1])
    for k in range(fan):
        sender = unfold_rows(picked, k * rows, rows, parts)
        kept[k] = sender.astype(LOW)
        hidden[k * rows : (k + 1) * rows, :] = silu(sender + own_term).astype(LOW)
    message[...] = product(hidden[...], weights[2])
    total = normalize(message[0:rows, :])[0]
    for k in range(1, fan):
        total = total + normalize(message[k * rows : (k + 1) * rows, :])[0]
    total_low = (total * gains[0:1, :]).astype(LOW)
    aggregate[...] = total_low
    node_mix = product(target_low, weights[3]) + product(total_low, weights[4])
    node_out = product(silu(node_mix).astype(LOW), weights[5])
    updated = wide[...].astype(WIDE) + normalize(node_out)[0] * gains[1:2, :]
    updated_low = updated.astype(LOW)
    update_low[...] = updated_low
    if has_next:
        update[...] = updated
        sent[...] = product(updated_low, head[0]).astype(LOW)


def in_hbm(shape, dtype):
    return pltpu.MemorySpace.HBM(shape, dtype)


def on_chip(shape, dtype):
    return pltpu.MemorySpace.VMEM(shape, dtype)


def kept_on_chip(array):
    return pltpu.with_memory_space_constraint(array, pltpu.MemorySpace.VMEM)


def pinned(array):
    return pltpu.with_memory_space_constraint(array, pltpu.MemorySpace.HBM)


def whole(shape):
    zeros = (0,) * len(shape)
    return pl.BlockSpec(shape, lambda step: zeros, pipeline_mode=pl.Buffered(1))


def matrix_spec(first, count, width):
    return pl.BlockSpec(
        (count, width, width), lambda step: (first // count, 0, 0), pipeline_mode=pl.Buffered(1)
    )


def tiled(rows, width):
    return pl.BlockSpec((rows, width), lambda step: (step, 0))


def fanned(fan, rows, width):
    return pl.BlockSpec((fan, rows, width), lambda step: (0, step, 0))


def forward_layer(slots, blocks, target_low, target, weights, next_weights, gains, halo_place):
    block_rows, width = target_low.shape
    fan = slots.shape[0] // block_rows
    parts = width // LANES
    rows = FORWARD_ROWS
    has_next = next_weights is not None
    shape = functools.partial(in_hbm, (block_rows, width))
    fan_shape = functools.partial(in_hbm, (fan, block_rows, width))
    tile = tiled(rows, width)
    in_specs = [pl.BlockSpec(memory_space=pltpu.SMEM)]
    in_specs += [whole((block_rows, width))] * 3 + [tile, tile]
    in_specs += [matrix_spec(weights[1], 6, width), whole(gains.shape)]
    out_specs = [tile, fanned(fan, rows, width), tile]
    out_shape = [shape(LOW), fan_shape(LOW), shape(LOW)]
    operands = [slots, *blocks, target_low, target, weights[0], gains]
    if has_next:
        in_specs += [matrix_spec(next_weights[1], 1, width)]
        operands += [next_weights[0]]
        out_specs = [tile, tile] + out_specs
        out_shape = [shape(LOW), shape(WIDE)] + out_shape
    return pl.pallas_call(
        functools.partial(forward_kernel, parts, has_next),
        grid=(block_rows // rows,),
        in_specs=in_specs,
        out_specs=out_specs,
        out_shape=out_shape,
        scratch_shapes=[
            pltpu.VMEM((3 * block_rows * parts, LANES), WIDE),
            pltpu.VMEM((fan * rows * parts, LANES), WIDE),
            pltpu.VMEM((fan * rows, width), LOW),
            pltpu.VMEM((fan * rows, width), WIDE),
        ],
        compiler_params=pltpu.CompilerParams(vmem_limit_bytes=54 << 20),
        cost_estimate=pl.CostEstimate(
            flops=2 * (fan + 5) * block_rows * width * width,
            transcendentals=(fan + 1) * block_rows * width,
            bytes_accessed=24 * block_rows * width * 2,
        ),
        name="forward_layer",
    )(
        operands[0],
        halo_place(operands[1]),
        pinned(operands[2]),
        halo_place(operands[3]),
        *map(pinned, operands[4:]),
    )


def backward_kernel(parts, mode, *refs):
    refs = list(refs)
    slots = refs.pop(0)
    if mode != "first":
        returned = [refs.pop(0) for _ in range(3)]
        head = refs.pop(0)
    if mode != "second":
        grad_part = refs.pop(0)
    low, kept, aggregate, weights, gains = refs[:5]
    refs = refs[5:]
    if mode != "first":
        sent_grad = refs.pop(0)
        grad_full = refs.pop(0)
    slot_grads = refs[:3]
    (grad_gains, grad_message, edge_hidden, grad_mix, grad_out, grad_own, hidden) = refs[3:10]
    sum_even, sum_odd, spread, stage = refs[10:]
    step = pl.program_id(0)
    rows, width = low.shape
    fan = kept.shape[0]
    block_rows = slot_grads[0].shape[0]

    @pl.when(step == 0)
    def _():
        sum_even[...] = jnp.zeros_like(sum_even)
        sum_odd[...] = jnp.zeros_like(sum_odd)
        grad_gains[...] = jnp.zeros_like(grad_gains)

    if mode == "first":
        grad_new = grad_part[...]
    else:
        sent_low = (
            returned[0][...].astype(WIDE)
            + returned[1][...].astype(WIDE)
            + returned[2][...].astype(WIDE)
        ).astype(LOW)
        sent_grad[...] = sent_low
        grad_new = product_right(sent_low, head[0])
        if mode == "third":
            grad_new = grad_part[...] + grad_new
        grad_full[...] = grad_new
    target_low = low[...]
    own_term = product(target_low, weights[1])
    node_mix = product(target_low, weights[3]) + product(aggregate[...], weights[4])
    for k in range(fan):
        edge_hidden[k] = silu(kept[k].astype(WIDE) + own_term).astype(LOW)
    stage[...] = product(edge_hidden[...].reshape(fan * rows, width), weights[2])
    half, bend = silu_parts(node_mix)
    node_hidden = (half * (1.0 + bend)).astype(LOW)
    hidden[...] = node_hidden
    out_unit, out_scale = normalize(product(node_hidden, weights[5]))
    gain_two = jnp.sum(grad_new * out_unit, axis=0, keepdims=True)
    out_low = normal_back(grad_new * gains[1:2, :], out_unit, out_scale).astype(LOW)
    grad_out[...] = out_low
    mix_low = (
        product_right(out_low, weights[5]) * ((0.5 + 0.5 * bend) * (1.0 + half * (1.0 - bend)))
    ).astype(LOW)
    grad_mix[...] = mix_low
    grad_sum = product_right(mix_low, weights[4])
    grad_unit = grad_sum * gains[0:1, :]
    unit_total = None
    for k in range(fan):
        unit_rows, inv_scale = normalize(stage[k * rows : (k + 1) * rows, :])
        unit_total = unit_rows if k == 0 else unit_total + unit_rows
        grad_message[k] = normal_back(grad_unit, unit_rows, inv_scale).astype(LOW)
    stage[...] = product_right(grad_message[...].reshape(fan * rows, width), weights[2])
    own_total = None
    for k in range(fan):
        half, bend = silu_parts(kept[k].astype(WIDE) + own_term)
        grad_pre = stage[k * rows : (k + 1) * rows, :] * (
            (0.5 + 0.5 * bend) * (1.0 + half * (1.0 - bend))
        )
        own_total = grad_pre if k == 0 else own_total + grad_pre
        fold_rows(spread, k * rows, rows, grad_pre)
    gain_one = jnp.sum(grad_sum * unit_total, axis=0, keepdims=True)
    grad_gains[...] += jnp.concatenate([gain_one, gain_two], axis=0)
    grad_own[...] = own_total.astype(LOW)

    for k in range(fan):

        def add(trip, carry):
            for lane in range(UNROLL // 2):
                places, values = [], []
                for store in (sum_even, sum_odd):
                    row = (trip * (UNROLL // 2) + lane) * 2 + len(places)
                    slot = slots[k * block_rows + step * rows + row]
                    place = pl.ds(pl.multiple_of(slot * parts, parts), parts)
                    value = spread[pl.ds(pl.multiple_of((k * rows + row) * parts, parts), parts), :]
                    places.append(place)
                    values.append(store[place, :] + value)
                sum_even[places[0], :] = values[0]
                sum_odd[places[1], :] = values[1]
            return carry

        lax.fori_loop(0, rows // UNROLL, add, 0)

    @pl.when(step == pl.num_programs(0) - 1)
    def _():
        for index in range(3):
            base = index * block_rows
            slot_grads[index][...] = (
                unfold_rows(sum_even, base, block_rows, parts)
                + unfold_rows(sum_odd, base, block_rows, parts)
            ).astype(LOW)


def backward_layer(slots, above, grad_part, stored, weights, gains, first_layer):
    target_low, kept, aggregate = stored
    block_rows, width = target_low.shape
    fan = kept.shape[0]
    parts = width // LANES
    rows = BACKWARD_ROWS
    tile = tiled(rows, width)
    fan_tile = fanned(fan, rows, width)
    in_specs = [pl.BlockSpec(memory_space=pltpu.SMEM)]
    operands = [slots]
    out_specs, out_shape = [], []
    shape = functools.partial(on_chip, (block_rows, width))
    fan_shape = functools.partial(on_chip, (fan, block_rows, width))
    mode = "first" if above is None else ("second" if grad_part is None else "third")
    if above is not None:
        from_before, slot_grad, from_after, head = above
        in_specs += [
            tile,
            tile,
            tile,
            matrix_spec(head[1], 1, width),
        ]
        operands += [from_before, slot_grad, from_after, head[0]]
        out_specs += [tile, tile]
        out_shape += [shape(LOW), shape(WIDE)]
    if grad_part is not None:
        in_specs += [tile]
        operands += [grad_part]
    in_specs += [tile, fan_tile, tile]
    in_specs += [matrix_spec(weights[1], 6, width), whole(gains.shape)]
    operands += [target_low, kept, aggregate, weights[0], gains]
    out_specs += [
        whole((block_rows, width)),
        whole((block_rows, width)),
        whole((block_rows, width)),
        whole((2, width)),
        fan_tile,
        fan_tile,
        tile,
        tile,
        tile,
        tile,
    ]
    out_shape += [
        in_hbm((block_rows, width), LOW),
        in_hbm((block_rows, width), LOW),
        in_hbm((block_rows, width), LOW),
        jax.ShapeDtypeStruct((2, width), WIDE),
        fan_shape(LOW),
        in_hbm((fan, block_rows, width), LOW) if first_layer else fan_shape(LOW),
        shape(LOW),
        shape(LOW),
        shape(LOW),
        shape(LOW),
    ]
    results = pl.pallas_call(
        functools.partial(backward_kernel, parts, mode),
        grid=(block_rows // rows,),
        in_specs=in_specs,
        out_specs=out_specs,
        out_shape=out_shape,
        scratch_shapes=[
            pltpu.VMEM((3 * block_rows * parts, LANES), WIDE),
            pltpu.VMEM((3 * block_rows * parts, LANES), WIDE),
            pltpu.VMEM((fan * rows * parts, LANES), WIDE),
            pltpu.VMEM((fan * rows, width), WIDE),
        ],
        compiler_params=pltpu.CompilerParams(vmem_limit_bytes=38 << 20),
        cost_estimate=pl.CostEstimate(
            flops=2 * (fan + 4) * block_rows * width * width,
            transcendentals=(fan + 1) * block_rows * width,
            bytes_accessed=24 * block_rows * width * 2,
        ),
        name="backward_layer",
    )(operands[0], *map(pinned, operands[1:]))
    if above is None:
        return (None, grad_part, *results)
    return tuple(results)


def deal(self_id, sums, outs):
    keep, send = outs
    share = keep.shape[1] // sums.shape[0]

    def move(node, carry):
        for core, out in enumerate((keep, send)):
            place = pl.multiple_of(((2 * node + core) ^ self_id[0]) * share, share)
            for index in range(sums.shape[0]):
                out[node, index * share : (index + 1) * share, :] = sums[
                    index, pl.ds(place, share), :
                ].astype(out.dtype)
        return carry

    lax.fori_loop(0, keep.shape[0], move, 0)


def weight_kernel(has_above, needs_target, direct, *refs):
    refs = list(refs)
    if direct:
        self_id = refs.pop(0)
    if has_above:
        source, sent_grad = refs[:2]
        refs = refs[2:]
    else:
        extra = refs.pop(0)
    low, aggregate, edge_hidden, grad_message, grad_mix, grad_out, grad_own, hidden = refs[:8]
    refs = refs[8:]
    if needs_target:
        grad_new, weights = refs[:2]
        grad_part = refs[2]
        refs = refs[3:]
    outs, sums = (refs[:2], refs[2]) if direct else (None, refs[0])
    step = pl.program_id(0)
    fan = edge_hidden.shape[0]

    @pl.when(step == 0)
    def _():
        sums[...] = jnp.zeros_like(sums)
        if not has_above:
            sums[0] = extra[...]

    target_low = low[...]
    mix_low = grad_mix[...]
    own_low = grad_own[...]
    if has_above:
        sums[0] += product_left(source[...], sent_grad[...])
    sums[1] += product_left(target_low, own_low)
    for k in range(fan):
        sums[2] += product_left(edge_hidden[k], grad_message[k])
    sums[3] += product_left(target_low, mix_low)
    sums[4] += product_left(aggregate[...], mix_low)
    sums[5] += product_left(hidden[...], grad_out[...])
    if needs_target:
        grad_part[...] = (
            grad_new[...] + product_right(own_low, weights[1]) + product_right(mix_low, weights[3])
        )
    if direct:

        @pl.when(step == pl.num_programs(0) - 1)
        def _():
            deal(self_id, sums, outs)


def share_outputs(count, width, device_count):
    shape = (device_count // 2, count * (width // device_count), width)
    return (
        [whole(shape)] * 2,
        [on_chip(shape, WIDE), on_chip(shape, SEND)],
    )


def weight_layer(self_id, device_count, above, extra, low, aggregate, back, grad_new, weights):
    block_rows, width = low.shape
    rows = WEIGHT_ROWS
    fan = back[0].shape[0]
    tile = tiled(rows, width)
    fan_tile = fanned(fan, rows, width)
    in_specs, operands = [], []
    direct = self_id is not None
    if direct:
        in_specs += [pl.BlockSpec(memory_space=pltpu.SMEM)]
        operands += [self_id]
    if above is not None:
        in_specs += [tile, tile]
        operands += [pinned(above[0]), kept_on_chip(above[1])]
    else:
        in_specs += [whole((width, width))]
        operands += [extra]
    in_specs += [tile, tile, fan_tile, fan_tile, tile, tile, tile, tile]
    place = pinned if grad_new is None else kept_on_chip
    operands += [pinned(low), pinned(aggregate), place(back[0]), *map(kept_on_chip, back[1:])]
    out_specs, out_shape, scratch = [], [], []
    if grad_new is not None:
        in_specs += [tile, matrix_spec(weights[1], 6, width)]
        operands += [kept_on_chip(grad_new), pinned(weights[0])]
        out_specs += [tile]
        out_shape += [in_hbm((block_rows, width), WIDE)]
    if direct:
        specs, shapes = share_outputs(6, width, device_count)
        out_specs += specs
        out_shape += shapes
        scratch = [pltpu.VMEM((6, width, width), WIDE)]
    else:
        out_specs += [whole((6, width, width))]
        out_shape += [jax.ShapeDtypeStruct((6, width, width), WIDE)]
    results = pl.pallas_call(
        functools.partial(weight_kernel, above is not None, grad_new is not None, direct),
        grid=(block_rows // rows,),
        in_specs=in_specs,
        out_specs=out_specs,
        out_shape=out_shape,
        scratch_shapes=scratch,
        compiler_params=pltpu.CompilerParams(vmem_limit_bytes=30 << 20),
        cost_estimate=pl.CostEstimate(
            flops=2 * (fan + 6) * block_rows * width * width,
            transcendentals=0,
            bytes_accessed=24 * block_rows * width,
        ),
        name="weight_layer",
    )(*operands)
    if grad_new is None:
        return (None, results)
    return (results[0], results[1:])


def place_rows(self_id, pieces, targets, width):
    share = width // (pieces[0].shape[0] * len(pieces))
    for index, piece in enumerate(pieces):
        base = (index // 2) + (index % 2) * 4

        def move(digit, carry, piece=piece, base=base):
            relative = (digit // 2) * 8 + (digit % 2) * 2 + base
            place = pl.multiple_of((relative ^ self_id[0]) * share, share)
            for j, target in enumerate(targets):
                target[pl.ds(place, share), :] = piece[digit, j * share : (j + 1) * share, :]
            return carry

        lax.fori_loop(0, piece.shape[0], move, 0)


def assemble_kernel(pieces_count, *refs):
    matrices = refs[-1]
    targets = [matrices.at[j] for j in range(matrices.shape[0])]
    place_rows(refs[0], refs[1 : 1 + pieces_count], targets, matrices.shape[1])


def assemble(self_id, pieces):
    digits, rows, width = pieces[0].shape
    count = rows * digits * len(pieces) // width
    return pl.pallas_call(
        functools.partial(assemble_kernel, len(pieces)),
        grid=(1,),
        in_specs=[pl.BlockSpec(memory_space=pltpu.SMEM)] + [whole(piece.shape) for piece in pieces],
        out_specs=whole((count, width, width)),
        out_shape=in_hbm((count, width, width), LOW),
        compiler_params=pltpu.CompilerParams(vmem_limit_bytes=20 << 20),
        cost_estimate=pl.CostEstimate(
            flops=0, transcendentals=0, bytes_accessed=4 * count * width * width
        ),
        name="assemble",
    )(self_id, *pieces)


def join_kernel(*refs):
    start = 0
    for part in refs[:-1]:
        refs[-1][start : start + part.shape[0]] = part[...]
        start += part.shape[0]


def join(parts):
    shape = (sum(part.shape[0] for part in parts), *parts[0].shape[1:])
    return pl.pallas_call(
        join_kernel,
        grid=(1,),
        in_specs=[whole(part.shape) for part in parts],
        out_specs=whole(shape),
        out_shape=on_chip(shape, parts[0].dtype),
        compiler_params=pltpu.CompilerParams(vmem_limit_bytes=8 << 20),
        cost_estimate=pl.CostEstimate(
            flops=0, transcendentals=0, bytes_accessed=4 * shape[0] * shape[1] * shape[2]
        ),
        name="join",
    )(*map(kept_on_chip, parts))


def embed_kernel(pieces_count, *refs):
    self_id = refs[0]
    pieces = refs[1 : 1 + pieces_count]
    before, middle, after = refs[1 + pieces_count : 4 + pieces_count]
    weights, latent, latent_low, sent_before, sent_middle, sent_after, table = refs[
        4 + pieces_count :
    ]

    @pl.when(pl.program_id(0) == 0)
    def _():
        targets = [weights.at[j] for j in range(weights.shape[0])] + [table]
        place_rows(self_id, pieces, targets, weights.shape[1])

    for block, sent in ((before, sent_before), (middle, sent_middle), (after, sent_after)):
        wide = product_right(block[...], table[...])
        low = wide.astype(LOW)
        sent[...] = product(low, weights[0]).astype(LOW)
        if block is middle:
            latent[...] = wide
            latent_low[...] = low


def embed(self_id, pieces, blocks):
    block_rows, width = blocks[1].shape
    rows = WEIGHT_ROWS
    tile = tiled(rows, width)
    return pl.pallas_call(
        functools.partial(embed_kernel, len(pieces)),
        grid=(block_rows // rows,),
        in_specs=[pl.BlockSpec(memory_space=pltpu.SMEM)]
        + [whole(piece.shape) for piece in pieces]
        + [tile] * 3,
        out_specs=[whole((7, width, width))] + [tile] * 5,
        out_shape=[
            in_hbm((7, width, width), LOW),
            in_hbm((block_rows, width), WIDE),
            in_hbm((block_rows, width), LOW),
            in_hbm((block_rows, width), LOW),
            in_hbm((block_rows, width), LOW),
            in_hbm((block_rows, width), LOW),
        ],
        scratch_shapes=[pltpu.VMEM((width, width), LOW)],
        compiler_params=pltpu.CompilerParams(vmem_limit_bytes=50 << 20),
        cost_estimate=pl.CostEstimate(
            flops=12 * block_rows * width * width,
            transcendentals=0,
            bytes_accessed=24 * block_rows * width,
        ),
        name="embed",
    )(self_id, *pieces, *blocks)


def tail_kernel(self_id, loss, before, middle, after, latent_low, inputs, grad_grid, head, *refs):
    gains = refs[:-3]
    keep, send, sums = refs[-3:]
    step = pl.program_id(0)
    rows, width = inputs.shape
    share = width // (2 * keep.shape[0])
    gain_count = 2 * len(gains)

    @pl.when(step == 0)
    def _():
        sums[...] = jnp.zeros_like(sums)

    sent_low = (
        before[...].astype(WIDE)
        + middle[...].astype(WIDE)
        + after[...].astype(WIDE)
    ).astype(LOW)
    grad_low = (grad_grid[...] + product_right(sent_low, head[0])).astype(LOW)
    sums[0] += product_left(latent_low[...], sent_low)
    sums[1] += product_left(grad_low, inputs[...])

    @pl.when(step == pl.num_programs(0) - 1)
    def _():
        size = sums.shape[0] * share
        main = [out.at[:, 0:size, :] for out in (keep, send)]
        deal(self_id, sums, main)
        gain_rows = jnp.concatenate([gain[...] for gain in gains], axis=0)
        lane = lax.broadcasted_iota(jnp.int32, gain_rows.shape, 1)

        def move(node, carry):
            for core, out in enumerate((keep, send)):
                device = (2 * node + core) ^ self_id[0]
                turned = pltpu.roll(gain_rows, width - device * share, axis=1)
                out[node, size : size + gain_count, :] = jnp.where(
                    lane == share, loss[0], turned
                ).astype(out.dtype)
            return carry

        lax.fori_loop(0, keep.shape[0], move, 0)


def tail_layer(
    self_id, device_count, loss, from_before, slot_grad, from_after, latent_low, inputs, grad_grid, head, gains
):
    block_rows, width = inputs.shape
    rows = WEIGHT_ROWS
    tile = tiled(rows, width)
    gain_count = 2 * len(gains)
    shape = (device_count // 2, 2 * (width // device_count) + gain_count, width)
    return pl.pallas_call(
        tail_kernel,
        grid=(block_rows // rows,),
        in_specs=[pl.BlockSpec(memory_space=pltpu.SMEM)] * 2
        + [tile] * 6
        + [matrix_spec(head[1], 1, width)]
        + [whole((2, width))] * len(gains),
        out_specs=[whole(shape)] * 2,
        out_shape=[on_chip(shape, WIDE), on_chip(shape, SEND)],
        scratch_shapes=[pltpu.VMEM((2, width, width), WIDE)],
        compiler_params=pltpu.CompilerParams(vmem_limit_bytes=56 << 20),
        cost_estimate=pl.CostEstimate(
            flops=6 * block_rows * width * width,
            transcendentals=0,
            bytes_accessed=24 * block_rows * width,
        ),
        name="tail_layer",
    )(
        self_id,
        loss,
        *map(pinned, (from_before, slot_grad, from_after, latent_low, inputs, grad_grid, head[0])),
        *gains,
    )


def combine_kernel(count, *refs):
    arrived, outs = refs[:count], refs[count:]
    for digit, out in enumerate(outs):
        total = arrived[0][0, digit].astype(WIDE)
        for part in arrived[1:]:
            total = total + part[0, digit].astype(WIDE)
        out[0] = total.astype(out.dtype)


def combine(arrived, radix):
    _, rows, width = arrived[0].shape
    rest = arrived[0].shape[0] // radix
    arrived = [part.reshape(rest, radix, rows, width) for part in arrived]
    spec = pl.BlockSpec((1, radix, rows, width), lambda step: (step, 0, 0, 0))
    shape = (rest, rows, width)
    return pl.pallas_call(
        functools.partial(combine_kernel, len(arrived)),
        grid=(rest,),
        in_specs=[spec] * len(arrived),
        out_specs=[pl.BlockSpec((1, rows, width), lambda step: (step, 0, 0))] * radix,
        out_shape=[on_chip(shape, WIDE)] + [on_chip(shape, SEND)] * (radix - 1),
        compiler_params=pltpu.CompilerParams(vmem_limit_bytes=20 << 20),
        cost_estimate=pl.CostEstimate(
            flops=rest * radix * rows * width * len(arrived),
            transcendentals=0,
            bytes_accessed=4 * rest * radix * rows * width * (len(arrived) + 1),
        ),
        name="combine",
    )(*map(kept_on_chip, arrived))


def swap(cells, count, mask):
    return lax.ppermute(cells, AXES, [(i, i ^ mask) for i in range(count)])


def spread_high(rows, count):
    return [rows] + [swap(rows, count, digit * 8) for digit in range(1, count // 8)]


def home(block, direct):
    return block ^ (((block >> 2) & 1) << 1) if direct else block


def bring(cells, count, step, direct):
    return lax.ppermute(cells, AXES, [(i, home((i + step) % count, direct)) for i in range(count)])


def shift(cells, count, step, direct):
    pairs = [(home(i, direct), home((i + step) % count, direct)) for i in range(count)]
    return lax.ppermute(cells, AXES, pairs)


def fan_out(pieces, count, unit):
    return [pieces[0]] + [
        swap(pieces[digit], count, digit * unit) for digit in range(1, len(pieces))
    ]


def together(first, second):
    joined = lax.optimization_barrier((tuple(first), tuple(second)))
    return list(joined[0]), list(joined[1])


def add_up(arrived):
    total = arrived[0][0]
    for part in arrived[1:]:
        total = total + part[0].astype(WIDE)
    return total


def adamw_update(weight, moment_one, moment_two, gradient, step_value, decay_rate):
    new_one = BETA_ONE * moment_one + (1.0 - BETA_ONE) * gradient
    new_two = BETA_TWO * moment_two + (1.0 - BETA_TWO) * gradient * gradient
    correct_one = 1.0 - jnp.power(BETA_ONE, step_value)
    correct_two = 1.0 - jnp.power(BETA_TWO, step_value)
    direction = new_one / correct_one / (jnp.sqrt(new_two / correct_two) + ADAM_EPS)
    return (new_one, new_two, weight - LEARN_RATE * (direction + decay_rate * weight))


def shards(
    grid_inputs,
    mesh_static,
    targets,
    area_weight,
    valid_rows,
    encoder_lists,
    mesh_lists,
    decoder_lists,
    step_count,
    w_in,
    moment_in,
    square_in,
    w_layers,
    moment_layers,
    square_layers,
    norm_gains,
    moment_gains,
    square_gains,
    w_out,
    moment_out,
    square_out,
):
    row_count = grid_inputs.shape[0]
    layer_total = w_layers.shape[0]
    device_count = lax.axis_size(AXES)
    width = mesh_static.shape[1]
    share = w_layers.shape[2]
    channels, outputs = w_in.shape[0], w_out.shape[1]
    direct = share == 16 and device_count % 8 == 0 and device_count & (device_count - 1) == 0
    slot_lists = [encoder_lists.T.reshape(-1), mesh_lists.T.reshape(-1), decoder_lists.T.reshape(-1)]
    local_rows = jnp.arange(row_count, dtype=jnp.int32)
    weight_rows = area_weight * (local_rows < valid_rows[0]).astype(WIDE)
    if direct:
        self_id = lax.axis_index(AXES).astype(jnp.int32)
        order = jnp.arange(device_count, dtype=jnp.int32) ^ self_id
        self_id = self_id.reshape(1)
        inputs = jnp.pad(grid_inputs, ((0, 0), (0, width - channels)))
        flat_gains = norm_gains.astype(LOW).reshape(1, -1)
        packed = jnp.concatenate(
            [
                w_layers[0].astype(LOW).reshape(-1, width),
                w_layers[1, 0].astype(LOW),
                jnp.pad(w_in.astype(LOW).T, ((0, 0), (0, width - channels))),
                jnp.pad(flat_gains, ((0, 7), (0, width - flat_gains.shape[1]))),
            ],
            axis=0,
        )
        second = jnp.concatenate([w_layers[2, :1], w_layers[1, 1:]], axis=0)
        second = second.astype(LOW).reshape(-1, width)
        rest = jnp.concatenate(
            [
                jnp.pad(w_out.astype(LOW), ((0, 0), (0, width - outputs)))[None],
                w_layers[2, 1:].astype(LOW),
                w_layers[3:].astype(LOW).reshape(-1, share, width),
            ],
            axis=0,
        )
        lists = jnp.concatenate(slot_lists).reshape(-1, LANES)
        goals = jnp.concatenate([targets, weight_rows[:, None]], axis=1)
        goals = jnp.pad(goals, ((0, 0), (0, -goals.shape[1] % LANES)))
        barrier = lax.optimization_barrier
        pairs = ((packed, swap(packed, device_count, 2)), (second, swap(second, device_count, 2)))
        lists = bring(lists, device_count, 0, direct)
        pairs, lists, inputs, mesh_static = barrier((pairs, lists, inputs, mesh_static))
        mesh_rows = bring(mesh_static, device_count, 0, direct)
        pair, second_pair = (jnp.stack(rows) for rows in pairs)
        column, mesh_rows, inputs, second_pair = barrier(
            (spread_high(pair, device_count), mesh_rows, inputs, second_pair)
        )
        sides = [bring(inputs, device_count, step, direct) for step in (1, 0, -1)]
        second_column = spread_high(second_pair, device_count)
        plane = join(column)
        near, sides, second_column, rest, goals = barrier(
            ((plane, swap(plane, device_count, 4)), sides, second_column, rest, goals)
        )
        pieces = [*near, *(swap(piece, device_count, 1) for piece in near)]
        rest = lax.all_gather(rest, AXES, axis=1, tiled=True)
        inputs = sides[1]
        lists = lists.reshape(len(slot_lists), -1)
        slot_lists = [lists[index] for index in range(len(slot_lists))]
        first, grid_latent, grid_start, *blocks = embed(
            self_id, pieces, sides
        )
        first, goals = barrier((first, goals))
        second_plane = join(second_column)
        second_near = (second_plane, swap(second_plane, device_count, 4))
        goals = bring(goals, device_count, 0, direct)
        targets, weight_rows = goals[:, :outputs], goals[:, outputs]
        weights = [(first, 0), None]
        weights += [(rest, 6 * layer_id) for layer_id in range(layer_total - 2)]
        heads = [(first, 0), (first, 6), None]
        heads += weights[3:]
        table_out = rest[0, :, :outputs]
        gain_rows = jnp.stack(pieces)[:, :, packed.shape[0] - 8, : flat_gains.shape[1]]
        gain_rows = gain_rows.reshape(2, 2, device_count // 8, 2, -1).transpose(2, 1, 3, 0, 4)
        gain_rows = gain_rows.reshape(device_count, -1)[order]
        gains = gain_rows.reshape(device_count, layer_total, 2, share).transpose(1, 2, 0, 3)
        gains = gains.reshape(layer_total, 2, width).astype(WIDE)
    else:
        self_id = None
        table_in = lax.all_gather(w_in.astype(LOW), AXES, axis=1, tiled=True)
        table_out = lax.all_gather(w_out.astype(LOW), AXES, axis=0, tiled=True)
        matrices = lax.all_gather(w_layers.astype(LOW), AXES, axis=2, tiled=True)
        matrices = matrices.reshape(-1, width, width)
        weights = [(matrices, 6 * layer_id) for layer_id in range(layer_total)]
        heads = weights
        gains = lax.all_gather(norm_gains.astype(LOW), AXES, axis=2, tiled=True).astype(WIDE)
        grid_latent = product(grid_inputs, table_in)
        grid_start = grid_latent.astype(LOW)
        sent = product(grid_start, matrices[0]).astype(LOW)
        blocks = (shift(sent, device_count, 1, direct), sent, shift(sent, device_count, -1, direct))
        mesh_rows = mesh_static
    slot_lists = [slot_lists[0]] + [slot_lists[1]] * (layer_total - 2) + [slot_lists[2]]
    target, target_low = mesh_rows, mesh_rows
    stored_list = []
    for layer_id in range(layer_total):
        if direct and layer_id == 1:
            second_near, target = lax.optimization_barrier((second_near, target))
            second_pieces = [*second_near, *(swap(piece, device_count, 1) for piece in second_near)]
            second = assemble(self_id, second_pieces)
            weights[1] = heads[2] = (second, 0)
        last_layer = layer_id == layer_total - 1
        if last_layer:
            source_low = target_low
            target, target_low = grid_latent, grid_start
        else:
            source_low = grid_start if layer_id == 0 else target_low
        results = forward_layer(
            slot_lists[layer_id],
            blocks,
            target_low,
            target,
            weights[layer_id],
            None if last_layer else heads[layer_id + 1],
            gains[layer_id],
            kept_on_chip if layer_id > 0 else pinned,
        )
        if last_layer:
            grid_low, kept, aggregate = results
        else:
            sent, updated, updated_low, kept, aggregate = results
            blocks = (shift(sent, device_count, 1, direct), sent, shift(sent, device_count, -1, direct))
        stored_list.append((source_low, (target_low, kept, aggregate), aggregate))
        if not last_layer:
            target, target_low = updated, updated_low
    prediction = product(grid_low, table_out)
    error_rows = prediction - targets
    loss_scale = 1.0 / (row_count * device_count * prediction.shape[1])
    loss_local = jnp.sum(weight_rows[:, None] * error_rows * error_rows) * loss_scale
    grad_pred = (2.0 * loss_scale * weight_rows[:, None] * error_rows).astype(LOW)
    grad_table_out = product_left(grid_low, grad_pred)
    grad_part = product_right(grad_pred, table_out)
    extra = jnp.pad(grad_table_out, ((0, 0), (0, width - outputs)))
    grad_grid = None
    above, above_source = None, None
    layer_grads = [None] * layer_total
    gain_grads = [None] * layer_total
    in_plane, in_slice = [], []
    for layer_id in reversed(range(layer_total)):
        source_low, stored, aggregate = stored_list[layer_id]
        sent_grad, grad_new, *slot_grads, grad_gain, grad_message, edge_hidden, b0, b1, b2, b3 = backward_layer(
            slot_lists[layer_id], above, grad_part, stored, weights[layer_id], gains[layer_id], layer_id == 0
        )
        far = []
        if in_plane:
            moved = len(in_plane)
            arrived, slot_grads = together(in_plane + in_slice, slot_grads)
            if in_slice:
                layer_grads[layer_id + 2] = add_up(arrived[moved:]).reshape(6, share, width)
            far = list(combine(arrived[:moved], device_count // 8))
        from_before = shift(slot_grads[2], device_count, 1, direct)
        from_after = shift(slot_grads[0], device_count, -1, direct)
        back = [edge_hidden, grad_message, b0, b1, b2, b3]
        grad_part, sums = weight_layer(
            self_id,
            device_count,
            None if above is None else (above_source, sent_grad),
            extra,
            stored[0],
            aggregate,
            back,
            None if layer_id == 0 else grad_new,
            weights[layer_id],
        )
        gain_grads[layer_id] = grad_gain
        if direct:
            halo, arrived = together([from_before, from_after], [*sums, *far])
            keep, send, far = arrived[0], arrived[1], arrived[2:]
            in_slice = fan_out(far, device_count, 8) if far else []
            other = swap(send, device_count, 1)
            if layer_id > 0:
                near = list(combine([keep, other], 4))
                halo, near = together(halo, near)
                in_plane = fan_out(near, device_count, 2)
            from_before, from_after = halo
        else:
            layer_grads[layer_id] = sums[0]
        if layer_id == layer_total - 1:
            grad_grid, grad_part = grad_part, None
        above = (from_before, slot_grads[1], from_after, heads[layer_id])
        above_source = source_low
    if direct:
        sums = tail_layer(
            self_id,
            device_count,
            loss_local.reshape(1),
            from_before,
            slot_grads[1],
            from_after,
            grid_start,
            inputs,
            grad_grid,
            heads[0],
            gain_grads,
        )
        arrived, sums = together([other] + in_slice, sums)
        other, in_slice = arrived[0], arrived[1:]
        near = combine([keep, other], 4)
        layer_grads[1] = add_up(in_slice).reshape(6, share, width)
        far = combine(fan_out(near, device_count, 2), device_count // 8)
        layer_grads[0] = add_up(fan_out(far, device_count, 8)).reshape(6, share, width)
        keep, send = sums
        pieces = combine([keep, swap(send, device_count, 1)], 4)
        pieces = combine(fan_out(pieces, device_count, 2), device_count // 8)
        total = add_up(fan_out(pieces, device_count, 8))
        grad_zero = total[:share]
        grad_in = total[share : 2 * share, :channels].T
        grad_gain_all = total[2 * share :, :share].reshape(layer_total, 2, share)
        loss_value = total[2 * share, share]
        grad_out = layer_grads[-1][0, :, :outputs]
    else:
        loss_value = lax.psum(loss_local, AXES)
        sent_grad = (
            from_before.astype(WIDE) + slot_grads[1].astype(WIDE) + from_after.astype(WIDE)
        ).astype(LOW)
        grad_zero = product_left(above_source, sent_grad)
        grad_grid = grad_grid + product_right(sent_grad, matrices[0])
        grad_table_in = product_left(grid_inputs, grad_grid.astype(LOW))
        grad_in = lax.psum_scatter(grad_table_in, AXES, scatter_dimension=1, tiled=True)
        grad_out = lax.psum_scatter(grad_table_out, AXES, scatter_dimension=0, tiled=True)
        grad_gain_all = lax.psum_scatter(
            jnp.stack(gain_grads), AXES, scatter_dimension=2, tiled=True
        )
    grad_layers = [grad_zero[None]]
    for layer_id in range(layer_total):
        grad_layers += [layer_grads[layer_id][1:]]
        if layer_id < layer_total - 1:
            grad_layers += [layer_grads[layer_id][0:1]]
    grad_layers = jnp.concatenate(grad_layers, axis=0)
    grad_layers = grad_layers.reshape(layer_total, 6, *grad_layers.shape[1:])
    if not direct:
        grad_layers = lax.psum_scatter(grad_layers, AXES, scatter_dimension=2, tiled=True)
    step_value = step_count[0].astype(WIDE)
    one_in, two_in, new_in = adamw_update(
        w_in, moment_in, square_in, grad_in, step_value, DECAY_RATE
    )
    one_layers, two_layers, new_layers = adamw_update(
        w_layers, moment_layers, square_layers, grad_layers, step_value, DECAY_RATE
    )
    one_gains, two_gains, new_gains = adamw_update(
        norm_gains, moment_gains, square_gains, grad_gain_all, step_value, 0.0
    )
    one_out, two_out, new_out = adamw_update(
        w_out, moment_out, square_out, grad_out, step_value, DECAY_RATE
    )
    return (
        loss_value,
        one_in,
        two_in,
        new_in,
        one_layers,
        two_layers,
        new_layers,
        one_gains,
        two_gains,
        new_gains,
        one_out,
        two_out,
        new_out,
    )


def solution(mesh):
    rows = P(AXES, None)
    layers = P(None, None, AXES, None)
    gains = P(None, None, AXES)
    columns = P(None, AXES)
    in_specs = (rows, rows, rows, P(AXES), P(AXES), rows, rows, rows, P())
    in_specs += (columns,) * 3 + (layers,) * 3 + (gains,) * 3 + (rows,) * 3
    out_specs = (P(),) + (columns,) * 3 + (layers,) * 3 + (gains,) * 3 + (rows,) * 3
    return jax.shard_map(shards, mesh=mesh, in_specs=in_specs, out_specs=out_specs, check_vma=False)
```

```python
import functools

import jax
import jax.numpy as jnp
from jax import lax
from jax.experimental import pallas as pl
from jax.experimental.pallas import tpu as pltpu
from jax.sharding import PartitionSpec as P

EPS_NORM = 1e-05
BETA_ONE = 0.5
BETA_TWO = 0.5
ADAM_EPS = 1e-08
LEARN_RATE = 0.04
DECAY_RATE = 0.1

AXES = ("nodes", "shard")
LANES = 128
FORWARD_ROWS = 256
BACKWARD_ROWS = 256
WEIGHT_ROWS = 256
UNROLL = 256
LOW = jnp.bfloat16
WIDE = jnp.float32
SEND = jnp.bfloat16


def product(left, right):
    return jnp.dot(left, right, preferred_element_type=WIDE)


def product_left(left, right):
    return lax.dot_general(left, right, (((0,), (0,)), ((), ())), preferred_element_type=WIDE)


def product_right(left, right):
    return lax.dot_general(left, right, (((1,), (1,)), ((), ())), preferred_element_type=WIDE)


def normalize(tensor):
    centre = tensor - jnp.mean(tensor, axis=-1, keepdims=True)
    inv_scale = lax.rsqrt(jnp.mean(centre * centre, axis=-1, keepdims=True) + EPS_NORM)
    return (centre * inv_scale, inv_scale)


def normal_back(grad_unit, unit_rows, inv_scale):
    centred = grad_unit - jnp.mean(grad_unit, axis=-1, keepdims=True)
    return inv_scale * (
        centred - unit_rows * jnp.mean(grad_unit * unit_rows, axis=-1, keepdims=True)
    )


def silu_parts(tensor):
    half = 0.5 * tensor
    return half, jnp.tanh(half)


def silu(tensor):
    half, bend = silu_parts(tensor)
    return half * (1.0 + bend)


def fold_rows(store, base, rows, tensor):
    parts = tensor.shape[1] // LANES
    for part in range(parts):
        store[pl.ds(base * parts + part, rows, stride=parts), :] = tensor[
            :, part * LANES : (part + 1) * LANES
        ]


def unfold_rows(store, base, rows, parts):
    return jnp.concatenate(
        [store[pl.ds(base * parts + part, rows, stride=parts), :] for part in range(parts)],
        axis=1,
    )


def forward_kernel(parts, has_next, *refs):
    if has_next:
        (slots, before, middle, after, low, wide, weights, gains, head) = refs[:9]
        (sent, update, update_low, kept, aggregate) = refs[9:14]
        window, picked, hidden, message = refs[14:]
    else:
        (slots, before, middle, after, low, wide, weights, gains) = refs[:8]
        (update_low, kept, aggregate) = refs[8:11]
        window, picked, hidden, message = refs[11:]
    step = pl.program_id(0)
    block_rows = before.shape[0]
    rows, width = low.shape
    fan = kept.shape[0]

    @pl.when(step == 0)
    def _():
        for index, block in enumerate((before, middle, after)):
            fold_rows(window, index * block_rows, block_rows, block[...].astype(WIDE))

    for k in range(fan):

        def pick(trip, carry):
            for lane in range(UNROLL):
                row = trip * UNROLL + lane
                slot = slots[k * block_rows + step * rows + row]
                picked[pl.ds(pl.multiple_of((k * rows + row) * parts, parts), parts), :] = window[
                    pl.ds(pl.multiple_of(slot * parts, parts), parts), :
                ]
            return carry

        lax.fori_loop(0, rows // UNROLL, pick, 0)
    target_low = low[...]
    own_term = product(target_low, weights[1])
    for k in range(fan):
        sender = unfold_rows(picked, k * rows, rows, parts)
        kept[k] = sender.astype(LOW)
        hidden[k * rows : (k + 1) * rows, :] = silu(sender + own_term).astype(LOW)
    message[...] = product(hidden[...], weights[2])
    total = normalize(message[0:rows, :])[0]
    for k in range(1, fan):
        total = total + normalize(message[k * rows : (k + 1) * rows, :])[0]
    total_low = (total * gains[0:1, :]).astype(LOW)
    aggregate[...] = total_low
    node_mix = product(target_low, weights[3]) + product(total_low, weights[4])
    node_out = product(silu(node_mix).astype(LOW), weights[5])
    updated = wide[...].astype(WIDE) + normalize(node_out)[0] * gains[1:2, :]
    updated_low = updated.astype(LOW)
    update_low[...] = updated_low
    if has_next:
        update[...] = updated
        sent[...] = product(updated_low, head[0]).astype(LOW)


def in_hbm(shape, dtype):
    return pltpu.MemorySpace.HBM(shape, dtype)


def on_chip(shape, dtype):
    return pltpu.MemorySpace.VMEM(shape, dtype)


def kept_on_chip(array):
    return pltpu.with_memory_space_constraint(array, pltpu.MemorySpace.VMEM)


def pinned(array):
    return pltpu.with_memory_space_constraint(array, pltpu.MemorySpace.HBM)


def whole(shape):
    zeros = (0,) * len(shape)
    return pl.BlockSpec(shape, lambda step: zeros, pipeline_mode=pl.Buffered(1))


def matrix_spec(first, count, width):
    return pl.BlockSpec(
        (count, width, width), lambda step: (first // count, 0, 0), pipeline_mode=pl.Buffered(1)
    )


def tiled(rows, width):
    return pl.BlockSpec((rows, width), lambda step: (step, 0))


def fanned(fan, rows, width):
    return pl.BlockSpec((fan, rows, width), lambda step: (0, step, 0))


def forward_layer(slots, blocks, target_low, target, weights, next_weights, gains, halo_place):
    block_rows, width = target_low.shape
    fan = slots.shape[0] // block_rows
    parts = width // LANES
    rows = FORWARD_ROWS
    has_next = next_weights is not None
    shape = functools.partial(in_hbm, (block_rows, width))
    fan_shape = functools.partial(in_hbm, (fan, block_rows, width))
    tile = tiled(rows, width)
    in_specs = [pl.BlockSpec(memory_space=pltpu.SMEM)]
    in_specs += [whole((block_rows, width))] * 3 + [tile, tile]
    in_specs += [matrix_spec(weights[1], 6, width), whole(gains.shape)]
    out_specs = [tile, fanned(fan, rows, width), tile]
    out_shape = [shape(LOW), fan_shape(LOW), shape(LOW)]
    operands = [slots, *blocks, target_low, target, weights[0], gains]
    if has_next:
        in_specs += [matrix_spec(next_weights[1], 1, width)]
        operands += [next_weights[0]]
        out_specs = [tile, tile] + out_specs
        out_shape = [shape(LOW), shape(WIDE)] + out_shape
    return pl.pallas_call(
        functools.partial(forward_kernel, parts, has_next),
        grid=(block_rows // rows,),
        in_specs=in_specs,
        out_specs=out_specs,
        out_shape=out_shape,
        scratch_shapes=[
            pltpu.VMEM((3 * block_rows * parts, LANES), WIDE),
            pltpu.VMEM((fan * rows * parts, LANES), WIDE),
            pltpu.VMEM((fan * rows, width), LOW),
            pltpu.VMEM((fan * rows, width), WIDE),
        ],
        compiler_params=pltpu.CompilerParams(vmem_limit_bytes=54 << 20),
        cost_estimate=pl.CostEstimate(
            flops=2 * (fan + 5) * block_rows * width * width,
            transcendentals=(fan + 1) * block_rows * width,
            bytes_accessed=24 * block_rows * width * 2,
        ),
        name="forward_layer",
    )(
        operands[0],
        halo_place(operands[1]),
        pinned(operands[2]),
        halo_place(operands[3]),
        *map(pinned, operands[4:]),
    )


def backward_kernel(parts, mode, *refs):
    refs = list(refs)
    slots = refs.pop(0)
    if mode != "first":
        returned = [refs.pop(0) for _ in range(3)]
        head = refs.pop(0)
    if mode != "second":
        grad_part = refs.pop(0)
    low, kept, aggregate, weights, gains = refs[:5]
    refs = refs[5:]
    if mode != "first":
        sent_grad = refs.pop(0)
        grad_full = refs.pop(0)
    slot_grads = refs[:3]
    (grad_gains, grad_message, edge_hidden, grad_mix, grad_out, grad_own, hidden) = refs[3:10]
    sum_even, sum_odd, spread, stage = refs[10:]
    step = pl.program_id(0)
    rows, width = low.shape
    fan = kept.shape[0]
    block_rows = slot_grads[0].shape[0]

    @pl.when(step == 0)
    def _():
        sum_even[...] = jnp.zeros_like(sum_even)
        sum_odd[...] = jnp.zeros_like(sum_odd)
        grad_gains[...] = jnp.zeros_like(grad_gains)

    if mode == "first":
        grad_new = grad_part[...]
    else:
        sent_low = (
            returned[0][...].astype(WIDE)
            + returned[1][...].astype(WIDE)
            + returned[2][...].astype(WIDE)
        ).astype(LOW)
        sent_grad[...] = sent_low
        grad_new = product_right(sent_low, head[0])
        if mode == "third":
            grad_new = grad_part[...] + grad_new
        grad_full[...] = grad_new
    target_low = low[...]
    own_term = product(target_low, weights[1])
    node_mix = product(target_low, weights[3]) + product(aggregate[...], weights[4])
    for k in range(fan):
        edge_hidden[k] = silu(kept[k].astype(WIDE) + own_term).astype(LOW)
    stage[...] = product(edge_hidden[...].reshape(fan * rows, width), weights[2])
    half, bend = silu_parts(node_mix)
    node_hidden = (half * (1.0 + bend)).astype(LOW)
    hidden[...] = node_hidden
    out_unit, out_scale = normalize(product(node_hidden, weights[5]))
    gain_two = jnp.sum(grad_new * out_unit, axis=0, keepdims=True)
    out_low = normal_back(grad_new * gains[1:2, :], out_unit, out_scale).astype(LOW)
    grad_out[...] = out_low
    mix_low = (
        product_right(out_low, weights[5]) * ((0.5 + 0.5 * bend) * (1.0 + half * (1.0 - bend)))
    ).astype(LOW)
    grad_mix[...] = mix_low
    grad_sum = product_right(mix_low, weights[4])
    grad_unit = grad_sum * gains[0:1, :]
    unit_total = None
    for k in range(fan):
        unit_rows, inv_scale = normalize(stage[k * rows : (k + 1) * rows, :])
        unit_total = unit_rows if k == 0 else unit_total + unit_rows
        grad_message[k] = normal_back(grad_unit, unit_rows, inv_scale).astype(LOW)
    stage[...] = product_right(grad_message[...].reshape(fan * rows, width), weights[2])
    own_total = None
    for k in range(fan):
        half, bend = silu_parts(kept[k].astype(WIDE) + own_term)
        grad_pre = stage[k * rows : (k + 1) * rows, :] * (
            (0.5 + 0.5 * bend) * (1.0 + half * (1.0 - bend))
        )
        own_total = grad_pre if k == 0 else own_total + grad_pre
        fold_rows(spread, k * rows, rows, grad_pre)
    gain_one = jnp.sum(grad_sum * unit_total, axis=0, keepdims=True)
    grad_gains[...] += jnp.concatenate([gain_one, gain_two], axis=0)
    grad_own[...] = own_total.astype(LOW)

    for k in range(fan):

        def add(trip, carry):
            for lane in range(UNROLL // 2):
                places, values = [], []
                for store in (sum_even, sum_odd):
                    row = (trip * (UNROLL // 2) + lane) * 2 + len(places)
                    slot = slots[k * block_rows + step * rows + row]
                    place = pl.ds(pl.multiple_of(slot * parts, parts), parts)
                    value = spread[pl.ds(pl.multiple_of((k * rows + row) * parts, parts), parts), :]
                    places.append(place)
                    values.append(store[place, :] + value)
                sum_even[places[0], :] = values[0]
                sum_odd[places[1], :] = values[1]
            return carry

        lax.fori_loop(0, rows // UNROLL, add, 0)

    @pl.when(step == pl.num_programs(0) - 1)
    def _():
        for index in range(3):
            base = index * block_rows
            slot_grads[index][...] = (
                unfold_rows(sum_even, base, block_rows, parts)
                + unfold_rows(sum_odd, base, block_rows, parts)
            ).astype(LOW)


def backward_layer(slots, above, grad_part, stored, weights, gains, first_layer):
    target_low, kept, aggregate = stored
    block_rows, width = target_low.shape
    fan = kept.shape[0]
    parts = width // LANES
    rows = BACKWARD_ROWS
    tile = tiled(rows, width)
    fan_tile = fanned(fan, rows, width)
    in_specs = [pl.BlockSpec(memory_space=pltpu.SMEM)]
    operands = [slots]
    out_specs, out_shape = [], []
    shape = functools.partial(on_chip, (block_rows, width))
    fan_shape = functools.partial(on_chip, (fan, block_rows, width))
    mode = "first" if above is None else ("second" if grad_part is None else "third")
    if above is not None:
        from_before, slot_grad, from_after, head = above
        in_specs += [
            tile,
            tile,
            tile,
            matrix_spec(head[1], 1, width),
        ]
        operands += [from_before, slot_grad, from_after, head[0]]
        out_specs += [tile, tile]
        out_shape += [shape(LOW), shape(WIDE)]
    if grad_part is not None:
        in_specs += [tile]
        operands += [grad_part]
    in_specs += [tile, fan_tile, tile]
    in_specs += [matrix_spec(weights[1], 6, width), whole(gains.shape)]
    operands += [target_low, kept, aggregate, weights[0], gains]
    out_specs += [
        whole((block_rows, width)),
        whole((block_rows, width)),
        whole((block_rows, width)),
        whole((2, width)),
        fan_tile,
        fan_tile,
        tile,
        tile,
        tile,
        tile,
    ]
    out_shape += [
        in_hbm((block_rows, width), LOW),
        in_hbm((block_rows, width), LOW),
        in_hbm((block_rows, width), LOW),
        jax.ShapeDtypeStruct((2, width), WIDE),
        fan_shape(LOW),
        in_hbm((fan, block_rows, width), LOW) if first_layer else fan_shape(LOW),
        shape(LOW),
        shape(LOW),
        shape(LOW),
        shape(LOW),
    ]
    results = pl.pallas_call(
        functools.partial(backward_kernel, parts, mode),
        grid=(block_rows // rows,),
        in_specs=in_specs,
        out_specs=out_specs,
        out_shape=out_shape,
        scratch_shapes=[
            pltpu.VMEM((3 * block_rows * parts, LANES), WIDE),
            pltpu.VMEM((3 * block_rows * parts, LANES), WIDE),
            pltpu.VMEM((fan * rows * parts, LANES), WIDE),
            pltpu.VMEM((fan * rows, width), WIDE),
        ],
        compiler_params=pltpu.CompilerParams(vmem_limit_bytes=38 << 20),
        cost_estimate=pl.CostEstimate(
            flops=2 * (fan + 4) * block_rows * width * width,
            transcendentals=(fan + 1) * block_rows * width,
            bytes_accessed=24 * block_rows * width * 2,
        ),
        name="backward_layer",
    )(operands[0], *map(pinned, operands[1:]))
    if above is None:
        return (None, grad_part, *results)
    return tuple(results)


def deal(self_id, sums, outs):
    keep, send = outs
    share = keep.shape[1] // sums.shape[0]

    def move(node, carry):
        for core, out in enumerate((keep, send)):
            place = pl.multiple_of(((2 * node + core) ^ self_id[0]) * share, share)
            for index in range(sums.shape[0]):
                out[node, index * share : (index + 1) * share, :] = sums[
                    index, pl.ds(place, share), :
                ].astype(out.dtype)
        return carry

    lax.fori_loop(0, keep.shape[0], move, 0)


def weight_kernel(has_above, needs_target, direct, *refs):
    refs = list(refs)
    if direct:
        self_id = refs.pop(0)
    if has_above:
        source, sent_grad = refs[:2]
        refs = refs[2:]
    else:
        extra = refs.pop(0)
    low, aggregate, edge_hidden, grad_message, grad_mix, grad_out, grad_own, hidden = refs[:8]
    refs = refs[8:]
    if needs_target:
        grad_new, weights = refs[:2]
        grad_part = refs[2]
        refs = refs[3:]
    outs, sums = (refs[:2], refs[2]) if direct else (None, refs[0])
    step = pl.program_id(0)
    fan = edge_hidden.shape[0]

    @pl.when(step == 0)
    def _():
        sums[...] = jnp.zeros_like(sums)
        if not has_above:
            sums[0] = extra[...]

    target_low = low[...]
    mix_low = grad_mix[...]
    own_low = grad_own[...]
    if has_above:
        sums[0] += product_left(source[...], sent_grad[...])
    sums[1] += product_left(target_low, own_low)
    for k in range(fan):
        sums[2] += product_left(edge_hidden[k], grad_message[k])
    sums[3] += product_left(target_low, mix_low)
    sums[4] += product_left(aggregate[...], mix_low)
    sums[5] += product_left(hidden[...], grad_out[...])
    if needs_target:
        grad_part[...] = (
            grad_new[...] + product_right(own_low, weights[1]) + product_right(mix_low, weights[3])
        )
    if direct:

        @pl.when(step == pl.num_programs(0) - 1)
        def _():
            deal(self_id, sums, outs)


def share_outputs(count, width, device_count):
    shape = (device_count // 2, count * (width // device_count), width)
    return (
        [whole(shape)] * 2,
        [on_chip(shape, WIDE), on_chip(shape, SEND)],
    )


def weight_layer(self_id, device_count, above, extra, low, aggregate, back, grad_new, weights):
    block_rows, width = low.shape
    rows = WEIGHT_ROWS
    fan = back[0].shape[0]
    tile = tiled(rows, width)
    fan_tile = fanned(fan, rows, width)
    in_specs, operands = [], []
    direct = self_id is not None
    if direct:
        in_specs += [pl.BlockSpec(memory_space=pltpu.SMEM)]
        operands += [self_id]
    if above is not None:
        in_specs += [tile, tile]
        operands += [pinned(above[0]), kept_on_chip(above[1])]
    else:
        in_specs += [whole((width, width))]
        operands += [extra]
    in_specs += [tile, tile, fan_tile, fan_tile, tile, tile, tile, tile]
    place = pinned if grad_new is None else kept_on_chip
    operands += [pinned(low), pinned(aggregate), place(back[0]), *map(kept_on_chip, back[1:])]
    out_specs, out_shape, scratch = [], [], []
    if grad_new is not None:
        in_specs += [tile, matrix_spec(weights[1], 6, width)]
        operands += [kept_on_chip(grad_new), pinned(weights[0])]
        out_specs += [tile]
        out_shape += [in_hbm((block_rows, width), WIDE)]
    if direct:
        specs, shapes = share_outputs(6, width, device_count)
        out_specs += specs
        out_shape += shapes
        scratch = [pltpu.VMEM((6, width, width), WIDE)]
    else:
        out_specs += [whole((6, width, width))]
        out_shape += [jax.ShapeDtypeStruct((6, width, width), WIDE)]
    results = pl.pallas_call(
        functools.partial(weight_kernel, above is not None, grad_new is not None, direct),
        grid=(block_rows // rows,),
        in_specs=in_specs,
        out_specs=out_specs,
        out_shape=out_shape,
        scratch_shapes=scratch,
        compiler_params=pltpu.CompilerParams(vmem_limit_bytes=30 << 20),
        cost_estimate=pl.CostEstimate(
            flops=2 * (fan + 6) * block_rows * width * width,
            transcendentals=0,
            bytes_accessed=24 * block_rows * width,
        ),
        name="weight_layer",
    )(*operands)
    if grad_new is None:
        return (None, results)
    return (results[0], results[1:])


def place_rows(self_id, pieces, targets, width):
    share = width // (pieces[0].shape[0] * len(pieces))
    for index, piece in enumerate(pieces):
        base = (index // 2) + (index % 2) * 4

        def move(digit, carry, piece=piece, base=base):
            relative = (digit // 2) * 8 + (digit % 2) * 2 + base
            place = pl.multiple_of((relative ^ self_id[0]) * share, share)
            for j, target in enumerate(targets):
                target[pl.ds(place, share), :] = piece[digit, j * share : (j + 1) * share, :]
            return carry

        lax.fori_loop(0, piece.shape[0], move, 0)


def assemble_kernel(pieces_count, *refs):
    matrices = refs[-1]
    targets = [matrices.at[j] for j in range(matrices.shape[0])]
    place_rows(refs[0], refs[1 : 1 + pieces_count], targets, matrices.shape[1])


def assemble(self_id, pieces):
    digits, rows, width = pieces[0].shape
    count = rows * digits * len(pieces) // width
    return pl.pallas_call(
        functools.partial(assemble_kernel, len(pieces)),
        grid=(1,),
        in_specs=[pl.BlockSpec(memory_space=pltpu.SMEM)] + [whole(piece.shape) for piece in pieces],
        out_specs=whole((count, width, width)),
        out_shape=in_hbm((count, width, width), LOW),
        compiler_params=pltpu.CompilerParams(vmem_limit_bytes=20 << 20),
        cost_estimate=pl.CostEstimate(
            flops=0, transcendentals=0, bytes_accessed=4 * count * width * width
        ),
        name="assemble",
    )(self_id, *pieces)


def join_kernel(*refs):
    start = 0
    for part in refs[:-1]:
        refs[-1][start : start + part.shape[0]] = part[...]
        start += part.shape[0]


def join(parts):
    shape = (sum(part.shape[0] for part in parts), *parts[0].shape[1:])
    return pl.pallas_call(
        join_kernel,
        grid=(1,),
        in_specs=[whole(part.shape) for part in parts],
        out_specs=whole(shape),
        out_shape=on_chip(shape, parts[0].dtype),
        compiler_params=pltpu.CompilerParams(vmem_limit_bytes=8 << 20),
        cost_estimate=pl.CostEstimate(
            flops=0, transcendentals=0, bytes_accessed=4 * shape[0] * shape[1] * shape[2]
        ),
        name="join",
    )(*map(kept_on_chip, parts))


def embed_kernel(pieces_count, *refs):
    self_id = refs[0]
    pieces = refs[1 : 1 + pieces_count]
    before, middle, after = refs[1 + pieces_count : 4 + pieces_count]
    weights, latent, latent_low, sent_before, sent_middle, sent_after, table = refs[
        4 + pieces_count :
    ]

    @pl.when(pl.program_id(0) == 0)
    def _():
        targets = [weights.at[j] for j in range(weights.shape[0])] + [table]
        place_rows(self_id, pieces, targets, weights.shape[1])

    for block, sent in ((before, sent_before), (middle, sent_middle), (after, sent_after)):
        wide = product_right(block[...], table[...])
        low = wide.astype(LOW)
        sent[...] = product(low, weights[0]).astype(LOW)
        if block is middle:
            latent[...] = wide
            latent_low[...] = low


def embed(self_id, pieces, blocks):
    block_rows, width = blocks[1].shape
    rows = WEIGHT_ROWS
    tile = tiled(rows, width)
    return pl.pallas_call(
        functools.partial(embed_kernel, len(pieces)),
        grid=(block_rows // rows,),
        in_specs=[pl.BlockSpec(memory_space=pltpu.SMEM)]
        + [whole(piece.shape) for piece in pieces]
        + [tile] * 3,
        out_specs=[whole((7, width, width))] + [tile] * 5,
        out_shape=[
            in_hbm((7, width, width), LOW),
            in_hbm((block_rows, width), WIDE),
            in_hbm((block_rows, width), LOW),
            in_hbm((block_rows, width), LOW),
            in_hbm((block_rows, width), LOW),
            in_hbm((block_rows, width), LOW),
        ],
        scratch_shapes=[pltpu.VMEM((width, width), LOW)],
        compiler_params=pltpu.CompilerParams(vmem_limit_bytes=50 << 20),
        cost_estimate=pl.CostEstimate(
            flops=12 * block_rows * width * width,
            transcendentals=0,
            bytes_accessed=24 * block_rows * width,
        ),
        name="embed",
    )(self_id, *pieces, *blocks)


def tail_kernel(self_id, loss, before, middle, after, latent_low, inputs, grad_grid, head, *refs):
    gains = refs[:-3]
    keep, send, sums = refs[-3:]
    step = pl.program_id(0)
    rows, width = inputs.shape
    share = width // (2 * keep.shape[0])
    gain_count = 2 * len(gains)

    @pl.when(step == 0)
    def _():
        sums[...] = jnp.zeros_like(sums)

    sent_low = (
        before[...].astype(WIDE)
        + middle[...].astype(WIDE)
        + after[...].astype(WIDE)
    ).astype(LOW)
    grad_low = (grad_grid[...] + product_right(sent_low, head[0])).astype(LOW)
    sums[0] += product_left(latent_low[...], sent_low)
    sums[1] += product_left(grad_low, inputs[...])

    @pl.when(step == pl.num_programs(0) - 1)
    def _():
        size = sums.shape[0] * share
        main = [out.at[:, 0:size, :] for out in (keep, send)]
        deal(self_id, sums, main)
        gain_rows = jnp.concatenate([gain[...] for gain in gains], axis=0)
        lane = lax.broadcasted_iota(jnp.int32, gain_rows.shape, 1)

        def move(node, carry):
            for core, out in enumerate((keep, send)):
                device = (2 * node + core) ^ self_id[0]
                turned = pltpu.roll(gain_rows, width - device * share, axis=1)
                out[node, size : size + gain_count, :] = jnp.where(
                    lane == share, loss[0], turned
                ).astype(out.dtype)
            return carry

        lax.fori_loop(0, keep.shape[0], move, 0)


def tail_layer(
    self_id, device_count, loss, from_before, slot_grad, from_after, latent_low, inputs, grad_grid, head, gains
):
    block_rows, width = inputs.shape
    rows = WEIGHT_ROWS
    tile = tiled(rows, width)
    gain_count = 2 * len(gains)
    shape = (device_count // 2, 2 * (width // device_count) + gain_count, width)
    return pl.pallas_call(
        tail_kernel,
        grid=(block_rows // rows,),
        in_specs=[pl.BlockSpec(memory_space=pltpu.SMEM)] * 2
        + [tile] * 6
        + [matrix_spec(head[1], 1, width)]
        + [whole((2, width))] * len(gains),
        out_specs=[whole(shape)] * 2,
        out_shape=[on_chip(shape, WIDE), on_chip(shape, SEND)],
        scratch_shapes=[pltpu.VMEM((2, width, width), WIDE)],
        compiler_params=pltpu.CompilerParams(vmem_limit_bytes=56 << 20),
        cost_estimate=pl.CostEstimate(
            flops=6 * block_rows * width * width,
            transcendentals=0,
            bytes_accessed=24 * block_rows * width,
        ),
        name="tail_layer",
    )(
        self_id,
        loss,
        *map(pinned, (from_before, slot_grad, from_after, latent_low, inputs, grad_grid, head[0])),
        *gains,
    )


def combine_kernel(counts, *refs):
    outs = refs[sum(counts) :]
    first, base = 0, 0
    for count in counts:
        arrived = refs[first : first + count]
        rows = arrived[0].shape[2]
        for digit, out in enumerate(outs):
            total = arrived[0][0, digit].astype(WIDE)
            for part in arrived[1:]:
                total = total + part[0, digit].astype(WIDE)
            out[0, base : base + rows, :] = total.astype(out.dtype)
        first, base = first + count, base + rows


def combine(radix, *groups):
    width = groups[0][0].shape[2]
    rest = groups[0][0].shape[0] // radix
    arrived, specs = [], []
    for group in groups:
        rows = group[0].shape[1]
        arrived += [part.reshape(rest, radix, rows, width) for part in group]
        specs += [pl.BlockSpec((1, radix, rows, width), lambda step: (step, 0, 0, 0))] * len(group)
    rows = sum(group[0].shape[1] for group in groups)
    shape = (rest, rows, width)
    return pl.pallas_call(
        functools.partial(combine_kernel, [len(group) for group in groups]),
        grid=(rest,),
        in_specs=specs,
        out_specs=[pl.BlockSpec((1, rows, width), lambda step: (step, 0, 0))] * radix,
        out_shape=[on_chip(shape, WIDE)] + [on_chip(shape, SEND)] * (radix - 1),
        compiler_params=pltpu.CompilerParams(vmem_limit_bytes=20 << 20),
        cost_estimate=pl.CostEstimate(
            flops=rest * radix * rows * width * 4,
            transcendentals=0,
            bytes_accessed=16 * rest * radix * rows * width,
        ),
        name="combine",
    )(*map(kept_on_chip, arrived))


def swap(cells, count, mask):
    return lax.ppermute(cells, AXES, [(i, i ^ mask) for i in range(count)])


def spread_high(rows, count):
    return [rows] + [swap(rows, count, digit * 8) for digit in range(1, count // 8)]


def home(block, direct):
    return block ^ (((block >> 2) & 1) << 1) if direct else block


def bring(cells, count, step, direct):
    return lax.ppermute(cells, AXES, [(i, home((i + step) % count, direct)) for i in range(count)])


def shift(cells, count, step, direct):
    pairs = [(home(i, direct), home((i + step) % count, direct)) for i in range(count)]
    return lax.ppermute(cells, AXES, pairs)


def fan_out(pieces, count, unit):
    return [pieces[0]] + [
        swap(pieces[digit], count, digit * unit) for digit in range(1, len(pieces))
    ]


def together(first, second):
    joined = lax.optimization_barrier((tuple(first), tuple(second)))
    return list(joined[0]), list(joined[1])


def add_up(arrived):
    total = arrived[0][0]
    for part in arrived[1:]:
        total = total + part[0].astype(WIDE)
    return total


def adamw_update(weight, moment_one, moment_two, gradient, step_value, decay_rate):
    new_one = BETA_ONE * moment_one + (1.0 - BETA_ONE) * gradient
    new_two = BETA_TWO * moment_two + (1.0 - BETA_TWO) * gradient * gradient
    correct_one = 1.0 - jnp.power(BETA_ONE, step_value)
    correct_two = 1.0 - jnp.power(BETA_TWO, step_value)
    direction = new_one / correct_one / (jnp.sqrt(new_two / correct_two) + ADAM_EPS)
    return (new_one, new_two, weight - LEARN_RATE * (direction + decay_rate * weight))


def shards(
    grid_inputs,
    mesh_static,
    targets,
    area_weight,
    valid_rows,
    encoder_lists,
    mesh_lists,
    decoder_lists,
    step_count,
    w_in,
    moment_in,
    square_in,
    w_layers,
    moment_layers,
    square_layers,
    norm_gains,
    moment_gains,
    square_gains,
    w_out,
    moment_out,
    square_out,
):
    row_count = grid_inputs.shape[0]
    layer_total = w_layers.shape[0]
    device_count = lax.axis_size(AXES)
    width = mesh_static.shape[1]
    share = w_layers.shape[2]
    channels, outputs = w_in.shape[0], w_out.shape[1]
    direct = share == 16 and device_count % 8 == 0 and device_count & (device_count - 1) == 0
    slot_lists = [encoder_lists.T.reshape(-1), mesh_lists.T.reshape(-1), decoder_lists.T.reshape(-1)]
    local_rows = jnp.arange(row_count, dtype=jnp.int32)
    weight_rows = area_weight * (local_rows < valid_rows[0]).astype(WIDE)
    if direct:
        self_id = lax.axis_index(AXES).astype(jnp.int32)
        order = jnp.arange(device_count, dtype=jnp.int32) ^ self_id
        self_id = self_id.reshape(1)
        inputs = jnp.pad(grid_inputs, ((0, 0), (0, width - channels)))
        flat_gains = norm_gains.astype(LOW).reshape(1, -1)
        packed = jnp.concatenate(
            [
                w_layers[0].astype(LOW).reshape(-1, width),
                w_layers[1, 0].astype(LOW),
                jnp.pad(w_in.astype(LOW).T, ((0, 0), (0, width - channels))),
                jnp.pad(flat_gains, ((0, 7), (0, width - flat_gains.shape[1]))),
            ],
            axis=0,
        )
        second = jnp.concatenate([w_layers[2, :1], w_layers[1, 1:]], axis=0)
        second = second.astype(LOW).reshape(-1, width)
        rest = jnp.concatenate(
            [
                jnp.pad(w_out.astype(LOW), ((0, 0), (0, width - outputs)))[None],
                w_layers[2, 1:].astype(LOW),
                w_layers[3:].astype(LOW).reshape(-1, share, width),
            ],
            axis=0,
        )
        lists = jnp.concatenate(slot_lists).reshape(-1, LANES)
        goals = jnp.concatenate([targets, weight_rows[:, None]], axis=1)
        goals = jnp.pad(goals, ((0, 0), (0, -goals.shape[1] % LANES)))
        barrier = lax.optimization_barrier
        pairs = ((packed, swap(packed, device_count, 2)), (second, swap(second, device_count, 2)))
        lists = bring(lists, device_count, 0, direct)
        pairs, lists, inputs, mesh_static = barrier((pairs, lists, inputs, mesh_static))
        own = bring(inputs, device_count, 0, direct)
        pair, second_pair = (jnp.stack(rows) for rows in pairs)
        column, own, mesh_static, second_pair = barrier(
            (spread_high(pair, device_count), own, mesh_static, second_pair)
        )
        sides = [shift(own, device_count, 1, direct), shift(own, device_count, -1, direct)]
        mesh_rows = bring(mesh_static, device_count, 0, direct)
        second_column = spread_high(second_pair, device_count)
        plane = join(column)
        near, sides, mesh_rows, second_column, rest, goals = barrier(
            ((plane, swap(plane, device_count, 4)), sides, mesh_rows, second_column, rest, goals)
        )
        sides = [sides[0], own, sides[1]]
        pieces = [*near, *(swap(piece, device_count, 1) for piece in near)]
        rest = lax.all_gather(rest, AXES, axis=1, tiled=True)
        inputs = sides[1]
        lists = lists.reshape(len(slot_lists), -1)
        slot_lists = [lists[index] for index in range(len(slot_lists))]
        first, grid_latent, grid_start, *blocks = embed(
            self_id, pieces, sides
        )
        first, goals = barrier((first, goals))
        second_plane = join(second_column)
        second_near = (second_plane, swap(second_plane, device_count, 4))
        goals = bring(goals, device_count, 0, direct)
        targets, weight_rows = goals[:, :outputs], goals[:, outputs]
        weights = [(first, 0), None]
        weights += [(rest, 6 * layer_id) for layer_id in range(layer_total - 2)]
        heads = [(first, 0), (first, 6), None]
        heads += weights[3:]
        table_out = rest[0, :, :outputs]
        gain_rows = jnp.stack(pieces)[:, :, packed.shape[0] - 8, : flat_gains.shape[1]]
        gain_rows = gain_rows.reshape(2, 2, device_count // 8, 2, -1).transpose(2, 1, 3, 0, 4)
        gain_rows = gain_rows.reshape(device_count, -1)[order]
        gains = gain_rows.reshape(device_count, layer_total, 2, share).transpose(1, 2, 0, 3)
        gains = gains.reshape(layer_total, 2, width).astype(WIDE)
    else:
        self_id = None
        table_in = lax.all_gather(w_in.astype(LOW), AXES, axis=1, tiled=True)
        table_out = lax.all_gather(w_out.astype(LOW), AXES, axis=0, tiled=True)
        matrices = lax.all_gather(w_layers.astype(LOW), AXES, axis=2, tiled=True)
        matrices = matrices.reshape(-1, width, width)
        weights = [(matrices, 6 * layer_id) for layer_id in range(layer_total)]
        heads = weights
        gains = lax.all_gather(norm_gains.astype(LOW), AXES, axis=2, tiled=True).astype(WIDE)
        grid_latent = product(grid_inputs, table_in)
        grid_start = grid_latent.astype(LOW)
        sent = product(grid_start, matrices[0]).astype(LOW)
        blocks = (shift(sent, device_count, 1, direct), sent, shift(sent, device_count, -1, direct))
        mesh_rows = mesh_static
    slot_lists = [slot_lists[0]] + [slot_lists[1]] * (layer_total - 2) + [slot_lists[2]]
    target, target_low = mesh_rows, mesh_rows
    stored_list = []
    for layer_id in range(layer_total):
        if direct and layer_id == 1:
            second_near, target = lax.optimization_barrier((second_near, target))
            second_pieces = [*second_near, *(swap(piece, device_count, 1) for piece in second_near)]
            second = assemble(self_id, second_pieces)
            weights[1] = heads[2] = (second, 0)
        last_layer = layer_id == layer_total - 1
        if last_layer:
            source_low = target_low
            target, target_low = grid_latent, grid_start
        else:
            source_low = grid_start if layer_id == 0 else target_low
        results = forward_layer(
            slot_lists[layer_id],
            blocks,
            target_low,
            target,
            weights[layer_id],
            None if last_layer else heads[layer_id + 1],
            gains[layer_id],
            kept_on_chip if layer_id > 0 else pinned,
        )
        if last_layer:
            grid_low, kept, aggregate = results
        else:
            sent, updated, updated_low, kept, aggregate = results
            blocks = (shift(sent, device_count, 1, direct), sent, shift(sent, device_count, -1, direct))
        stored_list.append((source_low, (target_low, kept, aggregate), aggregate))
        if not last_layer:
            target, target_low = updated, updated_low
    prediction = product(grid_low, table_out)
    error_rows = prediction - targets
    loss_scale = 1.0 / (row_count * device_count * prediction.shape[1])
    loss_local = jnp.sum(weight_rows[:, None] * error_rows * error_rows) * loss_scale
    grad_pred = (2.0 * loss_scale * weight_rows[:, None] * error_rows).astype(LOW)
    grad_table_out = product_left(grid_low, grad_pred)
    grad_part = product_right(grad_pred, table_out)
    extra = jnp.pad(grad_table_out, ((0, 0), (0, width - outputs)))
    grad_grid = None
    above, above_source = None, None
    layer_grads = [None] * layer_total
    gain_grads = [None] * layer_total
    in_plane, in_slice = [], []
    for layer_id in reversed(range(layer_total)):
        source_low, stored, aggregate = stored_list[layer_id]
        sent_grad, grad_new, *slot_grads, grad_gain, grad_message, edge_hidden, b0, b1, b2, b3 = backward_layer(
            slot_lists[layer_id], above, grad_part, stored, weights[layer_id], gains[layer_id], layer_id == 0
        )
        far = []
        if in_plane:
            moved = len(in_plane)
            arrived, slot_grads = together(in_plane + in_slice, slot_grads)
            if in_slice:
                layer_grads[layer_id + 2] = add_up(arrived[moved:]).reshape(6, share, width)
            far = list(combine(device_count // 8, arrived[:moved]))
        from_before = shift(slot_grads[2], device_count, 1, direct)
        from_after = shift(slot_grads[0], device_count, -1, direct)
        back = [edge_hidden, grad_message, b0, b1, b2, b3]
        grad_part, sums = weight_layer(
            self_id,
            device_count,
            None if above is None else (above_source, sent_grad),
            extra,
            stored[0],
            aggregate,
            back,
            None if layer_id == 0 else grad_new,
            weights[layer_id],
        )
        gain_grads[layer_id] = grad_gain
        if direct:
            tied = [*sums, *far] if layer_id > 0 else sums
            halo, arrived = together([from_before, from_after], tied)
            keep, send = arrived[:2]
            far = arrived[2:] if layer_id > 0 else far
            in_slice = fan_out(far, device_count, 8) if far else []
            other = swap(send, device_count, 1)
            near = list(combine(4, [keep, other]))
            halo, near = together(halo, near)
            in_plane = fan_out(near, device_count, 2)
            from_before, from_after = halo
        else:
            layer_grads[layer_id] = sums[0]
        if layer_id == layer_total - 1:
            grad_grid, grad_part = grad_part, None
        above = (from_before, slot_grads[1], from_after, heads[layer_id])
        above_source = source_low
    if direct:
        sums = tail_layer(
            self_id,
            device_count,
            loss_local.reshape(1),
            from_before,
            slot_grads[1],
            from_after,
            grid_start,
            inputs,
            grad_grid,
            heads[0],
            gain_grads,
        )
        early, sums = together(in_plane[1:3], sums)
        in_plane = [in_plane[0], *early, in_plane[3]]
        keep, send = sums
        last_plane = combine(4, [keep, swap(send, device_count, 1)])
        last_plane, in_slice = together(fan_out(last_plane, device_count, 2), in_slice)
        layer_grads[1] = add_up(in_slice).reshape(6, share, width)
        far = combine(device_count // 8, in_plane, last_plane)
        total = add_up(fan_out(far, device_count, 8))
        layer_grads[0] = total[: 6 * share].reshape(6, share, width)
        total = total[6 * share :]
        grad_zero = total[:share]
        grad_in = total[share : 2 * share, :channels].T
        grad_gain_all = total[2 * share :, :share].reshape(layer_total, 2, share)
        loss_value = total[2 * share, share]
        grad_out = layer_grads[-1][0, :, :outputs]
    else:
        loss_value = lax.psum(loss_local, AXES)
        sent_grad = (
            from_before.astype(WIDE) + slot_grads[1].astype(WIDE) + from_after.astype(WIDE)
        ).astype(LOW)
        grad_zero = product_left(above_source, sent_grad)
        grad_grid = grad_grid + product_right(sent_grad, matrices[0])
        grad_table_in = product_left(grid_inputs, grad_grid.astype(LOW))
        grad_in = lax.psum_scatter(grad_table_in, AXES, scatter_dimension=1, tiled=True)
        grad_out = lax.psum_scatter(grad_table_out, AXES, scatter_dimension=0, tiled=True)
        grad_gain_all = lax.psum_scatter(
            jnp.stack(gain_grads), AXES, scatter_dimension=2, tiled=True
        )
    grad_layers = [grad_zero[None]]
    for layer_id in range(layer_total):
        grad_layers += [layer_grads[layer_id][1:]]
        if layer_id < layer_total - 1:
            grad_layers += [layer_grads[layer_id][0:1]]
    grad_layers = jnp.concatenate(grad_layers, axis=0)
    grad_layers = grad_layers.reshape(layer_total, 6, *grad_layers.shape[1:])
    if not direct:
        grad_layers = lax.psum_scatter(grad_layers, AXES, scatter_dimension=2, tiled=True)
    step_value = step_count[0].astype(WIDE)
    one_in, two_in, new_in = adamw_update(
        w_in, moment_in, square_in, grad_in, step_value, DECAY_RATE
    )
    one_layers, two_layers, new_layers = adamw_update(
        w_layers, moment_layers, square_layers, grad_layers, step_value, DECAY_RATE
    )
    one_gains, two_gains, new_gains = adamw_update(
        norm_gains, moment_gains, square_gains, grad_gain_all, step_value, 0.0
    )
    one_out, two_out, new_out = adamw_update(
        w_out, moment_out, square_out, grad_out, step_value, DECAY_RATE
    )
    return (
        loss_value,
        one_in,
        two_in,
        new_in,
        one_layers,
        two_layers,
        new_layers,
        one_gains,
        two_gains,
        new_gains,
        one_out,
        two_out,
        new_out,
    )


def solution(mesh):
    rows = P(AXES, None)
    layers = P(None, None, AXES, None)
    gains = P(None, None, AXES)
    columns = P(None, AXES)
    in_specs = (rows, rows, rows, P(AXES), P(AXES), rows, rows, rows, P())
    in_specs += (columns,) * 3 + (layers,) * 3 + (gains,) * 3 + (rows,) * 3
    out_specs = (P(),) + (columns,) * 3 + (layers,) * 3 + (gains,) * 3 + (rows,) * 3
    return jax.shard_map(shards, mesh=mesh, in_specs=in_specs, out_specs=out_specs, check_vma=False)
```

```python
import functools

import jax
import jax.numpy as jnp
from jax import lax
from jax.experimental import pallas as pl
from jax.experimental.pallas import tpu as pltpu
from jax.sharding import PartitionSpec as P

EPS_NORM = 1e-05
BETA_ONE = 0.5
BETA_TWO = 0.5
ADAM_EPS = 1e-08
LEARN_RATE = 0.04
DECAY_RATE = 0.1

AXES = ("nodes", "shard")
LANES = 128
FORWARD_ROWS = 256
BACKWARD_ROWS = 256
WEIGHT_ROWS = 256
UNROLL = 256
LOW = jnp.bfloat16
WIDE = jnp.float32
SEND = jnp.bfloat16


def product(left, right):
    return jnp.dot(left, right, preferred_element_type=WIDE)


def product_left(left, right):
    return lax.dot_general(left, right, (((0,), (0,)), ((), ())), preferred_element_type=WIDE)


def product_right(left, right):
    return lax.dot_general(left, right, (((1,), (1,)), ((), ())), preferred_element_type=WIDE)


def normalize(tensor):
    centre = tensor - jnp.mean(tensor, axis=-1, keepdims=True)
    inv_scale = lax.rsqrt(jnp.mean(centre * centre, axis=-1, keepdims=True) + EPS_NORM)
    return (centre * inv_scale, inv_scale)


def normal_back(grad_unit, unit_rows, inv_scale):
    centred = grad_unit - jnp.mean(grad_unit, axis=-1, keepdims=True)
    return inv_scale * (
        centred - unit_rows * jnp.mean(grad_unit * unit_rows, axis=-1, keepdims=True)
    )


def silu_parts(tensor):
    half = 0.5 * tensor
    return half, jnp.tanh(half)


def silu(tensor):
    half, bend = silu_parts(tensor)
    return half * (1.0 + bend)


def fold_rows(store, base, rows, tensor):
    parts = tensor.shape[1] // LANES
    for part in range(parts):
        store[pl.ds(base * parts + part, rows, stride=parts), :] = tensor[
            :, part * LANES : (part + 1) * LANES
        ]


def unfold_rows(store, base, rows, parts):
    return jnp.concatenate(
        [store[pl.ds(base * parts + part, rows, stride=parts), :] for part in range(parts)],
        axis=1,
    )


def forward_kernel(parts, has_next, *refs):
    if has_next:
        (slots, before, middle, after, low, wide, weights, gains, head) = refs[:9]
        (sent, update, update_low, kept, aggregate) = refs[9:14]
        window, picked, hidden, message = refs[14:]
    else:
        (slots, before, middle, after, low, wide, weights, gains) = refs[:8]
        (update_low, kept, aggregate) = refs[8:11]
        window, picked, hidden, message = refs[11:]
    step = pl.program_id(0)
    block_rows = before.shape[0]
    rows, width = low.shape
    fan = kept.shape[0]

    @pl.when(step == 0)
    def _():
        for index, block in enumerate((before, middle, after)):
            fold_rows(window, index * block_rows, block_rows, block[...].astype(WIDE))

    for k in range(fan):

        def pick(trip, carry):
            for lane in range(UNROLL):
                row = trip * UNROLL + lane
                slot = slots[k * block_rows + step * rows + row]
                picked[pl.ds(pl.multiple_of((k * rows + row) * parts, parts), parts), :] = window[
                    pl.ds(pl.multiple_of(slot * parts, parts), parts), :
                ]
            return carry

        lax.fori_loop(0, rows // UNROLL, pick, 0)
    target_low = low[...]
    own_term = product(target_low, weights[1])
    for k in range(fan):
        sender = unfold_rows(picked, k * rows, rows, parts)
        kept[k] = sender.astype(LOW)
        hidden[k * rows : (k + 1) * rows, :] = silu(sender + own_term).astype(LOW)
    message[...] = product(hidden[...], weights[2])
    total = normalize(message[0:rows, :])[0]
    for k in range(1, fan):
        total = total + normalize(message[k * rows : (k + 1) * rows, :])[0]
    total_low = (total * gains[0:1, :]).astype(LOW)
    aggregate[...] = total_low
    node_mix = product(target_low, weights[3]) + product(total_low, weights[4])
    node_out = product(silu(node_mix).astype(LOW), weights[5])
    updated = wide[...].astype(WIDE) + normalize(node_out)[0] * gains[1:2, :]
    updated_low = updated.astype(LOW)
    update_low[...] = updated_low
    if has_next:
        update[...] = updated
        sent[...] = product(updated_low, head[0]).astype(LOW)


def in_hbm(shape, dtype):
    return pltpu.MemorySpace.HBM(shape, dtype)


def on_chip(shape, dtype):
    return pltpu.MemorySpace.VMEM(shape, dtype)


def kept_on_chip(array):
    return pltpu.with_memory_space_constraint(array, pltpu.MemorySpace.VMEM)


def pinned(array):
    return pltpu.with_memory_space_constraint(array, pltpu.MemorySpace.HBM)


def whole(shape):
    zeros = (0,) * len(shape)
    return pl.BlockSpec(shape, lambda step: zeros, pipeline_mode=pl.Buffered(1))


def matrix_spec(first, count, width):
    return pl.BlockSpec(
        (count, width, width), lambda step: (first // count, 0, 0), pipeline_mode=pl.Buffered(1)
    )


def tiled(rows, width):
    return pl.BlockSpec((rows, width), lambda step: (step, 0))


def fanned(fan, rows, width):
    return pl.BlockSpec((fan, rows, width), lambda step: (0, step, 0))


def forward_layer(slots, blocks, target_low, target, weights, next_weights, gains, halo_place):
    block_rows, width = target_low.shape
    fan = slots.shape[0] // block_rows
    parts = width // LANES
    rows = FORWARD_ROWS
    has_next = next_weights is not None
    shape = functools.partial(in_hbm, (block_rows, width))
    fan_shape = functools.partial(in_hbm, (fan, block_rows, width))
    tile = tiled(rows, width)
    in_specs = [pl.BlockSpec(memory_space=pltpu.SMEM)]
    in_specs += [whole((block_rows, width))] * 3 + [tile, tile]
    in_specs += [matrix_spec(weights[1], 6, width), whole(gains.shape)]
    out_specs = [tile, fanned(fan, rows, width), tile]
    out_shape = [shape(LOW), fan_shape(LOW), shape(LOW)]
    operands = [slots, *blocks, target_low, target, weights[0], gains]
    if has_next:
        in_specs += [matrix_spec(next_weights[1], 1, width)]
        operands += [next_weights[0]]
        out_specs = [tile, tile] + out_specs
        out_shape = [shape(LOW), shape(WIDE)] + out_shape
    return pl.pallas_call(
        functools.partial(forward_kernel, parts, has_next),
        grid=(block_rows // rows,),
        in_specs=in_specs,
        out_specs=out_specs,
        out_shape=out_shape,
        scratch_shapes=[
            pltpu.VMEM((3 * block_rows * parts, LANES), WIDE),
            pltpu.VMEM((fan * rows * parts, LANES), WIDE),
            pltpu.VMEM((fan * rows, width), LOW),
            pltpu.VMEM((fan * rows, width), WIDE),
        ],
        compiler_params=pltpu.CompilerParams(vmem_limit_bytes=54 << 20),
        cost_estimate=pl.CostEstimate(
            flops=2 * (fan + 5) * block_rows * width * width,
            transcendentals=(fan + 1) * block_rows * width,
            bytes_accessed=24 * block_rows * width * 2,
        ),
        name="forward_layer",
    )(
        operands[0],
        halo_place(operands[1]),
        pinned(operands[2]),
        halo_place(operands[3]),
        *map(pinned, operands[4:]),
    )


def backward_kernel(parts, mode, *refs):
    refs = list(refs)
    slots = refs.pop(0)
    if mode != "first":
        returned = [refs.pop(0) for _ in range(3)]
        head = refs.pop(0)
    if mode != "second":
        grad_part = refs.pop(0)
    low, kept, aggregate, weights, gains = refs[:5]
    refs = refs[5:]
    if mode != "first":
        sent_grad = refs.pop(0)
        grad_full = refs.pop(0)
    slot_grads = refs[:3]
    (grad_gains, grad_message, edge_hidden, grad_mix, grad_out, grad_own, hidden) = refs[3:10]
    sum_even, sum_odd, spread, stage = refs[10:]
    step = pl.program_id(0)
    rows, width = low.shape
    fan = kept.shape[0]
    block_rows = slot_grads[0].shape[0]

    @pl.when(step == 0)
    def _():
        sum_even[...] = jnp.zeros_like(sum_even)
        sum_odd[...] = jnp.zeros_like(sum_odd)
        grad_gains[...] = jnp.zeros_like(grad_gains)

    if mode == "first":
        grad_new = grad_part[...]
    else:
        sent_low = (
            returned[0][...].astype(WIDE)
            + returned[1][...].astype(WIDE)
            + returned[2][...].astype(WIDE)
        ).astype(LOW)
        sent_grad[...] = sent_low
        grad_new = product_right(sent_low, head[0])
        if mode == "third":
            grad_new = grad_part[...] + grad_new
        grad_full[...] = grad_new
    target_low = low[...]
    own_term = product(target_low, weights[1])
    node_mix = product(target_low, weights[3]) + product(aggregate[...], weights[4])
    for k in range(fan):
        edge_hidden[k] = silu(kept[k].astype(WIDE) + own_term).astype(LOW)
    stage[...] = product(edge_hidden[...].reshape(fan * rows, width), weights[2])
    half, bend = silu_parts(node_mix)
    node_hidden = (half * (1.0 + bend)).astype(LOW)
    hidden[...] = node_hidden
    out_unit, out_scale = normalize(product(node_hidden, weights[5]))
    gain_two = jnp.sum(grad_new * out_unit, axis=0, keepdims=True)
    out_low = normal_back(grad_new * gains[1:2, :], out_unit, out_scale).astype(LOW)
    grad_out[...] = out_low
    mix_low = (
        product_right(out_low, weights[5]) * ((0.5 + 0.5 * bend) * (1.0 + half * (1.0 - bend)))
    ).astype(LOW)
    grad_mix[...] = mix_low
    grad_sum = product_right(mix_low, weights[4])
    grad_unit = grad_sum * gains[0:1, :]
    unit_total = None
    for k in range(fan):
        unit_rows, inv_scale = normalize(stage[k * rows : (k + 1) * rows, :])
        unit_total = unit_rows if k == 0 else unit_total + unit_rows
        grad_message[k] = normal_back(grad_unit, unit_rows, inv_scale).astype(LOW)
    stage[...] = product_right(grad_message[...].reshape(fan * rows, width), weights[2])
    own_total = None
    for k in range(fan):
        half, bend = silu_parts(kept[k].astype(WIDE) + own_term)
        grad_pre = stage[k * rows : (k + 1) * rows, :] * (
            (0.5 + 0.5 * bend) * (1.0 + half * (1.0 - bend))
        )
        own_total = grad_pre if k == 0 else own_total + grad_pre
        fold_rows(spread, k * rows, rows, grad_pre)
    gain_one = jnp.sum(grad_sum * unit_total, axis=0, keepdims=True)
    grad_gains[...] += jnp.concatenate([gain_one, gain_two], axis=0)
    grad_own[...] = own_total.astype(LOW)

    for k in range(fan):

        def add(trip, carry):
            for lane in range(UNROLL // 2):
                places, values = [], []
                for store in (sum_even, sum_odd):
                    row = (trip * (UNROLL // 2) + lane) * 2 + len(places)
                    slot = slots[k * block_rows + step * rows + row]
                    place = pl.ds(pl.multiple_of(slot * parts, parts), parts)
                    value = spread[pl.ds(pl.multiple_of((k * rows + row) * parts, parts), parts), :]
                    places.append(place)
                    values.append(store[place, :] + value)
                sum_even[places[0], :] = values[0]
                sum_odd[places[1], :] = values[1]
            return carry

        lax.fori_loop(0, rows // UNROLL, add, 0)

    @pl.when(step == pl.num_programs(0) - 1)
    def _():
        for index in range(3):
            base = index * block_rows
            slot_grads[index][...] = (
                unfold_rows(sum_even, base, block_rows, parts)
                + unfold_rows(sum_odd, base, block_rows, parts)
            ).astype(LOW)


def backward_layer(slots, above, grad_part, stored, weights, gains, first_layer):
    target_low, kept, aggregate = stored
    block_rows, width = target_low.shape
    fan = kept.shape[0]
    parts = width // LANES
    rows = BACKWARD_ROWS
    tile = tiled(rows, width)
    fan_tile = fanned(fan, rows, width)
    in_specs = [pl.BlockSpec(memory_space=pltpu.SMEM)]
    operands = [slots]
    out_specs, out_shape = [], []
    shape = functools.partial(on_chip, (block_rows, width))
    fan_shape = functools.partial(on_chip, (fan, block_rows, width))
    mode = "first" if above is None else ("second" if grad_part is None else "third")
    if above is not None:
        from_before, slot_grad, from_after, head = above
        in_specs += [
            tile,
            tile,
            tile,
            matrix_spec(head[1], 1, width),
        ]
        operands += [from_before, slot_grad, from_after, head[0]]
        out_specs += [tile, tile]
        out_shape += [shape(LOW), shape(WIDE)]
    if grad_part is not None:
        in_specs += [tile]
        operands += [grad_part]
    in_specs += [tile, fan_tile, tile]
    in_specs += [matrix_spec(weights[1], 6, width), whole(gains.shape)]
    operands += [target_low, kept, aggregate, weights[0], gains]
    out_specs += [
        whole((block_rows, width)),
        whole((block_rows, width)),
        whole((block_rows, width)),
        whole((2, width)),
        fan_tile,
        fan_tile,
        tile,
        tile,
        tile,
        tile,
    ]
    out_shape += [
        in_hbm((block_rows, width), LOW),
        in_hbm((block_rows, width), LOW),
        in_hbm((block_rows, width), LOW),
        jax.ShapeDtypeStruct((2, width), WIDE),
        fan_shape(LOW),
        in_hbm((fan, block_rows, width), LOW) if first_layer else fan_shape(LOW),
        shape(LOW),
        shape(LOW),
        shape(LOW),
        shape(LOW),
    ]
    results = pl.pallas_call(
        functools.partial(backward_kernel, parts, mode),
        grid=(block_rows // rows,),
        in_specs=in_specs,
        out_specs=out_specs,
        out_shape=out_shape,
        scratch_shapes=[
            pltpu.VMEM((3 * block_rows * parts, LANES), WIDE),
            pltpu.VMEM((3 * block_rows * parts, LANES), WIDE),
            pltpu.VMEM((fan * rows * parts, LANES), WIDE),
            pltpu.VMEM((fan * rows, width), WIDE),
        ],
        compiler_params=pltpu.CompilerParams(vmem_limit_bytes=38 << 20),
        cost_estimate=pl.CostEstimate(
            flops=2 * (fan + 4) * block_rows * width * width,
            transcendentals=(fan + 1) * block_rows * width,
            bytes_accessed=24 * block_rows * width * 2,
        ),
        name="backward_layer",
    )(operands[0], *map(pinned, operands[1:]))
    if above is None:
        return (None, grad_part, *results)
    return tuple(results)


def deal(self_id, sums, outs):
    keep, send = outs
    share = keep.shape[1] // sums.shape[0]

    def move(node, carry):
        for core, out in enumerate((keep, send)):
            place = pl.multiple_of(((2 * node + core) ^ self_id[0]) * share, share)
            for index in range(sums.shape[0]):
                out[node, index * share : (index + 1) * share, :] = sums[
                    index, pl.ds(place, share), :
                ].astype(out.dtype)
        return carry

    lax.fori_loop(0, keep.shape[0], move, 0)


def weight_kernel(has_above, needs_target, direct, *refs):
    refs = list(refs)
    if direct:
        self_id = refs.pop(0)
    if has_above:
        source, sent_grad = refs[:2]
        refs = refs[2:]
    else:
        extra = refs.pop(0)
    low, aggregate, edge_hidden, grad_message, grad_mix, grad_out, grad_own, hidden = refs[:8]
    refs = refs[8:]
    if needs_target:
        grad_new, weights = refs[:2]
        grad_part = refs[2]
        refs = refs[3:]
    outs, sums = (refs[:2], refs[2]) if direct else (None, refs[0])
    step = pl.program_id(0)
    fan = edge_hidden.shape[0]

    @pl.when(step == 0)
    def _():
        sums[...] = jnp.zeros_like(sums)
        if not has_above:
            sums[0] = extra[...]

    target_low = low[...]
    mix_low = grad_mix[...]
    own_low = grad_own[...]
    if has_above:
        sums[0] += product_left(source[...], sent_grad[...])
    sums[1] += product_left(target_low, own_low)
    for k in range(fan):
        sums[2] += product_left(edge_hidden[k], grad_message[k])
    sums[3] += product_left(target_low, mix_low)
    sums[4] += product_left(aggregate[...], mix_low)
    sums[5] += product_left(hidden[...], grad_out[...])
    if needs_target:
        grad_part[...] = (
            grad_new[...] + product_right(own_low, weights[1]) + product_right(mix_low, weights[3])
        )
    if direct:

        @pl.when(step == pl.num_programs(0) - 1)
        def _():
            deal(self_id, sums, outs)


def share_outputs(count, width, device_count):
    shape = (device_count // 2, count * (width // device_count), width)
    return (
        [whole(shape)] * 2,
        [on_chip(shape, WIDE), on_chip(shape, SEND)],
    )


def weight_layer(self_id, device_count, above, extra, low, aggregate, back, grad_new, weights):
    block_rows, width = low.shape
    rows = WEIGHT_ROWS
    fan = back[0].shape[0]
    tile = tiled(rows, width)
    fan_tile = fanned(fan, rows, width)
    in_specs, operands = [], []
    direct = self_id is not None
    if direct:
        in_specs += [pl.BlockSpec(memory_space=pltpu.SMEM)]
        operands += [self_id]
    if above is not None:
        in_specs += [tile, tile]
        operands += [pinned(above[0]), kept_on_chip(above[1])]
    else:
        in_specs += [whole((width, width))]
        operands += [extra]
    in_specs += [tile, tile, fan_tile, fan_tile, tile, tile, tile, tile]
    place = pinned if grad_new is None else kept_on_chip
    operands += [pinned(low), pinned(aggregate), place(back[0]), *map(kept_on_chip, back[1:])]
    out_specs, out_shape, scratch = [], [], []
    if grad_new is not None:
        in_specs += [tile, matrix_spec(weights[1], 6, width)]
        operands += [kept_on_chip(grad_new), pinned(weights[0])]
        out_specs += [tile]
        out_shape += [in_hbm((block_rows, width), WIDE)]
    if direct:
        specs, shapes = share_outputs(6, width, device_count)
        out_specs += specs
        out_shape += shapes
        scratch = [pltpu.VMEM((6, width, width), WIDE)]
    else:
        out_specs += [whole((6, width, width))]
        out_shape += [jax.ShapeDtypeStruct((6, width, width), WIDE)]
    results = pl.pallas_call(
        functools.partial(weight_kernel, above is not None, grad_new is not None, direct),
        grid=(block_rows // rows,),
        in_specs=in_specs,
        out_specs=out_specs,
        out_shape=out_shape,
        scratch_shapes=scratch,
        compiler_params=pltpu.CompilerParams(vmem_limit_bytes=30 << 20),
        cost_estimate=pl.CostEstimate(
            flops=2 * (fan + 6) * block_rows * width * width,
            transcendentals=0,
            bytes_accessed=24 * block_rows * width,
        ),
        name="weight_layer",
    )(*operands)
    if grad_new is None:
        return (None, results)
    return (results[0], results[1:])


def place_rows(self_id, pieces, targets, width):
    share = width // (pieces[0].shape[0] * len(pieces))
    for index, piece in enumerate(pieces):
        base = (index // 2) + (index % 2) * 4

        def move(digit, carry, piece=piece, base=base):
            relative = (digit // 2) * 8 + (digit % 2) * 2 + base
            place = pl.multiple_of((relative ^ self_id[0]) * share, share)
            for j, target in enumerate(targets):
                target[pl.ds(place, share), :] = piece[digit, j * share : (j + 1) * share, :]
            return carry

        lax.fori_loop(0, piece.shape[0], move, 0)


def assemble_kernel(pieces_count, *refs):
    matrices = refs[-1]
    targets = [matrices.at[j] for j in range(matrices.shape[0])]
    place_rows(refs[0], refs[1 : 1 + pieces_count], targets, matrices.shape[1])


def assemble(self_id, pieces):
    digits, rows, width = pieces[0].shape
    count = rows * digits * len(pieces) // width
    return pl.pallas_call(
        functools.partial(assemble_kernel, len(pieces)),
        grid=(1,),
        in_specs=[pl.BlockSpec(memory_space=pltpu.SMEM)] + [whole(piece.shape) for piece in pieces],
        out_specs=whole((count, width, width)),
        out_shape=in_hbm((count, width, width), LOW),
        compiler_params=pltpu.CompilerParams(vmem_limit_bytes=20 << 20),
        cost_estimate=pl.CostEstimate(
            flops=0, transcendentals=0, bytes_accessed=4 * count * width * width
        ),
        name="assemble",
    )(self_id, *pieces)


def join_kernel(*refs):
    start = 0
    for part in refs[:-1]:
        refs[-1][start : start + part.shape[0]] = part[...]
        start += part.shape[0]


def join(parts):
    shape = (sum(part.shape[0] for part in parts), *parts[0].shape[1:])
    return pl.pallas_call(
        join_kernel,
        grid=(1,),
        in_specs=[whole(part.shape) for part in parts],
        out_specs=whole(shape),
        out_shape=on_chip(shape, parts[0].dtype),
        compiler_params=pltpu.CompilerParams(vmem_limit_bytes=8 << 20),
        cost_estimate=pl.CostEstimate(
            flops=0, transcendentals=0, bytes_accessed=4 * shape[0] * shape[1] * shape[2]
        ),
        name="join",
    )(*map(kept_on_chip, parts))


def embed_kernel(pieces_count, *refs):
    self_id = refs[0]
    pieces = refs[1 : 1 + pieces_count]
    before, middle, after = refs[1 + pieces_count : 4 + pieces_count]
    weights, latent, latent_low, sent_before, sent_middle, sent_after, table = refs[
        4 + pieces_count :
    ]

    @pl.when(pl.program_id(0) == 0)
    def _():
        targets = [weights.at[j] for j in range(weights.shape[0])] + [table]
        place_rows(self_id, pieces, targets, weights.shape[1])

    for block, sent in ((before, sent_before), (middle, sent_middle), (after, sent_after)):
        wide = product_right(block[...], table[...])
        low = wide.astype(LOW)
        sent[...] = product(low, weights[0]).astype(LOW)
        if block is middle:
            latent[...] = wide
            latent_low[...] = low


def embed(self_id, pieces, blocks):
    block_rows, width = blocks[1].shape
    rows = WEIGHT_ROWS
    tile = tiled(rows, width)
    return pl.pallas_call(
        functools.partial(embed_kernel, len(pieces)),
        grid=(block_rows // rows,),
        in_specs=[pl.BlockSpec(memory_space=pltpu.SMEM)]
        + [whole(piece.shape) for piece in pieces]
        + [tile] * 3,
        out_specs=[whole((7, width, width))] + [tile] * 5,
        out_shape=[
            in_hbm((7, width, width), LOW),
            in_hbm((block_rows, width), WIDE),
            in_hbm((block_rows, width), LOW),
            in_hbm((block_rows, width), LOW),
            in_hbm((block_rows, width), LOW),
            in_hbm((block_rows, width), LOW),
        ],
        scratch_shapes=[pltpu.VMEM((width, width), LOW)],
        compiler_params=pltpu.CompilerParams(vmem_limit_bytes=50 << 20),
        cost_estimate=pl.CostEstimate(
            flops=12 * block_rows * width * width,
            transcendentals=0,
            bytes_accessed=24 * block_rows * width,
        ),
        name="embed",
    )(self_id, *pieces, *blocks)


def tail_kernel(self_id, loss, before, middle, after, latent_low, inputs, grad_grid, head, *refs):
    gains = refs[:-3]
    keep, send, sums = refs[-3:]
    step = pl.program_id(0)
    rows, width = inputs.shape
    share = width // (2 * keep.shape[0])
    gain_count = 2 * len(gains)

    @pl.when(step == 0)
    def _():
        sums[...] = jnp.zeros_like(sums)

    sent_low = (
        before[...].astype(WIDE)
        + middle[...].astype(WIDE)
        + after[...].astype(WIDE)
    ).astype(LOW)
    grad_low = (grad_grid[...] + product_right(sent_low, head[0])).astype(LOW)
    sums[0] += product_left(latent_low[...], sent_low)
    sums[1] += product_left(grad_low, inputs[...])

    @pl.when(step == pl.num_programs(0) - 1)
    def _():
        size = sums.shape[0] * share
        main = [out.at[:, 0:size, :] for out in (keep, send)]
        deal(self_id, sums, main)
        gain_rows = jnp.concatenate([gain[...] for gain in gains], axis=0)
        lane = lax.broadcasted_iota(jnp.int32, gain_rows.shape, 1)

        def move(node, carry):
            for core, out in enumerate((keep, send)):
                device = (2 * node + core) ^ self_id[0]
                turned = pltpu.roll(gain_rows, width - device * share, axis=1)
                out[node, size : size + gain_count, :] = jnp.where(
                    lane == share, loss[0], turned
                ).astype(out.dtype)
            return carry

        lax.fori_loop(0, keep.shape[0], move, 0)


def tail_layer(
    self_id, device_count, loss, from_before, slot_grad, from_after, latent_low, inputs, grad_grid, head, gains
):
    block_rows, width = inputs.shape
    rows = WEIGHT_ROWS
    tile = tiled(rows, width)
    gain_count = 2 * len(gains)
    shape = (device_count // 2, 2 * (width // device_count) + gain_count, width)
    return pl.pallas_call(
        tail_kernel,
        grid=(block_rows // rows,),
        in_specs=[pl.BlockSpec(memory_space=pltpu.SMEM)] * 2
        + [tile] * 6
        + [matrix_spec(head[1], 1, width)]
        + [whole((2, width))] * len(gains),
        out_specs=[whole(shape)] * 2,
        out_shape=[on_chip(shape, WIDE), on_chip(shape, SEND)],
        scratch_shapes=[pltpu.VMEM((2, width, width), WIDE)],
        compiler_params=pltpu.CompilerParams(vmem_limit_bytes=56 << 20),
        cost_estimate=pl.CostEstimate(
            flops=6 * block_rows * width * width,
            transcendentals=0,
            bytes_accessed=24 * block_rows * width,
        ),
        name="tail_layer",
    )(
        self_id,
        loss,
        *map(pinned, (from_before, slot_grad, from_after, latent_low, inputs, grad_grid, head[0])),
        *gains,
    )


def combine_kernel(counts, *refs):
    outs = refs[sum(counts) :]
    first, base = 0, 0
    for count in counts:
        arrived = refs[first : first + count]
        rows = arrived[0].shape[2]
        for digit, out in enumerate(outs):
            total = arrived[0][0, digit].astype(WIDE)
            for part in arrived[1:]:
                total = total + part[0, digit].astype(WIDE)
            out[0, base : base + rows, :] = total.astype(out.dtype)
        first, base = first + count, base + rows


def combine(radix, *groups):
    width = groups[0][0].shape[2]
    rest = groups[0][0].shape[0] // radix
    arrived, specs = [], []
    for group in groups:
        rows = group[0].shape[1]
        arrived += [part.reshape(rest, radix, rows, width) for part in group]
        specs += [pl.BlockSpec((1, radix, rows, width), lambda step: (step, 0, 0, 0))] * len(group)
    rows = sum(group[0].shape[1] for group in groups)
    shape = (rest, rows, width)
    return pl.pallas_call(
        functools.partial(combine_kernel, [len(group) for group in groups]),
        grid=(rest,),
        in_specs=specs,
        out_specs=[pl.BlockSpec((1, rows, width), lambda step: (step, 0, 0))] * radix,
        out_shape=[on_chip(shape, WIDE)] + [on_chip(shape, SEND)] * (radix - 1),
        compiler_params=pltpu.CompilerParams(vmem_limit_bytes=20 << 20),
        cost_estimate=pl.CostEstimate(
            flops=rest * radix * rows * width * 4,
            transcendentals=0,
            bytes_accessed=16 * rest * radix * rows * width,
        ),
        name="combine",
    )(*map(kept_on_chip, arrived))


def swap(cells, count, mask):
    return lax.ppermute(cells, AXES, [(i, i ^ mask) for i in range(count)])


def spread_high(rows, count):
    return [rows] + [swap(rows, count, digit * 8) for digit in range(1, count // 8)]


def home(block, direct):
    return block ^ (((block >> 2) & 1) << 1) if direct else block


def bring(cells, count, step, direct):
    return lax.ppermute(cells, AXES, [(i, home((i + step) % count, direct)) for i in range(count)])


def shift(cells, count, step, direct):
    pairs = [(home(i, direct), home((i + step) % count, direct)) for i in range(count)]
    return lax.ppermute(cells, AXES, pairs)


def fan_out(pieces, count, unit):
    return [pieces[0]] + [
        swap(pieces[digit], count, digit * unit) for digit in range(1, len(pieces))
    ]


def together(first, second):
    joined = lax.optimization_barrier((tuple(first), tuple(second)))
    return list(joined[0]), list(joined[1])


def add_up(arrived):
    total = arrived[0][0]
    for part in arrived[1:]:
        total = total + part[0].astype(WIDE)
    return total


def adamw_update(weight, moment_one, moment_two, gradient, step_value, decay_rate):
    new_one = BETA_ONE * moment_one + (1.0 - BETA_ONE) * gradient
    new_two = BETA_TWO * moment_two + (1.0 - BETA_TWO) * gradient * gradient
    correct_one = 1.0 - jnp.power(BETA_ONE, step_value)
    correct_two = 1.0 - jnp.power(BETA_TWO, step_value)
    direction = new_one / correct_one / (jnp.sqrt(new_two / correct_two) + ADAM_EPS)
    return (new_one, new_two, weight - LEARN_RATE * (direction + decay_rate * weight))


def shards(
    grid_inputs,
    mesh_static,
    targets,
    area_weight,
    valid_rows,
    encoder_lists,
    mesh_lists,
    decoder_lists,
    step_count,
    w_in,
    moment_in,
    square_in,
    w_layers,
    moment_layers,
    square_layers,
    norm_gains,
    moment_gains,
    square_gains,
    w_out,
    moment_out,
    square_out,
):
    row_count = grid_inputs.shape[0]
    layer_total = w_layers.shape[0]
    device_count = lax.axis_size(AXES)
    width = mesh_static.shape[1]
    share = w_layers.shape[2]
    channels, outputs = w_in.shape[0], w_out.shape[1]
    direct = share == 16 and device_count % 8 == 0 and device_count & (device_count - 1) == 0
    slot_lists = [encoder_lists.T.reshape(-1), mesh_lists.T.reshape(-1), decoder_lists.T.reshape(-1)]
    local_rows = jnp.arange(row_count, dtype=jnp.int32)
    weight_rows = area_weight * (local_rows < valid_rows[0]).astype(WIDE)
    if direct:
        self_id = lax.axis_index(AXES).astype(jnp.int32)
        order = jnp.arange(device_count, dtype=jnp.int32) ^ self_id
        self_id = self_id.reshape(1)
        inputs = jnp.pad(grid_inputs, ((0, 0), (0, width - channels)))
        flat_gains = norm_gains.astype(LOW).reshape(1, -1)
        packed = jnp.concatenate(
            [
                w_layers[0].astype(LOW).reshape(-1, width),
                w_layers[1, 0].astype(LOW),
                jnp.pad(w_in.astype(LOW).T, ((0, 0), (0, width - channels))),
                jnp.pad(flat_gains, ((0, 7), (0, width - flat_gains.shape[1]))),
            ],
            axis=0,
        )
        second = jnp.concatenate([w_layers[2, :1], w_layers[1, 1:]], axis=0)
        second = second.astype(LOW).reshape(-1, width)
        rest = jnp.concatenate(
            [
                jnp.pad(w_out.astype(LOW), ((0, 0), (0, width - outputs)))[None],
                w_layers[2, 1:].astype(LOW),
                w_layers[3:].astype(LOW).reshape(-1, share, width),
            ],
            axis=0,
        )
        lists = jnp.concatenate(slot_lists).reshape(-1, LANES)
        goals = jnp.concatenate([targets, weight_rows[:, None]], axis=1)
        goals = jnp.pad(goals, ((0, 0), (0, -goals.shape[1] % LANES)))
        barrier = lax.optimization_barrier
        pairs = ((packed, swap(packed, device_count, 2)), (second, swap(second, device_count, 2)))
        lists = bring(lists, device_count, 0, direct)
        pairs, lists, inputs, mesh_static = barrier((pairs, lists, inputs, mesh_static))
        own = bring(inputs, device_count, 0, direct)
        pair, second_pair = (jnp.stack(rows) for rows in pairs)
        column, own, mesh_static, second_pair = barrier(
            (spread_high(pair, device_count), own, mesh_static, second_pair)
        )
        sides = [shift(own, device_count, 1, direct), shift(own, device_count, -1, direct)]
        mesh_rows = bring(mesh_static, device_count, 0, direct)
        second_column = spread_high(second_pair, device_count)
        plane = join(column)
        second_last = second_column.pop()
        near, sides, mesh_rows, second_column, rest, goals = barrier(
            ((plane, swap(plane, device_count, 4)), sides, mesh_rows, second_column, rest, goals)
        )
        sides = [sides[0], own, sides[1]]
        pieces = [*near, *(swap(piece, device_count, 1) for piece in near)]
        rest = lax.all_gather(rest, AXES, axis=1, tiled=True)
        inputs = sides[1]
        lists = lists.reshape(len(slot_lists), -1)
        slot_lists = [lists[index] for index in range(len(slot_lists))]
        first, grid_latent, grid_start, *blocks = embed(
            self_id, pieces, sides
        )
        first, goals, second_last = barrier((first, goals, second_last))
        second_plane = join([*second_column, second_last])
        second_near = (second_plane, swap(second_plane, device_count, 4))
        goals = bring(goals, device_count, 0, direct)
        targets, weight_rows = goals[:, :outputs], goals[:, outputs]
        weights = [(first, 0), None]
        weights += [(rest, 6 * layer_id) for layer_id in range(layer_total - 2)]
        heads = [(first, 0), (first, 6), None]
        heads += weights[3:]
        table_out = rest[0, :, :outputs]
        gain_rows = jnp.stack(pieces)[:, :, packed.shape[0] - 8, : flat_gains.shape[1]]
        gain_rows = gain_rows.reshape(2, 2, device_count // 8, 2, -1).transpose(2, 1, 3, 0, 4)
        gain_rows = gain_rows.reshape(device_count, -1)[order]
        gains = gain_rows.reshape(device_count, layer_total, 2, share).transpose(1, 2, 0, 3)
        gains = gains.reshape(layer_total, 2, width).astype(WIDE)
    else:
        self_id = None
        table_in = lax.all_gather(w_in.astype(LOW), AXES, axis=1, tiled=True)
        table_out = lax.all_gather(w_out.astype(LOW), AXES, axis=0, tiled=True)
        matrices = lax.all_gather(w_layers.astype(LOW), AXES, axis=2, tiled=True)
        matrices = matrices.reshape(-1, width, width)
        weights = [(matrices, 6 * layer_id) for layer_id in range(layer_total)]
        heads = weights
        gains = lax.all_gather(norm_gains.astype(LOW), AXES, axis=2, tiled=True).astype(WIDE)
        grid_latent = product(grid_inputs, table_in)
        grid_start = grid_latent.astype(LOW)
        sent = product(grid_start, matrices[0]).astype(LOW)
        blocks = (shift(sent, device_count, 1, direct), sent, shift(sent, device_count, -1, direct))
        mesh_rows = mesh_static
    slot_lists = [slot_lists[0]] + [slot_lists[1]] * (layer_total - 2) + [slot_lists[2]]
    target, target_low = mesh_rows, mesh_rows
    stored_list = []
    for layer_id in range(layer_total):
        if direct and layer_id == 1:
            second_near, target = lax.optimization_barrier((second_near, target))
            second_pieces = [*second_near, *(swap(piece, device_count, 1) for piece in second_near)]
            second = assemble(self_id, second_pieces)
            weights[1] = heads[2] = (second, 0)
        last_layer = layer_id == layer_total - 1
        if last_layer:
            source_low = target_low
            target, target_low = grid_latent, grid_start
        else:
            source_low = grid_start if layer_id == 0 else target_low
        results = forward_layer(
            slot_lists[layer_id],
            blocks,
            target_low,
            target,
            weights[layer_id],
            None if last_layer else heads[layer_id + 1],
            gains[layer_id],
            kept_on_chip if layer_id > 0 else pinned,
        )
        if last_layer:
            grid_low, kept, aggregate = results
        else:
            sent, updated, updated_low, kept, aggregate = results
            blocks = (shift(sent, device_count, 1, direct), sent, shift(sent, device_count, -1, direct))
        stored_list.append((source_low, (target_low, kept, aggregate), aggregate))
        if not last_layer:
            target, target_low = updated, updated_low
    prediction = product(grid_low, table_out)
    error_rows = prediction - targets
    loss_scale = 1.0 / (row_count * device_count * prediction.shape[1])
    loss_local = jnp.sum(weight_rows[:, None] * error_rows * error_rows) * loss_scale
    grad_pred = (2.0 * loss_scale * weight_rows[:, None] * error_rows).astype(LOW)
    grad_table_out = product_left(grid_low, grad_pred)
    grad_part = product_right(grad_pred, table_out)
    extra = jnp.pad(grad_table_out, ((0, 0), (0, width - outputs)))
    grad_grid = None
    above, above_source = None, None
    layer_grads = [None] * layer_total
    gain_grads = [None] * layer_total
    in_plane = []
    for layer_id in reversed(range(layer_total)):
        source_low, stored, aggregate = stored_list[layer_id]
        sent_grad, grad_new, *slot_grads, grad_gain, grad_message, edge_hidden, b0, b1, b2, b3 = backward_layer(
            slot_lists[layer_id], above, grad_part, stored, weights[layer_id], gains[layer_id], layer_id == 0
        )
        in_slice = []
        if in_plane:
            arrived, slot_grads = together(in_plane, slot_grads)
            in_slice = fan_out(combine(device_count // 8, arrived), device_count, 8)
        from_before = shift(slot_grads[2], device_count, 1, direct)
        from_after = shift(slot_grads[0], device_count, -1, direct)
        back = [edge_hidden, grad_message, b0, b1, b2, b3]
        grad_part, sums = weight_layer(
            self_id,
            device_count,
            None if above is None else (above_source, sent_grad),
            extra,
            stored[0],
            aggregate,
            back,
            None if layer_id == 0 else grad_new,
            weights[layer_id],
        )
        gain_grads[layer_id] = grad_gain
        if direct:
            halo, arrived = together([from_before, from_after], [*sums, *in_slice])
            keep, send = arrived[:2]
            if in_slice:
                layer_grads[layer_id + 1] = add_up(arrived[2:]).reshape(6, share, width)
            other = swap(send, device_count, 1)
            near = list(combine(4, [keep, other]))
            halo, near = together(halo, near)
            in_plane = fan_out(near, device_count, 2)
            from_before, from_after = halo
        else:
            layer_grads[layer_id] = sums[0]
        if layer_id == layer_total - 1:
            grad_grid, grad_part = grad_part, None
        above = (from_before, slot_grads[1], from_after, heads[layer_id])
        above_source = source_low
    if direct:
        sums = tail_layer(
            self_id,
            device_count,
            loss_local.reshape(1),
            from_before,
            slot_grads[1],
            from_after,
            grid_start,
            inputs,
            grad_grid,
            heads[0],
            gain_grads,
        )
        early, sums = together(in_plane[1:3], sums)
        in_plane = [in_plane[0], *early, in_plane[3]]
        keep, send = sums
        last_plane = combine(4, [keep, swap(send, device_count, 1)])
        last_plane = fan_out(last_plane, device_count, 2)
        far = combine(device_count // 8, in_plane, last_plane)
        total = add_up(fan_out(far, device_count, 8))
        layer_grads[0] = total[: 6 * share].reshape(6, share, width)
        total = total[6 * share :]
        grad_zero = total[:share]
        grad_in = total[share : 2 * share, :channels].T
        grad_gain_all = total[2 * share :, :share].reshape(layer_total, 2, share)
        loss_value = total[2 * share, share]
        grad_out = layer_grads[-1][0, :, :outputs]
    else:
        loss_value = lax.psum(loss_local, AXES)
        sent_grad = (
            from_before.astype(WIDE) + slot_grads[1].astype(WIDE) + from_after.astype(WIDE)
        ).astype(LOW)
        grad_zero = product_left(above_source, sent_grad)
        grad_grid = grad_grid + product_right(sent_grad, matrices[0])
        grad_table_in = product_left(grid_inputs, grad_grid.astype(LOW))
        grad_in = lax.psum_scatter(grad_table_in, AXES, scatter_dimension=1, tiled=True)
        grad_out = lax.psum_scatter(grad_table_out, AXES, scatter_dimension=0, tiled=True)
        grad_gain_all = lax.psum_scatter(
            jnp.stack(gain_grads), AXES, scatter_dimension=2, tiled=True
        )
    grad_layers = [grad_zero[None]]
    for layer_id in range(layer_total):
        grad_layers += [layer_grads[layer_id][1:]]
        if layer_id < layer_total - 1:
            grad_layers += [layer_grads[layer_id][0:1]]
    grad_layers = jnp.concatenate(grad_layers, axis=0)
    grad_layers = grad_layers.reshape(layer_total, 6, *grad_layers.shape[1:])
    if not direct:
        grad_layers = lax.psum_scatter(grad_layers, AXES, scatter_dimension=2, tiled=True)
    step_value = step_count[0].astype(WIDE)
    one_in, two_in, new_in = adamw_update(
        w_in, moment_in, square_in, grad_in, step_value, DECAY_RATE
    )
    one_layers, two_layers, new_layers = adamw_update(
        w_layers, moment_layers, square_layers, grad_layers, step_value, DECAY_RATE
    )
    one_gains, two_gains, new_gains = adamw_update(
        norm_gains, moment_gains, square_gains, grad_gain_all, step_value, 0.0
    )
    one_out, two_out, new_out = adamw_update(
        w_out, moment_out, square_out, grad_out, step_value, DECAY_RATE
    )
    return (
        loss_value,
        one_in,
        two_in,
        new_in,
        one_layers,
        two_layers,
        new_layers,
        one_gains,
        two_gains,
        new_gains,
        one_out,
        two_out,
        new_out,
    )


def solution(mesh):
    rows = P(AXES, None)
    layers = P(None, None, AXES, None)
    gains = P(None, None, AXES)
    columns = P(None, AXES)
    in_specs = (rows, rows, rows, P(AXES), P(AXES), rows, rows, rows, P())
    in_specs += (columns,) * 3 + (layers,) * 3 + (gains,) * 3 + (rows,) * 3
    out_specs = (P(),) + (columns,) * 3 + (layers,) * 3 + (gains,) * 3 + (rows,) * 3
    return jax.shard_map(shards, mesh=mesh, in_specs=in_specs, out_specs=out_specs, check_vma=False)
```

```python
import functools

import jax
import jax.numpy as jnp
from jax import lax
from jax.experimental import pallas as pl
from jax.experimental.pallas import tpu as pltpu
from jax.sharding import PartitionSpec as P

EPS_NORM = 1e-05
BETA_ONE = 0.5
BETA_TWO = 0.5
ADAM_EPS = 1e-08
LEARN_RATE = 0.04
DECAY_RATE = 0.1

AXES = ("nodes", "shard")
LANES = 128
FORWARD_ROWS = 256
BACKWARD_ROWS = 256
WEIGHT_ROWS = 256
UNROLL = 256
LOW = jnp.bfloat16
WIDE = jnp.float32
SEND = jnp.bfloat16


def product(left, right):
    return jnp.dot(left, right, preferred_element_type=WIDE)


def product_left(left, right):
    return lax.dot_general(left, right, (((0,), (0,)), ((), ())), preferred_element_type=WIDE)


def product_right(left, right):
    return lax.dot_general(left, right, (((1,), (1,)), ((), ())), preferred_element_type=WIDE)


def normalize(tensor):
    centre = tensor - jnp.mean(tensor, axis=-1, keepdims=True)
    inv_scale = lax.rsqrt(jnp.mean(centre * centre, axis=-1, keepdims=True) + EPS_NORM)
    return (centre * inv_scale, inv_scale)


def normal_back(grad_unit, unit_rows, inv_scale):
    centred = grad_unit - jnp.mean(grad_unit, axis=-1, keepdims=True)
    return inv_scale * (
        centred - unit_rows * jnp.mean(grad_unit * unit_rows, axis=-1, keepdims=True)
    )


def silu_parts(tensor):
    half = 0.5 * tensor
    return half, jnp.tanh(half)


def silu(tensor):
    half, bend = silu_parts(tensor)
    return half * (1.0 + bend)


def fold_rows(store, base, rows, tensor):
    parts = tensor.shape[1] // LANES
    for part in range(parts):
        store[pl.ds(base * parts + part, rows, stride=parts), :] = tensor[
            :, part * LANES : (part + 1) * LANES
        ]


def unfold_rows(store, base, rows, parts):
    return jnp.concatenate(
        [store[pl.ds(base * parts + part, rows, stride=parts), :] for part in range(parts)],
        axis=1,
    )


def forward_kernel(parts, has_next, *refs):
    if has_next:
        (slots, before, middle, after, low, wide, weights, gains, head) = refs[:9]
        (sent, update, update_low, kept, aggregate) = refs[9:14]
        window, picked, hidden, message = refs[14:]
    else:
        (slots, before, middle, after, low, wide, weights, gains) = refs[:8]
        (update_low, kept, aggregate) = refs[8:11]
        window, picked, hidden, message = refs[11:]
    step = pl.program_id(0)
    block_rows = before.shape[0]
    rows, width = low.shape
    fan = kept.shape[0]

    @pl.when(step == 0)
    def _():
        for index, block in enumerate((before, middle, after)):
            fold_rows(window, index * block_rows, block_rows, block[...].astype(WIDE))

    for k in range(fan):

        def pick(trip, carry):
            for lane in range(UNROLL):
                row = trip * UNROLL + lane
                slot = slots[k * block_rows + step * rows + row]
                picked[pl.ds(pl.multiple_of((k * rows + row) * parts, parts), parts), :] = window[
                    pl.ds(pl.multiple_of(slot * parts, parts), parts), :
                ]
            return carry

        lax.fori_loop(0, rows // UNROLL, pick, 0)
    target_low = low[...]
    own_term = product(target_low, weights[1])
    for k in range(fan):
        sender = unfold_rows(picked, k * rows, rows, parts)
        kept[k] = sender.astype(LOW)
        hidden[k * rows : (k + 1) * rows, :] = silu(sender + own_term).astype(LOW)
    message[...] = product(hidden[...], weights[2])
    total = normalize(message[0:rows, :])[0]
    for k in range(1, fan):
        total = total + normalize(message[k * rows : (k + 1) * rows, :])[0]
    total_low = (total * gains[0:1, :]).astype(LOW)
    aggregate[...] = total_low
    node_mix = product(target_low, weights[3]) + product(total_low, weights[4])
    node_out = product(silu(node_mix).astype(LOW), weights[5])
    updated = wide[...].astype(WIDE) + normalize(node_out)[0] * gains[1:2, :]
    updated_low = updated.astype(LOW)
    update_low[...] = updated_low
    if has_next:
        update[...] = updated
        sent[...] = product(updated_low, head[0]).astype(LOW)


def in_hbm(shape, dtype):
    return pltpu.MemorySpace.HBM(shape, dtype)


def on_chip(shape, dtype):
    return pltpu.MemorySpace.VMEM(shape, dtype)


def kept_on_chip(array):
    return pltpu.with_memory_space_constraint(array, pltpu.MemorySpace.VMEM)


def pinned(array):
    return pltpu.with_memory_space_constraint(array, pltpu.MemorySpace.HBM)


def whole(shape):
    zeros = (0,) * len(shape)
    return pl.BlockSpec(shape, lambda step: zeros, pipeline_mode=pl.Buffered(1))


def matrix_spec(first, count, width):
    return pl.BlockSpec(
        (count, width, width), lambda step: (first // count, 0, 0), pipeline_mode=pl.Buffered(1)
    )


def tiled(rows, width):
    return pl.BlockSpec((rows, width), lambda step: (step, 0))


def fanned(fan, rows, width):
    return pl.BlockSpec((fan, rows, width), lambda step: (0, step, 0))


def forward_layer(slots, blocks, target_low, target, weights, next_weights, gains, halo_place):
    block_rows, width = target_low.shape
    fan = slots.shape[0] // block_rows
    parts = width // LANES
    rows = FORWARD_ROWS
    has_next = next_weights is not None
    shape = functools.partial(in_hbm, (block_rows, width))
    fan_shape = functools.partial(in_hbm, (fan, block_rows, width))
    tile = tiled(rows, width)
    in_specs = [pl.BlockSpec(memory_space=pltpu.SMEM)]
    in_specs += [whole((block_rows, width))] * 3 + [tile, tile]
    in_specs += [matrix_spec(weights[1], 6, width), whole(gains.shape)]
    out_specs = [tile, fanned(fan, rows, width), tile]
    out_shape = [shape(LOW), fan_shape(LOW), shape(LOW)]
    operands = [slots, *blocks, target_low, target, weights[0], gains]
    if has_next:
        in_specs += [matrix_spec(next_weights[1], 1, width)]
        operands += [next_weights[0]]
        out_specs = [tile, tile] + out_specs
        out_shape = [shape(LOW), shape(WIDE)] + out_shape
    return pl.pallas_call(
        functools.partial(forward_kernel, parts, has_next),
        grid=(block_rows // rows,),
        in_specs=in_specs,
        out_specs=out_specs,
        out_shape=out_shape,
        scratch_shapes=[
            pltpu.VMEM((3 * block_rows * parts, LANES), WIDE),
            pltpu.VMEM((fan * rows * parts, LANES), WIDE),
            pltpu.VMEM((fan * rows, width), LOW),
            pltpu.VMEM((fan * rows, width), WIDE),
        ],
        compiler_params=pltpu.CompilerParams(vmem_limit_bytes=54 << 20),
        cost_estimate=pl.CostEstimate(
            flops=2 * (fan + 5) * block_rows * width * width,
            transcendentals=(fan + 1) * block_rows * width,
            bytes_accessed=24 * block_rows * width * 2,
        ),
        name="forward_layer",
    )(
        operands[0],
        halo_place(operands[1]),
        pinned(operands[2]),
        halo_place(operands[3]),
        *map(pinned, operands[4:]),
    )


def backward_kernel(parts, mode, *refs):
    refs = list(refs)
    slots = refs.pop(0)
    if mode != "first":
        returned = [refs.pop(0) for _ in range(3)]
        head = refs.pop(0)
    if mode != "second":
        grad_part = refs.pop(0)
    low, kept, aggregate, weights, gains = refs[:5]
    refs = refs[5:]
    if mode != "first":
        sent_grad = refs.pop(0)
        grad_full = refs.pop(0)
    slot_grads = refs[:3]
    (grad_gains, grad_message, edge_hidden, grad_mix, grad_out, grad_own, hidden) = refs[3:10]
    sum_even, sum_odd, spread, stage = refs[10:]
    step = pl.program_id(0)
    rows, width = low.shape
    fan = kept.shape[0]
    block_rows = slot_grads[0].shape[0]

    @pl.when(step == 0)
    def _():
        sum_even[...] = jnp.zeros_like(sum_even)
        sum_odd[...] = jnp.zeros_like(sum_odd)
        grad_gains[...] = jnp.zeros_like(grad_gains)

    if mode == "first":
        grad_new = grad_part[...]
    else:
        sent_low = (
            returned[0][...].astype(WIDE)
            + returned[1][...].astype(WIDE)
            + returned[2][...].astype(WIDE)
        ).astype(LOW)
        sent_grad[...] = sent_low
        grad_new = product_right(sent_low, head[0])
        if mode == "third":
            grad_new = grad_part[...] + grad_new
        grad_full[...] = grad_new
    target_low = low[...]
    own_term = product(target_low, weights[1])
    node_mix = product(target_low, weights[3]) + product(aggregate[...], weights[4])
    for k in range(fan):
        edge_hidden[k] = silu(kept[k].astype(WIDE) + own_term).astype(LOW)
    stage[...] = product(edge_hidden[...].reshape(fan * rows, width), weights[2])
    half, bend = silu_parts(node_mix)
    node_hidden = (half * (1.0 + bend)).astype(LOW)
    hidden[...] = node_hidden
    out_unit, out_scale = normalize(product(node_hidden, weights[5]))
    gain_two = jnp.sum(grad_new * out_unit, axis=0, keepdims=True)
    out_low = normal_back(grad_new * gains[1:2, :], out_unit, out_scale).astype(LOW)
    grad_out[...] = out_low
    mix_low = (
        product_right(out_low, weights[5]) * ((0.5 + 0.5 * bend) * (1.0 + half * (1.0 - bend)))
    ).astype(LOW)
    grad_mix[...] = mix_low
    grad_sum = product_right(mix_low, weights[4])
    grad_unit = grad_sum * gains[0:1, :]
    unit_total = None
    for k in range(fan):
        unit_rows, inv_scale = normalize(stage[k * rows : (k + 1) * rows, :])
        unit_total = unit_rows if k == 0 else unit_total + unit_rows
        grad_message[k] = normal_back(grad_unit, unit_rows, inv_scale).astype(LOW)
    stage[...] = product_right(grad_message[...].reshape(fan * rows, width), weights[2])
    own_total = None
    for k in range(fan):
        half, bend = silu_parts(kept[k].astype(WIDE) + own_term)
        grad_pre = stage[k * rows : (k + 1) * rows, :] * (
            (0.5 + 0.5 * bend) * (1.0 + half * (1.0 - bend))
        )
        own_total = grad_pre if k == 0 else own_total + grad_pre
        fold_rows(spread, k * rows, rows, grad_pre)
    gain_one = jnp.sum(grad_sum * unit_total, axis=0, keepdims=True)
    grad_gains[...] += jnp.concatenate([gain_one, gain_two], axis=0)
    grad_own[...] = own_total.astype(LOW)

    for k in range(fan):

        def add(trip, carry):
            for lane in range(UNROLL // 2):
                places, values = [], []
                for store in (sum_even, sum_odd):
                    row = (trip * (UNROLL // 2) + lane) * 2 + len(places)
                    slot = slots[k * block_rows + step * rows + row]
                    place = pl.ds(pl.multiple_of(slot * parts, parts), parts)
                    value = spread[pl.ds(pl.multiple_of((k * rows + row) * parts, parts), parts), :]
                    places.append(place)
                    values.append(store[place, :] + value)
                sum_even[places[0], :] = values[0]
                sum_odd[places[1], :] = values[1]
            return carry

        lax.fori_loop(0, rows // UNROLL, add, 0)

    @pl.when(step == pl.num_programs(0) - 1)
    def _():
        for index in range(3):
            base = index * block_rows
            slot_grads[index][...] = (
                unfold_rows(sum_even, base, block_rows, parts)
                + unfold_rows(sum_odd, base, block_rows, parts)
            ).astype(LOW)


def backward_layer(slots, above, grad_part, stored, weights, gains, first_layer):
    target_low, kept, aggregate = stored
    block_rows, width = target_low.shape
    fan = kept.shape[0]
    parts = width // LANES
    rows = BACKWARD_ROWS
    tile = tiled(rows, width)
    fan_tile = fanned(fan, rows, width)
    in_specs = [pl.BlockSpec(memory_space=pltpu.SMEM)]
    operands = [slots]
    out_specs, out_shape = [], []
    shape = functools.partial(on_chip, (block_rows, width))
    fan_shape = functools.partial(on_chip, (fan, block_rows, width))
    mode = "first" if above is None else ("second" if grad_part is None else "third")
    if above is not None:
        from_before, slot_grad, from_after, head = above
        in_specs += [
            tile,
            tile,
            tile,
            matrix_spec(head[1], 1, width),
        ]
        operands += [from_before, slot_grad, from_after, head[0]]
        out_specs += [tile, tile]
        out_shape += [shape(LOW), shape(WIDE)]
    if grad_part is not None:
        in_specs += [tile]
        operands += [grad_part]
    in_specs += [tile, fan_tile, tile]
    in_specs += [matrix_spec(weights[1], 6, width), whole(gains.shape)]
    operands += [target_low, kept, aggregate, weights[0], gains]
    out_specs += [
        whole((block_rows, width)),
        whole((block_rows, width)),
        whole((block_rows, width)),
        whole((2, width)),
        fan_tile,
        fan_tile,
        tile,
        tile,
        tile,
        tile,
    ]
    out_shape += [
        in_hbm((block_rows, width), LOW),
        in_hbm((block_rows, width), LOW),
        in_hbm((block_rows, width), LOW),
        jax.ShapeDtypeStruct((2, width), WIDE),
        fan_shape(LOW),
        in_hbm((fan, block_rows, width), LOW) if first_layer else fan_shape(LOW),
        shape(LOW),
        shape(LOW),
        shape(LOW),
        shape(LOW),
    ]
    results = pl.pallas_call(
        functools.partial(backward_kernel, parts, mode),
        grid=(block_rows // rows,),
        in_specs=in_specs,
        out_specs=out_specs,
        out_shape=out_shape,
        scratch_shapes=[
            pltpu.VMEM((3 * block_rows * parts, LANES), WIDE),
            pltpu.VMEM((3 * block_rows * parts, LANES), WIDE),
            pltpu.VMEM((fan * rows * parts, LANES), WIDE),
            pltpu.VMEM((fan * rows, width), WIDE),
        ],
        compiler_params=pltpu.CompilerParams(vmem_limit_bytes=38 << 20),
        cost_estimate=pl.CostEstimate(
            flops=2 * (fan + 4) * block_rows * width * width,
            transcendentals=(fan + 1) * block_rows * width,
            bytes_accessed=24 * block_rows * width * 2,
        ),
        name="backward_layer",
    )(operands[0], *map(pinned, operands[1:]))
    if above is None:
        return (None, grad_part, *results)
    return tuple(results)


def deal(self_id, sums, outs):
    keep, send = outs
    share = keep.shape[1] // sums.shape[0]

    def move(node, carry):
        for core, out in enumerate((keep, send)):
            place = pl.multiple_of(((2 * node + core) ^ self_id[0]) * share, share)
            for index in range(sums.shape[0]):
                out[node, index * share : (index + 1) * share, :] = sums[
                    index, pl.ds(place, share), :
                ].astype(out.dtype)
        return carry

    lax.fori_loop(0, keep.shape[0], move, 0)


def weight_kernel(has_above, needs_target, direct, *refs):
    refs = list(refs)
    if direct:
        self_id = refs.pop(0)
    if has_above:
        source, sent_grad = refs[:2]
        refs = refs[2:]
    else:
        extra = refs.pop(0)
    low, aggregate, edge_hidden, grad_message, grad_mix, grad_out, grad_own, hidden = refs[:8]
    refs = refs[8:]
    if needs_target:
        grad_new, weights = refs[:2]
        grad_part = refs[2]
        refs = refs[3:]
    outs, sums = (refs[:2], refs[2]) if direct else (None, refs[0])
    step = pl.program_id(0)
    fan = edge_hidden.shape[0]

    @pl.when(step == 0)
    def _():
        sums[...] = jnp.zeros_like(sums)
        if not has_above:
            sums[0] = extra[...]

    target_low = low[...]
    mix_low = grad_mix[...]
    own_low = grad_own[...]
    if has_above:
        sums[0] += product_left(source[...], sent_grad[...])
    sums[1] += product_left(target_low, own_low)
    for k in range(fan):
        sums[2] += product_left(edge_hidden[k], grad_message[k])
    sums[3] += product_left(target_low, mix_low)
    sums[4] += product_left(aggregate[...], mix_low)
    sums[5] += product_left(hidden[...], grad_out[...])
    if needs_target:
        grad_part[...] = (
            grad_new[...] + product_right(own_low, weights[1]) + product_right(mix_low, weights[3])
        )
    if direct:

        @pl.when(step == pl.num_programs(0) - 1)
        def _():
            deal(self_id, sums, outs)


def share_outputs(count, width, device_count):
    shape = (device_count // 2, count * (width // device_count), width)
    return (
        [whole(shape)] * 2,
        [on_chip(shape, WIDE), on_chip(shape, SEND)],
    )


def weight_layer(self_id, device_count, above, extra, low, aggregate, back, grad_new, weights):
    block_rows, width = low.shape
    rows = WEIGHT_ROWS
    fan = back[0].shape[0]
    tile = tiled(rows, width)
    fan_tile = fanned(fan, rows, width)
    in_specs, operands = [], []
    direct = self_id is not None
    if direct:
        in_specs += [pl.BlockSpec(memory_space=pltpu.SMEM)]
        operands += [self_id]
    if above is not None:
        in_specs += [tile, tile]
        operands += [pinned(above[0]), kept_on_chip(above[1])]
    else:
        in_specs += [whole((width, width))]
        operands += [extra]
    in_specs += [tile, tile, fan_tile, fan_tile, tile, tile, tile, tile]
    place = pinned if grad_new is None else kept_on_chip
    operands += [pinned(low), pinned(aggregate), place(back[0]), *map(kept_on_chip, back[1:])]
    out_specs, out_shape, scratch = [], [], []
    if grad_new is not None:
        in_specs += [tile, matrix_spec(weights[1], 6, width)]
        operands += [kept_on_chip(grad_new), pinned(weights[0])]
        out_specs += [tile]
        out_shape += [in_hbm((block_rows, width), WIDE)]
    if direct:
        specs, shapes = share_outputs(6, width, device_count)
        out_specs += specs
        out_shape += shapes
        scratch = [pltpu.VMEM((6, width, width), WIDE)]
    else:
        out_specs += [whole((6, width, width))]
        out_shape += [jax.ShapeDtypeStruct((6, width, width), WIDE)]
    results = pl.pallas_call(
        functools.partial(weight_kernel, above is not None, grad_new is not None, direct),
        grid=(block_rows // rows,),
        in_specs=in_specs,
        out_specs=out_specs,
        out_shape=out_shape,
        scratch_shapes=scratch,
        compiler_params=pltpu.CompilerParams(vmem_limit_bytes=30 << 20),
        cost_estimate=pl.CostEstimate(
            flops=2 * (fan + 6) * block_rows * width * width,
            transcendentals=0,
            bytes_accessed=24 * block_rows * width,
        ),
        name="weight_layer",
    )(*operands)
    if grad_new is None:
        return (None, results)
    return (results[0], results[1:])


def place_rows(self_id, pieces, targets, width):
    share = width // (pieces[0].shape[0] * len(pieces))
    for index, piece in enumerate(pieces):
        base = (index // 2) + (index % 2) * 4

        def move(digit, carry, piece=piece, base=base):
            relative = (digit // 2) * 8 + (digit % 2) * 2 + base
            place = pl.multiple_of((relative ^ self_id[0]) * share, share)
            for j, target in enumerate(targets):
                target[pl.ds(place, share), :] = piece[digit, j * share : (j + 1) * share, :]
            return carry

        lax.fori_loop(0, piece.shape[0], move, 0)


def assemble_kernel(pieces_count, *refs):
    matrices = refs[-1]
    targets = [matrices.at[j] for j in range(matrices.shape[0])]
    place_rows(refs[0], refs[1 : 1 + pieces_count], targets, matrices.shape[1])


def assemble(self_id, pieces):
    digits, rows, width = pieces[0].shape
    count = rows * digits * len(pieces) // width
    return pl.pallas_call(
        functools.partial(assemble_kernel, len(pieces)),
        grid=(1,),
        in_specs=[pl.BlockSpec(memory_space=pltpu.SMEM)] + [whole(piece.shape) for piece in pieces],
        out_specs=whole((count, width, width)),
        out_shape=in_hbm((count, width, width), LOW),
        compiler_params=pltpu.CompilerParams(vmem_limit_bytes=20 << 20),
        cost_estimate=pl.CostEstimate(
            flops=0, transcendentals=0, bytes_accessed=4 * count * width * width
        ),
        name="assemble",
    )(self_id, *pieces)


def join_kernel(*refs):
    start = 0
    for part in refs[:-1]:
        refs[-1][start : start + part.shape[0]] = part[...]
        start += part.shape[0]


def join(parts):
    shape = (sum(part.shape[0] for part in parts), *parts[0].shape[1:])
    return pl.pallas_call(
        join_kernel,
        grid=(1,),
        in_specs=[whole(part.shape) for part in parts],
        out_specs=whole(shape),
        out_shape=on_chip(shape, parts[0].dtype),
        compiler_params=pltpu.CompilerParams(vmem_limit_bytes=8 << 20),
        cost_estimate=pl.CostEstimate(
            flops=0, transcendentals=0, bytes_accessed=4 * shape[0] * shape[1] * shape[2]
        ),
        name="join",
    )(*map(kept_on_chip, parts))


def embed_kernel(pieces_count, *refs):
    self_id = refs[0]
    pieces = refs[1 : 1 + pieces_count]
    before, middle, after = refs[1 + pieces_count : 4 + pieces_count]
    weights, latent, latent_low, sent_before, sent_middle, sent_after, table = refs[
        4 + pieces_count :
    ]

    @pl.when(pl.program_id(0) == 0)
    def _():
        targets = [weights.at[j] for j in range(weights.shape[0])] + [table]
        place_rows(self_id, pieces, targets, weights.shape[1])

    for block, sent in ((before, sent_before), (middle, sent_middle), (after, sent_after)):
        wide = product_right(block[...], table[...])
        low = wide.astype(LOW)
        sent[...] = product(low, weights[0]).astype(LOW)
        if block is middle:
            latent[...] = wide
            latent_low[...] = low


def embed(self_id, pieces, blocks):
    block_rows, width = blocks[1].shape
    rows = WEIGHT_ROWS
    tile = tiled(rows, width)
    return pl.pallas_call(
        functools.partial(embed_kernel, len(pieces)),
        grid=(block_rows // rows,),
        in_specs=[pl.BlockSpec(memory_space=pltpu.SMEM)]
        + [whole(piece.shape) for piece in pieces]
        + [tile] * 3,
        out_specs=[whole((7, width, width))] + [tile] * 5,
        out_shape=[
            in_hbm((7, width, width), LOW),
            in_hbm((block_rows, width), WIDE),
            in_hbm((block_rows, width), LOW),
            in_hbm((block_rows, width), LOW),
            in_hbm((block_rows, width), LOW),
            in_hbm((block_rows, width), LOW),
        ],
        scratch_shapes=[pltpu.VMEM((width, width), LOW)],
        compiler_params=pltpu.CompilerParams(vmem_limit_bytes=50 << 20),
        cost_estimate=pl.CostEstimate(
            flops=12 * block_rows * width * width,
            transcendentals=0,
            bytes_accessed=24 * block_rows * width,
        ),
        name="embed",
    )(self_id, *pieces, *blocks)


def tail_kernel(self_id, loss, before, middle, after, latent_low, inputs, grad_grid, head, *refs):
    gains = refs[:-3]
    keep, send, sums = refs[-3:]
    step = pl.program_id(0)
    rows, width = inputs.shape
    share = width // (2 * keep.shape[0])
    gain_count = 2 * len(gains)

    @pl.when(step == 0)
    def _():
        sums[...] = jnp.zeros_like(sums)

    sent_low = (
        before[...].astype(WIDE)
        + middle[...].astype(WIDE)
        + after[...].astype(WIDE)
    ).astype(LOW)
    grad_low = (grad_grid[...] + product_right(sent_low, head[0])).astype(LOW)
    sums[0] += product_left(latent_low[...], sent_low)
    sums[1] += product_left(grad_low, inputs[...])

    @pl.when(step == pl.num_programs(0) - 1)
    def _():
        size = sums.shape[0] * share
        main = [out.at[:, 0:size, :] for out in (keep, send)]
        deal(self_id, sums, main)
        gain_rows = jnp.concatenate([gain[...] for gain in gains], axis=0)
        lane = lax.broadcasted_iota(jnp.int32, gain_rows.shape, 1)

        def move(node, carry):
            for core, out in enumerate((keep, send)):
                device = (2 * node + core) ^ self_id[0]
                turned = pltpu.roll(gain_rows, width - device * share, axis=1)
                out[node, size : size + gain_count, :] = jnp.where(
                    lane == share, loss[0], turned
                ).astype(out.dtype)
            return carry

        lax.fori_loop(0, keep.shape[0], move, 0)


def tail_layer(
    self_id, device_count, loss, from_before, slot_grad, from_after, latent_low, inputs, grad_grid, head, gains
):
    block_rows, width = inputs.shape
    rows = WEIGHT_ROWS
    tile = tiled(rows, width)
    gain_count = 2 * len(gains)
    shape = (device_count // 2, 2 * (width // device_count) + gain_count, width)
    return pl.pallas_call(
        tail_kernel,
        grid=(block_rows // rows,),
        in_specs=[pl.BlockSpec(memory_space=pltpu.SMEM)] * 2
        + [tile] * 6
        + [matrix_spec(head[1], 1, width)]
        + [whole((2, width))] * len(gains),
        out_specs=[whole(shape)] * 2,
        out_shape=[on_chip(shape, WIDE), on_chip(shape, SEND)],
        scratch_shapes=[pltpu.VMEM((2, width, width), WIDE)],
        compiler_params=pltpu.CompilerParams(vmem_limit_bytes=56 << 20),
        cost_estimate=pl.CostEstimate(
            flops=6 * block_rows * width * width,
            transcendentals=0,
            bytes_accessed=24 * block_rows * width,
        ),
        name="tail_layer",
    )(
        self_id,
        loss,
        *map(pinned, (from_before, slot_grad, from_after, latent_low, inputs, grad_grid, head[0])),
        *gains,
    )


def combine_kernel(counts, *refs):
    outs = refs[sum(counts) :]
    first, base = 0, 0
    for count in counts:
        arrived = refs[first : first + count]
        rows = arrived[0].shape[2]
        for digit, out in enumerate(outs):
            total = arrived[0][0, digit].astype(WIDE)
            for part in arrived[1:]:
                total = total + part[0, digit].astype(WIDE)
            out[0, base : base + rows, :] = total.astype(out.dtype)
        first, base = first + count, base + rows


def combine(radix, *groups):
    width = groups[0][0].shape[2]
    rest = groups[0][0].shape[0] // radix
    arrived, specs = [], []
    for group in groups:
        rows = group[0].shape[1]
        arrived += [part.reshape(rest, radix, rows, width) for part in group]
        specs += [pl.BlockSpec((1, radix, rows, width), lambda step: (step, 0, 0, 0))] * len(group)
    rows = sum(group[0].shape[1] for group in groups)
    shape = (rest, rows, width)
    return pl.pallas_call(
        functools.partial(combine_kernel, [len(group) for group in groups]),
        grid=(rest,),
        in_specs=specs,
        out_specs=[pl.BlockSpec((1, rows, width), lambda step: (step, 0, 0))] * radix,
        out_shape=[on_chip(shape, WIDE)] + [on_chip(shape, SEND)] * (radix - 1),
        compiler_params=pltpu.CompilerParams(vmem_limit_bytes=20 << 20),
        cost_estimate=pl.CostEstimate(
            flops=rest * radix * rows * width * 4,
            transcendentals=0,
            bytes_accessed=16 * rest * radix * rows * width,
        ),
        name="combine",
    )(*map(kept_on_chip, arrived))


def swap(cells, count, mask):
    return lax.ppermute(cells, AXES, [(i, i ^ mask) for i in range(count)])


def spread_high(rows, count):
    return [rows] + [swap(rows, count, digit * 8) for digit in range(1, count // 8)]


def home(block, direct):
    return block ^ (((block >> 2) & 1) << 1) if direct else block


def bring(cells, count, step, direct):
    return lax.ppermute(cells, AXES, [(i, home((i + step) % count, direct)) for i in range(count)])


def shift(cells, count, step, direct):
    pairs = [(home(i, direct), home((i + step) % count, direct)) for i in range(count)]
    return lax.ppermute(cells, AXES, pairs)


def fan_out(pieces, count, unit):
    return [pieces[0]] + [
        swap(pieces[digit], count, digit * unit) for digit in range(1, len(pieces))
    ]


def together(first, second):
    joined = lax.optimization_barrier((tuple(first), tuple(second)))
    return list(joined[0]), list(joined[1])


def add_up(arrived):
    total = arrived[0][0]
    for part in arrived[1:]:
        total = total + part[0].astype(WIDE)
    return total


def adamw_update(weight, moment_one, moment_two, gradient, step_value, decay_rate):
    new_one = BETA_ONE * moment_one + (1.0 - BETA_ONE) * gradient
    new_two = BETA_TWO * moment_two + (1.0 - BETA_TWO) * gradient * gradient
    correct_one = 1.0 - jnp.power(BETA_ONE, step_value)
    correct_two = 1.0 - jnp.power(BETA_TWO, step_value)
    direction = new_one / correct_one / (jnp.sqrt(new_two / correct_two) + ADAM_EPS)
    return (new_one, new_two, weight - LEARN_RATE * (direction + decay_rate * weight))


def shards(
    grid_inputs,
    mesh_static,
    targets,
    area_weight,
    valid_rows,
    encoder_lists,
    mesh_lists,
    decoder_lists,
    step_count,
    w_in,
    moment_in,
    square_in,
    w_layers,
    moment_layers,
    square_layers,
    norm_gains,
    moment_gains,
    square_gains,
    w_out,
    moment_out,
    square_out,
):
    row_count = grid_inputs.shape[0]
    layer_total = w_layers.shape[0]
    device_count = lax.axis_size(AXES)
    width = mesh_static.shape[1]
    share = w_layers.shape[2]
    channels, outputs = w_in.shape[0], w_out.shape[1]
    direct = share == 16 and device_count % 8 == 0 and device_count & (device_count - 1) == 0
    slot_lists = [encoder_lists.T.reshape(-1), mesh_lists.T.reshape(-1), decoder_lists.T.reshape(-1)]
    local_rows = jnp.arange(row_count, dtype=jnp.int32)
    weight_rows = area_weight * (local_rows < valid_rows[0]).astype(WIDE)
    if direct:
        self_id = lax.axis_index(AXES).astype(jnp.int32)
        order = jnp.arange(device_count, dtype=jnp.int32) ^ self_id
        self_id = self_id.reshape(1)
        inputs = jnp.pad(grid_inputs, ((0, 0), (0, width - channels)))
        flat_gains = norm_gains.astype(LOW).reshape(1, -1)
        packed = jnp.concatenate(
            [
                w_layers[0].astype(LOW).reshape(-1, width),
                w_layers[1, 0].astype(LOW),
                jnp.pad(w_in.astype(LOW).T, ((0, 0), (0, width - channels))),
                jnp.pad(flat_gains, ((0, 7), (0, width - flat_gains.shape[1]))),
            ],
            axis=0,
        )
        second = jnp.concatenate([w_layers[2, :1], w_layers[1, 1:]], axis=0)
        second = second.astype(LOW).reshape(-1, width)
        rest = jnp.concatenate(
            [
                jnp.pad(w_out.astype(LOW), ((0, 0), (0, width - outputs)))[None],
                w_layers[2, 1:].astype(LOW),
                w_layers[3:].astype(LOW).reshape(-1, share, width),
            ],
            axis=0,
        )
        lists = jnp.concatenate(slot_lists).reshape(-1, LANES)
        goals = jnp.concatenate([targets, weight_rows[:, None]], axis=1)
        goals = jnp.pad(goals, ((0, 0), (0, -goals.shape[1] % LANES)))
        barrier = lax.optimization_barrier
        pairs = ((packed, swap(packed, device_count, 2)), (second, swap(second, device_count, 2)))
        lists = bring(lists, device_count, 0, direct)
        pairs, lists, inputs, mesh_static = barrier((pairs, lists, inputs, mesh_static))
        own = bring(inputs, device_count, 0, direct)
        pair, second_pair = (jnp.stack(rows) for rows in pairs)
        column, own, mesh_static, second_pair = barrier(
            (spread_high(pair, device_count), own, mesh_static, second_pair)
        )
        sides = [shift(own, device_count, 1, direct), shift(own, device_count, -1, direct)]
        mesh_rows = bring(mesh_static, device_count, 0, direct)
        second_column = spread_high(second_pair, device_count)
        plane = join(column)
        second_last = second_column.pop()
        near, sides, mesh_rows, second_column, rest, goals = barrier(
            ((plane, swap(plane, device_count, 4)), sides, mesh_rows, second_column, rest, goals)
        )
        sides = [sides[0], own, sides[1]]
        pieces = [*near, *(swap(piece, device_count, 1) for piece in near)]
        rest = lax.all_gather(rest, AXES, axis=1, tiled=True)
        inputs = sides[1]
        lists = lists.reshape(len(slot_lists), -1)
        slot_lists = [lists[index] for index in range(len(slot_lists))]
        first, grid_latent, grid_start, *blocks = embed(
            self_id, pieces, sides
        )
        first, goals, second_last = barrier((first, goals, second_last))
        second_plane = join([*second_column, second_last])
        second_near = (second_plane, swap(second_plane, device_count, 4))
        goals = bring(goals, device_count, 0, direct)
        targets, weight_rows = goals[:, :outputs], goals[:, outputs]
        weights = [(first, 0), None]
        weights += [(rest, 6 * layer_id) for layer_id in range(layer_total - 2)]
        heads = [(first, 0), (first, 6), None]
        heads += weights[3:]
        table_out = rest[0, :, :outputs]
        gain_rows = jnp.stack(pieces)[:, :, packed.shape[0] - 8, : flat_gains.shape[1]]
        gain_rows = gain_rows.reshape(2, 2, device_count // 8, 2, -1).transpose(2, 1, 3, 0, 4)
        gain_rows = gain_rows.reshape(device_count, -1)[order]
        gains = gain_rows.reshape(device_count, layer_total, 2, share).transpose(1, 2, 0, 3)
        gains = gains.reshape(layer_total, 2, width).astype(WIDE)
    else:
        self_id = None
        table_in = lax.all_gather(w_in.astype(LOW), AXES, axis=1, tiled=True)
        table_out = lax.all_gather(w_out.astype(LOW), AXES, axis=0, tiled=True)
        matrices = lax.all_gather(w_layers.astype(LOW), AXES, axis=2, tiled=True)
        matrices = matrices.reshape(-1, width, width)
        weights = [(matrices, 6 * layer_id) for layer_id in range(layer_total)]
        heads = weights
        gains = lax.all_gather(norm_gains.astype(LOW), AXES, axis=2, tiled=True).astype(WIDE)
        grid_latent = product(grid_inputs, table_in)
        grid_start = grid_latent.astype(LOW)
        sent = product(grid_start, matrices[0]).astype(LOW)
        blocks = (shift(sent, device_count, 1, direct), sent, shift(sent, device_count, -1, direct))
        mesh_rows = mesh_static
    slot_lists = [slot_lists[0]] + [slot_lists[1]] * (layer_total - 2) + [slot_lists[2]]
    target, target_low = mesh_rows, mesh_rows
    stored_list = []
    for layer_id in range(layer_total):
        if direct and layer_id == 1:
            second_near, target = lax.optimization_barrier((second_near, target))
            second_pieces = [*second_near, *(swap(piece, device_count, 1) for piece in second_near)]
            second = assemble(self_id, second_pieces)
            weights[1] = heads[2] = (second, 0)
        last_layer = layer_id == layer_total - 1
        if last_layer:
            source_low = target_low
            target, target_low = grid_latent, grid_start
        else:
            source_low = grid_start if layer_id == 0 else target_low
        results = forward_layer(
            slot_lists[layer_id],
            blocks,
            target_low,
            target,
            weights[layer_id],
            None if last_layer else heads[layer_id + 1],
            gains[layer_id],
            kept_on_chip if layer_id > 0 else pinned,
        )
        if last_layer:
            grid_low, kept, aggregate = results
        else:
            sent, updated, updated_low, kept, aggregate = results
            blocks = (shift(sent, device_count, 1, direct), sent, shift(sent, device_count, -1, direct))
        stored_list.append((source_low, (target_low, kept, aggregate), aggregate))
        if not last_layer:
            target, target_low = updated, updated_low
    prediction = product(grid_low, table_out)
    error_rows = prediction - targets
    loss_scale = 1.0 / (row_count * device_count * prediction.shape[1])
    loss_local = jnp.sum(weight_rows[:, None] * error_rows * error_rows) * loss_scale
    grad_pred = (2.0 * loss_scale * weight_rows[:, None] * error_rows).astype(LOW)
    grad_table_out = product_left(grid_low, grad_pred)
    grad_part = product_right(grad_pred, table_out)
    extra = jnp.pad(grad_table_out, ((0, 0), (0, width - outputs)))
    grad_grid = None
    above, above_source = None, None
    layer_grads = [None] * layer_total
    gain_grads = [None] * layer_total
    in_plane, in_slice = [], []
    for layer_id in reversed(range(layer_total)):
        source_low, stored, aggregate = stored_list[layer_id]
        sent_grad, grad_new, *slot_grads, grad_gain, grad_message, edge_hidden, b0, b1, b2, b3 = backward_layer(
            slot_lists[layer_id], above, grad_part, stored, weights[layer_id], gains[layer_id], layer_id == 0
        )
        far = []
        if in_plane:
            moved = len(in_plane)
            arrived, slot_grads = together(in_plane + in_slice, slot_grads)
            if in_slice:
                layer_grads[layer_id + 2] = add_up(arrived[moved:]).reshape(6, share, width)
            far = list(combine(device_count // 8, arrived[:moved]))
        from_before = shift(slot_grads[2], device_count, 1, direct)
        from_after = shift(slot_grads[0], device_count, -1, direct)
        back = [edge_hidden, grad_message, b0, b1, b2, b3]
        grad_part, sums = weight_layer(
            self_id,
            device_count,
            None if above is None else (above_source, sent_grad),
            extra,
            stored[0],
            aggregate,
            back,
            None if layer_id == 0 else grad_new,
            weights[layer_id],
        )
        gain_grads[layer_id] = grad_gain
        if direct:
            tied = [*sums, *far] if layer_id > 0 else sums
            halo, arrived = together([from_before, from_after], tied)
            keep, send = arrived[:2]
            far = arrived[2:] if layer_id > 0 else far
            in_slice = fan_out(far, device_count, 8) if far else []
            other = swap(send, device_count, 1)
            near = list(combine(4, [keep, other]))
            halo, near = together(halo, near)
            in_plane = fan_out(near, device_count, 2)
            from_before, from_after = halo
        else:
            layer_grads[layer_id] = sums[0]
        if layer_id == layer_total - 1:
            grad_grid, grad_part = grad_part, None
        above = (from_before, slot_grads[1], from_after, heads[layer_id])
        above_source = source_low
    if direct:
        sums = tail_layer(
            self_id,
            device_count,
            loss_local.reshape(1),
            from_before,
            slot_grads[1],
            from_after,
            grid_start,
            inputs,
            grad_grid,
            heads[0],
            gain_grads,
        )
        early, sums = together(in_plane[1:3] + in_slice, sums)
        in_plane = [in_plane[0], *early[:2], in_plane[3]]
        layer_grads[1] = add_up(early[2:]).reshape(6, share, width)
        keep, send = sums
        last_plane = combine(4, [keep, swap(send, device_count, 1)])
        last_plane = fan_out(last_plane, device_count, 2)
        far = combine(device_count // 8, in_plane, last_plane)
        total = add_up(fan_out(far, device_count, 8))
        layer_grads[0] = total[: 6 * share].reshape(6, share, width)
        total = total[6 * share :]
        grad_zero = total[:share]
        grad_in = total[share : 2 * share, :channels].T
        grad_gain_all = total[2 * share :, :share].reshape(layer_total, 2, share)
        loss_value = total[2 * share, share]
        grad_out = layer_grads[-1][0, :, :outputs]
    else:
        loss_value = lax.psum(loss_local, AXES)
        sent_grad = (
            from_before.astype(WIDE) + slot_grads[1].astype(WIDE) + from_after.astype(WIDE)
        ).astype(LOW)
        grad_zero = product_left(above_source, sent_grad)
        grad_grid = grad_grid + product_right(sent_grad, matrices[0])
        grad_table_in = product_left(grid_inputs, grad_grid.astype(LOW))
        grad_in = lax.psum_scatter(grad_table_in, AXES, scatter_dimension=1, tiled=True)
        grad_out = lax.psum_scatter(grad_table_out, AXES, scatter_dimension=0, tiled=True)
        grad_gain_all = lax.psum_scatter(
            jnp.stack(gain_grads), AXES, scatter_dimension=2, tiled=True
        )
    grad_layers = [grad_zero[None]]
    for layer_id in range(layer_total):
        grad_layers += [layer_grads[layer_id][1:]]
        if layer_id < layer_total - 1:
            grad_layers += [layer_grads[layer_id][0:1]]
    grad_layers = jnp.concatenate(grad_layers, axis=0)
    grad_layers = grad_layers.reshape(layer_total, 6, *grad_layers.shape[1:])
    if not direct:
        grad_layers = lax.psum_scatter(grad_layers, AXES, scatter_dimension=2, tiled=True)
    step_value = step_count[0].astype(WIDE)
    one_in, two_in, new_in = adamw_update(
        w_in, moment_in, square_in, grad_in, step_value, DECAY_RATE
    )
    one_layers, two_layers, new_layers = adamw_update(
        w_layers, moment_layers, square_layers, grad_layers, step_value, DECAY_RATE
    )
    one_gains, two_gains, new_gains = adamw_update(
        norm_gains, moment_gains, square_gains, grad_gain_all, step_value, 0.0
    )
    one_out, two_out, new_out = adamw_update(
        w_out, moment_out, square_out, grad_out, step_value, DECAY_RATE
    )
    return (
        loss_value,
        one_in,
        two_in,
        new_in,
        one_layers,
        two_layers,
        new_layers,
        one_gains,
        two_gains,
        new_gains,
        one_out,
        two_out,
        new_out,
    )


def solution(mesh):
    rows = P(AXES, None)
    layers = P(None, None, AXES, None)
    gains = P(None, None, AXES)
    columns = P(None, AXES)
    in_specs = (rows, rows, rows, P(AXES), P(AXES), rows, rows, rows, P())
    in_specs += (columns,) * 3 + (layers,) * 3 + (gains,) * 3 + (rows,) * 3
    out_specs = (P(),) + (columns,) * 3 + (layers,) * 3 + (gains,) * 3 + (rows,) * 3
    return jax.shard_map(shards, mesh=mesh, in_specs=in_specs, out_specs=out_specs, check_vma=False)
```

```python
import functools

import jax
import jax.numpy as jnp
from jax import lax
from jax.experimental import pallas as pl
from jax.experimental.pallas import tpu as pltpu
from jax.sharding import PartitionSpec as P

EPS_NORM = 1e-05
BETA_ONE = 0.5
BETA_TWO = 0.5
ADAM_EPS = 1e-08
LEARN_RATE = 0.04
DECAY_RATE = 0.1

AXES = ("nodes", "shard")
LANES = 128
FORWARD_ROWS = 256
BACKWARD_ROWS = 256
WEIGHT_ROWS = 256
UNROLL = 256
LOW = jnp.bfloat16
WIDE = jnp.float32
SEND = jnp.bfloat16


def product(left, right):
    return jnp.dot(left, right, preferred_element_type=WIDE)


def product_left(left, right):
    return lax.dot_general(left, right, (((0,), (0,)), ((), ())), preferred_element_type=WIDE)


def product_right(left, right):
    return lax.dot_general(left, right, (((1,), (1,)), ((), ())), preferred_element_type=WIDE)


def normalize(tensor):
    centre = tensor - jnp.mean(tensor, axis=-1, keepdims=True)
    inv_scale = lax.rsqrt(jnp.mean(centre * centre, axis=-1, keepdims=True) + EPS_NORM)
    return (centre * inv_scale, inv_scale)


def normal_back(grad_unit, unit_rows, inv_scale):
    centred = grad_unit - jnp.mean(grad_unit, axis=-1, keepdims=True)
    return inv_scale * (
        centred - unit_rows * jnp.mean(grad_unit * unit_rows, axis=-1, keepdims=True)
    )


def silu_parts(tensor):
    half = 0.5 * tensor
    return half, jnp.tanh(half)


def silu(tensor):
    half, bend = silu_parts(tensor)
    return half * (1.0 + bend)


def fold_rows(store, base, rows, tensor):
    parts = tensor.shape[1] // LANES
    for part in range(parts):
        store[pl.ds(base * parts + part, rows, stride=parts), :] = tensor[
            :, part * LANES : (part + 1) * LANES
        ]


def unfold_rows(store, base, rows, parts):
    return jnp.concatenate(
        [store[pl.ds(base * parts + part, rows, stride=parts), :] for part in range(parts)],
        axis=1,
    )


def forward_kernel(parts, has_next, *refs):
    if has_next:
        (slots, before, middle, after, low, wide, weights, gains, head) = refs[:9]
        (sent, update, update_low, kept, aggregate) = refs[9:14]
        window, picked, hidden, message = refs[14:]
    else:
        (slots, before, middle, after, low, wide, weights, gains) = refs[:8]
        (update_low, kept, aggregate) = refs[8:11]
        window, picked, hidden, message = refs[11:]
    step = pl.program_id(0)
    block_rows = before.shape[0]
    rows, width = low.shape
    fan = kept.shape[0]

    @pl.when(step == 0)
    def _():
        for index, block in enumerate((before, middle, after)):
            fold_rows(window, index * block_rows, block_rows, block[...].astype(WIDE))

    for k in range(fan):

        def pick(trip, carry):
            for lane in range(UNROLL):
                row = trip * UNROLL + lane
                slot = slots[k * block_rows + step * rows + row]
                picked[pl.ds(pl.multiple_of((k * rows + row) * parts, parts), parts), :] = window[
                    pl.ds(pl.multiple_of(slot * parts, parts), parts), :
                ]
            return carry

        lax.fori_loop(0, rows // UNROLL, pick, 0)
    target_low = low[...]
    own_term = product(target_low, weights[1])
    for k in range(fan):
        sender = unfold_rows(picked, k * rows, rows, parts)
        kept[k] = sender.astype(LOW)
        hidden[k * rows : (k + 1) * rows, :] = silu(sender + own_term).astype(LOW)
    message[...] = product(hidden[...], weights[2])
    total = normalize(message[0:rows, :])[0]
    for k in range(1, fan):
        total = total + normalize(message[k * rows : (k + 1) * rows, :])[0]
    total_low = (total * gains[0:1, :]).astype(LOW)
    aggregate[...] = total_low
    node_mix = product(target_low, weights[3]) + product(total_low, weights[4])
    node_out = product(silu(node_mix).astype(LOW), weights[5])
    updated = wide[...].astype(WIDE) + normalize(node_out)[0] * gains[1:2, :]
    updated_low = updated.astype(LOW)
    update_low[...] = updated_low
    if has_next:
        update[...] = updated
        sent[...] = product(updated_low, head[0]).astype(LOW)


def in_hbm(shape, dtype):
    return pltpu.MemorySpace.HBM(shape, dtype)


def on_chip(shape, dtype):
    return pltpu.MemorySpace.VMEM(shape, dtype)


def kept_on_chip(array):
    return pltpu.with_memory_space_constraint(array, pltpu.MemorySpace.VMEM)


def pinned(array):
    return pltpu.with_memory_space_constraint(array, pltpu.MemorySpace.HBM)


def whole(shape):
    zeros = (0,) * len(shape)
    return pl.BlockSpec(shape, lambda step: zeros, pipeline_mode=pl.Buffered(1))


def matrix_spec(first, count, width):
    return pl.BlockSpec(
        (count, width, width), lambda step: (first // count, 0, 0), pipeline_mode=pl.Buffered(1)
    )


def tiled(rows, width):
    return pl.BlockSpec((rows, width), lambda step: (step, 0))


def fanned(fan, rows, width):
    return pl.BlockSpec((fan, rows, width), lambda step: (0, step, 0))


def forward_layer(slots, blocks, target_low, target, weights, next_weights, gains, halo_place):
    block_rows, width = target_low.shape
    fan = slots.shape[0] // block_rows
    parts = width // LANES
    rows = FORWARD_ROWS
    has_next = next_weights is not None
    shape = functools.partial(in_hbm, (block_rows, width))
    fan_shape = functools.partial(in_hbm, (fan, block_rows, width))
    tile = tiled(rows, width)
    in_specs = [pl.BlockSpec(memory_space=pltpu.SMEM)]
    in_specs += [whole((block_rows, width))] * 3 + [tile, tile]
    in_specs += [matrix_spec(weights[1], 6, width), whole(gains.shape)]
    out_specs = [tile, fanned(fan, rows, width), tile]
    out_shape = [shape(LOW), fan_shape(LOW), shape(LOW)]
    operands = [slots, *blocks, target_low, target, weights[0], gains]
    if has_next:
        in_specs += [matrix_spec(next_weights[1], 1, width)]
        operands += [next_weights[0]]
        out_specs = [tile, tile] + out_specs
        out_shape = [shape(LOW), shape(WIDE)] + out_shape
    return pl.pallas_call(
        functools.partial(forward_kernel, parts, has_next),
        grid=(block_rows // rows,),
        in_specs=in_specs,
        out_specs=out_specs,
        out_shape=out_shape,
        scratch_shapes=[
            pltpu.VMEM((3 * block_rows * parts, LANES), WIDE),
            pltpu.VMEM((fan * rows * parts, LANES), WIDE),
            pltpu.VMEM((fan * rows, width), LOW),
            pltpu.VMEM((fan * rows, width), WIDE),
        ],
        compiler_params=pltpu.CompilerParams(vmem_limit_bytes=54 << 20),
        cost_estimate=pl.CostEstimate(
            flops=2 * (fan + 5) * block_rows * width * width,
            transcendentals=(fan + 1) * block_rows * width,
            bytes_accessed=24 * block_rows * width * 2,
        ),
        name="forward_layer",
    )(
        operands[0],
        halo_place(operands[1]),
        pinned(operands[2]),
        halo_place(operands[3]),
        *map(pinned, operands[4:]),
    )


def backward_kernel(parts, mode, *refs):
    refs = list(refs)
    slots = refs.pop(0)
    if mode != "first":
        returned = [refs.pop(0) for _ in range(3)]
        head = refs.pop(0)
    if mode != "second":
        grad_part = refs.pop(0)
    low, kept, aggregate, weights, gains = refs[:5]
    refs = refs[5:]
    if mode != "first":
        sent_grad = refs.pop(0)
        grad_full = refs.pop(0)
    slot_grads = refs[:3]
    (grad_gains, grad_message, edge_hidden, grad_mix, grad_out, grad_own, hidden) = refs[3:10]
    sum_even, sum_odd, spread, stage = refs[10:]
    step = pl.program_id(0)
    rows, width = low.shape
    fan = kept.shape[0]
    block_rows = slot_grads[0].shape[0]

    @pl.when(step == 0)
    def _():
        sum_even[...] = jnp.zeros_like(sum_even)
        sum_odd[...] = jnp.zeros_like(sum_odd)
        grad_gains[...] = jnp.zeros_like(grad_gains)

    if mode == "first":
        grad_new = grad_part[...]
    else:
        sent_low = (
            returned[0][...].astype(WIDE)
            + returned[1][...].astype(WIDE)
            + returned[2][...].astype(WIDE)
        ).astype(LOW)
        sent_grad[...] = sent_low
        grad_new = product_right(sent_low, head[0])
        if mode == "third":
            grad_new = grad_part[...] + grad_new
        grad_full[...] = grad_new
    target_low = low[...]
    own_term = product(target_low, weights[1])
    node_mix = product(target_low, weights[3]) + product(aggregate[...], weights[4])
    for k in range(fan):
        edge_hidden[k] = silu(kept[k].astype(WIDE) + own_term).astype(LOW)
    stage[...] = product(edge_hidden[...].reshape(fan * rows, width), weights[2])
    half, bend = silu_parts(node_mix)
    node_hidden = (half * (1.0 + bend)).astype(LOW)
    hidden[...] = node_hidden
    out_unit, out_scale = normalize(product(node_hidden, weights[5]))
    gain_two = jnp.sum(grad_new * out_unit, axis=0, keepdims=True)
    out_low = normal_back(grad_new * gains[1:2, :], out_unit, out_scale).astype(LOW)
    grad_out[...] = out_low
    mix_low = (
        product_right(out_low, weights[5]) * ((0.5 + 0.5 * bend) * (1.0 + half * (1.0 - bend)))
    ).astype(LOW)
    grad_mix[...] = mix_low
    grad_sum = product_right(mix_low, weights[4])
    grad_unit = grad_sum * gains[0:1, :]
    unit_total = None
    for k in range(fan):
        unit_rows, inv_scale = normalize(stage[k * rows : (k + 1) * rows, :])
        unit_total = unit_rows if k == 0 else unit_total + unit_rows
        grad_message[k] = normal_back(grad_unit, unit_rows, inv_scale).astype(LOW)
    stage[...] = product_right(grad_message[...].reshape(fan * rows, width), weights[2])
    own_total = None
    for k in range(fan):
        half, bend = silu_parts(kept[k].astype(WIDE) + own_term)
        grad_pre = stage[k * rows : (k + 1) * rows, :] * (
            (0.5 + 0.5 * bend) * (1.0 + half * (1.0 - bend))
        )
        own_total = grad_pre if k == 0 else own_total + grad_pre
        fold_rows(spread, k * rows, rows, grad_pre)
    gain_one = jnp.sum(grad_sum * unit_total, axis=0, keepdims=True)
    grad_gains[...] += jnp.concatenate([gain_one, gain_two], axis=0)
    grad_own[...] = own_total.astype(LOW)

    for k in range(fan):

        def add(trip, carry):
            for lane in range(UNROLL // 2):
                places, values = [], []
                for store in (sum_even, sum_odd):
                    row = (trip * (UNROLL // 2) + lane) * 2 + len(places)
                    slot = slots[k * block_rows + step * rows + row]
                    place = pl.ds(pl.multiple_of(slot * parts, parts), parts)
                    value = spread[pl.ds(pl.multiple_of((k * rows + row) * parts, parts), parts), :]
                    places.append(place)
                    values.append(store[place, :] + value)
                sum_even[places[0], :] = values[0]
                sum_odd[places[1], :] = values[1]
            return carry

        lax.fori_loop(0, rows // UNROLL, add, 0)

    @pl.when(step == pl.num_programs(0) - 1)
    def _():
        for index in range(3):
            base = index * block_rows
            slot_grads[index][...] = (
                unfold_rows(sum_even, base, block_rows, parts)
                + unfold_rows(sum_odd, base, block_rows, parts)
            ).astype(LOW)


def backward_layer(slots, above, grad_part, stored, weights, gains, first_layer):
    target_low, kept, aggregate = stored
    block_rows, width = target_low.shape
    fan = kept.shape[0]
    parts = width // LANES
    rows = BACKWARD_ROWS
    tile = tiled(rows, width)
    fan_tile = fanned(fan, rows, width)
    in_specs = [pl.BlockSpec(memory_space=pltpu.SMEM)]
    operands = [slots]
    out_specs, out_shape = [], []
    shape = functools.partial(on_chip, (block_rows, width))
    fan_shape = functools.partial(on_chip, (fan, block_rows, width))
    mode = "first" if above is None else ("second" if grad_part is None else "third")
    if above is not None:
        from_before, slot_grad, from_after, head = above
        in_specs += [
            tile,
            tile,
            tile,
            matrix_spec(head[1], 1, width),
        ]
        operands += [from_before, slot_grad, from_after, head[0]]
        out_specs += [tile, tile]
        out_shape += [shape(LOW), shape(WIDE)]
    if grad_part is not None:
        in_specs += [tile]
        operands += [grad_part]
    in_specs += [tile, fan_tile, tile]
    in_specs += [matrix_spec(weights[1], 6, width), whole(gains.shape)]
    operands += [target_low, kept, aggregate, weights[0], gains]
    out_specs += [
        whole((block_rows, width)),
        whole((block_rows, width)),
        whole((block_rows, width)),
        whole((2, width)),
        fan_tile,
        fan_tile,
        tile,
        tile,
        tile,
        tile,
    ]
    out_shape += [
        in_hbm((block_rows, width), LOW),
        in_hbm((block_rows, width), LOW),
        in_hbm((block_rows, width), LOW),
        jax.ShapeDtypeStruct((2, width), WIDE),
        fan_shape(LOW),
        in_hbm((fan, block_rows, width), LOW) if first_layer else fan_shape(LOW),
        shape(LOW),
        shape(LOW),
        shape(LOW),
        shape(LOW),
    ]
    results = pl.pallas_call(
        functools.partial(backward_kernel, parts, mode),
        grid=(block_rows // rows,),
        in_specs=in_specs,
        out_specs=out_specs,
        out_shape=out_shape,
        scratch_shapes=[
            pltpu.VMEM((3 * block_rows * parts, LANES), WIDE),
            pltpu.VMEM((3 * block_rows * parts, LANES), WIDE),
            pltpu.VMEM((fan * rows * parts, LANES), WIDE),
            pltpu.VMEM((fan * rows, width), WIDE),
        ],
        compiler_params=pltpu.CompilerParams(vmem_limit_bytes=38 << 20),
        cost_estimate=pl.CostEstimate(
            flops=2 * (fan + 4) * block_rows * width * width,
            transcendentals=(fan + 1) * block_rows * width,
            bytes_accessed=24 * block_rows * width * 2,
        ),
        name="backward_layer",
    )(operands[0], *map(pinned, operands[1:]))
    if above is None:
        return (None, grad_part, *results)
    return tuple(results)


def deal(self_id, sums, outs):
    keep, send = outs
    share = keep.shape[1] // sums.shape[0]

    def move(node, carry):
        for core, out in enumerate((keep, send)):
            place = pl.multiple_of(((2 * node + core) ^ self_id[0]) * share, share)
            for index in range(sums.shape[0]):
                out[node, index * share : (index + 1) * share, :] = sums[
                    index, pl.ds(place, share), :
                ].astype(out.dtype)
        return carry

    lax.fori_loop(0, keep.shape[0], move, 0)


def weight_kernel(has_above, needs_target, direct, *refs):
    refs = list(refs)
    if direct:
        self_id = refs.pop(0)
    if has_above:
        source, sent_grad = refs[:2]
        refs = refs[2:]
    else:
        extra = refs.pop(0)
    low, aggregate, edge_hidden, grad_message, grad_mix, grad_out, grad_own, hidden = refs[:8]
    refs = refs[8:]
    if needs_target:
        grad_new, weights = refs[:2]
        grad_part = refs[2]
        refs = refs[3:]
    outs, sums = (refs[:2], refs[2]) if direct else (None, refs[0])
    step = pl.program_id(0)
    fan = edge_hidden.shape[0]

    @pl.when(step == 0)
    def _():
        sums[...] = jnp.zeros_like(sums)
        if not has_above:
            sums[0] = extra[...]

    target_low = low[...]
    mix_low = grad_mix[...]
    own_low = grad_own[...]
    if has_above:
        sums[0] += product_left(source[...], sent_grad[...])
    sums[1] += product_left(target_low, own_low)
    for k in range(fan):
        sums[2] += product_left(edge_hidden[k], grad_message[k])
    sums[3] += product_left(target_low, mix_low)
    sums[4] += product_left(aggregate[...], mix_low)
    sums[5] += product_left(hidden[...], grad_out[...])
    if needs_target:
        grad_part[...] = (
            grad_new[...] + product_right(own_low, weights[1]) + product_right(mix_low, weights[3])
        )
    if direct:

        @pl.when(step == pl.num_programs(0) - 1)
        def _():
            deal(self_id, sums, outs)


def share_outputs(count, width, device_count):
    shape = (device_count // 2, count * (width // device_count), width)
    return (
        [whole(shape)] * 2,
        [on_chip(shape, WIDE), on_chip(shape, SEND)],
    )


def weight_layer(self_id, device_count, above, extra, low, aggregate, back, grad_new, weights):
    block_rows, width = low.shape
    rows = WEIGHT_ROWS
    fan = back[0].shape[0]
    tile = tiled(rows, width)
    fan_tile = fanned(fan, rows, width)
    in_specs, operands = [], []
    direct = self_id is not None
    if direct:
        in_specs += [pl.BlockSpec(memory_space=pltpu.SMEM)]
        operands += [self_id]
    if above is not None:
        in_specs += [tile, tile]
        operands += [pinned(above[0]), kept_on_chip(above[1])]
    else:
        in_specs += [whole((width, width))]
        operands += [extra]
    in_specs += [tile, tile, fan_tile, fan_tile, tile, tile, tile, tile]
    place = pinned if grad_new is None else kept_on_chip
    operands += [pinned(low), pinned(aggregate), place(back[0]), *map(kept_on_chip, back[1:])]
    out_specs, out_shape, scratch = [], [], []
    if grad_new is not None:
        in_specs += [tile, matrix_spec(weights[1], 6, width)]
        operands += [kept_on_chip(grad_new), pinned(weights[0])]
        out_specs += [tile]
        out_shape += [in_hbm((block_rows, width), WIDE)]
    if direct:
        specs, shapes = share_outputs(6, width, device_count)
        out_specs += specs
        out_shape += shapes
        scratch = [pltpu.VMEM((6, width, width), WIDE)]
    else:
        out_specs += [whole((6, width, width))]
        out_shape += [jax.ShapeDtypeStruct((6, width, width), WIDE)]
    results = pl.pallas_call(
        functools.partial(weight_kernel, above is not None, grad_new is not None, direct),
        grid=(block_rows // rows,),
        in_specs=in_specs,
        out_specs=out_specs,
        out_shape=out_shape,
        scratch_shapes=scratch,
        compiler_params=pltpu.CompilerParams(vmem_limit_bytes=30 << 20),
        cost_estimate=pl.CostEstimate(
            flops=2 * (fan + 6) * block_rows * width * width,
            transcendentals=0,
            bytes_accessed=24 * block_rows * width,
        ),
        name="weight_layer",
    )(*operands)
    if grad_new is None:
        return (None, results)
    return (results[0], results[1:])


def place_rows(self_id, pieces, targets, width):
    share = width // (pieces[0].shape[0] * len(pieces))
    for index, piece in enumerate(pieces):
        base = (index // 2) + (index % 2) * 4

        def move(digit, carry, piece=piece, base=base):
            relative = (digit // 2) * 8 + (digit % 2) * 2 + base
            place = pl.multiple_of((relative ^ self_id[0]) * share, share)
            for j, target in enumerate(targets):
                target[pl.ds(place, share), :] = piece[digit, j * share : (j + 1) * share, :]
            return carry

        lax.fori_loop(0, piece.shape[0], move, 0)


def assemble_kernel(pieces_count, *refs):
    matrices = refs[-1]
    targets = [matrices.at[j] for j in range(matrices.shape[0])]
    place_rows(refs[0], refs[1 : 1 + pieces_count], targets, matrices.shape[1])


def assemble(self_id, pieces):
    digits, rows, width = pieces[0].shape
    count = rows * digits * len(pieces) // width
    return pl.pallas_call(
        functools.partial(assemble_kernel, len(pieces)),
        grid=(1,),
        in_specs=[pl.BlockSpec(memory_space=pltpu.SMEM)] + [whole(piece.shape) for piece in pieces],
        out_specs=whole((count, width, width)),
        out_shape=in_hbm((count, width, width), LOW),
        compiler_params=pltpu.CompilerParams(vmem_limit_bytes=20 << 20),
        cost_estimate=pl.CostEstimate(
            flops=0, transcendentals=0, bytes_accessed=4 * count * width * width
        ),
        name="assemble",
    )(self_id, *pieces)


def join_kernel(*refs):
    start = 0
    for part in refs[:-1]:
        refs[-1][start : start + part.shape[0]] = part[...]
        start += part.shape[0]


def join(parts):
    shape = (sum(part.shape[0] for part in parts), *parts[0].shape[1:])
    return pl.pallas_call(
        join_kernel,
        grid=(1,),
        in_specs=[whole(part.shape) for part in parts],
        out_specs=whole(shape),
        out_shape=on_chip(shape, parts[0].dtype),
        compiler_params=pltpu.CompilerParams(vmem_limit_bytes=8 << 20),
        cost_estimate=pl.CostEstimate(
            flops=0, transcendentals=0, bytes_accessed=4 * shape[0] * shape[1] * shape[2]
        ),
        name="join",
    )(*map(kept_on_chip, parts))


def embed_kernel(pieces_count, *refs):
    self_id = refs[0]
    pieces = refs[1 : 1 + pieces_count]
    before, middle, after = refs[1 + pieces_count : 4 + pieces_count]
    weights, latent, latent_low, sent_before, sent_middle, sent_after, table = refs[
        4 + pieces_count :
    ]

    @pl.when(pl.program_id(0) == 0)
    def _():
        targets = [weights.at[j] for j in range(weights.shape[0])] + [table]
        place_rows(self_id, pieces, targets, weights.shape[1])

    for block, sent in ((before, sent_before), (middle, sent_middle), (after, sent_after)):
        wide = product_right(block[...], table[...])
        low = wide.astype(LOW)
        sent[...] = product(low, weights[0]).astype(LOW)
        if block is middle:
            latent[...] = wide
            latent_low[...] = low


def embed(self_id, pieces, blocks):
    block_rows, width = blocks[1].shape
    rows = WEIGHT_ROWS
    tile = tiled(rows, width)
    return pl.pallas_call(
        functools.partial(embed_kernel, len(pieces)),
        grid=(block_rows // rows,),
        in_specs=[pl.BlockSpec(memory_space=pltpu.SMEM)]
        + [whole(piece.shape) for piece in pieces]
        + [tile] * 3,
        out_specs=[whole((7, width, width))] + [tile] * 5,
        out_shape=[
            in_hbm((7, width, width), LOW),
            in_hbm((block_rows, width), WIDE),
            in_hbm((block_rows, width), LOW),
            in_hbm((block_rows, width), LOW),
            in_hbm((block_rows, width), LOW),
            in_hbm((block_rows, width), LOW),
        ],
        scratch_shapes=[pltpu.VMEM((width, width), LOW)],
        compiler_params=pltpu.CompilerParams(vmem_limit_bytes=50 << 20),
        cost_estimate=pl.CostEstimate(
            flops=12 * block_rows * width * width,
            transcendentals=0,
            bytes_accessed=24 * block_rows * width,
        ),
        name="embed",
    )(self_id, *pieces, *blocks)


def tail_kernel(self_id, loss, before, middle, after, latent_low, inputs, grad_grid, head, *refs):
    gains = refs[:-3]
    keep, send, sums = refs[-3:]
    step = pl.program_id(0)
    rows, width = inputs.shape
    share = width // (2 * keep.shape[0])
    gain_count = 2 * len(gains)

    @pl.when(step == 0)
    def _():
        sums[...] = jnp.zeros_like(sums)

    sent_low = (
        before[...].astype(WIDE)
        + middle[...].astype(WIDE)
        + after[...].astype(WIDE)
    ).astype(LOW)
    grad_low = (grad_grid[...] + product_right(sent_low, head[0])).astype(LOW)
    sums[0] += product_left(latent_low[...], sent_low)
    sums[1] += product_left(grad_low, inputs[...])

    @pl.when(step == pl.num_programs(0) - 1)
    def _():
        size = sums.shape[0] * share
        main = [out.at[:, 0:size, :] for out in (keep, send)]
        deal(self_id, sums, main)
        gain_rows = jnp.concatenate([gain[...] for gain in gains], axis=0)
        lane = lax.broadcasted_iota(jnp.int32, gain_rows.shape, 1)

        def move(node, carry):
            for core, out in enumerate((keep, send)):
                device = (2 * node + core) ^ self_id[0]
                turned = pltpu.roll(gain_rows, width - device * share, axis=1)
                out[node, size : size + gain_count, :] = jnp.where(
                    lane == share, loss[0], turned
                ).astype(out.dtype)
            return carry

        lax.fori_loop(0, keep.shape[0], move, 0)


def tail_layer(
    self_id, device_count, loss, from_before, slot_grad, from_after, latent_low, inputs, grad_grid, head, gains
):
    block_rows, width = inputs.shape
    rows = WEIGHT_ROWS
    tile = tiled(rows, width)
    gain_count = 2 * len(gains)
    shape = (device_count // 2, 2 * (width // device_count) + gain_count, width)
    return pl.pallas_call(
        tail_kernel,
        grid=(block_rows // rows,),
        in_specs=[pl.BlockSpec(memory_space=pltpu.SMEM)] * 2
        + [tile] * 6
        + [matrix_spec(head[1], 1, width)]
        + [whole((2, width))] * len(gains),
        out_specs=[whole(shape)] * 2,
        out_shape=[on_chip(shape, WIDE), on_chip(shape, SEND)],
        scratch_shapes=[pltpu.VMEM((2, width, width), WIDE)],
        compiler_params=pltpu.CompilerParams(vmem_limit_bytes=56 << 20),
        cost_estimate=pl.CostEstimate(
            flops=6 * block_rows * width * width,
            transcendentals=0,
            bytes_accessed=24 * block_rows * width,
        ),
        name="tail_layer",
    )(
        self_id,
        loss,
        *map(pinned, (from_before, slot_grad, from_after, latent_low, inputs, grad_grid, head[0])),
        *gains,
    )


def combine_kernel(counts, *refs):
    outs = refs[sum(counts) :]
    first, base = 0, 0
    for count in counts:
        arrived = refs[first : first + count]
        rows = arrived[0].shape[2]
        for digit, out in enumerate(outs):
            total = arrived[0][0, digit].astype(WIDE)
            for part in arrived[1:]:
                total = total + part[0, digit].astype(WIDE)
            out[0, base : base + rows, :] = total.astype(out.dtype)
        first, base = first + count, base + rows


def combine(radix, *groups):
    width = groups[0][0].shape[2]
    rest = groups[0][0].shape[0] // radix
    arrived, specs = [], []
    for group in groups:
        rows = group[0].shape[1]
        arrived += [part.reshape(rest, radix, rows, width) for part in group]
        specs += [pl.BlockSpec((1, radix, rows, width), lambda step: (step, 0, 0, 0))] * len(group)
    rows = sum(group[0].shape[1] for group in groups)
    shape = (rest, rows, width)
    return pl.pallas_call(
        functools.partial(combine_kernel, [len(group) for group in groups]),
        grid=(rest,),
        in_specs=specs,
        out_specs=[pl.BlockSpec((1, rows, width), lambda step: (step, 0, 0))] * radix,
        out_shape=[on_chip(shape, WIDE)] + [on_chip(shape, SEND)] * (radix - 1),
        compiler_params=pltpu.CompilerParams(vmem_limit_bytes=20 << 20),
        cost_estimate=pl.CostEstimate(
            flops=rest * radix * rows * width * 4,
            transcendentals=0,
            bytes_accessed=16 * rest * radix * rows * width,
        ),
        name="combine",
    )(*map(kept_on_chip, arrived))


def swap(cells, count, mask):
    return lax.ppermute(cells, AXES, [(i, i ^ mask) for i in range(count)])


def spread_high(rows, count):
    return [rows] + [swap(rows, count, digit * 8) for digit in range(1, count // 8)]


def home(block, direct):
    return block ^ (((block >> 2) & 1) << 1) if direct else block


def bring(cells, count, step, direct):
    return lax.ppermute(cells, AXES, [(i, home((i + step) % count, direct)) for i in range(count)])


def shift(cells, count, step, direct):
    pairs = [(home(i, direct), home((i + step) % count, direct)) for i in range(count)]
    return lax.ppermute(cells, AXES, pairs)


def fan_out(pieces, count, unit):
    return [pieces[0]] + [
        swap(pieces[digit], count, digit * unit) for digit in range(1, len(pieces))
    ]


def together(first, second):
    joined = lax.optimization_barrier((tuple(first), tuple(second)))
    return list(joined[0]), list(joined[1])


def add_up(arrived):
    total = arrived[0][0]
    for part in arrived[1:]:
        total = total + part[0].astype(WIDE)
    return total


def adamw_update(weight, moment_one, moment_two, gradient, step_value, decay_rate):
    new_one = BETA_ONE * moment_one + (1.0 - BETA_ONE) * gradient
    new_two = BETA_TWO * moment_two + (1.0 - BETA_TWO) * gradient * gradient
    correct_one = 1.0 - jnp.power(BETA_ONE, step_value)
    correct_two = 1.0 - jnp.power(BETA_TWO, step_value)
    direction = new_one / correct_one / (jnp.sqrt(new_two / correct_two) + ADAM_EPS)
    return (new_one, new_two, weight - LEARN_RATE * (direction + decay_rate * weight))


def shards(
    grid_inputs,
    mesh_static,
    targets,
    area_weight,
    valid_rows,
    encoder_lists,
    mesh_lists,
    decoder_lists,
    step_count,
    w_in,
    moment_in,
    square_in,
    w_layers,
    moment_layers,
    square_layers,
    norm_gains,
    moment_gains,
    square_gains,
    w_out,
    moment_out,
    square_out,
):
    row_count = grid_inputs.shape[0]
    layer_total = w_layers.shape[0]
    device_count = lax.axis_size(AXES)
    width = mesh_static.shape[1]
    share = w_layers.shape[2]
    channels, outputs = w_in.shape[0], w_out.shape[1]
    direct = share == 16 and device_count % 8 == 0 and device_count & (device_count - 1) == 0
    slot_lists = [encoder_lists.T.reshape(-1), mesh_lists.T.reshape(-1), decoder_lists.T.reshape(-1)]
    local_rows = jnp.arange(row_count, dtype=jnp.int32)
    weight_rows = area_weight * (local_rows < valid_rows[0]).astype(WIDE)
    if direct:
        self_id = lax.axis_index(AXES).astype(jnp.int32)
        order = jnp.arange(device_count, dtype=jnp.int32) ^ self_id
        self_id = self_id.reshape(1)
        inputs = jnp.pad(grid_inputs, ((0, 0), (0, width - channels)))
        flat_gains = norm_gains.astype(LOW).reshape(1, -1)
        packed = jnp.concatenate(
            [
                w_layers[0].astype(LOW).reshape(-1, width),
                w_layers[1, 0].astype(LOW),
                jnp.pad(w_in.astype(LOW).T, ((0, 0), (0, width - channels))),
                jnp.pad(flat_gains, ((0, 7), (0, width - flat_gains.shape[1]))),
            ],
            axis=0,
        )
        second = jnp.concatenate([w_layers[2, :1], w_layers[1, 1:]], axis=0)
        second = second.astype(LOW).reshape(-1, width)
        rest = jnp.concatenate(
            [
                jnp.pad(w_out.astype(LOW), ((0, 0), (0, width - outputs)))[None],
                w_layers[2, 1:].astype(LOW),
                w_layers[3:].astype(LOW).reshape(-1, share, width),
            ],
            axis=0,
        )
        lists = jnp.concatenate(slot_lists).reshape(-1, LANES)
        goals = jnp.concatenate([targets, weight_rows[:, None]], axis=1)
        goals = jnp.pad(goals, ((0, 0), (0, -goals.shape[1] % LANES)))
        barrier = lax.optimization_barrier
        pairs = ((packed, swap(packed, device_count, 2)), (second, swap(second, device_count, 2)))
        lists = bring(lists, device_count, 0, direct)
        pairs, lists, inputs, mesh_static = barrier((pairs, lists, inputs, mesh_static))
        own = bring(inputs, device_count, 0, direct)
        pair, second_pair = (jnp.stack(rows) for rows in pairs)
        column, own, mesh_static, second_pair = barrier(
            (spread_high(pair, device_count), own, mesh_static, second_pair)
        )
        sides = [shift(own, device_count, 1, direct), shift(own, device_count, -1, direct)]
        mesh_rows = bring(mesh_static, device_count, 0, direct)
        second_column = spread_high(second_pair, device_count)
        plane = join(column)
        second_last = second_column.pop()
        near, sides, mesh_rows, second_column, rest, goals = barrier(
            ((plane, swap(plane, device_count, 4)), sides, mesh_rows, second_column, rest, goals)
        )
        sides = [sides[0], own, sides[1]]
        pieces = [*near, *(swap(piece, device_count, 1) for piece in near)]
        rest = lax.all_gather(rest, AXES, axis=1, tiled=True)
        inputs = sides[1]
        lists = lists.reshape(len(slot_lists), -1)
        slot_lists = [lists[index] for index in range(len(slot_lists))]
        first, grid_latent, grid_start, *blocks = embed(
            self_id, pieces, sides
        )
        first, goals, second_last = barrier((first, goals, second_last))
        second_plane = join([*second_column, second_last])
        second_near = (second_plane, swap(second_plane, device_count, 4))
        goals = bring(goals, device_count, 0, direct)
        targets, weight_rows = goals[:, :outputs], goals[:, outputs]
        weights = [(first, 0), None]
        weights += [(rest, 6 * layer_id) for layer_id in range(layer_total - 2)]
        heads = [(first, 0), (first, 6), None]
        heads += weights[3:]
        table_out = rest[0, :, :outputs]
        gain_rows = jnp.stack(pieces)[:, :, packed.shape[0] - 8, : flat_gains.shape[1]]
        gain_rows = gain_rows.reshape(2, 2, device_count // 8, 2, -1).transpose(2, 1, 3, 0, 4)
        gain_rows = gain_rows.reshape(device_count, -1)[order]
        gains = gain_rows.reshape(device_count, layer_total, 2, share).transpose(1, 2, 0, 3)
        gains = gains.reshape(layer_total, 2, width).astype(WIDE)
    else:
        self_id = None
        table_in = lax.all_gather(w_in.astype(LOW), AXES, axis=1, tiled=True)
        table_out = lax.all_gather(w_out.astype(LOW), AXES, axis=0, tiled=True)
        matrices = lax.all_gather(w_layers.astype(LOW), AXES, axis=2, tiled=True)
        matrices = matrices.reshape(-1, width, width)
        weights = [(matrices, 6 * layer_id) for layer_id in range(layer_total)]
        heads = weights
        gains = lax.all_gather(norm_gains.astype(LOW), AXES, axis=2, tiled=True).astype(WIDE)
        grid_latent = product(grid_inputs, table_in)
        grid_start = grid_latent.astype(LOW)
        sent = product(grid_start, matrices[0]).astype(LOW)
        blocks = (shift(sent, device_count, 1, direct), sent, shift(sent, device_count, -1, direct))
        mesh_rows = mesh_static
    slot_lists = [slot_lists[0]] + [slot_lists[1]] * (layer_total - 2) + [slot_lists[2]]
    target, target_low = mesh_rows, mesh_rows
    stored_list = []
    for layer_id in range(layer_total):
        if direct and layer_id == 1:
            second_near, target = lax.optimization_barrier((second_near, target))
            second_pieces = [*second_near, *(swap(piece, device_count, 1) for piece in second_near)]
            second = assemble(self_id, second_pieces)
            weights[1] = heads[2] = (second, 0)
        last_layer = layer_id == layer_total - 1
        if last_layer:
            source_low = target_low
            target, target_low = grid_latent, grid_start
        else:
            source_low = grid_start if layer_id == 0 else target_low
        results = forward_layer(
            slot_lists[layer_id],
            blocks,
            target_low,
            target,
            weights[layer_id],
            None if last_layer else heads[layer_id + 1],
            gains[layer_id],
            kept_on_chip if layer_id > 0 else pinned,
        )
        if last_layer:
            grid_low, kept, aggregate = results
        else:
            sent, updated, updated_low, kept, aggregate = results
            blocks = (shift(sent, device_count, 1, direct), sent, shift(sent, device_count, -1, direct))
        stored_list.append((source_low, (target_low, kept, aggregate), aggregate))
        if not last_layer:
            target, target_low = updated, updated_low
    prediction = product(grid_low, table_out)
    error_rows = prediction - targets
    loss_scale = 1.0 / (row_count * device_count * prediction.shape[1])
    loss_local = jnp.sum(weight_rows[:, None] * error_rows * error_rows) * loss_scale
    grad_pred = (2.0 * loss_scale * weight_rows[:, None] * error_rows).astype(LOW)
    grad_table_out = product_left(grid_low, grad_pred)
    grad_part = product_right(grad_pred, table_out)
    extra = jnp.pad(grad_table_out, ((0, 0), (0, width - outputs)))
    grad_grid = None
    above, above_source = None, None
    layer_grads = [None] * layer_total
    gain_grads = [None] * layer_total
    in_plane, in_slice, waiting = [], [], []
    for layer_id in reversed(range(layer_total)):
        source_low, stored, aggregate = stored_list[layer_id]
        sent_grad, grad_new, *slot_grads, grad_gain, grad_message, edge_hidden, b0, b1, b2, b3 = backward_layer(
            slot_lists[layer_id], above, grad_part, stored, weights[layer_id], gains[layer_id], layer_id == 0
        )
        far = []
        if in_plane:
            moved = len(in_plane)
            arrived, slot_grads = together(in_plane + in_slice, slot_grads)
            if in_slice:
                total = add_up(arrived[moved:]).reshape(-1, 6, share, width)
                for index in range(total.shape[0]):
                    layer_grads[layer_total - 1 - index] = total[index]
            waiting.append(arrived[:moved])
            if layer_id < layer_total - 2:
                far = list(combine(device_count // 8, *waiting))
                waiting = []
        from_before = shift(slot_grads[2], device_count, 1, direct)
        from_after = shift(slot_grads[0], device_count, -1, direct)
        back = [edge_hidden, grad_message, b0, b1, b2, b3]
        grad_part, sums = weight_layer(
            self_id,
            device_count,
            None if above is None else (above_source, sent_grad),
            extra,
            stored[0],
            aggregate,
            back,
            None if layer_id == 0 else grad_new,
            weights[layer_id],
        )
        gain_grads[layer_id] = grad_gain
        if direct:
            tied = [*sums, *far] if layer_id > 0 else sums
            halo, arrived = together([from_before, from_after], tied)
            keep, send = arrived[:2]
            far = arrived[2:] if layer_id > 0 else far
            in_slice = fan_out(far, device_count, 8) if far else []
            other = swap(send, device_count, 1)
            near = list(combine(4, [keep, other]))
            halo, near = together(halo, near)
            in_plane = fan_out(near, device_count, 2)
            from_before, from_after = halo
        else:
            layer_grads[layer_id] = sums[0]
        if layer_id == layer_total - 1:
            grad_grid, grad_part = grad_part, None
        above = (from_before, slot_grads[1], from_after, heads[layer_id])
        above_source = source_low
    if direct:
        sums = tail_layer(
            self_id,
            device_count,
            loss_local.reshape(1),
            from_before,
            slot_grads[1],
            from_after,
            grid_start,
            inputs,
            grad_grid,
            heads[0],
            gain_grads,
        )
        early, sums = together(in_plane[1:3] + in_slice, sums)
        in_plane = [in_plane[0], *early[:2], in_plane[3]]
        layer_grads[1] = add_up(early[2:]).reshape(6, share, width)
        keep, send = sums
        last_plane = combine(4, [keep, swap(send, device_count, 1)])
        last_plane = fan_out(last_plane, device_count, 2)
        far = combine(device_count // 8, in_plane, last_plane)
        total = add_up(fan_out(far, device_count, 8))
        layer_grads[0] = total[: 6 * share].reshape(6, share, width)
        total = total[6 * share :]
        grad_zero = total[:share]
        grad_in = total[share : 2 * share, :channels].T
        grad_gain_all = total[2 * share :, :share].reshape(layer_total, 2, share)
        loss_value = total[2 * share, share]
        grad_out = layer_grads[-1][0, :, :outputs]
    else:
        loss_value = lax.psum(loss_local, AXES)
        sent_grad = (
            from_before.astype(WIDE) + slot_grads[1].astype(WIDE) + from_after.astype(WIDE)
        ).astype(LOW)
        grad_zero = product_left(above_source, sent_grad)
        grad_grid = grad_grid + product_right(sent_grad, matrices[0])
        grad_table_in = product_left(grid_inputs, grad_grid.astype(LOW))
        grad_in = lax.psum_scatter(grad_table_in, AXES, scatter_dimension=1, tiled=True)
        grad_out = lax.psum_scatter(grad_table_out, AXES, scatter_dimension=0, tiled=True)
        grad_gain_all = lax.psum_scatter(
            jnp.stack(gain_grads), AXES, scatter_dimension=2, tiled=True
        )
    grad_layers = [grad_zero[None]]
    for layer_id in range(layer_total):
        grad_layers += [layer_grads[layer_id][1:]]
        if layer_id < layer_total - 1:
            grad_layers += [layer_grads[layer_id][0:1]]
    grad_layers = jnp.concatenate(grad_layers, axis=0)
    grad_layers = grad_layers.reshape(layer_total, 6, *grad_layers.shape[1:])
    if not direct:
        grad_layers = lax.psum_scatter(grad_layers, AXES, scatter_dimension=2, tiled=True)
    step_value = step_count[0].astype(WIDE)
    one_in, two_in, new_in = adamw_update(
        w_in, moment_in, square_in, grad_in, step_value, DECAY_RATE
    )
    one_layers, two_layers, new_layers = adamw_update(
        w_layers, moment_layers, square_layers, grad_layers, step_value, DECAY_RATE
    )
    one_gains, two_gains, new_gains = adamw_update(
        norm_gains, moment_gains, square_gains, grad_gain_all, step_value, 0.0
    )
    one_out, two_out, new_out = adamw_update(
        w_out, moment_out, square_out, grad_out, step_value, DECAY_RATE
    )
    return (
        loss_value,
        one_in,
        two_in,
        new_in,
        one_layers,
        two_layers,
        new_layers,
        one_gains,
        two_gains,
        new_gains,
        one_out,
        two_out,
        new_out,
    )


def solution(mesh):
    rows = P(AXES, None)
    layers = P(None, None, AXES, None)
    gains = P(None, None, AXES)
    columns = P(None, AXES)
    in_specs = (rows, rows, rows, P(AXES), P(AXES), rows, rows, rows, P())
    in_specs += (columns,) * 3 + (layers,) * 3 + (gains,) * 3 + (rows,) * 3
    out_specs = (P(),) + (columns,) * 3 + (layers,) * 3 + (gains,) * 3 + (rows,) * 3
    return jax.shard_map(shards, mesh=mesh, in_specs=in_specs, out_specs=out_specs, check_vma=False)
```
